32 devices in a mesh: dp: 4 (over z), mp: 8 (over y, x, core).
Axes of the slice: x: 2, y: 2, z: 4, core: 2. Of those that a mesh axis runs over, the one named last changes fastest.
Arguments:
- patches: bfloat16 [32, 256, 1152], P('dp'), may hold values from -6 to 6
- condition: bfloat16 [32, 1152], P('dp'), may hold values from -6 to 6
- lengths: int32 [32], P('dp'), may hold values from 144 to 192, as said below
- keep_order: int32 [32, 256], P('dp'), may hold values from 0 to 255, each once within a row
- cotangent: bfloat16 [32, 192, 1152], P('dp'), may hold values from -6 to 6
- projection_weight: bfloat16 [3, 1152, 1152], P(None, None, 'mp'), may hold values from -0.1875 to 0.1875
- query_value_bias: bfloat16 [2, 1152], P(None, 'mp'), may hold values from -3 to 3
- merge_weight: bfloat16 [1152, 1152], P('mp'), may hold values from -0.75 to 0.75
- merge_output_bias: bfloat16 [1152], replicated, may hold values from -3 to 3
- up_weight: bfloat16 [1152, 4608], P(None, 'mp'), may hold values from -0.1875 to 0.1875
- up_projection_bias: bfloat16 [4608], P('mp'), may hold values from -3 to 3
- down_weight: bfloat16 [4608, 1152], P('mp'), may hold values from -0.09375 to 0.09375
- down_projection_bias: bfloat16 [1152], replicated, may hold values from -3 to 3
- w_modulate: bfloat16 [1152, 6912], P(None, 'mp'), may hold values from -0.1875 to 0.1875
- bias_modulate: bfloat16 [6912], P('mp'), may hold values from -3 to 3
- bias_table: bfloat16 [16, 961], P('mp'), may hold values from -5 to 5
Outputs:
- block_out: bfloat16 [32, 192, 1152], P('dp')
- patch_grad: float32 [32, 256, 1152], P('dp')
- project_grad: float32 [3, 1152, 1152], P(None, None, 'mp')
- project_bias_grad: float32 [2, 1152], P(None, 'mp')
- merge_grad: float32 [1152, 1152], P('mp')
- merge_bias_grad: float32 [1152], replicated
- up_grad: float32 [1152, 4608], P(None, 'mp')
- up_bias_grad: float32 [4608], P('mp')
- down_grad: float32 [4608, 1152], P('mp')
- down_bias_grad: float32 [1152], replicated
- modulate_grad: float32 [1152, 6912], P(None, 'mp')
- modulate_bias_grad: float32 [6912], P('mp')
- table_grad: float32 [16, 961], P('mp')
The draws below stay inside these ranges and needn't reach their ends.
Inputs may be any that keep to these rules, and one draw needn't show every extreme that they name: `lengths`: some sample keeps exactly 192 tokens. Each row holds every patch position once; slot j of sample b holds patch keep_order[b, j] when j < lengths[b].
All inputs are finite; a program needn't handle non-finite values.
Results may differ from the reference program's by a relative error of at most 0.02.
The reference program's roundings to bfloat16 on the way count: a program that leaves them out, or rounds other values in their place, can miss the bound.
Values may be sent and summed in bfloat16 or wider, within the bound.
A program may use at most 256 MiB of HBM per device.

```python
import jax
import jax.numpy as jnp
from jax import lax

D = 1152
HEADS = 16
HD = 72
FF = 4608
GRID = 16
L = 256
KEEP = 192
BATCH = 32
BUCKETS = 961


def draw_lengths(key, part):
    first_key = jax.random.fold_in(key, 11)
    second_key = jax.random.fold_in(key, 12)
    drawn = jax.random.randint(first_key, (BATCH,), 3 * KEEP // 4, KEEP + 1)
    chosen = jax.random.randint(second_key, (), 0, BATCH)
    return jnp.where(jnp.arange(BATCH) == chosen, KEEP, drawn).astype(jnp.int32)


def levels(rng, shape, split, smallest, high):
    def one(axis_at, blocks):
        draws = jax.random.uniform(jax.random.fold_in(jax.random.fold_in(rng, 6), axis_at), (blocks,), jnp.float32, smallest / len(split), high / len(split))
        return jnp.repeat(jnp.exp(draws), shape[axis_at] // blocks).reshape((-1,) + (1,) * (len(shape) - axis_at - 1))

    factor_of = one(*split[0])
    for cut in split[1:]:
        factor_of = factor_of * one(*cut)
    return factor_of


def scatter_about(stream_key, dims, deviation, reach, pieces=(), kind=jnp.bfloat16):
    values = jax.random.normal(stream_key, dims, jnp.float32) * deviation
    if len(pieces) > 0:
        values = levels(stream_key, dims, pieces, -0.22, 0.18) * values
    return jnp.clip(values, min=-reach, max=reach).astype(kind)


def setup_inputs(seed: int = 0) -> dict:
    streams_of = jax.random.split(jax.random.key(seed), 17)
    patches = scatter_about(streams_of[0], (BATCH, L, D), 1.0, 6.0, ((0, 4),))
    condition = scatter_about(streams_of[1], (BATCH, D), 1.0, 6.0, ((0, 4),))
    lengths = draw_lengths(jax.random.fold_in(streams_of[16], 71), 0)
    keep_order = jax.vmap(lambda own: jax.random.permutation(own, L))(jax.random.split(streams_of[3], BATCH)).reshape((BATCH, L)).astype(jnp.int32)
    cotangent = scatter_about(streams_of[4], (BATCH, KEEP, D), 1.0, 6.0, ((0, 4),))
    projection_weight = scatter_about(streams_of[5], (3, D, D), D ** -0.5, 0.1875, ((2, 8),))
    query_value_bias = scatter_about(streams_of[6], (2, D), 0.5, 3.0, ((1, 8),))
    merge_weight = scatter_about(streams_of[7], (D, D), (D // 16) ** -0.5, 0.75, ((0, 8),))
    merge_output_bias = scatter_about(streams_of[8], (D,), 0.5, 3.0)
    up_weight = scatter_about(streams_of[9], (D, FF), D ** -0.5, 0.1875, ((1, 8),))
    up_projection_bias = scatter_about(streams_of[10], (FF,), 0.5, 3.0, ((0, 8),))
    down_weight = scatter_about(streams_of[11], (FF, D), FF ** -0.5, 0.09375, ((0, 8),))
    down_projection_bias = scatter_about(streams_of[12], (D,), 0.5, 3.0)
    w_modulate = scatter_about(streams_of[13], (D, 6 * D), D ** -0.5, 0.1875, ((1, 8),))
    bias_modulate = scatter_about(streams_of[14], (6 * D,), 0.5, 3.0, ((0, 8),))
    bias_table = scatter_about(streams_of[15], (HEADS, BUCKETS), 1.0, 5.0, ((0, 8),))
    return dict(patches=patches, condition=condition, lengths=lengths, keep_order=keep_order, cotangent=cotangent, projection_weight=projection_weight, query_value_bias=query_value_bias, merge_weight=merge_weight, merge_output_bias=merge_output_bias, up_weight=up_weight, up_projection_bias=up_projection_bias, down_weight=down_weight, down_projection_bias=down_projection_bias, w_modulate=w_modulate, bias_modulate=bias_modulate, bias_table=bias_table)


EXACT_PRECISION = lax.Precision.HIGHEST
EPSILON = 1e-06
MASKED = -1000000000.0

@jax.custom_vjp
def low(v):
    return lax.optimization_barrier(v.astype(jnp.bfloat16)).astype(jnp.float32)

@jax.custom_vjp
def reduced_backward(v):
    return v

def low_keep(v):
    return (low(v), None)

def low_pass(kept, grad):
    return (grad,)

def back_keep(v):
    return (v, None)

def back_low(kept, grad):
    return (low(grad),)
low.defvjp(low_keep, low_pass)
reduced_backward.defvjp(back_keep, back_low)

def layer_norm(values):
    centre = lax.optimization_barrier(jnp.mean(values, axis=-1, keepdims=True))
    shifted = values - centre
    spread = lax.optimization_barrier(jnp.mean(shifted * shifted, axis=-1, keepdims=True))
    return shifted * lax.rsqrt(spread + EPSILON)

def block_forward(patches, projection_weight, query_value_bias, merge_weight, merge_output_bias, up_weight, up_projection_bias, down_weight, down_projection_bias, w_modulate, bias_modulate, bias_table, cond_float, row_picker, live_slots, buckets):
    batch_size = patches.shape[0]
    signal = low(jax.nn.silu(cond_float))
    modulation = jnp.dot(signal, w_modulate, precision=EXACT_PRECISION) + bias_modulate
    blocks = [modulation[:, None, column * D:(column + 1) * D] for column in range(6)]
    shift_one, scale_one, gate_one, shift_two, scale_two, gate_two = blocks
    retained_rows = jnp.einsum('fuq,fqt->fut', row_picker, patches, precision=EXACT_PRECISION)
    normed_one = layer_norm(retained_rows)
    attention_entry = low(normed_one * (1.0 + scale_one) + shift_one)
    query_rows = jnp.einsum('ipq,qc->ipc', attention_entry, projection_weight[0], precision=EXACT_PRECISION) + query_value_bias[0]
    every_key = jnp.einsum('ipq,qc->ipc', attention_entry, projection_weight[1], precision=EXACT_PRECISION)
    every_value = jnp.einsum('ipq,qc->ipc', attention_entry, projection_weight[2], precision=EXACT_PRECISION) + query_value_bias[1]
    head_shape = (batch_size, KEEP, HEADS, HD)
    query_rows = low(reduced_backward(query_rows)).reshape(head_shape)
    every_key = low(reduced_backward(every_key)).reshape(head_shape)
    every_value = low(reduced_backward(every_value)).reshape(head_shape)
    logits = reduced_backward(jnp.einsum('bqhe,bkhe->bhqk', query_rows, every_key, precision=EXACT_PRECISION) * HD ** (-0.5))
    pair_bias = jnp.transpose(bias_table[:, buckets], (1, 0, 2, 3))
    scores = jnp.where(live_slots[:, None, None, :] > 0.5, logits + pair_bias, MASKED)
    row_max = lax.optimization_barrier(jnp.max(scores, axis=-1, keepdims=True))
    exponent = jnp.exp(scores - row_max)
    attention_probs = exponent / lax.optimization_barrier(jnp.sum(exponent, axis=-1, keepdims=True))
    attended_values = jnp.einsum('bhqk,bkhe->bqhe', low(attention_probs), every_value, precision=EXACT_PRECISION).reshape(batch_size, KEEP, D)
    attended_values = low(reduced_backward(attended_values))
    attention_result = reduced_backward(jnp.einsum('ipq,qc->ipc', attended_values, merge_weight, precision=EXACT_PRECISION) + merge_output_bias)
    hidden_one = retained_rows + gate_one * attention_result
    normed_two = layer_norm(hidden_one)
    feedforward_entry = low(normed_two * (1.0 + scale_two) + shift_two)
    preactivation_hidden = reduced_backward(jnp.einsum('hou,us->hos', feedforward_entry, up_weight, precision=EXACT_PRECISION) + up_projection_bias)
    activated_hidden = low(jax.nn.gelu(preactivation_hidden, approximate=True))
    feedforward_result = reduced_backward(jnp.einsum('ouz,zh->ouh', activated_hidden, down_weight, precision=EXACT_PRECISION) + down_projection_bias)
    return (hidden_one + gate_two * feedforward_result) * live_slots[:, :, None]

def reference(patches, condition, lengths, keep_order, cotangent, projection_weight, query_value_bias, merge_weight, merge_output_bias, up_weight, up_projection_bias, down_weight, down_projection_bias, w_modulate, bias_modulate, bias_table):
    slot_ids = jnp.arange(KEEP, dtype=jnp.int32)
    live_slots = (slot_ids[None, :] < lengths[:, None]).astype(jnp.float32)
    positions = keep_order[:, :KEEP]
    patch_ids = jnp.arange(GRID * GRID, dtype=jnp.int32)
    row_picker = (positions[:, :, None] == patch_ids[None, None, :]).astype(jnp.float32) * live_slots[:, :, None]
    row_index = positions // GRID
    column_index = positions % GRID
    buckets = ((row_index[:, :, None] - row_index[:, None, :] + GRID - 1) * (2 * GRID - 1) + column_index[:, :, None] - column_index[:, None, :] + GRID - 1).astype(jnp.int32)
    weights = tuple((weight.astype(jnp.float32) for weight in (projection_weight, query_value_bias, merge_weight, merge_output_bias, up_weight, up_projection_bias, down_weight, down_projection_bias, w_modulate, bias_modulate, bias_table)))
    cond_float = condition.astype(jnp.float32)

    def closed_block(patch_float, *params):
        return block_forward(patch_float, *params, cond_float, row_picker, live_slots, buckets)
    block_out, pull_back = jax.vjp(closed_block, patches.astype(jnp.float32), *weights)
    gradients = pull_back(cotangent.astype(jnp.float32))
    return (block_out.astype(jnp.bfloat16), gradients[0], gradients[1], gradients[2], gradients[3], gradients[4], gradients[5], gradients[6], gradients[7], gradients[8], gradients[9], gradients[10], gradients[11])
```

```python
import functools
import math

import jax
import jax.numpy as jnp
import numpy as np
from jax import lax
from jax.experimental import pallas as pl
from jax.experimental.pallas import tpu as pltpu
from jax.sharding import PartitionSpec as P

MESH = pl.DeviceIdType.MESH
F32 = jnp.float32
BF16 = jnp.bfloat16
EPSILON = 1e-06
MASKED = -1000000000.0
GELU_C = math.sqrt(2.0 / math.pi)
GELU_A = 0.044715
VMEM = pl.BlockSpec(memory_space=pltpu.VMEM)
HEAD_PAD = 128


def dot(a, b, ca=1, cb=0):
    return lax.dot_general(a, b, (((ca,), (cb,)), ((), ())), preferred_element_type=F32)


def bit_of(value, k):
    return lax.rem(value // (1 << k), 2)


def flip(value, mask):
    out = value
    k = 0
    while (1 << k) <= mask:
        if mask & (1 << k):
            out = out + (1 << k) * (1 - 2 * bit_of(value, k))
        k += 1
    return out


def xor(a, b, bits):
    out = 0
    for k in range(bits):
        out = out + (1 << k) * lax.rem(bit_of(a, k) + bit_of(b, k), 2)
    return out


class Sizes:
    def __init__(self, mp, samples, slots, width):
        self.mp, self.samples, self.slots, self.width = mp, samples, slots, width
        self.bits = mp.bit_length() - 1
        self.rows = samples * slots
        self.block = self.rows // mp
        self.half = self.block // 2
        self.per = self.block and slots // self.block
        rest = [1 << k for k in range(1, self.bits)]
        self.orders = (rest, rest[::-1])
        self.sends = {}
        count = 0
        for h in range(2):
            live = list(range(0, mp, 2))
            for t, bit in enumerate(self.orders[h]):
                moved = [d for d in live if d & bit]
                live = [d for d in live if not d & bit]
                self.sends[h, t] = [(d, bit, count + i) for i, d in enumerate(moved)]
                count += len(moved)
        self.steps = len(rest)
        self.far = count
        self.near = mp // 2


def my_index():
    return lax.axis_index("dp"), lax.axis_index("mp")


def enter(sz):
    dp, me = my_index()
    barrier = pltpu.get_barrier_semaphore()
    for d in range(1, sz.mp):
        pl.semaphore_signal(barrier, inc=1, device_id=(dp, flip(me, d)), device_id_type=MESH)
    pl.semaphore_wait(barrier, sz.mp - 1)


def rows_of(ref, start, size):
    return ref.at[pl.ds(start, size)]


class Reduce:
    def __init__(self, sz, part, near_buf, far_buf, sems):
        self.sz, self.part, self.near_buf, self.far_buf = sz, part, near_buf, far_buf
        self.near_send, self.near_recv, self.far_send, self.far_recv = sems
        self.dp, self.me = my_index()

    def near_copy(self, pair):
        b = self.sz.block
        return pltpu.make_async_remote_copy(
            src_ref=rows_of(self.part, (2 * pair + 1) * b, b),
            dst_ref=rows_of(self.near_buf, pair * b, b),
            send_sem=self.near_send.at[pair],
            recv_sem=self.near_recv.at[pair],
            device_id=(self.dp, flip(self.me, 1)),
            device_id_type=MESH,
        )

    def far_copy(self, h, d, bit, i):
        b, hb = self.sz.block, self.sz.half
        return pltpu.make_async_remote_copy(
            src_ref=rows_of(self.part, d * b + h * hb, hb),
            dst_ref=rows_of(self.far_buf, i * hb, hb),
            send_sem=self.far_send.at[i],
            recv_sem=self.far_recv.at[i],
            device_id=(self.dp, flip(self.me, bit)),
            device_id_type=MESH,
        )

    def add(self, start, buf, at, size):
        a = self.part[pl.ds(start, size), :].astype(F32) + buf[pl.ds(at, size), :].astype(F32)
        self.part[pl.ds(start, size), :] = a.astype(BF16)

    def near_finish(self):
        b = self.sz.block

        def one(i, carry):
            pair = self.sz.near - 1 - i
            self.near_copy(pair).wait()
            self.add(2 * pair * b, self.near_buf, pair * b, b)
            return carry

        lax.fori_loop(0, self.sz.near, one, 0)

    def far_start(self, t):
        for h in range(2):
            for d, bit, i in self.sz.sends[h, t]:
                self.far_copy(h, d, bit, i).start()

    def far_finish(self, t):
        b, hb = self.sz.block, self.sz.half
        for h in range(2):
            for d, bit, i in self.sz.sends[h, t]:
                self.far_copy(h, d, bit, i).wait()
                if t < self.sz.steps - 1:
                    self.add((d - bit) * b + h * hb, self.far_buf, i * hb, hb)

    def own_sum(self):
        hb = self.sz.half
        out = []
        for h in range(2):
            (_, _, i), = self.sz.sends[h, self.sz.steps - 1]
            out.append(self.part[h * hb : (h + 1) * hb, :].astype(F32) + self.far_buf[i * hb : (i + 1) * hb, :].astype(F32))
        return jnp.concatenate(out, axis=0)


class Gather:
    def __init__(self, sz, out, sems):
        self.sz, self.out = sz, out
        self.near_send, self.near_recv, self.far_send, self.far_recv = sems
        self.dp, self.me = my_index()
        self.plan = {}
        count = 0
        for h in range(2):
            have = [0]
            for t, bit in enumerate(sz.orders[h][::-1]):
                self.plan[h, t] = [(d, bit, count + i) for i, d in enumerate(have)]
                count += len(have)
                have = have + [d | bit for d in have]

    def near_copy(self, d, h):
        b, hb = self.sz.block, self.sz.half
        return pltpu.make_async_remote_copy(
            src_ref=rows_of(self.out, d * b + h * hb, hb),
            dst_ref=rows_of(self.out, (d + 1) * b + h * hb, hb),
            send_sem=self.near_send.at[d + h],
            recv_sem=self.near_recv.at[d + h],
            device_id=(self.dp, flip(self.me, 1)),
            device_id_type=MESH,
        )

    def far_copy(self, h, d, bit, i):
        b, hb = self.sz.block, self.sz.half
        return pltpu.make_async_remote_copy(
            src_ref=rows_of(self.out, d * b + h * hb, hb),
            dst_ref=rows_of(self.out, (d + bit) * b + h * hb, hb),
            send_sem=self.far_send.at[i],
            recv_sem=self.far_recv.at[i],
            device_id=(self.dp, flip(self.me, bit)),
            device_id_type=MESH,
        )

    def start(self):
        for h in range(2):
            for d, bit, i in self.plan[h, 0]:
                self.far_copy(h, d, bit, i).start()
        for h in range(2):
            self.near_copy(0, h).start()

    def step(self, t):
        for h in range(2):
            for d, bit, i in self.plan[h, t]:
                self.far_copy(h, d, bit, i).wait()
            if t + 1 < self.sz.steps:
                for d, bit, i in self.plan[h, t + 1]:
                    self.far_copy(h, d, bit, i).start()
            for d, bit, i in self.plan[h, t]:
                self.near_copy(d + bit, h).start()

    def finish(self):
        for d in range(0, self.sz.mp, 2):
            for h in range(2):
                self.near_copy(d, h).wait()


def reduce_scratch(sz):
    return [
        pltpu.VMEM((sz.near * sz.block, sz.width), BF16),
        pltpu.VMEM((sz.far * sz.half, sz.width), BF16),
        pltpu.SemaphoreType.DMA((sz.near,)),
        pltpu.SemaphoreType.DMA((sz.near,)),
        pltpu.SemaphoreType.DMA((sz.far,)),
        pltpu.SemaphoreType.DMA((sz.far,)),
    ]


def gather_scratch(sz):
    return [
        pltpu.SemaphoreType.DMA((sz.mp,)),
        pltpu.SemaphoreType.DMA((sz.mp,)),
        pltpu.SemaphoreType.DMA((sz.far,)),
        pltpu.SemaphoreType.DMA((sz.far,)),
    ]


def sample_loops(sz, body, send, middle=None):
    if sz.per == 1:
        n = sz.samples // 2

        def odd(i, carry):
            body(2 * i + 1)
            send(i)
            return carry

        def even(i, carry):
            body(2 * (n - 1 - i))
            return carry

        lax.fori_loop(0, n, odd, 0)
        if middle is not None:
            middle()
        lax.fori_loop(0, n, even, 0)
    else:
        pairs = sz.per // 2

        def one(i, carry):
            slot = sz.samples - 1 - i
            body(slot)
            for p in range(pairs):
                send(slot * pairs + p)
            return carry

        lax.fori_loop(0, sz.samples, one, 0)
        if middle is not None:
            middle()


def layer_stats(values):
    centre = jnp.mean(values, axis=-1, keepdims=True)
    shifted = values - centre
    spread = jnp.mean(shifted * shifted, axis=-1, keepdims=True)
    inv_std = lax.rsqrt(spread + EPSILON)
    return shifted * inv_std, inv_std


def layer_back(gradient, normed, inv_std):
    mean_grad = jnp.mean(gradient, axis=-1, keepdims=True)
    mean_mix = jnp.mean(gradient * normed, axis=-1, keepdims=True)
    return inv_std * (gradient - mean_grad - normed * mean_mix)


def picker(pos_ref, s, slots, patches):
    ids = lax.broadcasted_iota(jnp.int32, (slots, patches), 1)
    return (pos_ref[s] == ids).astype(F32).astype(BF16)


def attention_forward_kernel(
    sz, heads, head_size, grid_side, cols,
    patches, condition, w_mod, b_mod, pos_col, pos_row, w_qkv, b_qkv, band, w_merge, b_merge,
    modv, attn_in, qkv, probs, att, normed1_own, inv1_own, res_own, hidden_own, normed2_own, inv2_own, mlp,
    mod_buf, mod_wide, normed, kept_own, bias_full, part, mod_send, mod_recv, *rest,
):
    dp, me = my_index()
    mine = me // sz.per
    sbits = sz.samples.bit_length() - 1
    D, n, L = sz.width, sz.slots, patches.shape[1]
    lanes = heads * HEAD_PAD
    red = Reduce(sz, part, rest[0], rest[1], rest[2:6])
    gat = Gather(sz, mlp, rest[6:10])
    wide = mod_buf.shape[2]

    cond = condition[...].astype(F32)
    signal = (cond / (1.0 + jnp.exp(-cond))).astype(BF16)
    local = dot(signal, w_mod[...]) + b_mod[...]
    mod_buf[me] = jnp.zeros((sz.samples, wide), F32)
    mod_buf[me, :, 0:cols] = local
    enter(sz)

    def mod_copy(d):
        return pltpu.make_async_remote_copy(
            src_ref=mod_buf.at[me],
            dst_ref=mod_buf.at[me],
            send_sem=mod_send.at[d],
            recv_sem=mod_recv.at[d],
            device_id=(dp, flip(me, d)),
            device_id_type=MESH,
        )

    def mod_arrival(d):
        return pltpu.make_async_remote_copy(
            src_ref=mod_buf.at[flip(me, d)],
            dst_ref=mod_buf.at[flip(me, d)],
            send_sem=mod_send.at[d],
            recv_sem=mod_recv.at[d],
            device_id=(dp, flip(me, d)),
            device_id_type=MESH,
        )

    for d in range(1, sz.mp):
        mod_copy(d).start()

    span = band.shape[2]
    for h in range(heads):
        strip = band[h]
        for r in range(grid_side):
            shift = (grid_side - 1 - r) * grid_side
            rolled = pltpu.roll(strip, (span - shift) % span, 1) if shift else strip
            bias_full[h, r * grid_side : (r + 1) * grid_side, :] = rolled[:, :L].astype(BF16)

    def norm_one(slot, carry):
        s = xor(mine, slot, sbits)
        kept = dot(picker(pos_col, s, n, L), patches[s])
        value, inv = layer_stats(kept)
        normed[pl.ds(slot * n, n), :] = value

        @pl.when(slot == 0)
        def _():
            kept_own[...] = kept[: sz.block]
            normed1_own[...] = value[: sz.block]
            inv1_own[...] = inv[: sz.block]

        return carry

    lax.fori_loop(0, sz.samples, norm_one, 0)

    for d in range(1, sz.mp):
        mod_copy(d).wait_send()
        mod_arrival(d).wait_recv()
    mod_wide[...] = jnp.zeros_like(mod_wide)
    for m in range(sz.mp):
        base = m * cols // 128 * 128
        phase = m * cols - base
        piece = mod_buf[m]
        if phase:
            piece = pltpu.roll(piece, phase, 1)
        mod_wide[:, base : base + wide] += piece
    modv[...] = mod_wide[:, : 6 * D]

    factor = head_size ** (-0.5)

    def body(slot):
        s = xor(mine, slot, sbits)
        at = pl.ds(slot * n, n)
        shift = modv[pl.ds(s, 1), 0:D]
        scale = modv[pl.ds(s, 1), D : 2 * D]
        entry = (normed[at, :] * (1.0 + scale) + shift).astype(BF16)
        attn_in[at, :] = entry
        proj = (dot(entry, w_qkv[...]) + b_qkv[...]).astype(BF16)
        qkv[at, :] = proj
        sel = picker(pos_col, s, n, L)
        live = pos_row[s] >= 0
        outs = []
        for h in range(heads):
            q = proj[:, h * HEAD_PAD : (h + 1) * HEAD_PAD]
            k = proj[:, lanes + h * HEAD_PAD : lanes + (h + 1) * HEAD_PAD]
            v = proj[:, 2 * lanes + h * HEAD_PAD : 2 * lanes + (h + 1) * HEAD_PAD]
            bias = dot(dot(sel, bias_full[h]).astype(BF16), sel, 1, 1)
            scores = jnp.where(live, dot(q, k, 1, 1) * factor + bias, MASKED)
            top = jnp.max(scores, axis=-1, keepdims=True)
            e = jnp.exp(scores - top)
            p = e / jnp.sum(e, axis=-1, keepdims=True)
            probs[slot, h] = p
            outs.append(dot(p.astype(BF16), v).astype(BF16))
        joined = jnp.concatenate(outs, axis=1) if heads > 1 else outs[0]
        att[at, :] = joined
        part[at, :] = dot(joined, w_merge[...]).astype(BF16)

    sample_loops(sz, body, lambda pair: red.near_copy(pair).start())
    red.near_finish()
    for t in range(sz.steps):
        red.far_start(t)
        red.far_finish(t)
    result = red.own_sum() + b_merge[...]
    res_own[...] = result
    gate = modv[pl.ds(mine, 1), 2 * D : 3 * D]
    hidden = kept_own[...] + gate * result
    hidden_own[...] = hidden
    value, inv = layer_stats(hidden)
    normed2_own[...] = value
    inv2_own[...] = inv
    shift = modv[pl.ds(mine, 1), 3 * D : 4 * D]
    scale = modv[pl.ds(mine, 1), 4 * D : 5 * D]
    mlp[: sz.block, :] = (value * (1.0 + scale) + shift).astype(BF16)
    gat.start()
    for t in range(sz.steps):
        gat.step(t)
    gat.finish()


def mlp_kernel(
    sz,
    mlp, w_up, b_up, w_down, b_down, cot, pos_col, modv, res_own, hidden_own, normed2_own, inv2_own,
    up_g, down_g, up_bg, down_bg, d_attn, out, dh_own, dmod,
    slope, act, d_mlp, d_pre, part_f, part_b, *rest,
):
    dp, me = my_index()
    mine = me // sz.per
    sbits = sz.samples.bit_length() - 1
    D, n = sz.width, sz.slots
    fwd = Reduce(sz, part_f, rest[0], rest[1], rest[2:6])
    bwd = Reduce(sz, part_b, rest[6], rest[7], rest[8:12])
    gat_d = Gather(sz, d_attn, rest[12:16])
    gat_o = Gather(sz, out, rest[16:20])
    enter(sz)

    def forward(slot):
        at = pl.ds(slot * n, n)
        v = dot(mlp[at, :], w_up[...]) + b_up[...]
        square = v * v
        t = jnp.tanh(GELU_C * (v + GELU_A * v * square))
        active = (0.5 * v * (1.0 + t)).astype(BF16)
        act[at, :] = active
        slope[at, :] = 0.5 * (1.0 + t) + 0.5 * v * (1.0 - t * t) * (GELU_C * (1.0 + 3.0 * GELU_A * square))
        part_f[at, :] = dot(active, w_down[...]).astype(BF16)

    sample_loops(sz, forward, lambda pair: fwd.near_copy(pair).start())
    fwd.near_finish()
    fwd.far_start(0)

    up_bg[...] = jnp.zeros_like(up_bg)
    down_bg[...] = jnp.zeros_like(down_bg)

    def d_out_of(s, rows):
        live = (pos_col[s, 0:rows, :] >= 0).astype(F32)
        return cot[pl.ds(s * n, rows), :].astype(F32) * live

    def backward(slot):
        s = xor(mine, slot, sbits)
        at = pl.ds(slot * n, n)
        gate = modv[pl.ds(s, 1), 5 * D : 6 * D]
        dm = (gate * d_out_of(s, n)).astype(BF16)
        d_mlp[at, :] = dm
        down_bg[...] += jnp.sum(dm.astype(F32), axis=0, keepdims=True)
        dpre = (dot(dm, w_down[...], 1, 1) * slope[at, :]).astype(BF16)
        d_pre[at, :] = dpre
        up_bg[...] += jnp.sum(dpre.astype(F32), axis=0, keepdims=True)
        part_b[at, :] = dot(dpre, w_up[...], 1, 1).astype(BF16)

    def middle():
        for t in range(sz.steps):
            fwd.far_finish(t)
            if t + 1 < sz.steps:
                fwd.far_start(t + 1)

    sample_loops(sz, backward, lambda pair: bwd.near_copy(pair).start(), middle)
    bwd.near_finish()
    bwd.far_start(0)

    tile = D // 3

    def down_tile(i, carry):
        cols = pl.ds(pl.multiple_of(i * tile, 128), tile)
        down_g[:, cols] = dot(act[...], d_mlp[:, cols], 0, 0).astype(BF16)
        return carry

    lax.fori_loop(0, 3, down_tile, 0)
    for t in range(sz.steps):
        bwd.far_finish(t)
        if t + 1 < sz.steps:
            bwd.far_start(t + 1)

    mrow = pl.ds(mine, 1)
    d_out = d_out_of(mine, sz.block)
    d_mlp_in = bwd.own_sum()
    normed2 = normed2_own[...]
    g = d_mlp_in * (1.0 + modv[mrow, 4 * D : 5 * D])
    dh = d_out + layer_back(g, normed2, inv2_own[...])
    dh_own[...] = dh
    d_attn[: sz.block, :] = (modv[mrow, 2 * D : 3 * D] * dh).astype(BF16)
    gat_d.start()

    dmod[0:2, :] = jnp.zeros((2, D), F32)
    dmod[2:3, :] = jnp.sum(dh * res_own[...], axis=0, keepdims=True)
    dmod[3:4, :] = jnp.sum(d_mlp_in, axis=0, keepdims=True)
    dmod[4:5, :] = jnp.sum(d_mlp_in * normed2, axis=0, keepdims=True)
    mlp_out = fwd.own_sum() + b_down[...]
    dmod[5:6, :] = jnp.sum(mlp_out * d_out, axis=0, keepdims=True)
    dmod[6:8, :] = jnp.zeros((2, D), F32)
    live = (pos_col[mine, 0 : sz.block, :] >= 0).astype(F32)
    out[: sz.block, :] = ((hidden_own[...] + modv[mrow, 5 * D : 6 * D] * mlp_out) * live).astype(BF16)

    def up_tile(i, carry):
        cols = pl.ds(pl.multiple_of(i * tile, 128), tile)
        up_g[cols, :] = dot(mlp[:, cols], d_pre[...], 0, 0).astype(BF16)
        return carry

    gat_d.step(0)
    gat_o.start()
    lax.fori_loop(0, 3, up_tile, 0)
    for t in range(1, sz.steps):
        gat_d.step(t)
    for t in range(sz.steps):
        gat_o.step(t)
    gat_d.finish()
    gat_o.finish()


def attention_backward_kernel(
    sz, heads, head_size, grid_side,
    d_attn, attn_in, qkv, probs, att, w_qkv, w_merge, pos_col, modv, normed1_own, inv1_own, dh_own, dmod_in,
    proj_g, proj_bg, merge_g, merge_bg, band_g, d_kept, dmod_all,
    dqkv, part, grid_g, dm_send, dm_recv, *rest,
):
    dp, me = my_index()
    mine = me // sz.per
    sbits = sz.samples.bit_length() - 1
    D, n, L = sz.width, sz.slots, grid_side * grid_side
    lanes = heads * HEAD_PAD
    red = Reduce(sz, part, rest[0], rest[1], rest[2:6])
    gat = Gather(sz, d_kept, rest[6:10])
    factor = head_size ** (-0.5)
    enter(sz)
    merge_bg[...] = jnp.zeros_like(merge_bg)
    proj_bg[...] = jnp.zeros_like(proj_bg)
    grid_g[...] = jnp.zeros_like(grid_g)

    def body(slot):
        s = xor(mine, slot, sbits)
        at = pl.ds(slot * n, n)
        da = d_attn[at, :]
        merge_bg[...] += jnp.sum(da.astype(F32), axis=0, keepdims=True)
        d_att = dot(da, w_merge[...], 1, 1).astype(BF16)
        sel = picker(pos_col, s, n, L)
        dq, dk, dv = [], [], []
        for h in range(heads):
            q = qkv[at, h * HEAD_PAD : (h + 1) * HEAD_PAD]
            k = qkv[at, lanes + h * HEAD_PAD : lanes + (h + 1) * HEAD_PAD]
            v = qkv[at, 2 * lanes + h * HEAD_PAD : 2 * lanes + (h + 1) * HEAD_PAD]
            dh = d_att[:, h * HEAD_PAD : (h + 1) * HEAD_PAD]
            p = probs[slot, h]
            dp_ = dot(dh, v, 1, 1)
            dv.append(dot(p.astype(BF16), dh, 0, 0).astype(BF16))
            ds = p * (dp_ - jnp.sum(p * dp_, axis=-1, keepdims=True))
            dl = ds.astype(BF16)
            dq.append((dot(dl, k) * factor).astype(BF16))
            dk.append((dot(dl, q, 0, 0) * factor).astype(BF16))
            grid_g[h] += dot(sel, dot(dl, sel).astype(BF16), 0, 0)
        joined = jnp.concatenate(dq + dk + dv, axis=1)
        dqkv[at, :] = joined
        proj_bg[...] += jnp.sum(joined.astype(F32), axis=0, keepdims=True)
        part[at, :] = dot(joined, w_qkv[...], 1, 1).astype(BF16)

    sample_loops(sz, body, lambda pair: red.near_copy(pair).start())
    red.near_finish()
    red.far_start(0)

    tile = D // 3

    def proj_tile(i, carry):
        cols = pl.ds(pl.multiple_of(i * tile, 128), tile)
        full = dot(attn_in[:, cols], dqkv[...], 0, 0)
        for c in range(3):
            piece = full[:, c * lanes : c * lanes + HEAD_PAD]
            if heads > 1:
                zero = jnp.zeros((tile, (heads - 1) * HEAD_PAD), F32)
                piece = jnp.concatenate([piece, zero], axis=1)
                for h in range(1, heads):
                    other = full[:, c * lanes + h * HEAD_PAD : c * lanes + (h + 1) * HEAD_PAD]
                    piece = piece + pltpu.roll(jnp.concatenate([other, zero], axis=1), h * head_size, 1)
            proj_g[c, cols, :] = piece[:, : heads * head_size].astype(BF16)
        return carry

    def merge_tile(i, carry):
        cols = pl.ds(pl.multiple_of(i * tile, 128), tile)
        merge_g[:, cols] = dot(att[...], d_attn[:, cols], 0, 0).astype(BF16)
        return carry

    lax.fori_loop(0, 3, proj_tile, 0)
    for t in range(sz.steps):
        red.far_finish(t)
        if t + 1 < sz.steps:
            red.far_start(t + 1)
    d_in = red.own_sum()
    normed1 = normed1_own[...]
    g = d_in * (1.0 + modv[pl.ds(mine, 1), D : 2 * D])
    d_kept[: sz.block, :] = (dh_own[...] + layer_back(g, normed1, inv1_own[...])).astype(BF16)
    gat.start()
    dmod_all[me] = dmod_in[...]
    dmod_all[me, 0:1, :] = jnp.sum(d_in, axis=0, keepdims=True)
    dmod_all[me, 1:2, :] = jnp.sum(d_in * normed1, axis=0, keepdims=True)

    def dm_copy(d, slot):
        return pltpu.make_async_remote_copy(
            src_ref=dmod_all.at[slot],
            dst_ref=dmod_all.at[slot],
            send_sem=dm_send.at[d],
            recv_sem=dm_recv.at[d],
            device_id=(dp, flip(me, d)),
            device_id_type=MESH,
        )

    for d in range(1, sz.mp):
        dm_copy(d, me).start()
    lax.fori_loop(0, 3, merge_tile, 0)
    span = band_g.shape[2]
    for h in range(heads):
        strip = jnp.zeros((grid_side, span), F32)
        for r in range(grid_side):
            shift = (grid_side - 1 - r) * grid_side
            piece = jnp.concatenate(
                [grid_g[h, r * grid_side : (r + 1) * grid_side, :], jnp.zeros((grid_side, span - L), F32)], axis=1
            )
            strip = strip + (pltpu.roll(piece, shift, 1) if shift else piece)
        band_g[h] = strip
    for t in range(sz.steps):
        gat.step(t)
    gat.finish()
    for d in range(1, sz.mp):
        dm_copy(d, me).wait_send()
        dm_copy(d, flip(me, d)).wait_recv()


def scatter_kernel(slot_ref, pos_row, d_kept, out_in, patch_grad, block_out):
    ids = lax.broadcasted_iota(jnp.int32, (patch_grad.shape[1], pos_row.shape[2]), 0)
    sel = (ids == pos_row[0]).astype(F32).astype(BF16)
    patch_grad[0] = dot(sel, d_kept[0])
    block_out[...] = out_in[...]


def body(
    patches,
    condition,
    lengths,
    keep_order,
    cotangent,
    projection_weight,
    query_value_bias,
    merge_weight,
    merge_output_bias,
    up_weight,
    up_projection_bias,
    down_weight,
    down_projection_bias,
    w_modulate,
    bias_modulate,
    bias_table,
):
    samples, L, D = patches.shape
    n = cotangent.shape[1]
    grid_side = math.isqrt(L)
    offsets = 2 * grid_side - 1
    heads = bias_table.shape[0]
    local = projection_weight.shape[2]
    hd = local // heads
    lanes = heads * HEAD_PAD
    F = up_weight.shape[1]
    cols = w_modulate.shape[1]
    mp = lax.axis_size("mp")
    me = lax.axis_index("mp")
    sz = Sizes(mp, samples, n, D)
    rows, block = sz.rows, sz.block

    ids = jnp.arange(n, dtype=jnp.int32)
    pos = jnp.where(ids[None, :] < lengths[:, None], keep_order[:, :n], -1)
    cot = cotangent
    if sz.per > 1:
        part_at = lax.rem(me, sz.per)
        order = (ids // block) ^ part_at
        order = order * block + ids % block
        pos = jnp.take(pos, order, axis=1)
        cot = jnp.take(cot, order, axis=1)
    pos_col = pos[:, :, None]
    pos_row = pos[:, None, :]
    cot = cot.reshape(rows, D)

    def pad_heads(a, axis):
        shape = a.shape[:axis] + (heads, hd) + a.shape[axis + 1 :]
        pads = [(0, 0)] * len(shape)
        pads[axis + 1] = (0, HEAD_PAD - hd)
        return jnp.pad(a.reshape(shape), pads).reshape(a.shape[:axis] + (lanes,) + a.shape[axis + 1 :])

    w_qkv = jnp.concatenate([pad_heads(projection_weight[c], 1) for c in range(3)], axis=1)
    qv = query_value_bias.astype(F32)
    b_qkv = jnp.concatenate([pad_heads(qv[0], 0), jnp.zeros((lanes,), F32), pad_heads(qv[1], 0)])[None, :]
    w_merge = pad_heads(merge_weight, 0)

    table = bias_table.reshape(heads, offsets, offsets)[:, ::-1, :]
    shift = np.arange(grid_side)
    pick = (np.arange(offsets)[:, None, None] == shift[None, :, None] - shift[None, None, :] + grid_side - 1)
    pick = jnp.asarray(pick, dtype=BF16)
    band = jnp.einsum("hab,bxy->hxay", table, pick, preferred_element_type=F32)
    band = band.reshape(heads, grid_side, offsets * grid_side)
    span = -(-offsets * grid_side // 128) * 128
    band = jnp.pad(band, ((0, 0), (0, 0), (0, span - offsets * grid_side)))

    def shape(*dims, dtype=F32):
        return jax.ShapeDtypeStruct(dims, dtype)

    def call(kernel, name, cid, outs, scratch, *args):
        return pl.pallas_call(
            kernel,
            out_shape=outs,
            in_specs=[VMEM] * len(args),
            out_specs=[VMEM] * len(outs),
            scratch_shapes=scratch,
            name=name,
            compiler_params=pltpu.CompilerParams(
                collective_id=cid, has_side_effects=True, vmem_limit_bytes=62 << 20
            ),
        )(*args)

    wide = -(-cols // 128) * 128 + 128
    modw = max(m * cols // 128 * 128 + wide for m in range(mp))
    act_like = functools.partial(shape, dtype=BF16)
    (modv, attn_in, qkv, probs, att, normed1, inv1, res, hidden, normed2, inv2, mlp) = call(
        functools.partial(attention_forward_kernel, sz, heads, hd, grid_side, cols),
        "attention_forward",
        0,
        [
            shape(samples, 6 * D),
            act_like(rows, D),
            act_like(rows, 3 * lanes),
            shape(samples, heads, n, n),
            act_like(rows, lanes),
            shape(block, D),
            shape(block, 1),
            shape(block, D),
            shape(block, D),
            shape(block, D),
            shape(block, 1),
            act_like(rows, D),
        ],
        [
            pltpu.VMEM((mp, samples, wide), F32),
            pltpu.VMEM((samples, modw), F32),
            pltpu.VMEM((rows, D), F32),
            pltpu.VMEM((block, D), F32),
            pltpu.VMEM((heads, L, L), BF16),
            pltpu.VMEM((rows, D), BF16),
            pltpu.SemaphoreType.DMA((mp,)),
            pltpu.SemaphoreType.DMA((mp,)),
        ]
        + reduce_scratch(sz)
        + gather_scratch(sz),
        patches,
        condition,
        w_modulate,
        bias_modulate.astype(F32)[None, :],
        pos_col,
        pos_row,
        w_qkv,
        b_qkv,
        band,
        w_merge,
        merge_output_bias.astype(F32)[None, :],
    )
    up_g, down_g, up_bg, down_bg, d_attn, out, dh, dmod = call(
        functools.partial(mlp_kernel, sz),
        "feed_forward",
        1,
        [
            act_like(D, F),
            act_like(F, D),
            shape(1, F),
            shape(1, D),
            act_like(rows, D),
            act_like(rows, D),
            shape(block, D),
            shape(8, D),
        ],
        [
            pltpu.VMEM((rows, F), F32),
            pltpu.VMEM((rows, F), BF16),
            pltpu.VMEM((rows, D), BF16),
            pltpu.VMEM((rows, F), BF16),
            pltpu.VMEM((rows, D), BF16),
            pltpu.VMEM((rows, D), BF16),
        ]
        + reduce_scratch(sz)
        + reduce_scratch(sz)
        + gather_scratch(sz)
        + gather_scratch(sz),
        mlp,
        up_weight,
        up_projection_bias.astype(F32)[None, :],
        down_weight,
        down_projection_bias.astype(F32)[None, :],
        cot,
        pos_col,
        modv,
        res,
        hidden,
        normed2,
        inv2,
    )
    up_grad, down_grad = lax.psum((up_g, down_g), "dp")
    proj_g, proj_bg, merge_g, merge_bg, band_g, d_kept, dmod_all = call(
        functools.partial(attention_backward_kernel, sz, heads, hd, grid_side),
        "attention_backward",
        2,
        [
            act_like(3, D, local),
            shape(1, 3 * lanes),
            act_like(lanes, D),
            shape(1, D),
            shape(heads, grid_side, span),
            act_like(rows, D),
            shape(mp, 8, D),
        ],
        [
            pltpu.VMEM((rows, 3 * lanes), BF16),
            pltpu.VMEM((rows, D), BF16),
            pltpu.VMEM((heads, L, L), F32),
            pltpu.SemaphoreType.DMA((mp,)),
            pltpu.SemaphoreType.DMA((mp,)),
        ]
        + reduce_scratch(sz)
        + gather_scratch(sz),
        d_attn,
        attn_in,
        qkv,
        probs,
        att,
        w_qkv,
        w_merge,
        pos_col,
        modv,
        normed1,
        inv1,
        dh,
        dmod,
    )
    project_grad, merge_grad = lax.psum(
        (proj_g, merge_g.reshape(heads, HEAD_PAD, D)[:, :hd].reshape(local, D)), "dp"
    )

    slot_of = jnp.arange(samples, dtype=jnp.int32) ^ (me // sz.per)
    own_cols = lax.dynamic_slice_in_dim(
        dmod_all[:, :6].reshape(samples, sz.per, 6 * D).sum(axis=1), me * cols, cols, 1
    )
    cond = condition.astype(F32)
    signal = jax.nn.silu(cond).astype(BF16).astype(F32)
    bias_parts = proj_bg.reshape(3, heads, HEAD_PAD)[:, :, :hd].reshape(3, local)
    smalls = [signal, own_cols, bias_parts, merge_bg, up_bg, down_bg, band_g]
    flat = jnp.concatenate([a.reshape(-1) for a in smalls])
    everyone = lax.all_gather(flat, "dp")
    got, at = [], 0
    for a in smalls:
        got.append(everyone[:, at : at + a.size].reshape((everyone.shape[0],) + a.shape))
        at += a.size
    signal_all = got[0].reshape(-1, D)
    dmod_cols = got[1].reshape(-1, cols)
    modulate_grad = jnp.dot(signal_all.T, dmod_cols, precision=lax.Precision.HIGHEST)
    modulate_bias_grad = jnp.sum(dmod_cols, axis=0)
    proj_bias, merge_bias, up_bias, down_bias, band_sum = [jnp.sum(a, axis=0) for a in got[2:]]
    band_sum = band_sum[:, :, : offsets * grid_side].reshape(heads, grid_side, offsets, grid_side)
    table_grad = jnp.einsum(
        "hxay,bxy->hab", band_sum, pick.astype(F32), precision=lax.Precision.HIGHEST
    )[:, ::-1, :].reshape(heads, offsets * offsets)

    by_sample = lambda s, slot_ref: (slot_ref[s], 0, 0)
    straight = lambda s, slot_ref: (s, 0, 0)
    patch_grad, block_out = pl.pallas_call(
        scatter_kernel,
        out_shape=[shape(samples, L, D), act_like(samples, n, D)],
        grid_spec=pltpu.PrefetchScalarGridSpec(
            num_scalar_prefetch=1,
            grid=(samples,),
            in_specs=[
                pl.BlockSpec((1, 1, n), straight),
                pl.BlockSpec((1, n, D), by_sample),
                pl.BlockSpec((1, n, D), by_sample),
            ],
            out_specs=[pl.BlockSpec((1, L, D), straight), pl.BlockSpec((1, n, D), straight)],
        ),
        name="scatter",
    )(slot_of, pos_row, d_kept.reshape(samples, n, D), out.reshape(samples, n, D))
    if sz.per > 1:
        block_out = jnp.take(block_out, order, axis=1)
    return (
        block_out,
        patch_grad,
        project_grad.astype(F32),
        proj_bias[jnp.array([0, 2])],
        merge_grad.astype(F32),
        merge_bias[0],
        up_grad.astype(F32),
        up_bias[0],
        down_grad.astype(F32),
        down_bias[0],
        modulate_grad,
        modulate_bias_grad,
        table_grad,
    )


def solution(mesh):
    placed = (
        P("dp", None, None),
        P("dp", None),
        P("dp"),
        P("dp", None),
        P("dp", None, None),
        P(None, None, "mp"),
        P(None, "mp"),
        P("mp", None),
        P(),
        P(None, "mp"),
        P("mp"),
        P("mp", None),
        P(),
        P(None, "mp"),
        P("mp"),
        P("mp", None),
    )
    return jax.shard_map(
        body,
        mesh=mesh,
        in_specs=placed,
        out_specs=(
            P("dp", None, None),
            P("dp", None, None),
            P(None, None, "mp"),
            P(None, "mp"),
            P("mp", None),
            P(),
            P(None, "mp"),
            P("mp"),
            P("mp", None),
            P(),
            P(None, "mp"),
            P("mp"),
            P("mp", None),
        ),
        check_vma=False,
    )
```

```python
import functools
import math
from types import SimpleNamespace

import jax
import jax.numpy as jnp
import numpy as np
from jax import lax
from jax.experimental import pallas as pl
from jax.experimental.pallas import tpu as pltpu
from jax.sharding import PartitionSpec as P

MESH = pl.DeviceIdType.MESH
F32 = jnp.float32
BF16 = jnp.bfloat16
EPSILON = 1e-06
MASKED = -1000000000.0
GELU_C = math.sqrt(2.0 / math.pi)
GELU_A = 0.044715
VMEM = pl.BlockSpec(memory_space=pltpu.VMEM)
HEAD_PAD = 128


def dot(a, b, ca=1, cb=0):
    return lax.dot_general(a, b, (((ca,), (cb,)), ((), ())), preferred_element_type=F32)


def bit_of(value, k):
    return lax.rem(value // (1 << k), 2)


def flip(value, mask):
    out = value
    k = 0
    while (1 << k) <= mask:
        if mask & (1 << k):
            out = out + (1 << k) * (1 - 2 * bit_of(value, k))
        k += 1
    return out


def xor(a, b, bits):
    out = 0
    for k in range(bits):
        out = out + (1 << k) * lax.rem(bit_of(a, k) + bit_of(b, k), 2)
    return out


class Sizes:
    def __init__(self, mp, samples, slots, width):
        self.mp, self.samples, self.slots, self.width = mp, samples, slots, width
        self.bits = mp.bit_length() - 1
        self.rows = samples * slots
        self.block = self.rows // mp
        self.half = self.block // 2
        self.per = self.block and slots // self.block
        rest = [1 << k for k in range(1, self.bits)]
        self.orders = (rest, rest[::-1])
        self.sends = {}
        count = 0
        for h in range(2):
            live = list(range(0, mp, 2))
            for t, bit in enumerate(self.orders[h]):
                moved = [d for d in live if d & bit]
                live = [d for d in live if not d & bit]
                self.sends[h, t] = [(d, bit, count + i) for i, d in enumerate(moved)]
                count += len(moved)
        self.steps = len(rest)
        self.far = count
        self.near = mp // 2
        self.fast = self.steps == 2 and self.per == 1


def my_index():
    return lax.axis_index("dp"), lax.axis_index("mp")


def enter(sz):
    dp, me = my_index()
    barrier = pltpu.get_barrier_semaphore()
    for d in range(1, sz.mp):
        pl.semaphore_signal(barrier, inc=1, device_id=(dp, flip(me, d)), device_id_type=MESH)
    pl.semaphore_wait(barrier, sz.mp - 1)


def rows_of(ref, start, size):
    return ref.at[pl.ds(start, size)]


class Reduce:
    def __init__(self, sz, part, refs):
        self.sz, self.part = sz, part
        self.near_buf, self.far_buf, self.near_send, self.near_recv, self.far_send, self.far_recv = refs
        self.dp, self.me = my_index()

    def near_copy(self, pair):
        b = self.sz.block
        return pltpu.make_async_remote_copy(
            src_ref=rows_of(self.part, (2 * pair + 1) * b, b),
            dst_ref=rows_of(self.near_buf, pair * b, b),
            send_sem=self.near_send.at[pair],
            recv_sem=self.near_recv.at[pair],
            device_id=(self.dp, flip(self.me, 1)),
            device_id_type=MESH,
        )

    def far_copy(self, h, d, bit, i):
        b, hb = self.sz.block, self.sz.half
        return pltpu.make_async_remote_copy(
            src_ref=rows_of(self.part, d * b + h * hb, hb),
            dst_ref=rows_of(self.far_buf, i * hb, hb),
            send_sem=self.far_send.at[i],
            recv_sem=self.far_recv.at[i],
            device_id=(self.dp, flip(self.me, bit)),
            device_id_type=MESH,
        )

    def add(self, start, buf, at, size):
        a = self.part[pl.ds(start, size), :].astype(F32) + buf[pl.ds(at, size), :].astype(F32)
        self.part[pl.ds(start, size), :] = a.astype(BF16)

    def near_add(self, pair):
        b = self.sz.block
        self.near_copy(pair).wait()
        self.add(2 * pair * b, self.near_buf, pair * b, b)

    def send(self, h, d):
        for t in range(self.sz.steps):
            for m in self.sz.sends[h, t]:
                if m[0] == d:
                    self.far_copy(h, *m).start()

    def take(self, h, d, bit, i, add=True):
        b, hb = self.sz.block, self.sz.half
        self.far_copy(h, d, bit, i).wait()
        if add:
            self.add((d - bit) * b + h * hb, self.far_buf, i * hb, hb)

    def after(self, k):
        if k == 0:
            self.send(0, 6)
            self.send(1, 6)
        if k == 1:
            self.send(0, 2)
        if k == 2:
            self.send(1, 4)
            self.take(1, *self.sz.sends[1, 0][1])
            self.send(1, 2)
            self.take(0, *self.sz.sends[0, 0][1])
            self.send(0, 4)

    def close(self):
        sz = self.sz
        if sz.fast:
            for h in range(2):
                for t in range(2):
                    for m in sz.sends[h, t]:
                        if m[0] == m[1]:
                            self.take(h, *m, add=False)
            return

        def one(i, carry):
            self.near_add(sz.near - 1 - i)
            return carry

        lax.fori_loop(0, sz.near, one, 0)
        for t in range(sz.steps):
            for h in range(2):
                for m in sz.sends[h, t]:
                    self.far_copy(h, *m).start()
            for h in range(2):
                for m in sz.sends[h, t]:
                    self.take(h, *m, add=t < sz.steps - 1)

    def own_sum(self):
        sz, hb = self.sz, self.sz.half
        out = []
        for h in range(2):
            total = self.part[h * hb : (h + 1) * hb, :].astype(F32)
            for t in range(0 if sz.fast else sz.steps - 1, sz.steps):
                for d, bit, i in sz.sends[h, t]:
                    if d == bit:
                        total = total + self.far_buf[i * hb : (i + 1) * hb, :].astype(F32)
            out.append(total)
        return jnp.concatenate(out, axis=0)


class Gather:
    def __init__(self, sz, out, sems):
        self.sz, self.out = sz, out
        self.near_send, self.near_recv, self.far_send, self.far_recv = sems
        self.dp, self.me = my_index()
        self.first, self.stages = [], []
        if sz.fast:
            x, y = sz.orders[0]
            self.first = [(1, 0, x, 0), (0, 0, y, 1), (0, 0, x, 2), (1, 0, y, 3)]
            on = {0: (1, x, y, 5), 1: (0, y, x, 4)}
            self.stages = [
                [(self.first[1], [on[1]]), (self.first[0], [on[0]])],
                [(self.first[2], []), (self.first[3], [])],
                [(on[1], []), (on[0], [])],
            ]
        else:
            count, plan = 0, {}
            for h in range(2):
                have = [0]
                for t, bit in enumerate(sz.orders[h][::-1]):
                    plan[h, t] = [(h, d, bit, count + i) for i, d in enumerate(have)]
                    count += len(have)
                    have = have + [d | bit for d in have]
            self.first = plan[0, 0] + plan[1, 0]
            for t in range(sz.steps):
                stage = []
                for h in range(2):
                    later = plan[h, t + 1] if t + 1 < sz.steps else []
                    for k, m in enumerate(plan[h, t]):
                        stage.append((m, later if k == len(plan[h, t]) - 1 else []))
                self.stages.append(stage)

    def near_copy(self, d, h):
        b, hb = self.sz.block, self.sz.half
        return pltpu.make_async_remote_copy(
            src_ref=rows_of(self.out, d * b + h * hb, hb),
            dst_ref=rows_of(self.out, (d + 1) * b + h * hb, hb),
            send_sem=self.near_send.at[d + h],
            recv_sem=self.near_recv.at[d + h],
            device_id=(self.dp, flip(self.me, 1)),
            device_id_type=MESH,
        )

    def far_copy(self, h, d, bit, i):
        b, hb = self.sz.block, self.sz.half
        return pltpu.make_async_remote_copy(
            src_ref=rows_of(self.out, d * b + h * hb, hb),
            dst_ref=rows_of(self.out, (d + bit) * b + h * hb, hb),
            send_sem=self.far_send.at[i],
            recv_sem=self.far_recv.at[i],
            device_id=(self.dp, flip(self.me, bit)),
            device_id_type=MESH,
        )

    def start(self):
        for m in self.first:
            self.far_copy(*m).start()
        for h in range(2):
            self.near_copy(0, h).start()

    def step(self, t):
        for m, later in self.stages[t]:
            self.far_copy(*m).wait()
            for n in later:
                self.far_copy(*n).start()
            h, d, bit, _ = m
            self.near_copy(d + bit, h).start()

    def finish(self, first=0):
        for d in range(first, self.sz.mp, 2):
            for h in range(2):
                self.near_copy(d, h).wait()


def reduce_scratch(sz):
    return [
        pltpu.VMEM((sz.near * sz.block, sz.width), BF16),
        pltpu.VMEM((sz.far * sz.half, sz.width), BF16),
        pltpu.SemaphoreType.DMA((sz.near,)),
        pltpu.SemaphoreType.DMA((sz.near,)),
        pltpu.SemaphoreType.DMA((sz.far,)),
        pltpu.SemaphoreType.DMA((sz.far,)),
    ]


def gather_scratch(sz):
    return [
        pltpu.SemaphoreType.DMA((sz.mp,)),
        pltpu.SemaphoreType.DMA((sz.mp,)),
        pltpu.SemaphoreType.DMA((sz.far,)),
        pltpu.SemaphoreType.DMA((sz.far,)),
    ]


def slot_loop(sz, body, red, extra=None):
    if sz.fast:

        def one(i, carry):
            q = i // 2
            pair = 2 * (1 - lax.rem(q, 2)) + 1 - q // 2
            other = 1 - lax.rem(i, 2)
            body(2 * pair + other)

            @pl.when(other == 1)
            def _():
                red.near_copy(pair).start()

            @pl.when(other == 0)
            def _():
                red.near_add(pair)

            for k in range(3):
                pl.when(i == 2 * k + 1)(functools.partial(red.after, k))
            if extra is not None:
                extra(i)
            return carry

    else:
        pairs = sz.per // 2

        def one(i, carry):
            slot = sz.samples - 1 - i
            body(slot)
            for p in range(pairs):
                red.near_copy(slot * pairs + p).start()
            return carry

    lax.fori_loop(0, sz.samples, one, 0)


def layer_stats(values):
    centre = jnp.mean(values, axis=-1, keepdims=True)
    shifted = values - centre
    spread = jnp.mean(shifted * shifted, axis=-1, keepdims=True)
    inv_std = lax.rsqrt(spread + EPSILON)
    return shifted * inv_std, inv_std


def layer_back(gradient, normed, inv_std):
    mean_grad = jnp.mean(gradient, axis=-1, keepdims=True)
    mean_mix = jnp.mean(gradient * normed, axis=-1, keepdims=True)
    return inv_std * (gradient - mean_grad - normed * mean_mix)


def pick_rows(ids_ref, s, count):
    ids = ids_ref[pl.ds(s, 1), :]
    return (lax.broadcasted_iota(jnp.int32, (count, ids.shape[1]), 0) == ids).astype(F32).astype(BF16)


def live_column(sel):
    ones = jnp.ones((sel.shape[0], 128), BF16)
    return dot(sel, ones, 0, 0)[:, 0:1]


class Call:
    def __init__(self):
        self.args, self.specs, self.outs, self.out_specs, self.scratch_of = {}, [], {}, [], {}

    def arg(self, space=pltpu.VMEM, **values):
        self.args.update(values)
        self.specs += [pl.BlockSpec(memory_space=space)] * len(values)

    def out(self, space=pltpu.VMEM, **results):
        for name, (shape, dtype) in results.items():
            self.outs[name] = jax.ShapeDtypeStruct(shape, dtype)
            self.out_specs.append(pl.BlockSpec(memory_space=space))

    def scratch(self, **buffers):
        self.scratch_of.update(buffers)

    def vmem(self, **buffers):
        for name, (shape, dtype) in buffers.items():
            self.scratch_of[name] = pltpu.VMEM(shape, dtype)

    def run(self, kernel, name, cid, limit):
        flat = []
        for value in self.scratch_of.values():
            flat += value if isinstance(value, list) else [value]

        def inner(*refs):
            r, refs = SimpleNamespace(), list(refs)
            for key in list(self.args) + list(self.outs):
                setattr(r, key, refs.pop(0))
            for key, value in self.scratch_of.items():
                count = len(value) if isinstance(value, list) else 0
                setattr(r, key, [refs.pop(0) for _ in range(count)] if count else refs.pop(0))
            kernel(r)

        got = pl.pallas_call(
            inner,
            out_shape=list(self.outs.values()),
            in_specs=self.specs,
            out_specs=self.out_specs,
            scratch_shapes=flat,
            name=name,
            compiler_params=pltpu.CompilerParams(
                collective_id=cid, has_side_effects=True, vmem_limit_bytes=limit
            ),
        )(*self.args.values())
        return SimpleNamespace(**dict(zip(self.outs, got)))


def attention_forward(sz, heads, hd, grid_side, cols, r):
    dp, me = my_index()
    mine = me // sz.per
    sbits = sz.samples.bit_length() - 1
    D, n, L = sz.width, sz.slots, grid_side * grid_side
    lanes = heads * HEAD_PAD
    red = Reduce(sz, r.part, r.red)
    mod_buf, mod_wide, modv, vec = r.mod_buf, r.mod_wide, r.modv, r.vec
    wide = mod_buf.shape[2]
    sem = r.sem

    load_mod = pltpu.make_async_copy(r.w_mod, r.w_mod_v, sem.at[0])
    load_mod.start()

    def load_patches(i, slot):
        return pltpu.make_async_copy(r.patches.at[xor(mine, slot, sbits)], r.patches_v.at[slot], r.load_sem.at[i])

    def start_load(slot, carry):
        load_patches(slot, slot).start()
        return carry

    lax.fori_loop(0, sz.samples, start_load, 0)
    cond = r.condition[...].astype(F32)
    signal = (cond / (1.0 + jnp.exp(-cond))).astype(BF16)
    mod_buf[me] = jnp.zeros((sz.samples, wide), F32)
    load_mod.wait()
    mod_buf[me, :, 0:cols] = dot(signal, r.w_mod_v[...], 1, 1) + vec[5:6, 0:cols]
    enter(sz)

    def mod_copy(d, slot):
        return pltpu.make_async_remote_copy(
            src_ref=mod_buf.at[slot],
            dst_ref=mod_buf.at[slot],
            send_sem=r.mod_send.at[d],
            recv_sem=r.mod_recv.at[d],
            device_id=(dp, flip(me, d)),
            device_id_type=MESH,
        )

    for d in range(1, sz.mp):
        mod_copy(d, me).start()

    w_qkv, w_merge = r.w_qkv_v, r.w_merge_v
    pad_rows = jnp.zeros((HEAD_PAD - hd, D), F32)
    for h in range(heads):
        for c in range(3):
            piece = r.w_in[c].astype(F32)[h * hd : (h + 1) * hd]
            w_qkv[c * lanes + h * HEAD_PAD : c * lanes + (h + 1) * HEAD_PAD, :] = jnp.concatenate(
                [piece, pad_rows], axis=0
            ).astype(BF16)
        piece = r.w_out[...].astype(F32)[h * hd : (h + 1) * hd]
        w_merge[h * HEAD_PAD : (h + 1) * HEAD_PAD, :] = jnp.concatenate([piece, pad_rows], axis=0).astype(BF16)
    save = [
        pltpu.make_async_copy(w_qkv, r.w_qkv, sem.at[1]),
        pltpu.make_async_copy(w_merge, r.w_merge, sem.at[2]),
    ]
    for copy in save:
        copy.start()

    bias_full = r.bias_full
    span = r.table.shape[1]
    for h in range(heads):
        line = r.table[h : h + 1, :]
        strip = jnp.concatenate([line] + [pltpu.roll(line, span - c, 1) for c in range(1, grid_side)], axis=0)
        for row in range(grid_side):
            rolled = pltpu.roll(strip, span - row * 2 * grid_side, 1) if row else strip
            bias_full[h, row * grid_side : (row + 1) * grid_side, :] = rolled[:, : 2 * L].astype(BF16)

    normed, kept_own = r.normed, r.kept_v

    def norm_one(slot, carry):
        load_patches(slot, slot).wait()
        sel = pick_rows(r.pos, xor(mine, slot, sbits), L)
        kept = dot(sel, r.patches_v[slot], 0, 0)
        value, _ = layer_stats(kept)
        normed[pl.ds(slot * n, n), :] = value

        @pl.when(slot == 0)
        def _():
            kept_own[...] = kept[: sz.block]

        return carry

    lax.fori_loop(0, sz.samples, norm_one, 0)
    save_kept = pltpu.make_async_copy(kept_own, r.kept, sem.at[3])
    save_kept.start()

    for d in range(1, sz.mp):
        mod_copy(d, me).wait_send()
        mod_copy(d, flip(me, d)).wait_recv()
    mod_wide[...] = jnp.zeros_like(mod_wide)
    for m in range(sz.mp):
        base = m * cols // 128 * 128
        phase = m * cols - base
        piece = mod_buf[m]
        if phase:
            piece = pltpu.roll(piece, phase, 1)
        mod_wide[:, base : base + wide] += piece
    modv[...] = mod_wide[:, : 6 * D]

    factor = hd ** (-0.5)
    stores = [(r.attn_in_v, r.attn_in), (r.qkv_v, r.qkv), (r.att_v, r.att)]

    def save_slot(i, slot):
        at = pl.ds(slot * n, n)
        copies = [
            pltpu.make_async_copy(a.at[at], b.at[at], r.save_sem.at[k, slot]) for k, (a, b) in enumerate(stores)
        ]
        copies.append(pltpu.make_async_copy(r.probs_v.at[slot], r.probs.at[slot], r.save_sem.at[3, slot]))
        return copies

    def body(slot):
        s = xor(mine, slot, sbits)
        at = pl.ds(slot * n, n)
        shift = modv[pl.ds(s, 1), 0:D]
        scale = modv[pl.ds(s, 1), D : 2 * D]
        entry = (normed[at, :] * (1.0 + scale) + shift).astype(BF16)
        r.attn_in_v[at, :] = entry
        proj = dot(entry, w_qkv[...], 1, 1)
        qs = (proj[:, :lanes] + vec[0:1, :lanes]).astype(BF16)
        ks = proj[:, lanes : 2 * lanes].astype(BF16)
        vs = (proj[:, 2 * lanes :] + vec[1:2, :lanes]).astype(BF16)
        r.qkv_v[at, 0:lanes] = qs
        r.qkv_v[at, lanes : 2 * lanes] = ks
        r.qkv_v[at, 2 * lanes :] = vs
        sel = pick_rows(r.pos, s, L)
        sel_wide = pick_rows(r.pos_wide, s, 2 * L)
        live = r.pos[pl.ds(s, 1), :] >= 0
        outs = []
        for h in range(heads):
            cut = slice(h * HEAD_PAD, (h + 1) * HEAD_PAD)
            bias = dot(dot(sel, bias_full[h], 0, 0).astype(BF16), sel_wide)
            scores = jnp.where(live, dot(qs[:, cut], ks[:, cut], 1, 1) * factor + bias, MASKED)
            top = jnp.max(scores, axis=-1, keepdims=True)
            e = jnp.exp(scores - top)
            p = e / jnp.sum(e, axis=-1, keepdims=True)
            r.probs_v[slot, h] = p
            outs.append(dot(p.astype(BF16), vs[:, cut]).astype(BF16))
        joined = jnp.concatenate(outs, axis=1) if heads > 1 else outs[0]
        r.att_v[at, :] = joined
        r.part[at, :] = dot(joined, w_merge[...]).astype(BF16)
        for copy in save_slot(0, slot):
            copy.start()

    slot_loop(sz, body, red)
    red.close()
    result = red.own_sum() + vec[2:3, :D]
    r.res_v[...] = result
    hidden = kept_own[...] + modv[pl.ds(mine, 1), 2 * D : 3 * D] * result
    r.hidden_v[...] = hidden
    value, _ = layer_stats(hidden)
    shift = modv[pl.ds(mine, 1), 3 * D : 4 * D]
    scale = modv[pl.ds(mine, 1), 4 * D : 5 * D]
    r.mlp_v[...] = (value * (1.0 + scale) + shift).astype(BF16)
    save_own = [
        pltpu.make_async_copy(r.res_v, r.res, sem.at[4]),
        pltpu.make_async_copy(r.hidden_v, r.hidden, sem.at[5]),
        pltpu.make_async_copy(r.mlp_v, r.mlp, sem.at[6]),
    ]
    for copy in save_own:
        copy.start()

    def wait_slot(slot, carry):
        for copy in save_slot(0, slot):
            copy.wait()
        return carry

    lax.fori_loop(0, sz.samples, wait_slot, 0)
    for copy in save + save_own + [save_kept]:
        copy.wait()


class Line:
    def __init__(self, r, chunk):
        self.r, self.chunk = r, chunk
        self.g, self.outer_buf, self.inner_buf = r.grads, r.z_outer, r.z_inner
        self.count = self.g.shape[1] // chunk
        self.dp, self.me = my_index()
        self.is_inner = (self.dp == 1) | (self.dp == 2)
        self.is_outer = (self.dp == 0) | (self.dp == 3)
        self.step_to = 1 + self.dp // 3
        self.back_to = (self.dp - 1) * 3
        self.other = 3 - self.dp
        self.mine = 2 - self.dp
        self.passed = self.dp - 1

    def rows(self, k):
        return pl.ds(k * self.chunk, self.chunk)

    def copy(self, src, dst, send, recv, to):
        return pltpu.make_async_remote_copy(
            src_ref=src, dst_ref=dst, send_sem=send, recv_sem=recv, device_id=(to, self.me), device_id_type=MESH
        )

    def out_copy(self, j, k):
        return self.copy(
            self.g.at[j, self.rows(k)], self.outer_buf.at[j, self.rows(k)],
            self.r.zs.at[j, k], self.r.zo.at[j, k], self.step_to,
        )

    def in_copy(self, k):
        return self.copy(
            self.g.at[self.passed, self.rows(k)], self.inner_buf.at[self.rows(k)],
            self.r.zf.at[k], self.r.zi.at[k], self.other,
        )

    def total_copy(self, j, k, which, to):
        return self.copy(
            self.outer_buf.at[j, self.rows(k)], self.outer_buf.at[j, self.rows(k)],
            self.r.zt.at[which, k], self.r.zr.at[j, k], to,
        )

    def begin(self, j, k0, k1):
        @pl.when(self.is_outer)
        def _():
            def one(k, carry):
                self.out_copy(j, k).start()
                return carry

            lax.fori_loop(k0, k1, one, 0)

    def add(self, to, j, k, more):
        def one(i, carry):
            at = pl.ds(k * self.chunk + i * 16, 16)
            v = self.g[j, at, :].astype(F32) + self.outer_buf[j, at, :].astype(F32)
            if more:
                v = v + self.inner_buf[at, :].astype(F32)
            to[j, at, :] = v.astype(BF16)
            return carry

        lax.fori_loop(0, self.chunk // 16, one, 0)

    def stage(self, number, j, k):
        if number == 1:

            @pl.when(self.passed == j)
            def _():
                self.out_copy(j, k).wait_recv()
                self.add(self.g, j, k, False)
                self.in_copy(k).start()

        elif number == 2:

            @pl.when(self.mine == j)
            def _():
                self.out_copy(j, k).wait_recv()
                self.in_copy(k).wait_recv()
                self.add(self.outer_buf, j, k, True)
                self.total_copy(j, k, 0, self.other).start()
                self.total_copy(j, k, 1, self.back_to).start()

        else:

            @pl.when(self.passed == j)
            def _():
                self.in_copy(k).wait_send()
                self.total_copy(j, k, 0, self.other).wait_recv()
                self.total_copy(j, k, 2, self.back_to).start()

    def finish(self):
        @pl.when(self.is_inner)
        def _():
            def one(k, carry):
                self.total_copy(self.mine, k, 0, self.other).wait_send()
                self.total_copy(self.mine, k, 1, self.back_to).wait_send()
                self.total_copy(self.passed, k, 2, self.back_to).wait_send()
                return carry

            lax.fori_loop(0, self.count, one, 0)

        @pl.when(self.is_outer)
        def _():
            def one(k, carry):
                for j in range(2):
                    self.out_copy(j, k).wait_send()
                    self.total_copy(j, k, 0, self.step_to).wait_recv()
                return carry

            lax.fori_loop(0, self.count, one, 0)


def block_backward(sz, heads, hd, grid_side, cols, dp_size, chunk, r):
    dp, me = my_index()
    mine = me // sz.per
    sbits = sz.samples.bit_length() - 1
    D, n, L = sz.width, sz.slots, grid_side * grid_side
    lanes = heads * HEAD_PAD
    local = heads * hd
    F = r.w_up_v.shape[0]
    block = sz.block
    vec, modv = r.vec, r.modv
    fwd = Reduce(sz, r.part_f, r.red_f)
    bwd = Reduce(sz, r.part_b, r.red_b)
    last = Reduce(sz, r.part_b, r.red_b[:2] + r.last_sems)
    gat_m = Gather(sz, r.mlp_v, r.gat_m)
    gat_d = Gather(sz, r.d_attn, r.gat_d)
    gat_o = Gather(sz, r.part_f, r.gat_o)
    gat_k = Gather(sz, r.mlp_v, r.gat_k)
    line = Line(r, chunk) if chunk else None
    grads = r.grads
    sem = r.sem

    per_up, per_local = (F // chunk, local // chunk) if chunk else (0, 0)
    marks = [0, per_up, per_up + per_local, per_up + 2 * per_local]
    following = {(number, j): 0 for number in (1, 2, 3) for j in range(2)}

    def tick(*steps):
        if line is None:
            return
        for number, j, count in steps:
            k0 = following[number, j]
            k1 = min(k0 + count, marks[3])
            assert number == 1 or k1 <= following[number - 1, j]
            following[number, j] = k1
            if k1 - k0 == 1:
                line.stage(number, j, k0)
            elif k1 > k0:

                def one(k, carry, number=number, j=j):
                    line.stage(number, j, k)
                    return carry

                lax.fori_loop(k0, k1, one, 0)

    def begin(j, group):
        if line is not None:
            line.begin(j, marks[group], marks[group + 1])

    def ticks_at(i, plan):
        if line is not None:
            for when, steps in plan.items():
                pl.when(i == when)(lambda steps=steps: tick(*steps))

    load_up = pltpu.make_async_copy(r.w_up, r.w_up_v, sem.at[0])
    load_down = pltpu.make_async_copy(r.w_down, r.w_down_v, sem.at[1])
    load_up.start()
    load_down.start()

    load_own = pltpu.make_async_copy(r.mlp, r.mlp_v.at[pl.ds(0, block)], sem.at[12])
    load_own.start()

    def load_cot(slot):
        at = pl.ds(slot * n, n)
        return pltpu.make_async_copy(r.cot.at[xor(mine, slot, sbits)], r.d_mlp.at[at], r.load_sem.at[1, slot])

    def start_cot(slot, carry):
        load_cot(slot).start()
        return carry

    lax.fori_loop(0, sz.samples, start_cot, 0)
    loads = [
        pltpu.make_async_copy(r.cot.at[mine, pl.ds(0, block)], r.cot_own, sem.at[2]),
        pltpu.make_async_copy(r.hidden, r.hidden_v, sem.at[3]),
        pltpu.make_async_copy(r.res, r.res_v, sem.at[4]),
    ]
    late = [
        pltpu.make_async_copy(r.qkv, r.qkv_v, sem.at[6]),
        pltpu.make_async_copy(r.probs, r.probs_v, sem.at[7]),
        pltpu.make_async_copy(r.w_qkv, r.w_qkv_v, sem.at[9]),
        pltpu.make_async_copy(r.w_merge, r.w_merge_v, sem.at[10]),
    ]
    for copy in loads + late:
        copy.start()
    load_attn = pltpu.make_async_copy(r.attn_in, r.d_mlp, sem.at[11])
    load_kept = pltpu.make_async_copy(r.kept, r.res_v, sem.at[5])
    load_att = pltpu.make_async_copy(r.att, r.act.at[:, pl.ds(0, lanes)], sem.at[8])

    barrier = pltpu.get_barrier_semaphore()
    for d in range(1, sz.mp):
        pl.semaphore_signal(barrier, inc=1, device_id=(dp, flip(me, d)), device_id_type=MESH)
    for e in range(1, dp_size):
        pl.semaphore_signal(barrier, inc=1, device_id=(lax.rem(dp + e, dp_size), me), device_id_type=MESH)
    pl.semaphore_wait(barrier, sz.mp + dp_size - 2)
    load_own.wait()
    gat_m.start()
    load_up.wait()
    load_down.wait()
    w_up, w_down, mlp = r.w_up_v, r.w_down_v, r.mlp_v
    act, d_pre, d_mlp, slope = r.act, r.d_pre, r.d_mlp, r.slope

    up_bg, down_bg = r.bias_g.at[dp, 0:1], r.bias_g.at[dp, 1:2]
    merge_bg, proj_bg = r.bias_g.at[dp, 2:3], r.bias_g.at[dp, 3:4]
    r.bias_g[dp] = jnp.zeros(r.bias_g.shape[1:], F32)
    cond = r.condition[...].astype(F32)
    r.signal_g[dp] = (cond / (1.0 + jnp.exp(-cond))).astype(BF16)
    shared = [r.bias_g, r.table_g, r.mod_g, r.signal_g]

    def dp_copy(k, e, slot):
        return pltpu.make_async_remote_copy(
            src_ref=shared[k].at[slot],
            dst_ref=shared[k].at[slot],
            send_sem=r.dp_send.at[k, e],
            recv_sem=r.dp_recv.at[k, e],
            device_id=(lax.rem(dp + e, dp_size), me),
            device_id_type=MESH,
        )

    def share(k):
        for e in range(1, dp_size):
            dp_copy(k, e, dp).start()

    share(3)

    def forward(slot, wide):
        at = pl.ds(slot * n, wide * n)
        v = dot(mlp[at, :], w_up[...], 1, 1) + vec[3:4, :F]
        square = v * v
        t = jnp.tanh(GELU_C * (v + GELU_A * v * square))
        active = (0.5 * v * (1.0 + t)).astype(BF16)
        act[at, :] = active
        slope[at, :] = 0.5 * (1.0 + t) + 0.5 * v * (1.0 - t * t) * (GELU_C * (1.0 + 3.0 * GELU_A * square))
        r.part_f[at, :] = dot(active, w_down[...]).astype(BF16)
        for k in range(wide):
            at = pl.ds((slot + k) * n, n)
            s = xor(mine, slot + k, sbits)
            load_cot(slot + k).wait()
            gate = modv[pl.ds(s, 1), 5 * D : 6 * D]
            live = live_column(pick_rows(r.pos, s, L))
            dm = (gate * (d_mlp[at, :].astype(F32) * live)).astype(BF16)
            d_mlp[at, :] = dm
            down_bg[...] += jnp.sum(dm.astype(F32), axis=0, keepdims=True)

    if sz.fast:
        def two_slots(i, carry):
            @pl.when(i == 1)
            def _():
                gat_m.step(0)
                gat_m.step(1)

            @pl.when(i == 3)
            def _():
                gat_m.step(2)

            for h in range(2):
                gat_m.near_copy(2 * i, h).wait()
            forward(2 * i, 2)
            fwd.near_copy(i).start()

            @pl.when(i > 0)
            def _():
                fwd.near_add(i - 1)

            pl.when(i == 2)(functools.partial(fwd.send, 0, 2))
            pl.when(i == 3)(functools.partial(fwd.send, 1, 4))
            return carry

        lax.fori_loop(0, 4, two_slots, 0)
    else:
        for t in range(len(gat_m.stages)):
            gat_m.step(t)
        gat_m.finish()
        slot_loop(sz, lambda slot: forward(slot, 1), fwd)

    def wide_grad(left, right, half):
        at = 0
        while at < F:
            size = min(256, F - at)
            grads[half, at : at + size, :] = dot(left[:, at : at + size], right[...], 0, 0).astype(BF16)
            at += size

    wide_grad(act, d_mlp, 1)
    begin(1, 0)
    if sz.fast:
        fwd.near_add(3)
        fwd.send(0, 6)
        fwd.send(1, 6)

    def backward(slot):
        at = pl.ds(slot * n, n)
        dpre = (dot(d_mlp[at, :], w_down[...], 1, 1) * slope[at, :]).astype(BF16)
        d_pre[at, :] = dpre
        up_bg[:, :F] += jnp.sum(dpre.astype(F32), axis=0, keepdims=True)
        r.part_b[at, :] = dot(dpre, w_up[...]).astype(BF16)

    plan = {
        1: [(1, 1, 1)],
        2: [(1, 1, 1)],
        3: [(1, 1, 1)],
        4: [(1, 1, 1), (2, 1, 1)],
        5: [(1, 1, 1), (2, 1, 1)],
        6: [(1, 1, 1), (2, 1, 1)],
        7: [(1, 1, 1), (2, 1, 1)],
    }

    slot_loop(sz, backward, bwd, lambda i: ticks_at(i, plan))
    load_attn.start()
    load_att.start()
    wide_grad(d_pre, mlp, 0)
    begin(0, 0)
    tick((1, 1, 1), (2, 1, 1), (3, 1, 2))
    for copy in loads:
        copy.wait()
    normed2, inv2 = layer_stats(r.hidden_v[...])
    r.normed_v[...] = normed2
    if sz.fast:
        fwd.take(1, *sz.sends[1, 0][1])
        fwd.take(0, *sz.sends[0, 0][1])
    bwd.close()
    tick((1, 1, 1), (2, 1, 1), (3, 1, 1))

    mrow = pl.ds(mine, 1)
    live = live_column(pick_rows(r.pos, mine, L)[:, :block])
    d_out = r.cot_own[...].astype(F32) * live
    d_mlp_in = bwd.own_sum()
    g = d_mlp_in * (1.0 + modv[mrow, 4 * D : 5 * D])
    dh = d_out + layer_back(g, r.normed_v[...], inv2)
    r.dh_v[...] = dh
    r.d_attn[:block, :] = (modv[mrow, 2 * D : 3 * D] * dh).astype(BF16)
    gat_d.start()

    early, late_sums = r.early, r.late_sums
    early[me, 0:1, :] = jnp.sum(dh * r.res_v[...], axis=0, keepdims=True)
    load_kept.start()
    early[me, 1:2, :] = jnp.sum(d_mlp_in, axis=0, keepdims=True)
    early[me, 2:3, :] = jnp.sum(d_mlp_in * r.normed_v[...], axis=0, keepdims=True)

    def finish_out():
        fwd.close()
        live = live_column(pick_rows(r.pos, mine, L)[:, :block])
        mlp_out = fwd.own_sum() + vec[4:5, :D]
        early[me, 3:4, :] = jnp.sum(mlp_out * (r.cot_own[...].astype(F32) * live), axis=0, keepdims=True)
        out_own = (r.hidden_v[...] + modv[mrow, 5 * D : 6 * D] * mlp_out) * live
        r.part_f[:block, :] = out_own.astype(BF16)

    def dm_copy(ref, k, d, slot):
        return pltpu.make_async_remote_copy(
            src_ref=ref.at[slot],
            dst_ref=ref.at[slot],
            send_sem=r.dm_send.at[k, d],
            recv_sem=r.dm_recv.at[k, d],
            device_id=(dp, flip(me, d)),
            device_id_type=MESH,
        )

    tick((1, 1, 1))

    def attention_grad(c, half, at):
        if c < 3:
            full = dot(qkv[:, c * lanes : (c + 1) * lanes], d_mlp[...], 0, 0)
        else:
            full = dot(r.act[:, :lanes], r.d_attn[...], 0, 0)
        rows = [full[h * HEAD_PAD : h * HEAD_PAD + hd] for h in range(heads)]
        rows = jnp.concatenate(rows, axis=0) if heads > 1 else rows[0]
        grads[half, at : at + local, :] = rows.astype(BF16)

    for copy in late:
        copy.wait()
    factor = hd ** (-0.5)
    grid_g = r.grid_g
    grid_g[...] = jnp.zeros_like(grid_g)
    qkv, w_qkv, w_merge = r.qkv_v, r.w_qkv_v, r.w_merge_v
    def attention(slot):
        s = xor(mine, slot, sbits)
        at = pl.ds(slot * n, n)
        da = r.d_attn[at, :]
        merge_bg[...] += jnp.sum(da.astype(F32), axis=0, keepdims=True)
        d_att = dot(da, w_merge[...], 1, 1).astype(BF16)
        sel = pick_rows(r.pos, s, L)
        sel_wide = pick_rows(r.pos_wide, s, 2 * L)
        dq, dk, dv = [], [], []
        for h in range(heads):
            q = qkv[at, h * HEAD_PAD : (h + 1) * HEAD_PAD]
            k = qkv[at, lanes + h * HEAD_PAD : lanes + (h + 1) * HEAD_PAD]
            v = qkv[at, 2 * lanes + h * HEAD_PAD : 2 * lanes + (h + 1) * HEAD_PAD]
            d_a = d_att[:, h * HEAD_PAD : (h + 1) * HEAD_PAD]
            p = r.probs_v[slot, h]
            d_p = dot(d_a, v, 1, 1)
            dv.append(dot(p.astype(BF16), d_a, 0, 0).astype(BF16))
            ds = p * (d_p - jnp.sum(p * d_p, axis=-1, keepdims=True))
            dl = ds.astype(BF16)
            dq.append((dot(dl, k) * factor).astype(BF16))
            dk.append((dot(dl, q, 0, 0) * factor).astype(BF16))
            grid_g[h] += dot(dot(sel, dl).astype(BF16), sel_wide, 1, 1)
        joined = jnp.concatenate(dq + dk + dv, axis=1)
        qkv[at, :] = joined
        proj_bg[:, : 3 * lanes] += jnp.sum(joined.astype(F32), axis=0, keepdims=True)
        r.part_b[at, :] = dot(joined, w_qkv[...]).astype(BF16)

    if sz.fast:
        plan_one = {1: [(1, 1, 1), (2, 1, 2), (3, 1, 2)], 2: [(1, 1, 1), (2, 1, 1), (3, 1, 2)]}
        plan_two = {
            3: [(1, 0, 2)],
            4: [(1, 0, 1), (2, 0, 1), (3, 1, 1)],
            5: [(1, 0, 2), (2, 0, 1), (3, 1, 1)],
            6: [(1, 0, 1), (2, 0, 1), (3, 0, 1), (3, 1, 1)],
            7: [(1, 0, 1), (2, 0, 1), (3, 0, 1)],
        }

        def one(i, carry):
            q = i // 2
            pair = q + lax.rem(q, 2) * (q // 2) * -1 + (q // 2) * (1 - lax.rem(q, 2))
            slot = jnp.where(i < 2, i, 2 * pair + 1 - lax.rem(i, 2))

            ticks_at(i, plan_one)

            @pl.when(i == 1)
            def _():
                for h in range(2):
                    gat_d.near_copy(0, h).wait()

            @pl.when(i == 2)
            def _():
                gat_d.step(0)
                tick((2, 1, 1), (3, 1, 1))
                gat_d.step(1)
                fwd.send(1, 2)
                fwd.send(0, 4)
                tick((2, 1, 2), (1, 0, 2), (3, 1, 1))
                for h in range(2):
                    gat_d.near_copy(2, h).wait()

            ticks_at(i, plan_two)

            @pl.when(i == 4)
            def _():
                gat_d.step(2)
                for d in (4, 6):
                    for h in range(2):
                        gat_d.near_copy(d, h).wait()

            attention(slot)

            @pl.when(i == 1)
            def _():
                last.near_copy(0).start()

            @pl.when((i > 1) & (lax.rem(i, 2) == 0))
            def _():
                last.near_copy(pair).start()

            @pl.when(i == 3)
            def _():
                last.near_add(0)
                last.near_add(1)
                last.send(0, 2)

            @pl.when(i == 6)
            def _():
                finish_out()

            @pl.when(i == 5)
            def _():
                last.near_add(3)
                last.send(0, 6)
                last.send(1, 6)

            @pl.when(i == 7)
            def _():
                last.near_add(2)
                last.after(2)

            return carry

        lax.fori_loop(0, 8, one, 0)
        tick((1, 0, 1), (2, 0, 1), (3, 0, 1))
    else:
        for t in range(len(gat_d.stages)):
            gat_d.step(t)
        gat_d.finish()
        finish_out()
        slot_loop(sz, attention, last)

    load_attn.wait()
    load_att.wait()
    attention_grad(3, 1, F)
    begin(1, 1)
    tick((1, 0, 1), (2, 0, 1))
    attention_grad(0, 0, F)
    begin(0, 1)
    attention_grad(2, 1, F + local)
    begin(1, 2)
    attention_grad(1, 0, F + local)
    begin(0, 2)
    tick((1, 0, 1), (2, 0, 1), (3, 0, 2))

    tables = r.table_g
    span = tables.shape[2]
    for h in range(heads):
        strip = jnp.zeros((grid_side, span), F32)
        for row in range(grid_side):
            piece = jnp.concatenate(
                [
                    grid_g[h, row * grid_side : (row + 1) * grid_side, :],
                    jnp.zeros((grid_side, span - 2 * L), F32),
                ],
                axis=1,
            )
            strip = strip + (pltpu.roll(piece, row * 2 * grid_side, 1) if row else piece)
        total_row = strip[0:1]
        for c in range(1, grid_side):
            total_row = total_row + pltpu.roll(strip[c : c + 1], c, 1)
        tables[dp, h : h + 1, :] = total_row

    share(0)
    share(1)
    load_kept.wait()
    normed1, inv1 = layer_stats(r.res_v[...])
    r.normed_v[...] = normed1
    last.close()
    tick((2, 0, 2), (3, 0, 1), (1, 1, 2))
    d_in = last.own_sum()
    g = d_in * (1.0 + modv[mrow, D : 2 * D])
    mlp[:block, :] = (r.dh_v[...] + layer_back(g, r.normed_v[...], inv1)).astype(BF16)
    late_sums[me, 0:1, :] = jnp.sum(d_in, axis=0, keepdims=True)
    late_sums[me, 1:2, :] = jnp.sum(d_in * r.normed_v[...], axis=0, keepdims=True)
    gat_k.start()
    tick((2, 0, 1), (1, 1, 1), (3, 0, 1))

    def out_copy(slot):
        return pltpu.make_async_copy(
            r.part_f.at[pl.ds(slot * n, n)], r.out.at[xor(mine, slot, sbits)], r.load_sem.at[0, slot]
        )

    def start_out(slot, carry):
        out_copy(slot).start()
        return carry

    def patch_copy(slot):
        return pltpu.make_async_copy(
            r.part_b.at[pl.ds(lax.rem(slot, 2) * L, L)], r.patch_g.at[xor(mine, slot, sbits)], r.load_sem.at[1, slot]
        )

    def patch(slot, carry):
        @pl.when(slot >= 2)
        def _():
            patch_copy(slot - 2).wait()

        sel = pick_rows(r.pos, xor(mine, slot, sbits), L)
        r.part_b[pl.ds(lax.rem(slot, 2) * L, L), :] = dot(sel, mlp[pl.ds(slot * n, n), :]).astype(BF16)
        patch_copy(slot).start()
        return carry

    for h in range(2):
        gat_k.near_copy(0, h).wait()
    if sz.fast:
        lax.fori_loop(0, 2, patch, 0)
    gat_k.step(0)
    for d in range(1, sz.mp):
        dm_copy(early, 0, d, me).start()
        dm_copy(late_sums, 1, d, me).start()
    gat_o.start()
    tick((2, 0, 2), (1, 0, 2), (3, 0, 2), (2, 1, 1))
    gat_k.step(1)
    tick((1, 0, 1), (1, 1, 1), (2, 1, 2), (2, 0, 1), (3, 0, 3))
    if sz.fast:
        for d in (2, 4):
            for h in range(2):
                gat_k.near_copy(d, h).wait()
        lax.fori_loop(2, 6, patch, 0)
        gat_k.step(2)
        tick((1, 1, 2), (2, 0, 2), (3, 1, 2))
        for h in range(2):
            gat_k.near_copy(6, h).wait()
        lax.fori_loop(6, 8, patch, 0)
    else:
        for t in range(2, len(gat_k.stages)):
            gat_k.step(t)
        gat_k.finish(2)
        lax.fori_loop(0, sz.samples, patch, 0)
    for d in range(1, sz.mp):
        dm_copy(early, 0, d, me).wait_send()
        dm_copy(early, 0, d, flip(me, d)).wait_recv()
        dm_copy(late_sums, 1, d, me).wait_send()
        dm_copy(late_sums, 1, d, flip(me, d)).wait_recv()
    flat, mod_g = r.flat, r.mod_g
    flat[:, 6 * D :] = jnp.zeros((sz.samples, flat.shape[1] - 6 * D), F32)
    for s in range(sz.samples):
        for c in range(6):
            v = 0
            for p in range(sz.per):
                m = s * sz.per + p
                v = v + (late_sums[m, c : c + 1, :] if c < 2 else early[m, c - 2 : c - 1, :])
            flat[s : s + 1, c * D : (c + 1) * D] = v
    base = pl.multiple_of(me * cols // 128 * 128, 128)
    mod_g[dp] = flat[:, pl.ds(base, mod_g.shape[2])]
    share(2)
    tick((1, 0, 1), (2, 0, 1))
    gat_o.step(0)
    tick((1, 0, 1), (2, 1, 1), (3, 1, 1), (3, 0, 1))
    gat_o.step(1)
    tick((2, 1, 1), (1, 0, 1), (3, 0, 1))
    for t in range(2, len(gat_o.stages)):
        gat_o.step(t)
    gat_o.finish()
    lax.fori_loop(0, sz.samples, start_out, 0)
    tick((2, 1, 1), (3, 0, 1), (2, 0, 1), (3, 1, 1), (2, 0, 1), (3, 1, 1), (2, 0, 1), (3, 1, 1), (3, 0, 3))
    if line is not None:
        assert all(k == marks[3] for k in following.values()), following
    for k in range(4):
        for e in range(1, dp_size):
            dp_copy(k, e, dp).wait_send()
            dp_copy(k, e, lax.rem(dp + dp_size - e, dp_size)).wait_recv()
    for slot in range(sz.samples - 2, sz.samples):
        patch_copy(slot).wait()

    def wait_out(slot, carry):
        out_copy(slot).wait()
        return carry

    lax.fori_loop(0, sz.samples, wait_out, 0)
    if line is not None:
        line.finish()


def body(
    patches,
    condition,
    lengths,
    keep_order,
    cotangent,
    projection_weight,
    query_value_bias,
    merge_weight,
    merge_output_bias,
    up_weight,
    up_projection_bias,
    down_weight,
    down_projection_bias,
    w_modulate,
    bias_modulate,
    bias_table,
):
    samples, L, D = patches.shape
    n = cotangent.shape[1]
    grid_side = math.isqrt(L)
    offsets = 2 * grid_side - 1
    heads = bias_table.shape[0]
    local = projection_weight.shape[2]
    hd = local // heads
    lanes = heads * HEAD_PAD
    F = up_weight.shape[1]
    cols = w_modulate.shape[1]
    mp, dp_size = lax.axis_size("mp"), lax.axis_size("dp")
    me = lax.axis_index("mp")
    sz = Sizes(mp, samples, n, D)
    rows, block = sz.rows, sz.block

    ids = jnp.arange(n, dtype=jnp.int32)
    pos = jnp.where(ids[None, :] < lengths[:, None], keep_order[:, :n], -1)
    cot = cotangent
    if sz.per > 1:
        order = ((ids // block) ^ lax.rem(me, sz.per)) * block + ids % block
        pos = jnp.take(pos, order, axis=1)
        cot = jnp.take(cot, order, axis=1)
    turned = L - 1 - pos
    pos_wide = jnp.where(pos < 0, -1, turned + turned // grid_side * grid_side)

    def wide_row(a):
        return jnp.pad(a.astype(F32), (0, D - a.shape[0]))

    def by_head(a):
        return jnp.pad(a.reshape(heads, hd), ((0, 0), (0, HEAD_PAD - hd))).reshape(lanes)

    vec = jnp.stack(
        [
            wide_row(by_head(query_value_bias[0])),
            wide_row(by_head(query_value_bias[1])),
            wide_row(merge_output_bias),
            wide_row(up_projection_bias),
            wide_row(down_projection_bias),
            wide_row(bias_modulate),
        ]
    )
    table = bias_table.astype(F32).reshape(heads, offsets, offsets)
    table = jnp.pad(table, ((0, 0), (0, 1), (0, 1))).reshape(heads, 4 * L)
    wide = -(-cols // 128) * 128 + 128
    modw = max(m * cols // 128 * 128 + wide for m in range(mp))
    dma = pltpu.SemaphoreType.DMA

    one = Call()
    one.arg(
        condition=condition,
        vec=vec,
        pos=pos,
        pos_wide=pos_wide,
        w_in=jnp.swapaxes(projection_weight, 1, 2),
        w_out=merge_weight,
        table=table,
    )
    one.arg(pl.ANY, patches=patches, w_mod=w_modulate.T)
    one.out(modv=((samples, 6 * D), F32))
    one.out(
        pl.ANY,
        attn_in=((rows, D), BF16),
        qkv=((rows, 3 * lanes), BF16),
        probs=((samples, heads, n, n), F32),
        att=((rows, lanes), BF16),
        kept=((block, D), F32),
        res=((block, D), F32),
        hidden=((block, D), F32),
        mlp=((block, D), BF16),
        w_qkv=((3 * lanes, D), BF16),
        w_merge=((lanes, D), BF16),
    )
    one.vmem(
        attn_in_v=((rows, D), BF16),
        qkv_v=((rows, 3 * lanes), BF16),
        probs_v=((samples, heads, n, n), F32),
        att_v=((rows, lanes), BF16),
        kept_v=((block, D), F32),
        res_v=((block, D), F32),
        hidden_v=((block, D), F32),
        mlp_v=((block, D), BF16),
        w_qkv_v=((3 * lanes, D), BF16),
        w_merge_v=((lanes, D), BF16),
        w_mod_v=((cols, D), BF16),
        patches_v=((samples, L, D), BF16),
        mod_buf=((mp, samples, wide), F32),
        mod_wide=((samples, modw), F32),
        normed=((rows, D), F32),
        bias_full=((heads, L, 2 * L), BF16),
        part=((rows, D), BF16),
    )
    one.scratch(
        mod_send=dma((mp,)),
        mod_recv=dma((mp,)),
        sem=dma((7,)),
        load_sem=dma((samples,)),
        save_sem=dma((4, samples)),
        red=reduce_scratch(sz),
    )
    first = one.run(
        functools.partial(attention_forward, sz, heads, hd, grid_side, cols), "attention_forward", 0, 62 << 20
    )

    chunk = 48 if dp_size == 4 and F % 48 == 0 and local % 48 == 0 else 0
    two = Call()
    two.arg(condition=condition, vec=vec, pos=pos, pos_wide=pos_wide, modv=first.modv)
    two.arg(
        pl.ANY,
        cot=cot,
        w_up=up_weight.T,
        w_down=down_weight,
        mlp=first.mlp,
        hidden=first.hidden,
        res=first.res,
        kept=first.kept,
        qkv=first.qkv,
        probs=first.probs,
        att=first.att,
        w_qkv=first.w_qkv,
        w_merge=first.w_merge,
        attn_in=first.attn_in,
    )
    both = ((2, F + 2 * local, D), BF16)
    if chunk:
        count = (F + 2 * local) // chunk
        two.out(z_outer=both)
        two.vmem(grads=both, z_inner=((F + 2 * local, D), BF16))
        two.scratch(
            zs=dma((2, count)),
            zo=dma((2, count)),
            zf=dma((count,)),
            zi=dma((count,)),
            zt=dma((3, count)),
            zr=dma((2, count)),
        )
    else:
        two.out(grads=both)
    two.out(
        bias_g=((dp_size, 4, D), F32),
        table_g=((dp_size, heads, 4 * L), F32),
        signal_g=((dp_size, samples, D), BF16),
        mod_g=((dp_size, samples, wide), F32),
    )
    two.out(pl.ANY, out=((samples, n, D), BF16), patch_g=((samples, L, D), BF16))
    two.vmem(
        w_up_v=((F, D), BF16),
        w_down_v=((F, D), BF16),
        mlp_v=((rows, D), BF16),
        d_mlp=((rows, D), BF16),
        slope=((rows, F), F32),
        act=((rows, F), BF16),
        d_pre=((rows, F), BF16),
        part_f=((rows, D), BF16),
        part_b=((rows, D), BF16),
        d_attn=((rows, D), BF16),
        cot_own=((block, D), BF16),
        hidden_v=((block, D), F32),
        res_v=((block, D), F32),
        normed_v=((block, D), F32),
        dh_v=((block, D), F32),
        qkv_v=((rows, 3 * lanes), BF16),
        probs_v=((samples, heads, n, n), F32),
        w_qkv_v=((3 * lanes, D), BF16),
        w_merge_v=((lanes, D), BF16),
        grid_g=((heads, L, 2 * L), F32),
        early=((mp, 4, D), F32),
        late_sums=((mp, 2, D), F32),
        flat=((samples, modw), F32),
    )
    two.scratch(
        sem=dma((13,)),
        load_sem=dma((3, samples)),
        dm_send=dma((2, mp)),
        dm_recv=dma((2, mp)),
        dp_send=dma((4, dp_size)),
        dp_recv=dma((4, dp_size)),
        red_f=reduce_scratch(sz),
        red_b=reduce_scratch(sz),
        last_sems=reduce_scratch(sz)[2:],
        gat_m=gather_scratch(sz),
        gat_d=gather_scratch(sz),
        gat_o=gather_scratch(sz),
        gat_k=gather_scratch(sz),
    )
    got = two.run(
        functools.partial(block_backward, sz, heads, hd, grid_side, cols, dp_size, chunk), "block_backward", 1, 64 << 20
    )

    grads = got.z_outer if chunk else lax.psum(got.grads, "dp")
    up_grad = grads[0, :F].astype(F32).T
    down_grad = grads[1, :F].astype(F32)
    projected = jnp.concatenate([grads[0, F:], grads[1, F + local :]]).reshape(3, local, D)
    project_grad = jnp.swapaxes(projected.astype(F32), 1, 2)
    merge_grad = grads[1, F : F + local].astype(F32)

    signal_all = got.signal_g.reshape(dp_size * samples, D)
    dmod_cols = got.mod_g.reshape(dp_size * samples, wide)
    dmod_cols = lax.dynamic_slice_in_dim(dmod_cols, lax.rem(me * cols, 128), cols, 1)
    upper = lax.reduce_precision(dmod_cols, 8, 7)
    parts = jnp.concatenate([upper, dmod_cols - upper]).astype(BF16)
    modulate_grad = lax.dot_general(
        parts,
        jnp.concatenate([signal_all, signal_all]),
        (((0,), (0,)), ((), ())),
        preferred_element_type=F32,
    ).T
    modulate_bias_grad = jnp.sum(dmod_cols, axis=0)
    biases = jnp.sum(got.bias_g, axis=0)
    proj_bias = biases[3, : 3 * lanes].reshape(3, heads, HEAD_PAD)[:, :, :hd].reshape(3, local)
    proj_bias = jnp.stack([proj_bias[0], proj_bias[2]])
    table_grad = jnp.sum(got.table_g, axis=0).reshape(heads, 2 * grid_side, 2 * grid_side)
    table_grad = table_grad[:, :offsets, :offsets].reshape(heads, offsets * offsets)
    block_out = got.out
    if sz.per > 1:
        block_out = jnp.take(block_out, order, axis=1)
    return (
        block_out,
        got.patch_g.astype(F32),
        project_grad,
        proj_bias,
        merge_grad,
        biases[2],
        up_grad,
        biases[0, :F],
        down_grad,
        biases[1],
        modulate_grad,
        modulate_bias_grad,
        table_grad,
    )


def solution(mesh):
    placed = (
        P("dp", None, None),
        P("dp", None),
        P("dp"),
        P("dp", None),
        P("dp", None, None),
        P(None, None, "mp"),
        P(None, "mp"),
        P("mp", None),
        P(),
        P(None, "mp"),
        P("mp"),
        P("mp", None),
        P(),
        P(None, "mp"),
        P("mp"),
        P("mp", None),
    )
    return jax.shard_map(
        body,
        mesh=mesh,
        in_specs=placed,
        out_specs=(
            P("dp", None, None),
            P("dp", None, None),
            P(None, None, "mp"),
            P(None, "mp"),
            P("mp", None),
            P(),
            P(None, "mp"),
            P("mp"),
            P("mp", None),
            P(),
            P(None, "mp"),
            P("mp"),
            P("mp", None),
        ),
        check_vma=False,
    )
```

```python
import functools
import math
from types import SimpleNamespace

import jax
import jax.numpy as jnp
import numpy as np
from jax import lax
from jax.experimental import pallas as pl
from jax.experimental.pallas import tpu as pltpu
from jax.sharding import PartitionSpec as P

MESH = pl.DeviceIdType.MESH
F32 = jnp.float32
BF16 = jnp.bfloat16
EPSILON = 1e-06
MASKED = -1000000000.0
GELU_C = math.sqrt(2.0 / math.pi)
GELU_A = 0.044715
VMEM = pl.BlockSpec(memory_space=pltpu.VMEM)
HEAD_PAD = 128


def dot(a, b, ca=1, cb=0):
    return lax.dot_general(a, b, (((ca,), (cb,)), ((), ())), preferred_element_type=F32)


def bit_of(value, k):
    return lax.rem(value // (1 << k), 2)


def flip(value, mask):
    out = value
    k = 0
    while (1 << k) <= mask:
        if mask & (1 << k):
            out = out + (1 << k) * (1 - 2 * bit_of(value, k))
        k += 1
    return out


def xor(a, b, bits):
    out = 0
    for k in range(bits):
        out = out + (1 << k) * lax.rem(bit_of(a, k) + bit_of(b, k), 2)
    return out


class Sizes:
    def __init__(self, mp, samples, slots, width):
        self.mp, self.samples, self.slots, self.width = mp, samples, slots, width
        self.bits = mp.bit_length() - 1
        self.rows = samples * slots
        self.block = self.rows // mp
        self.half = self.block // 2
        self.per = self.block and slots // self.block
        rest = [1 << k for k in range(1, self.bits)]
        self.orders = (rest, rest[::-1])
        self.sends = {}
        count = 0
        for h in range(2):
            live = list(range(0, mp, 2))
            for t, bit in enumerate(self.orders[h]):
                moved = [d for d in live if d & bit]
                live = [d for d in live if not d & bit]
                self.sends[h, t] = [(d, bit, count + i) for i, d in enumerate(moved)]
                count += len(moved)
        self.steps = len(rest)
        self.far = count
        self.near = mp // 2
        self.fast = self.steps == 2 and self.per == 1


def my_index():
    return lax.axis_index("dp"), lax.axis_index("mp")


def enter(sz):
    dp, me = my_index()
    barrier = pltpu.get_barrier_semaphore()
    for d in range(1, sz.mp):
        pl.semaphore_signal(barrier, inc=1, device_id=(dp, flip(me, d)), device_id_type=MESH)
    pl.semaphore_wait(barrier, sz.mp - 1)


def rows_of(ref, start, size):
    return ref.at[pl.ds(start, size)]


class Reduce:
    def __init__(self, sz, part, refs):
        self.sz, self.part = sz, part
        self.near_buf, self.far_buf, self.near_send, self.near_recv, self.far_send, self.far_recv = refs
        self.dp, self.me = my_index()

    def near_copy(self, pair):
        b = self.sz.block
        return pltpu.make_async_remote_copy(
            src_ref=rows_of(self.part, (2 * pair + 1) * b, b),
            dst_ref=rows_of(self.near_buf, pair * b, b),
            send_sem=self.near_send.at[pair],
            recv_sem=self.near_recv.at[pair],
            device_id=(self.dp, flip(self.me, 1)),
            device_id_type=MESH,
        )

    def far_copy(self, h, d, bit, i):
        b, hb = self.sz.block, self.sz.half
        return pltpu.make_async_remote_copy(
            src_ref=rows_of(self.part, d * b + h * hb, hb),
            dst_ref=rows_of(self.far_buf, i * hb, hb),
            send_sem=self.far_send.at[i],
            recv_sem=self.far_recv.at[i],
            device_id=(self.dp, flip(self.me, bit)),
            device_id_type=MESH,
        )

    def add(self, start, buf, at, size):
        a = self.part[pl.ds(start, size), :].astype(F32) + buf[pl.ds(at, size), :].astype(F32)
        self.part[pl.ds(start, size), :] = a.astype(BF16)

    def near_add(self, pair):
        b = self.sz.block
        self.near_copy(pair).wait()
        self.add(2 * pair * b, self.near_buf, pair * b, b)

    def send(self, h, d):
        for t in range(self.sz.steps):
            for m in self.sz.sends[h, t]:
                if m[0] == d:
                    self.far_copy(h, *m).start()

    def take(self, h, d, bit, i, add=True):
        b, hb = self.sz.block, self.sz.half
        self.far_copy(h, d, bit, i).wait()
        if add:
            self.add((d - bit) * b + h * hb, self.far_buf, i * hb, hb)

    def after(self, k):
        if k == 0:
            self.send(0, 6)
            self.send(1, 6)
        if k == 1:
            self.send(0, 2)
        if k == 2:
            self.send(1, 4)
            self.take(1, *self.sz.sends[1, 0][1])
            self.send(1, 2)
            self.take(0, *self.sz.sends[0, 0][1])
            self.send(0, 4)

    def close(self):
        sz = self.sz
        if sz.fast:
            for h in range(2):
                for t in range(2):
                    for m in sz.sends[h, t]:
                        if m[0] == m[1]:
                            self.take(h, *m, add=False)
            return

        def one(i, carry):
            self.near_add(sz.near - 1 - i)
            return carry

        lax.fori_loop(0, sz.near, one, 0)
        for t in range(sz.steps):
            for h in range(2):
                for m in sz.sends[h, t]:
                    self.far_copy(h, *m).start()
            for h in range(2):
                for m in sz.sends[h, t]:
                    self.take(h, *m, add=t < sz.steps - 1)

    def own_sum(self):
        sz, hb = self.sz, self.sz.half
        out = []
        for h in range(2):
            total = self.part[h * hb : (h + 1) * hb, :].astype(F32)
            for t in range(0 if sz.fast else sz.steps - 1, sz.steps):
                for d, bit, i in sz.sends[h, t]:
                    if d == bit:
                        total = total + self.far_buf[i * hb : (i + 1) * hb, :].astype(F32)
            out.append(total)
        return jnp.concatenate(out, axis=0)


class Gather:
    def __init__(self, sz, out, sems):
        self.sz, self.out = sz, out
        self.near_send, self.near_recv, self.far_send, self.far_recv = sems
        self.dp, self.me = my_index()
        self.first, self.stages = [], []
        if sz.fast:
            x, y = sz.orders[0]
            self.first = [(1, 0, x, 0), (0, 0, y, 1), (0, 0, x, 2), (1, 0, y, 3)]
            on = {0: (1, x, y, 5), 1: (0, y, x, 4)}
            self.stages = [
                [(self.first[1], [on[1]]), (self.first[0], [on[0]])],
                [(self.first[2], []), (self.first[3], [])],
                [(on[1], []), (on[0], [])],
            ]
        else:
            count, plan = 0, {}
            for h in range(2):
                have = [0]
                for t, bit in enumerate(sz.orders[h][::-1]):
                    plan[h, t] = [(h, d, bit, count + i) for i, d in enumerate(have)]
                    count += len(have)
                    have = have + [d | bit for d in have]
            self.first = plan[0, 0] + plan[1, 0]
            for t in range(sz.steps):
                stage = []
                for h in range(2):
                    later = plan[h, t + 1] if t + 1 < sz.steps else []
                    for k, m in enumerate(plan[h, t]):
                        stage.append((m, later if k == len(plan[h, t]) - 1 else []))
                self.stages.append(stage)

    def near_copy(self, d, h):
        b, hb = self.sz.block, self.sz.half
        return pltpu.make_async_remote_copy(
            src_ref=rows_of(self.out, d * b + h * hb, hb),
            dst_ref=rows_of(self.out, (d + 1) * b + h * hb, hb),
            send_sem=self.near_send.at[d + h],
            recv_sem=self.near_recv.at[d + h],
            device_id=(self.dp, flip(self.me, 1)),
            device_id_type=MESH,
        )

    def far_copy(self, h, d, bit, i):
        b, hb = self.sz.block, self.sz.half
        return pltpu.make_async_remote_copy(
            src_ref=rows_of(self.out, d * b + h * hb, hb),
            dst_ref=rows_of(self.out, (d + bit) * b + h * hb, hb),
            send_sem=self.far_send.at[i],
            recv_sem=self.far_recv.at[i],
            device_id=(self.dp, flip(self.me, bit)),
            device_id_type=MESH,
        )

    def start(self):
        for m in self.first:
            self.far_copy(*m).start()
        for h in range(2):
            self.near_copy(0, h).start()

    def step(self, t):
        for m, later in self.stages[t]:
            self.far_copy(*m).wait()
            for n in later:
                self.far_copy(*n).start()
            h, d, bit, _ = m
            self.near_copy(d + bit, h).start()

    def finish(self, first=0):
        for d in range(first, self.sz.mp, 2):
            for h in range(2):
                self.near_copy(d, h).wait()


def reduce_scratch(sz):
    return [
        pltpu.VMEM((sz.near * sz.block, sz.width), BF16),
        pltpu.VMEM((sz.far * sz.half, sz.width), BF16),
        pltpu.SemaphoreType.DMA((sz.near,)),
        pltpu.SemaphoreType.DMA((sz.near,)),
        pltpu.SemaphoreType.DMA((sz.far,)),
        pltpu.SemaphoreType.DMA((sz.far,)),
    ]


def gather_scratch(sz):
    return [
        pltpu.SemaphoreType.DMA((sz.mp,)),
        pltpu.SemaphoreType.DMA((sz.mp,)),
        pltpu.SemaphoreType.DMA((sz.far,)),
        pltpu.SemaphoreType.DMA((sz.far,)),
    ]


def slot_loop(sz, body, red, extra=None):
    if sz.fast:

        def one(i, carry):
            q = i // 2
            pair = 2 * (1 - lax.rem(q, 2)) + 1 - q // 2
            other = 1 - lax.rem(i, 2)
            body(2 * pair + other)

            @pl.when(other == 1)
            def _():
                red.near_copy(pair).start()

            @pl.when(other == 0)
            def _():
                red.near_add(pair)

            for k in range(3):
                pl.when(i == 2 * k + 1)(functools.partial(red.after, k))
            if extra is not None:
                extra(i)
            return carry

    else:
        pairs = sz.per // 2

        def one(i, carry):
            slot = sz.samples - 1 - i
            body(slot)
            for p in range(pairs):
                red.near_copy(slot * pairs + p).start()
            return carry

    lax.fori_loop(0, sz.samples, one, 0)


def layer_stats(values):
    centre = jnp.mean(values, axis=-1, keepdims=True)
    shifted = values - centre
    spread = jnp.mean(shifted * shifted, axis=-1, keepdims=True)
    inv_std = lax.rsqrt(spread + EPSILON)
    return shifted * inv_std, inv_std


def layer_back(gradient, normed, inv_std):
    mean_grad = jnp.mean(gradient, axis=-1, keepdims=True)
    mean_mix = jnp.mean(gradient * normed, axis=-1, keepdims=True)
    return inv_std * (gradient - mean_grad - normed * mean_mix)


def pick_rows(ids_ref, s, count):
    ids = ids_ref[pl.ds(s, 1), :]
    return (lax.broadcasted_iota(jnp.int32, (count, ids.shape[1]), 0) == ids).astype(F32).astype(BF16)


def live_column(sel):
    ones = jnp.ones((sel.shape[0], 128), BF16)
    return dot(sel, ones, 0, 0)[:, 0:1]


class Call:
    def __init__(self):
        self.args, self.specs, self.outs, self.out_specs, self.scratch_of = {}, [], {}, [], {}

    def arg(self, space=pltpu.VMEM, **values):
        self.args.update(values)
        self.specs += [pl.BlockSpec(memory_space=space)] * len(values)

    def out(self, space=pltpu.VMEM, **results):
        for name, (shape, dtype) in results.items():
            self.outs[name] = jax.ShapeDtypeStruct(shape, dtype)
            self.out_specs.append(pl.BlockSpec(memory_space=space))

    def scratch(self, **buffers):
        self.scratch_of.update(buffers)

    def vmem(self, **buffers):
        for name, (shape, dtype) in buffers.items():
            self.scratch_of[name] = pltpu.VMEM(shape, dtype)

    def run(self, kernel, name, cid, limit):
        flat = []
        for value in self.scratch_of.values():
            flat += value if isinstance(value, list) else [value]

        def inner(*refs):
            r, refs = SimpleNamespace(), list(refs)
            for key in list(self.args) + list(self.outs):
                setattr(r, key, refs.pop(0))
            for key, value in self.scratch_of.items():
                count = len(value) if isinstance(value, list) else 0
                setattr(r, key, [refs.pop(0) for _ in range(count)] if count else refs.pop(0))
            kernel(r)

        got = pl.pallas_call(
            inner,
            out_shape=list(self.outs.values()),
            in_specs=self.specs,
            out_specs=self.out_specs,
            scratch_shapes=flat,
            name=name,
            compiler_params=pltpu.CompilerParams(vmem_limit_bytes=limit)
            if cid is None
            else pltpu.CompilerParams(collective_id=cid, has_side_effects=True, vmem_limit_bytes=limit),
        )(*self.args.values())
        return SimpleNamespace(**dict(zip(self.outs, got)))


def attention_forward(sz, heads, hd, grid_side, cols, r):
    dp, me = my_index()
    mine = me // sz.per
    sbits = sz.samples.bit_length() - 1
    D, n, L = sz.width, sz.slots, grid_side * grid_side
    lanes = heads * HEAD_PAD
    red = Reduce(sz, r.part, r.red)
    mod_buf, mod_wide, modv, vec = r.mod_buf, r.mod_wide, r.modv, r.vec
    wide = mod_buf.shape[2]
    sem = r.sem

    load_mod = pltpu.make_async_copy(r.w_mod, r.w_mod_v, sem.at[0])
    load_mod.start()

    def load_patches(i, slot):
        return pltpu.make_async_copy(r.patches.at[xor(mine, slot, sbits)], r.patches_v.at[slot], r.load_sem.at[i])

    def start_load(slot, carry):
        load_patches(slot, slot).start()
        return carry

    lax.fori_loop(0, sz.samples, start_load, 0)
    cond = r.condition[...].astype(F32)
    signal = (cond / (1.0 + jnp.exp(-cond))).astype(BF16)
    mod_buf[me] = jnp.zeros((sz.samples, wide), F32)
    load_mod.wait()
    mod_buf[me, :, 0:cols] = dot(signal, r.w_mod_v[...], 1, 1) + vec[5:6, 0:cols]
    enter(sz)

    def mod_copy(d, slot):
        return pltpu.make_async_remote_copy(
            src_ref=mod_buf.at[slot],
            dst_ref=mod_buf.at[slot],
            send_sem=r.mod_send.at[d],
            recv_sem=r.mod_recv.at[d],
            device_id=(dp, flip(me, d)),
            device_id_type=MESH,
        )

    for d in range(1, sz.mp):
        mod_copy(d, me).start()

    w_qkv, w_merge = r.w_qkv_v, r.w_merge_v
    pad_rows = jnp.zeros((HEAD_PAD - hd, D), F32)
    for h in range(heads):
        for c in range(3):
            piece = r.w_in[c].astype(F32)[h * hd : (h + 1) * hd]
            w_qkv[c * lanes + h * HEAD_PAD : c * lanes + (h + 1) * HEAD_PAD, :] = jnp.concatenate(
                [piece, pad_rows], axis=0
            ).astype(BF16)
        piece = r.w_out[...].astype(F32)[h * hd : (h + 1) * hd]
        w_merge[h * HEAD_PAD : (h + 1) * HEAD_PAD, :] = jnp.concatenate([piece, pad_rows], axis=0).astype(BF16)
    save = [
        pltpu.make_async_copy(w_qkv, r.w_qkv, sem.at[1]),
        pltpu.make_async_copy(w_merge, r.w_merge, sem.at[2]),
    ]
    for copy in save:
        copy.start()

    bias_full = r.bias_full
    span = r.table.shape[1]
    for h in range(heads):
        line = r.table[h : h + 1, :]
        strip = jnp.concatenate([line] + [pltpu.roll(line, span - c, 1) for c in range(1, grid_side)], axis=0)
        for row in range(grid_side):
            rolled = pltpu.roll(strip, span - row * 2 * grid_side, 1) if row else strip
            bias_full[h, row * grid_side : (row + 1) * grid_side, :] = rolled[:, : 2 * L].astype(BF16)

    normed, kept_own = r.normed, r.kept_v

    def norm_one(slot, carry):
        load_patches(slot, slot).wait()
        sel = pick_rows(r.pos, xor(mine, slot, sbits), L)
        kept = dot(sel, r.patches_v[slot], 0, 0)
        value, _ = layer_stats(kept)
        normed[pl.ds(slot * n, n), :] = value

        @pl.when(slot == 0)
        def _():
            kept_own[...] = kept[: sz.block]

        return carry

    lax.fori_loop(0, sz.samples, norm_one, 0)
    save_kept = pltpu.make_async_copy(kept_own, r.kept, sem.at[3])
    save_kept.start()

    for d in range(1, sz.mp):
        mod_copy(d, me).wait_send()
        mod_copy(d, flip(me, d)).wait_recv()
    mod_wide[...] = jnp.zeros_like(mod_wide)
    for m in range(sz.mp):
        base = m * cols // 128 * 128
        phase = m * cols - base
        piece = mod_buf[m]
        if phase:
            piece = pltpu.roll(piece, phase, 1)
        mod_wide[:, base : base + wide] += piece
    modv[...] = mod_wide[:, : 6 * D]

    factor = hd ** (-0.5)
    stores = [(r.attn_in_v, r.attn_in), (r.qkv_v, r.qkv), (r.att_v, r.att)]

    def save_slot(i, slot):
        at = pl.ds(slot * n, n)
        copies = [
            pltpu.make_async_copy(a.at[at], b.at[at], r.save_sem.at[k, slot]) for k, (a, b) in enumerate(stores)
        ]
        copies.append(pltpu.make_async_copy(r.probs_v.at[slot], r.probs.at[slot], r.save_sem.at[3, slot]))
        return copies

    def body(slot):
        s = xor(mine, slot, sbits)
        at = pl.ds(slot * n, n)
        shift = modv[pl.ds(s, 1), 0:D]
        scale = modv[pl.ds(s, 1), D : 2 * D]
        entry = (normed[at, :] * (1.0 + scale) + shift).astype(BF16)
        r.attn_in_v[at, :] = entry
        proj = dot(entry, w_qkv[...], 1, 1)
        qs = (proj[:, :lanes] + vec[0:1, :lanes]).astype(BF16)
        ks = proj[:, lanes : 2 * lanes].astype(BF16)
        vs = (proj[:, 2 * lanes :] + vec[1:2, :lanes]).astype(BF16)
        r.qkv_v[at, 0:lanes] = qs
        r.qkv_v[at, lanes : 2 * lanes] = ks
        r.qkv_v[at, 2 * lanes :] = vs
        sel = pick_rows(r.pos, s, L)
        sel_wide = pick_rows(r.pos_wide, s, 2 * L)
        live = r.pos[pl.ds(s, 1), :] >= 0
        outs = []
        for h in range(heads):
            cut = slice(h * HEAD_PAD, (h + 1) * HEAD_PAD)
            bias = dot(dot(sel, bias_full[h], 0, 0).astype(BF16), sel_wide)
            scores = jnp.where(live, dot(qs[:, cut], ks[:, cut], 1, 1) * factor + bias, MASKED)
            top = jnp.max(scores, axis=-1, keepdims=True)
            e = jnp.exp(scores - top)
            p = e / jnp.sum(e, axis=-1, keepdims=True)
            r.probs_v[slot, h] = p
            outs.append(dot(p.astype(BF16), vs[:, cut]).astype(BF16))
        joined = jnp.concatenate(outs, axis=1) if heads > 1 else outs[0]
        r.att_v[at, :] = joined
        r.part[at, :] = dot(joined, w_merge[...]).astype(BF16)
        for copy in save_slot(0, slot):
            copy.start()

    slot_loop(sz, body, red)
    red.close()
    result = red.own_sum() + vec[2:3, :D]
    r.res_v[...] = result
    hidden = kept_own[...] + modv[pl.ds(mine, 1), 2 * D : 3 * D] * result
    r.hidden_v[...] = hidden
    value, _ = layer_stats(hidden)
    shift = modv[pl.ds(mine, 1), 3 * D : 4 * D]
    scale = modv[pl.ds(mine, 1), 4 * D : 5 * D]
    r.mlp_v[...] = (value * (1.0 + scale) + shift).astype(BF16)
    save_own = [
        pltpu.make_async_copy(r.res_v, r.res, sem.at[4]),
        pltpu.make_async_copy(r.hidden_v, r.hidden, sem.at[5]),
        pltpu.make_async_copy(r.mlp_v, r.mlp, sem.at[6]),
    ]
    for copy in save_own:
        copy.start()

    def wait_slot(slot, carry):
        for copy in save_slot(0, slot):
            copy.wait()
        return carry

    lax.fori_loop(0, sz.samples, wait_slot, 0)
    for copy in save + save_own + [save_kept]:
        copy.wait()


class Line:
    def __init__(self, r, chunk):
        self.r, self.chunk = r, chunk
        self.g, self.outer_buf, self.inner_buf = r.grads, r.z_outer, r.z_inner
        self.count = self.g.shape[1] // chunk
        self.dp, self.me = my_index()
        self.is_inner = (self.dp == 1) | (self.dp == 2)
        self.is_outer = (self.dp == 0) | (self.dp == 3)
        self.step_to = 1 + self.dp // 3
        self.back_to = (self.dp - 1) * 3
        self.other = 3 - self.dp
        self.mine = 2 - self.dp
        self.passed = self.dp - 1

    def rows(self, k):
        return pl.ds(k * self.chunk, self.chunk)

    def copy(self, src, dst, send, recv, to):
        return pltpu.make_async_remote_copy(
            src_ref=src, dst_ref=dst, send_sem=send, recv_sem=recv, device_id=(to, self.me), device_id_type=MESH
        )

    def out_copy(self, j, k):
        return self.copy(
            self.g.at[j, self.rows(k)], self.outer_buf.at[j, self.rows(k)],
            self.r.zs.at[j, k], self.r.zo.at[j, k], self.step_to,
        )

    def in_copy(self, k):
        return self.copy(
            self.g.at[self.passed, self.rows(k)], self.inner_buf.at[self.rows(k)],
            self.r.zf.at[k], self.r.zi.at[k], self.other,
        )

    def total_copy(self, j, k, which, to):
        return self.copy(
            self.outer_buf.at[j, self.rows(k)], self.outer_buf.at[j, self.rows(k)],
            self.r.zt.at[which, k], self.r.zr.at[j, k], to,
        )

    def begin(self, halves, k0, k1):
        @pl.when(self.is_outer)
        def _():
            def one(k, carry):
                for j in halves:
                    self.out_copy(j, k).start()
                return carry

            lax.fori_loop(k0, k1, one, 0)

    def add(self, to, j, k, more):
        def one(i, carry):
            at = pl.ds(k * self.chunk + i * 16, 16)
            v = self.g[j, at, :].astype(F32) + self.outer_buf[j, at, :].astype(F32)
            if more:
                v = v + self.inner_buf[at, :].astype(F32)
            to[j, at, :] = v.astype(BF16)
            return carry

        lax.fori_loop(0, self.chunk // 16, one, 0)

    def stage(self, number, j, k):
        if number == 1:

            @pl.when(self.passed == j)
            def _():
                self.out_copy(j, k).wait_recv()
                self.add(self.g, j, k, False)
                self.in_copy(k).start()

        elif number == 2:

            @pl.when(self.mine == j)
            def _():
                self.out_copy(j, k).wait_recv()
                self.in_copy(k).wait_recv()
                self.add(self.outer_buf, j, k, True)
                self.total_copy(j, k, 0, self.other).start()
                self.total_copy(j, k, 1, self.back_to).start()

        else:

            @pl.when(self.passed == j)
            def _():
                self.in_copy(k).wait_send()
                self.total_copy(j, k, 0, self.other).wait_recv()
                self.total_copy(j, k, 2, self.back_to).start()

    def finish(self):
        @pl.when(self.is_inner)
        def _():
            def one(k, carry):
                self.total_copy(self.mine, k, 0, self.other).wait_send()
                self.total_copy(self.mine, k, 1, self.back_to).wait_send()
                self.total_copy(self.passed, k, 2, self.back_to).wait_send()
                return carry

            lax.fori_loop(0, self.count, one, 0)

        @pl.when(self.is_outer)
        def _():
            def one(k, carry):
                for j in range(2):
                    self.out_copy(j, k).wait_send()
                    self.total_copy(j, k, 0, self.step_to).wait_recv()
                return carry

            lax.fori_loop(0, self.count, one, 0)


def block_backward(sz, heads, hd, grid_side, cols, dp_size, chunk, r):
    dp, me = my_index()
    mine = me // sz.per
    sbits = sz.samples.bit_length() - 1
    D, n, L = sz.width, sz.slots, grid_side * grid_side
    lanes = heads * HEAD_PAD
    local = heads * hd
    F = r.w_up_v.shape[0]
    block = sz.block
    vec, modv = r.vec, r.modv
    fwd = Reduce(sz, r.part_f, r.red_f)
    bwd = Reduce(sz, r.part_b, r.red_b)
    last = Reduce(sz, r.part_b, r.red_b[:2] + r.last_sems)
    gat_m = Gather(sz, r.mlp_v, r.gat_m)
    gat_d = Gather(sz, r.d_attn, r.gat_d)
    gat_o = Gather(sz, r.part_f, r.gat_o)
    gat_k = Gather(sz, r.mlp_v, r.gat_k)
    line = Line(r, chunk) if chunk else None
    grads = r.grads
    sem = r.sem

    per_half, per_local = (F // 2 // chunk, local // chunk) if chunk else (0, 0)
    marks = [0, per_half, 2 * per_half, 2 * per_half + per_local, 2 * per_half + 2 * per_local]
    following = {(number, j): 0 for number in (1, 2, 3) for j in range(2)}

    def tick(*steps):
        if line is None:
            return
        for number, j, count in steps:
            k0 = following[number, j]
            k1 = min(k0 + count, marks[4])
            assert number == 1 or k1 <= following[number - 1, j]
            following[number, j] = k1
            if k1 - k0 == 1:
                line.stage(number, j, k0)
            elif k1 > k0:

                def one(k, carry, number=number, j=j):
                    line.stage(number, j, k)
                    return carry

                lax.fori_loop(k0, k1, one, 0)

    def begin(group, *halves):
        if line is not None:
            line.begin(halves or (0, 1), marks[group], marks[group + 1])

    def ticks_at(i, plan):
        if line is not None:
            for when, steps in plan.items():
                pl.when(i == when)(lambda steps=steps: tick(*steps))

    load_up = pltpu.make_async_copy(r.w_up, r.w_up_v, sem.at[0])
    load_down = pltpu.make_async_copy(r.w_down, r.w_down_v, sem.at[1])
    load_up.start()
    load_down.start()

    load_own = pltpu.make_async_copy(r.mlp, r.mlp_v.at[pl.ds(0, block)], sem.at[12])
    load_own.start()

    def load_cot(slot):
        at = pl.ds(slot * n, n)
        return pltpu.make_async_copy(r.cot.at[xor(mine, slot, sbits)], r.d_mlp.at[at], r.load_sem.at[1, slot])

    def start_cot(slot, carry):
        load_cot(slot).start()
        return carry

    lax.fori_loop(0, sz.samples, start_cot, 0)
    loads = [
        pltpu.make_async_copy(r.cot.at[mine, pl.ds(0, block)], r.cot_own, sem.at[2]),
        pltpu.make_async_copy(r.hidden, r.hidden_v, sem.at[3]),
        pltpu.make_async_copy(r.res, r.res_v, sem.at[4]),
    ]
    late = [
        pltpu.make_async_copy(r.qkv, r.qkv_v, sem.at[6]),
        pltpu.make_async_copy(r.probs, r.probs_v, sem.at[7]),
        pltpu.make_async_copy(r.w_qkv, r.w_qkv_v, sem.at[9]),
        pltpu.make_async_copy(r.w_merge, r.w_merge_v, sem.at[10]),
    ]
    for copy in loads + late:
        copy.start()
    load_attn = pltpu.make_async_copy(r.attn_in, r.d_mlp, sem.at[11])
    load_kept = pltpu.make_async_copy(r.kept, r.res_v, sem.at[5])
    load_att = pltpu.make_async_copy(r.att, r.act.at[:, pl.ds(0, lanes)], sem.at[8])

    barrier = pltpu.get_barrier_semaphore()
    for d in range(1, sz.mp):
        pl.semaphore_signal(barrier, inc=1, device_id=(dp, flip(me, d)), device_id_type=MESH)
    for e in range(1, dp_size):
        pl.semaphore_signal(barrier, inc=1, device_id=(lax.rem(dp + e, dp_size), me), device_id_type=MESH)
    pl.semaphore_wait(barrier, sz.mp + dp_size - 2)
    load_own.wait()
    gat_m.start()
    load_up.wait()
    load_down.wait()
    w_up, w_down, mlp = r.w_up_v, r.w_down_v, r.mlp_v
    act, d_pre, d_mlp, slope = r.act, r.d_pre, r.d_mlp, r.slope

    up_bg, down_bg = r.bias_g.at[dp, 0:1], r.bias_g.at[dp, 1:2]
    merge_bg, proj_bg = r.bias_g.at[dp, 2:3], r.bias_g.at[dp, 3:4]
    r.bias_g[dp] = jnp.zeros(r.bias_g.shape[1:], F32)
    cond = r.condition[...].astype(F32)
    r.signal_g[dp] = (cond / (1.0 + jnp.exp(-cond))).astype(BF16)
    shared = [r.bias_g, r.table_g, r.mod_g, r.signal_g]

    def dp_copy(k, e, slot):
        return pltpu.make_async_remote_copy(
            src_ref=shared[k].at[slot],
            dst_ref=shared[k].at[slot],
            send_sem=r.dp_send.at[k, e],
            recv_sem=r.dp_recv.at[k, e],
            device_id=(lax.rem(dp + e, dp_size), me),
            device_id_type=MESH,
        )

    def share(k):
        for e in range(1, dp_size):
            dp_copy(k, e, dp).start()

    share(3)

    def forward(slot, wide):
        at = pl.ds(slot * n, wide * n)
        v = dot(mlp[at, :], w_up[...], 1, 1) + vec[3:4, :F]
        square = v * v
        t = jnp.tanh(GELU_C * (v + GELU_A * v * square))
        active = (0.5 * v * (1.0 + t)).astype(BF16)
        act[at, :] = active
        slope[at, :] = 0.5 * (1.0 + t) + 0.5 * v * (1.0 - t * t) * (GELU_C * (1.0 + 3.0 * GELU_A * square))
        r.part_f[at, :] = dot(active, w_down[...]).astype(BF16)

    def output_grad(slot, carry):
        at = pl.ds(slot * n, n)
        s = xor(mine, slot, sbits)
        load_cot(slot).wait()
        gate = modv[pl.ds(s, 1), 5 * D : 6 * D]
        live = live_column(pick_rows(r.pos, s, L))
        dm = (gate * (d_mlp[at, :].astype(F32) * live)).astype(BF16)
        d_mlp[at, :] = dm
        down_bg[...] += jnp.sum(dm.astype(F32), axis=0, keepdims=True)
        return carry

    if sz.fast:
        def two_slots(i, carry):
            @pl.when(i == 1)
            def _():
                lax.fori_loop(0, sz.samples, output_grad, 0)
                gat_m.step(0)
                gat_m.step(1)

            @pl.when(i == 3)
            def _():
                gat_m.step(2)

            for h in range(2):
                gat_m.near_copy(2 * i, h).wait()
            forward(2 * i, 2)
            fwd.near_copy(i).start()

            @pl.when(i > 0)
            def _():
                fwd.near_add(i - 1)

            pl.when(i == 2)(functools.partial(fwd.send, 0, 2))
            pl.when(i == 3)(functools.partial(fwd.send, 1, 4))
            return carry

        lax.fori_loop(0, 4, two_slots, 0)
    else:
        for t in range(len(gat_m.stages)):
            gat_m.step(t)
        gat_m.finish()
        lax.fori_loop(0, sz.samples, output_grad, 0)
        slot_loop(sz, lambda slot: forward(slot, 1), fwd)

    def wide_grad(left, right, base):
        at = 0
        while at < F:
            size = min(256, F - at)
            value = dot(left[:, at : at + size], right[...], 0, 0).astype(BF16)
            cut = min(max(F // 2 - at, 0), size)
            if cut:
                grads[0, base + at : base + at + cut, :] = value[:cut]
            if cut < size:
                start = base + at + cut - F // 2
                grads[1, start : start + size - cut, :] = value[cut:]
            at += size

    wide_grad(act, d_mlp, 0)
    begin(0)

    def backward(slot):
        at = pl.ds(slot * n, n)
        dpre = (dot(d_mlp[at, :], w_down[...], 1, 1) * slope[at, :]).astype(BF16)
        d_pre[at, :] = dpre
        up_bg[:, :F] += jnp.sum(dpre.astype(F32), axis=0, keepdims=True)
        r.part_b[at, :] = dot(dpre, w_up[...]).astype(BF16)

    plan = {
        4: [(1, 0, 1), (1, 1, 1)],
        6: [(1, 1, 1), (2, 0, 1), (2, 1, 1)],
        7: [(1, 0, 1)],
    }

    def bwd_extra(i):
        ticks_at(i, plan)

        @pl.when(i == 5)
        def _():
            fwd.near_add(3)
            fwd.send(0, 6)
            fwd.send(1, 6)

    slot_loop(sz, backward, bwd, bwd_extra)
    load_attn.start()
    load_att.start()
    wide_grad(d_pre, mlp, F // 2)
    begin(1)
    tick((1, 1, 1), (2, 1, 1))
    for copy in loads:
        copy.wait()
    normed2, inv2 = layer_stats(r.hidden_v[...])
    r.normed_v[...] = normed2
    bwd.close()
    tick((1, 0, 1), (1, 1, 1), (2, 0, 1), (2, 1, 1), (3, 0, 1), (3, 1, 2))

    mrow = pl.ds(mine, 1)
    live = live_column(pick_rows(r.pos, mine, L)[:, :block])
    d_out = r.cot_own[...].astype(F32) * live
    d_mlp_in = bwd.own_sum()
    g = d_mlp_in * (1.0 + modv[mrow, 4 * D : 5 * D])
    dh = d_out + layer_back(g, r.normed_v[...], inv2)
    r.dh_v[...] = dh
    r.d_attn[:block, :] = (modv[mrow, 2 * D : 3 * D] * dh).astype(BF16)
    gat_d.start()
    tick((1, 0, 1))

    early, late_sums = r.early, r.late_sums
    early[me, 0:1, :] = jnp.sum(dh * r.res_v[...], axis=0, keepdims=True)
    load_kept.start()
    early[me, 1:2, :] = jnp.sum(d_mlp_in, axis=0, keepdims=True)
    early[me, 2:3, :] = jnp.sum(d_mlp_in * r.normed_v[...], axis=0, keepdims=True)

    def finish_out():
        fwd.close()
        live = live_column(pick_rows(r.pos, mine, L)[:, :block])
        mlp_out = fwd.own_sum() + vec[4:5, :D]
        early[me, 3:4, :] = jnp.sum(mlp_out * (r.cot_own[...].astype(F32) * live), axis=0, keepdims=True)
        out_own = (r.hidden_v[...] + modv[mrow, 5 * D : 6 * D] * mlp_out) * live
        r.part_f[:block, :] = out_own.astype(BF16)

    def dm_copy(ref, k, d, slot):
        return pltpu.make_async_remote_copy(
            src_ref=ref.at[slot],
            dst_ref=ref.at[slot],
            send_sem=r.dm_send.at[k, d],
            recv_sem=r.dm_recv.at[k, d],
            device_id=(dp, flip(me, d)),
            device_id_type=MESH,
        )

    def attention_grad(c, half, at):
        if c < 3:
            full = dot(qkv[:, c * lanes : (c + 1) * lanes], d_mlp[...], 0, 0)
        else:
            full = dot(r.act[:, :lanes], r.d_attn[...], 0, 0)
        rows = [full[h * HEAD_PAD : h * HEAD_PAD + hd] for h in range(heads)]
        rows = jnp.concatenate(rows, axis=0) if heads > 1 else rows[0]
        grads[half, at : at + local, :] = rows.astype(BF16)

    for copy in late:
        copy.wait()
    factor = hd ** (-0.5)
    grid_g = r.grid_g
    grid_g[...] = jnp.zeros_like(grid_g)
    qkv, w_qkv, w_merge = r.qkv_v, r.w_qkv_v, r.w_merge_v
    def attention(slot):
        s = xor(mine, slot, sbits)
        at = pl.ds(slot * n, n)
        da = r.d_attn[at, :]
        merge_bg[...] += jnp.sum(da.astype(F32), axis=0, keepdims=True)
        d_att = dot(da, w_merge[...], 1, 1).astype(BF16)
        sel = pick_rows(r.pos, s, L)
        sel_wide = pick_rows(r.pos_wide, s, 2 * L)
        dq, dk, dv = [], [], []
        for h in range(heads):
            q = qkv[at, h * HEAD_PAD : (h + 1) * HEAD_PAD]
            k = qkv[at, lanes + h * HEAD_PAD : lanes + (h + 1) * HEAD_PAD]
            v = qkv[at, 2 * lanes + h * HEAD_PAD : 2 * lanes + (h + 1) * HEAD_PAD]
            d_a = d_att[:, h * HEAD_PAD : (h + 1) * HEAD_PAD]
            p = r.probs_v[slot, h]
            d_p = dot(d_a, v, 1, 1)
            dv.append(dot(p.astype(BF16), d_a, 0, 0).astype(BF16))
            ds = p * (d_p - jnp.sum(p * d_p, axis=-1, keepdims=True))
            dl = ds.astype(BF16)
            dq.append((dot(dl, k) * factor).astype(BF16))
            dk.append((dot(dl, q, 0, 0) * factor).astype(BF16))
            grid_g[h] += dot(dot(sel, dl).astype(BF16), sel_wide, 1, 1)
        joined = jnp.concatenate(dq + dk + dv, axis=1)
        qkv[at, :] = joined
        proj_bg[:, : 3 * lanes] += jnp.sum(joined.astype(F32), axis=0, keepdims=True)
        r.part_b[at, :] = dot(joined, w_qkv[...]).astype(BF16)

    if sz.fast:
        plan_one = {1: [(2, 0, 1), (2, 1, 1)], 2: [(1, 0, 1), (1, 1, 1), (3, 0, 1), (3, 1, 1)]}
        plan_two = {
            3: [(1, 0, 1), (1, 1, 1), (2, 0, 2), (2, 1, 1), (3, 0, 1)],
            4: [(1, 0, 1), (1, 1, 1), (3, 1, 1)],
            5: [(1, 1, 1), (2, 0, 1), (2, 1, 1), (3, 0, 1)],
            6: [(1, 0, 1), (2, 0, 1), (3, 0, 1), (3, 1, 1)],
            7: [(1, 0, 1), (1, 1, 1), (2, 1, 1), (3, 1, 1)],
        }

        def one(i, carry):
            q = i // 2
            pair = q + lax.rem(q, 2) * (q // 2) * -1 + (q // 2) * (1 - lax.rem(q, 2))
            slot = jnp.where(i < 2, i, 2 * pair + 1 - lax.rem(i, 2))

            ticks_at(i, plan_one)

            @pl.when(i == 1)
            def _():
                for h in range(2):
                    gat_d.near_copy(0, h).wait()

            @pl.when(i == 2)
            def _():
                gat_d.step(0)
                tick((2, 0, 1), (3, 0, 1))
                gat_d.step(1)
                fwd.take(1, *sz.sends[1, 0][1])
                fwd.take(0, *sz.sends[0, 0][1])
                fwd.send(1, 2)
                fwd.send(0, 4)
                tick((1, 0, 1), (1, 1, 1), (2, 1, 1), (3, 1, 1))
                for h in range(2):
                    gat_d.near_copy(2, h).wait()

            ticks_at(i, plan_two)

            @pl.when(i == 4)
            def _():
                gat_d.step(2)
                for d in (4, 6):
                    for h in range(2):
                        gat_d.near_copy(d, h).wait()

            attention(slot)

            @pl.when(i == 1)
            def _():
                last.near_copy(0).start()

            @pl.when((i > 1) & (lax.rem(i, 2) == 0))
            def _():
                last.near_copy(pair).start()

            @pl.when(i == 3)
            def _():
                last.near_add(0)
                last.near_add(1)
                last.send(0, 2)

            @pl.when(i == 6)
            def _():
                finish_out()

            @pl.when(i == 5)
            def _():
                last.near_add(3)
                last.send(0, 6)
                last.send(1, 6)

            @pl.when(i == 7)
            def _():
                last.near_add(2)
                last.after(2)

            return carry

        lax.fori_loop(0, 8, one, 0)
        tick((1, 1, 1), (2, 0, 1), (2, 1, 1), (3, 0, 1))
    else:
        for t in range(len(gat_d.stages)):
            gat_d.step(t)
        gat_d.finish()
        finish_out()
        slot_loop(sz, attention, last)

    load_attn.wait()
    load_att.wait()
    attention_grad(3, 1, F)
    begin(2, 1)
    tick((1, 0, 1), (2, 0, 1))
    attention_grad(0, 0, F)
    begin(2, 0)
    attention_grad(2, 1, F + local)
    begin(3, 1)
    attention_grad(1, 0, F + local)
    begin(3, 0)
    tick((1, 1, 1), (2, 1, 1), (3, 0, 1), (3, 1, 1))

    tables = r.table_g
    span = tables.shape[2]
    for h in range(heads):
        strip = jnp.zeros((grid_side, span), F32)
        for row in range(grid_side):
            piece = jnp.concatenate(
                [
                    grid_g[h, row * grid_side : (row + 1) * grid_side, :],
                    jnp.zeros((grid_side, span - 2 * L), F32),
                ],
                axis=1,
            )
            strip = strip + (pltpu.roll(piece, row * 2 * grid_side, 1) if row else piece)
        total_row = strip[0:1]
        for c in range(1, grid_side):
            total_row = total_row + pltpu.roll(strip[c : c + 1], c, 1)
        tables[dp, h : h + 1, :] = total_row

    share(0)
    share(1)
    load_kept.wait()
    normed1, inv1 = layer_stats(r.res_v[...])
    r.normed_v[...] = normed1
    last.close()
    tick((1, 0, 1), (1, 1, 1), (2, 0, 1), (2, 1, 1), (3, 1, 1))
    d_in = last.own_sum()
    g = d_in * (1.0 + modv[mrow, D : 2 * D])
    mlp[:block, :] = (r.dh_v[...] + layer_back(g, r.normed_v[...], inv1)).astype(BF16)
    late_sums[me, 0:1, :] = jnp.sum(d_in, axis=0, keepdims=True)
    late_sums[me, 1:2, :] = jnp.sum(d_in * r.normed_v[...], axis=0, keepdims=True)
    gat_k.start()
    tick((1, 1, 2), (3, 0, 1), (3, 1, 1))

    def out_copy(slot):
        return pltpu.make_async_copy(
            r.part_f.at[pl.ds(slot * n, n)], r.out.at[xor(mine, slot, sbits)], r.load_sem.at[0, slot]
        )

    def start_out(slot, carry):
        out_copy(slot).start()
        return carry

    def patch_copy(slot):
        return pltpu.make_async_copy(
            r.part_b.at[pl.ds(lax.rem(slot, 2) * L, L)], r.patch_g.at[xor(mine, slot, sbits)], r.load_sem.at[1, slot]
        )

    def patch(slot, carry):
        @pl.when(slot >= 2)
        def _():
            patch_copy(slot - 2).wait()

        sel = pick_rows(r.pos, xor(mine, slot, sbits), L)
        r.part_b[pl.ds(lax.rem(slot, 2) * L, L), :] = dot(sel, mlp[pl.ds(slot * n, n), :]).astype(BF16)
        patch_copy(slot).start()
        return carry

    for h in range(2):
        gat_k.near_copy(0, h).wait()
    if sz.fast:
        lax.fori_loop(0, 2, patch, 0)
    gat_k.step(0)
    for d in range(1, sz.mp):
        dm_copy(early, 0, d, me).start()
        dm_copy(late_sums, 1, d, me).start()
    gat_o.start()
    tick((2, 0, 1), (2, 1, 2), (3, 0, 1), (3, 1, 1))
    gat_k.step(1)
    tick((1, 0, 2), (1, 1, 1), (3, 0, 1), (3, 1, 1))
    if sz.fast:
        for d in (2, 4):
            for h in range(2):
                gat_k.near_copy(d, h).wait()
        lax.fori_loop(2, 6, patch, 0)
        gat_k.step(2)
        tick((1, 0, 1), (1, 1, 1), (2, 0, 1), (2, 1, 2), (3, 1, 1))
        for h in range(2):
            gat_k.near_copy(6, h).wait()
        lax.fori_loop(6, 8, patch, 0)
    else:
        for t in range(2, len(gat_k.stages)):
            gat_k.step(t)
        gat_k.finish(2)
        lax.fori_loop(0, sz.samples, patch, 0)
    for d in range(1, sz.mp):
        dm_copy(early, 0, d, me).wait_send()
        dm_copy(early, 0, d, flip(me, d)).wait_recv()
        dm_copy(late_sums, 1, d, me).wait_send()
        dm_copy(late_sums, 1, d, flip(me, d)).wait_recv()
    flat, mod_g = r.flat, r.mod_g
    flat[:, 6 * D :] = jnp.zeros((sz.samples, flat.shape[1] - 6 * D), F32)
    for s in range(sz.samples):
        for c in range(6):
            v = 0
            for p in range(sz.per):
                m = s * sz.per + p
                v = v + (late_sums[m, c : c + 1, :] if c < 2 else early[m, c - 2 : c - 1, :])
            flat[s : s + 1, c * D : (c + 1) * D] = v
    base = pl.multiple_of(me * cols // 128 * 128, 128)
    mod_g[dp] = flat[:, pl.ds(base, mod_g.shape[2])]
    share(2)
    tick((1, 1, 1), (2, 0, 1), (2, 1, 1), (3, 0, 1))
    tick((2, 0, 1), (2, 1, 1))
    gat_o.step(0)
    tick((1, 0, 1), (3, 1, 1), (3, 0, 1), (1, 0, 1))
    tick((3, 1, 1), (2, 1, 1))
    gat_o.step(1)
    tick((1, 0, 1), (3, 1, 1), (3, 0, 1), (3, 1, 1))
    tick((3, 0, 1), (2, 0, 1))
    for t in range(2, len(gat_o.stages)):
        gat_o.step(t)
    gat_o.finish()
    lax.fori_loop(0, sz.samples, start_out, 0)
    tick((2, 0, 1), (3, 0, 1), (3, 1, 1), (3, 0, 1))
    tick((2, 0, 1), (3, 0, 1))
    if line is not None:
        assert all(k == marks[4] for k in following.values()), following
    for k in range(4):
        for e in range(1, dp_size):
            dp_copy(k, e, dp).wait_send()
            dp_copy(k, e, lax.rem(dp + dp_size - e, dp_size)).wait_recv()
    for slot in range(sz.samples - 2, sz.samples):
        patch_copy(slot).wait()

    def wait_out(slot, carry):
        out_copy(slot).wait()
        return carry

    lax.fori_loop(0, sz.samples, wait_out, 0)
    if line is not None:
        line.finish()


def write_results(cols, r):
    total = r.total
    F, local = r.up.shape[0], r.merge.shape[0]
    D = total.shape[2]
    depth = r.narrow.shape[0]
    samples = r.out.shape[0]

    def out_in(s):
        return pltpu.make_async_copy(r.out.at[s], r.out_v.at[s], r.out_sem.at[0, s])

    def out_back(s):
        return pltpu.make_async_copy(r.out_v.at[s], r.block_out.at[s], r.out_sem.at[1, s])

    jobs = []
    for s in range(samples):
        jobs.append((r.patch_g.at[s], r.patch.at[s], r.patch.shape[1]))
    rows_most = r.narrow.shape[1]

    def add(half, start, to, at, count):
        while count:
            size = min(rows_most, count)
            jobs.append((total.at[half, pl.ds(start, size)], to.at[pl.ds(at, size)], size))
            start, at, count = start + size, at + size, count - size

    for half in range(2):
        add(half, 0, r.down, half * (F // 2), F // 2)
        add(half, F // 2, r.up, half * (F // 2), F // 2)
    add(0, F, r.project, 0, 2 * local)
    add(1, F + local, r.project, 2 * local, local)
    add(1, F, r.merge, 0, local)

    def load(k):
        src, _, size = jobs[k]
        return pltpu.make_async_copy(src, r.narrow.at[k % depth, pl.ds(0, size)], r.load_sem.at[k % depth])

    def save(k):
        _, dst, size = jobs[k]
        return pltpu.make_async_copy(r.wide.at[k % depth, pl.ds(0, size)], dst, r.save_sem.at[k % depth])

    for k in range(depth):
        load(k).start()
    for s in range(samples):
        out_in(s).start()

    members, _, width = r.mod_g.shape
    shift = lax.rem(lax.axis_index("mp") * cols, 128)
    dmod = jnp.concatenate([r.mod_g[m] for m in range(members)], axis=0)
    dmod = pltpu.roll(dmod, lax.rem(width - shift, width), 1)
    upper = dmod.astype(BF16)
    parts = jnp.concatenate([upper, (dmod - upper.astype(F32)).astype(BF16)], axis=0)
    signal = jnp.concatenate([r.signal_g[m].astype(F32) for m in range(members)], axis=0).astype(BF16)
    r.mod_v[...] = dot(parts, jnp.concatenate([signal, signal], axis=0), 0, 0)[:cols]
    modulate = pltpu.make_async_copy(r.mod_v, r.modulate, r.sem.at[0])
    modulate.start()
    r.mod_bias[...] = jnp.sum(dmod, axis=0, keepdims=True)
    bias, table = r.bias_g[0], r.table_g[0]
    for m in range(1, members):
        bias, table = bias + r.bias_g[m], table + r.table_g[m]
    r.bias[...] = bias
    r.table[...] = table

    for k, (_, _, size) in enumerate(jobs):
        load(k).wait()
        if k >= depth:
            save(k - depth).wait()
        r.wide[k % depth, :size] = r.narrow[k % depth, :size].astype(F32)
        save(k).start()
        if k + depth < len(jobs):
            load(k + depth).start()
        if k < samples:
            out_in(k).wait()
            out_back(k).start()
    for k in range(max(0, len(jobs) - depth), len(jobs)):
        save(k).wait()
    for s in range(samples):
        out_back(s).wait()
    modulate.wait()


def body(
    patches,
    condition,
    lengths,
    keep_order,
    cotangent,
    projection_weight,
    query_value_bias,
    merge_weight,
    merge_output_bias,
    up_weight,
    up_projection_bias,
    down_weight,
    down_projection_bias,
    w_modulate,
    bias_modulate,
    bias_table,
):
    samples, L, D = patches.shape
    n = cotangent.shape[1]
    grid_side = math.isqrt(L)
    offsets = 2 * grid_side - 1
    heads = bias_table.shape[0]
    local = projection_weight.shape[2]
    hd = local // heads
    lanes = heads * HEAD_PAD
    F = up_weight.shape[1]
    cols = w_modulate.shape[1]
    mp, dp_size = lax.axis_size("mp"), lax.axis_size("dp")
    me = lax.axis_index("mp")
    sz = Sizes(mp, samples, n, D)
    rows, block = sz.rows, sz.block

    ids = jnp.arange(n, dtype=jnp.int32)
    pos = jnp.where(ids[None, :] < lengths[:, None], keep_order[:, :n], -1)
    cot = cotangent
    if sz.per > 1:
        order = ((ids // block) ^ lax.rem(me, sz.per)) * block + ids % block
        pos = jnp.take(pos, order, axis=1)
        cot = jnp.take(cot, order, axis=1)
    turned = L - 1 - pos
    pos_wide = jnp.where(pos < 0, -1, turned + turned // grid_side * grid_side)

    def wide_row(a):
        return jnp.pad(a.astype(F32), (0, D - a.shape[0]))

    def by_head(a):
        return jnp.pad(a.reshape(heads, hd), ((0, 0), (0, HEAD_PAD - hd))).reshape(lanes)

    vec = jnp.stack(
        [
            wide_row(by_head(query_value_bias[0])),
            wide_row(by_head(query_value_bias[1])),
            wide_row(merge_output_bias),
            wide_row(up_projection_bias),
            wide_row(down_projection_bias),
            wide_row(bias_modulate),
        ]
    )
    table = bias_table.astype(F32).reshape(heads, offsets, offsets)
    table = jnp.pad(table, ((0, 0), (0, 1), (0, 1))).reshape(heads, 4 * L)
    wide = -(-cols // 128) * 128 + 128
    modw = max(m * cols // 128 * 128 + wide for m in range(mp))
    dma = pltpu.SemaphoreType.DMA

    one = Call()
    one.arg(
        condition=condition,
        vec=vec,
        pos=pos,
        pos_wide=pos_wide,
        w_in=jnp.swapaxes(projection_weight, 1, 2),
        w_out=merge_weight,
        table=table,
    )
    one.arg(pl.ANY, patches=patches, w_mod=w_modulate.T)
    one.out(modv=((samples, 6 * D), F32))
    one.out(
        pl.ANY,
        attn_in=((rows, D), BF16),
        qkv=((rows, 3 * lanes), BF16),
        probs=((samples, heads, n, n), F32),
        att=((rows, lanes), BF16),
        kept=((block, D), F32),
        res=((block, D), F32),
        hidden=((block, D), F32),
        mlp=((block, D), BF16),
        w_qkv=((3 * lanes, D), BF16),
        w_merge=((lanes, D), BF16),
    )
    one.vmem(
        attn_in_v=((rows, D), BF16),
        qkv_v=((rows, 3 * lanes), BF16),
        probs_v=((samples, heads, n, n), F32),
        att_v=((rows, lanes), BF16),
        kept_v=((block, D), F32),
        res_v=((block, D), F32),
        hidden_v=((block, D), F32),
        mlp_v=((block, D), BF16),
        w_qkv_v=((3 * lanes, D), BF16),
        w_merge_v=((lanes, D), BF16),
        w_mod_v=((cols, D), BF16),
        patches_v=((samples, L, D), BF16),
        mod_buf=((mp, samples, wide), F32),
        mod_wide=((samples, modw), F32),
        normed=((rows, D), F32),
        bias_full=((heads, L, 2 * L), BF16),
        part=((rows, D), BF16),
    )
    one.scratch(
        mod_send=dma((mp,)),
        mod_recv=dma((mp,)),
        sem=dma((7,)),
        load_sem=dma((samples,)),
        save_sem=dma((4, samples)),
        red=reduce_scratch(sz),
    )
    first = one.run(
        functools.partial(attention_forward, sz, heads, hd, grid_side, cols), "attention_forward", 0, 62 << 20
    )

    chunk = 48 if dp_size == 4 and F % 96 == 0 and local % 48 == 0 else 0
    two = Call()
    two.arg(condition=condition, vec=vec, pos=pos, pos_wide=pos_wide, modv=first.modv)
    two.arg(
        pl.ANY,
        cot=cot,
        w_up=up_weight.T,
        w_down=down_weight,
        mlp=first.mlp,
        hidden=first.hidden,
        res=first.res,
        kept=first.kept,
        qkv=first.qkv,
        probs=first.probs,
        att=first.att,
        w_qkv=first.w_qkv,
        w_merge=first.w_merge,
        attn_in=first.attn_in,
    )
    both = ((2, F + 2 * local, D), BF16)
    if chunk:
        count = (F + 2 * local) // chunk
        two.out(z_outer=both)
        two.vmem(grads=both, z_inner=((F + 2 * local, D), BF16))
        two.scratch(
            zs=dma((2, count)),
            zo=dma((2, count)),
            zf=dma((count,)),
            zi=dma((count,)),
            zt=dma((3, count)),
            zr=dma((2, count)),
        )
    else:
        two.out(grads=both)
    two.out(
        bias_g=((dp_size, 4, D), F32),
        table_g=((dp_size, heads, 4 * L), F32),
        signal_g=((dp_size, samples, D), BF16),
        mod_g=((dp_size, samples, wide), F32),
    )
    two.out(pl.ANY, out=((samples, n, D), BF16), patch_g=((samples, L, D), BF16))
    two.vmem(
        w_up_v=((F, D), BF16),
        w_down_v=((F, D), BF16),
        mlp_v=((rows, D), BF16),
        d_mlp=((rows, D), BF16),
        slope=((rows, F), F32),
        act=((rows, F), BF16),
        d_pre=((rows, F), BF16),
        part_f=((rows, D), BF16),
        part_b=((rows, D), BF16),
        d_attn=((rows, D), BF16),
        cot_own=((block, D), BF16),
        hidden_v=((block, D), F32),
        res_v=((block, D), F32),
        normed_v=((block, D), F32),
        dh_v=((block, D), F32),
        qkv_v=((rows, 3 * lanes), BF16),
        probs_v=((samples, heads, n, n), F32),
        w_qkv_v=((3 * lanes, D), BF16),
        w_merge_v=((lanes, D), BF16),
        grid_g=((heads, L, 2 * L), F32),
        early=((mp, 4, D), F32),
        late_sums=((mp, 2, D), F32),
        flat=((samples, modw), F32),
    )
    two.scratch(
        sem=dma((13,)),
        load_sem=dma((3, samples)),
        dm_send=dma((2, mp)),
        dm_recv=dma((2, mp)),
        dp_send=dma((4, dp_size)),
        dp_recv=dma((4, dp_size)),
        red_f=reduce_scratch(sz),
        red_b=reduce_scratch(sz),
        last_sems=reduce_scratch(sz)[2:],
        gat_m=gather_scratch(sz),
        gat_d=gather_scratch(sz),
        gat_o=gather_scratch(sz),
        gat_k=gather_scratch(sz),
    )
    got = two.run(
        functools.partial(block_backward, sz, heads, hd, grid_side, cols, dp_size, chunk), "block_backward", 1, 64 << 20
    )

    total = got.z_outer if chunk else lax.psum(got.grads, "dp")
    three = Call()
    three.arg(mod_g=got.mod_g, signal_g=got.signal_g, bias_g=got.bias_g, table_g=got.table_g)
    three.arg(pl.ANY, total=total, out=got.out, patch_g=got.patch_g)
    three.out(mod_bias=((1, wide), F32), bias=((4, D), F32), table=((heads, 4 * L), F32))
    three.out(
        pl.ANY,
        block_out=((samples, n, D), BF16),
        patch=((samples, L, D), F32),
        up=((F, D), F32),
        down=((F, D), F32),
        project=((3 * local, D), F32),
        merge=((local, D), F32),
        modulate=((cols, D), F32),
    )
    depth = 4
    three.vmem(narrow=((depth, 288, D), BF16), wide=((depth, 288, D), F32), mod_v=((cols, D), F32), out_v=((samples, n, D), BF16))
    three.scratch(sem=dma((1,)), out_sem=dma((2, samples)), load_sem=dma((depth,)), save_sem=dma((depth,)))
    end = three.run(functools.partial(write_results, cols), "write_results", None, 63 << 20)

    block_out = end.block_out
    if sz.per > 1:
        block_out = jnp.take(block_out, order, axis=1)
    proj_bias = end.bias[3, : 3 * lanes].reshape(3, heads, HEAD_PAD)[:, :, :hd].reshape(3, local)
    proj_bias = jnp.stack([proj_bias[0], proj_bias[2]])
    table_grad = end.table.reshape(heads, 2 * grid_side, 2 * grid_side)
    table_grad = table_grad[:, :offsets, :offsets].reshape(heads, offsets * offsets)
    return (
        block_out,
        end.patch,
        jnp.swapaxes(end.project.reshape(3, local, D), 1, 2),
        proj_bias,
        end.merge,
        end.bias[2],
        end.up.T,
        end.bias[0, :F],
        end.down,
        end.bias[1],
        end.modulate.T,
        end.mod_bias[0, :cols],
        table_grad,
    )


def solution(mesh):
    placed = (
        P("dp", None, None),
        P("dp", None),
        P("dp"),
        P("dp", None),
        P("dp", None, None),
        P(None, None, "mp"),
        P(None, "mp"),
        P("mp", None),
        P(),
        P(None, "mp"),
        P("mp"),
        P("mp", None),
        P(),
        P(None, "mp"),
        P("mp"),
        P("mp", None),
    )
    return jax.shard_map(
        body,
        mesh=mesh,
        in_specs=placed,
        out_specs=(
            P("dp", None, None),
            P("dp", None, None),
            P(None, None, "mp"),
            P(None, "mp"),
            P("mp", None),
            P(),
            P(None, "mp"),
            P("mp"),
            P("mp", None),
            P(),
            P(None, "mp"),
            P("mp"),
            P("mp", None),
        ),
        check_vma=False,
    )
```

```python
import functools
import math
from types import SimpleNamespace

import jax
import jax.numpy as jnp
from jax import lax
from jax.experimental import pallas as pl
from jax.experimental.pallas import tpu as pltpu
from jax.sharding import PartitionSpec as P

MESH = pl.DeviceIdType.MESH
F32 = jnp.float32
BF16 = jnp.bfloat16
EPSILON = 1e-06
MASKED = -1000000000.0
GELU_C = math.sqrt(2.0 / math.pi)
GELU_A = 0.044715
VMEM = pl.BlockSpec(memory_space=pltpu.VMEM)
HEAD_PAD = 128


def dot(a, b, ca=1, cb=0):
    return lax.dot_general(a, b, (((ca,), (cb,)), ((), ())), preferred_element_type=F32)


def bit_of(value, k):
    return lax.rem(value // (1 << k), 2)


def flip(value, mask):
    out = value
    k = 0
    while (1 << k) <= mask:
        if mask & (1 << k):
            out = out + (1 << k) * (1 - 2 * bit_of(value, k))
        k += 1
    return out


def xor(a, b, bits):
    out = 0
    for k in range(bits):
        out = out + (1 << k) * lax.rem(bit_of(a, k) + bit_of(b, k), 2)
    return out


class Sizes:
    def __init__(self, mp, samples, slots, width):
        self.mp, self.samples, self.slots, self.width = mp, samples, slots, width
        self.bits = mp.bit_length() - 1
        self.rows = samples * slots
        self.block = self.rows // mp
        self.half = self.block // 2
        self.per = self.block and slots // self.block
        rest = [1 << k for k in range(1, self.bits)]
        self.orders = (rest, rest[::-1])
        self.sends = {}
        count = 0
        for h in range(2):
            live = list(range(0, mp, 2))
            for t, bit in enumerate(self.orders[h]):
                moved = [d for d in live if d & bit]
                live = [d for d in live if not d & bit]
                self.sends[h, t] = [(d, bit, count + i) for i, d in enumerate(moved)]
                count += len(moved)
        self.steps = len(rest)
        self.far = count
        self.near = mp // 2
        self.fast = self.steps == 2 and self.per == 1


def my_index():
    return lax.axis_index("dp"), lax.axis_index("mp")


def enter(sz):
    dp, me = my_index()
    barrier = pltpu.get_barrier_semaphore()
    for d in range(1, sz.mp):
        pl.semaphore_signal(barrier, inc=1, device_id=(dp, flip(me, d)), device_id_type=MESH)
    pl.semaphore_wait(barrier, sz.mp - 1)


def rows_of(ref, start, size):
    return ref.at[pl.ds(start, size)]


class Reduce:
    def __init__(self, sz, part, refs):
        self.sz, self.part = sz, part
        self.near_buf, self.far_buf, self.near_send, self.near_recv, self.far_send, self.far_recv = refs
        self.dp, self.me = my_index()

    def near_copy(self, pair):
        b = self.sz.block
        return pltpu.make_async_remote_copy(
            src_ref=rows_of(self.part, (2 * pair + 1) * b, b),
            dst_ref=rows_of(self.near_buf, pair * b, b),
            send_sem=self.near_send.at[pair],
            recv_sem=self.near_recv.at[pair],
            device_id=(self.dp, flip(self.me, 1)),
            device_id_type=MESH,
        )

    def far_copy(self, h, d, bit, i):
        b, hb = self.sz.block, self.sz.half
        return pltpu.make_async_remote_copy(
            src_ref=rows_of(self.part, d * b + h * hb, hb),
            dst_ref=rows_of(self.far_buf, i * hb, hb),
            send_sem=self.far_send.at[i],
            recv_sem=self.far_recv.at[i],
            device_id=(self.dp, flip(self.me, bit)),
            device_id_type=MESH,
        )

    def add(self, start, buf, at, size):
        a = self.part[pl.ds(start, size), :].astype(F32) + buf[pl.ds(at, size), :].astype(F32)
        self.part[pl.ds(start, size), :] = a.astype(BF16)

    def near_add(self, pair):
        b = self.sz.block
        self.near_copy(pair).wait()
        self.add(2 * pair * b, self.near_buf, pair * b, b)

    def send(self, h, d):
        for t in range(self.sz.steps):
            for m in self.sz.sends[h, t]:
                if m[0] == d:
                    self.far_copy(h, *m).start()

    def take(self, h, d, bit, i, add=True):
        b, hb = self.sz.block, self.sz.half
        self.far_copy(h, d, bit, i).wait()
        if add:
            self.add((d - bit) * b + h * hb, self.far_buf, i * hb, hb)

    def after(self, k):
        if k == 0:
            self.send(0, 6)
            self.send(1, 6)
        if k == 1:
            self.send(0, 2)
        if k == 2:
            self.send(1, 4)
            self.take(1, *self.sz.sends[1, 0][1])
            self.send(1, 2)
            self.take(0, *self.sz.sends[0, 0][1])
            self.send(0, 4)

    def close(self):
        sz = self.sz
        if sz.fast:
            for h in range(2):
                for t in range(2):
                    for m in sz.sends[h, t]:
                        if m[0] == m[1]:
                            self.take(h, *m, add=False)
            return

        def one(i, carry):
            self.near_add(sz.near - 1 - i)
            return carry

        lax.fori_loop(0, sz.near, one, 0)
        for t in range(sz.steps):
            for h in range(2):
                for m in sz.sends[h, t]:
                    self.far_copy(h, *m).start()
            for h in range(2):
                for m in sz.sends[h, t]:
                    self.take(h, *m, add=t < sz.steps - 1)

    def own_sum(self):
        sz, hb = self.sz, self.sz.half
        out = []
        for h in range(2):
            total = self.part[h * hb : (h + 1) * hb, :].astype(F32)
            for t in range(0 if sz.fast else sz.steps - 1, sz.steps):
                for d, bit, i in sz.sends[h, t]:
                    if d == bit:
                        total = total + self.far_buf[i * hb : (i + 1) * hb, :].astype(F32)
            out.append(total)
        return jnp.concatenate(out, axis=0)


class Gather:
    def __init__(self, sz, out, sems):
        self.sz, self.out = sz, out
        self.near_send, self.near_recv, self.far_send, self.far_recv = sems
        self.dp, self.me = my_index()
        self.first, self.stages = [], []
        if sz.fast:
            x, y = sz.orders[0]
            self.first = [(1, 0, x, 0), (0, 0, y, 1), (0, 0, x, 2), (1, 0, y, 3)]
            on = {0: (1, x, y, 5), 1: (0, y, x, 4)}
            self.stages = [
                [(self.first[1], [on[1]]), (self.first[0], [on[0]])],
                [(self.first[2], []), (self.first[3], [])],
                [(on[1], []), (on[0], [])],
            ]
        else:
            count, plan = 0, {}
            for h in range(2):
                have = [0]
                for t, bit in enumerate(sz.orders[h][::-1]):
                    plan[h, t] = [(h, d, bit, count + i) for i, d in enumerate(have)]
                    count += len(have)
                    have = have + [d | bit for d in have]
            self.first = plan[0, 0] + plan[1, 0]
            for t in range(sz.steps):
                stage = []
                for h in range(2):
                    later = plan[h, t + 1] if t + 1 < sz.steps else []
                    for k, m in enumerate(plan[h, t]):
                        stage.append((m, later if k == len(plan[h, t]) - 1 else []))
                self.stages.append(stage)

    def near_copy(self, d, h):
        b, hb = self.sz.block, self.sz.half
        return pltpu.make_async_remote_copy(
            src_ref=rows_of(self.out, d * b + h * hb, hb),
            dst_ref=rows_of(self.out, (d + 1) * b + h * hb, hb),
            send_sem=self.near_send.at[d + h],
            recv_sem=self.near_recv.at[d + h],
            device_id=(self.dp, flip(self.me, 1)),
            device_id_type=MESH,
        )

    def far_copy(self, h, d, bit, i):
        b, hb = self.sz.block, self.sz.half
        return pltpu.make_async_remote_copy(
            src_ref=rows_of(self.out, d * b + h * hb, hb),
            dst_ref=rows_of(self.out, (d + bit) * b + h * hb, hb),
            send_sem=self.far_send.at[i],
            recv_sem=self.far_recv.at[i],
            device_id=(self.dp, flip(self.me, bit)),
            device_id_type=MESH,
        )

    def start(self):
        for m in self.first:
            self.far_copy(*m).start()
        for h in range(2):
            self.near_copy(0, h).start()

    def step(self, t):
        for m, later in self.stages[t]:
            self.far_copy(*m).wait()
            for n in later:
                self.far_copy(*n).start()
            h, d, bit, _ = m
            self.near_copy(d + bit, h).start()

    def finish(self, first=0):
        for d in range(first, self.sz.mp, 2):
            for h in range(2):
                self.near_copy(d, h).wait()


def reduce_scratch(sz):
    return [
        pltpu.VMEM((sz.near * sz.block, sz.width), BF16),
        pltpu.VMEM((sz.far * sz.half, sz.width), BF16),
        pltpu.SemaphoreType.DMA((sz.near,)),
        pltpu.SemaphoreType.DMA((sz.near,)),
        pltpu.SemaphoreType.DMA((sz.far,)),
        pltpu.SemaphoreType.DMA((sz.far,)),
    ]


def gather_scratch(sz):
    return [
        pltpu.SemaphoreType.DMA((sz.mp,)),
        pltpu.SemaphoreType.DMA((sz.mp,)),
        pltpu.SemaphoreType.DMA((sz.far,)),
        pltpu.SemaphoreType.DMA((sz.far,)),
    ]


def slot_loop(sz, body, red, extra=None):
    if sz.fast:

        def one(i, carry):
            q = i // 2
            pair = 2 * (1 - lax.rem(q, 2)) + 1 - q // 2
            other = 1 - lax.rem(i, 2)
            body(2 * pair + other)

            @pl.when(other == 1)
            def _():
                red.near_copy(pair).start()

            @pl.when(other == 0)
            def _():
                red.near_add(pair)

            for k in range(3):
                pl.when(i == 2 * k + 1)(functools.partial(red.after, k))
            if extra is not None:
                extra(i)
            return carry

    else:
        pairs = sz.per // 2

        def one(i, carry):
            slot = sz.samples - 1 - i
            body(slot)
            for p in range(pairs):
                red.near_copy(slot * pairs + p).start()
            return carry

    lax.fori_loop(0, sz.samples, one, 0)


def layer_stats(values):
    centre = jnp.mean(values, axis=-1, keepdims=True)
    shifted = values - centre
    spread = jnp.mean(shifted * shifted, axis=-1, keepdims=True)
    inv_std = lax.rsqrt(spread + EPSILON)
    return shifted * inv_std, inv_std


def layer_back(gradient, normed, inv_std):
    mean_grad = jnp.mean(gradient, axis=-1, keepdims=True)
    mean_mix = jnp.mean(gradient * normed, axis=-1, keepdims=True)
    return inv_std * (gradient - mean_grad - normed * mean_mix)


def pick_rows(ids_ref, s, count):
    ids = ids_ref[pl.ds(s, 1), :]
    return (lax.broadcasted_iota(jnp.int32, (count, ids.shape[1]), 0) == ids).astype(F32).astype(BF16)


def spread(row, pieces, size, step):
    width = row.shape[1]
    lane = lax.broadcasted_iota(jnp.int32, row.shape, 1)
    total = jnp.zeros_like(row)
    for p in range(pieces):
        start = p * (size + step) if step > 0 else p * size
        moved = pltpu.roll(row, (p * step) % width, 1) if p else row
        total = jnp.where((lane >= start) & (lane < start + size), moved, total)
    return total


def spread_heads(row, heads, hd):
    return spread(row, heads, hd, HEAD_PAD - hd)


def live_column(sel):
    ones = jnp.ones((sel.shape[0], 128), BF16)
    return dot(sel, ones, 0, 0)[:, 0:1]


class Call:
    def __init__(self):
        self.args, self.specs, self.outs, self.out_specs, self.scratch_of = {}, [], {}, [], {}

    def arg(self, space=pltpu.VMEM, **values):
        self.args.update(values)
        self.specs += [pl.BlockSpec(memory_space=space)] * len(values)

    def out(self, space=pltpu.VMEM, **results):
        for name, (shape, dtype) in results.items():
            self.outs[name] = jax.ShapeDtypeStruct(shape, dtype)
            self.out_specs.append(pl.BlockSpec(memory_space=space))

    def scratch(self, **buffers):
        self.scratch_of.update(buffers)

    def vmem(self, **buffers):
        for name, (shape, dtype) in buffers.items():
            self.scratch_of[name] = pltpu.VMEM(shape, dtype)

    def run(self, kernel, name, cid, limit):
        flat = []
        for value in self.scratch_of.values():
            flat += value if isinstance(value, list) else [value]

        def inner(*refs):
            r, refs = SimpleNamespace(), list(refs)
            for key in list(self.args) + list(self.outs):
                setattr(r, key, refs.pop(0))
            for key, value in self.scratch_of.items():
                count = len(value) if isinstance(value, list) else 0
                setattr(r, key, [refs.pop(0) for _ in range(count)] if count else refs.pop(0))
            kernel(r)

        got = pl.pallas_call(
            inner,
            out_shape=list(self.outs.values()),
            in_specs=self.specs,
            out_specs=self.out_specs,
            scratch_shapes=flat,
            name=name,
            compiler_params=pltpu.CompilerParams(vmem_limit_bytes=limit)
            if cid is None
            else pltpu.CompilerParams(collective_id=cid, has_side_effects=True, vmem_limit_bytes=limit),
        )(*self.args.values())
        return SimpleNamespace(**dict(zip(self.outs, got)))


def attention_forward(sz, heads, hd, grid_side, cols, r):
    dp, me = my_index()
    mine = me // sz.per
    sbits = sz.samples.bit_length() - 1
    D, n, L = sz.width, sz.slots, grid_side * grid_side
    lanes = heads * HEAD_PAD
    red = Reduce(sz, r.part, r.red)
    mod_buf, mod_wide, modv = r.mod_buf, r.mod_wide, r.modv
    wide = mod_buf.shape[2]
    sem = r.sem

    load_mod = pltpu.make_async_copy(r.w_mod, r.w_mod_v, sem.at[0])
    load_mod.start()

    def load_patches(i, slot):
        return pltpu.make_async_copy(r.patches.at[xor(mine, slot, sbits)], r.patches_v.at[slot], r.load_sem.at[i])

    def start_load(slot, carry):
        load_patches(slot, slot).start()
        return carry

    lax.fori_loop(0, sz.samples, start_load, 0)
    slots = lax.broadcasted_iota(jnp.int32, (1, n), 1)
    for s in range(sz.samples):
        pos = jnp.where(slots < r.lengths[s], r.keep[s : s + 1, 0:n], -1)
        r.pos[s : s + 1, :] = pos
        turned = L - 1 - pos
        r.pos_wide[s : s + 1, :] = jnp.where(pos < 0, -1, turned + turned // grid_side * grid_side)
    r.qv_wide[...] = jnp.zeros_like(r.qv_wide)
    r.qv_wide[:, 0 : heads * hd] = r.b_qv[...].astype(F32)
    r.qv_wide[...] = spread_heads(r.qv_wide[...], heads, hd)
    r.table_v[...] = jnp.zeros_like(r.table_v)
    offsets = 2 * grid_side - 1
    r.table_v[:, 0 : offsets * offsets] = r.b_table[...].astype(F32)
    r.table_v[...] = spread(r.table_v[...], offsets, offsets, 1)
    cond = r.condition[...].astype(F32)
    signal = (cond / (1.0 + jnp.exp(-cond))).astype(BF16)
    mod_buf[me] = jnp.zeros((sz.samples, wide), F32)
    load_mod.wait()
    mod_buf[me, :, 0:cols] = dot(signal, r.w_mod_v[...], 1, 1) + r.b_mod[...].astype(F32).reshape(1, cols)
    enter(sz)

    def mod_copy(d, slot):
        return pltpu.make_async_remote_copy(
            src_ref=mod_buf.at[slot],
            dst_ref=mod_buf.at[slot],
            send_sem=r.mod_send.at[d],
            recv_sem=r.mod_recv.at[d],
            device_id=(dp, flip(me, d)),
            device_id_type=MESH,
        )

    for d in range(1, sz.mp):
        mod_copy(d, me).start()

    w_qkv, w_merge = r.w_qkv_v, r.w_merge_v
    pad_rows = jnp.zeros((HEAD_PAD - hd, D), F32)
    for h in range(heads):
        for c in range(3):
            piece = r.w_in[c].astype(F32)[h * hd : (h + 1) * hd]
            w_qkv[c * lanes + h * HEAD_PAD : c * lanes + (h + 1) * HEAD_PAD, :] = jnp.concatenate(
                [piece, pad_rows], axis=0
            ).astype(BF16)
        piece = r.w_out[...].astype(F32)[h * hd : (h + 1) * hd]
        w_merge[h * HEAD_PAD : (h + 1) * HEAD_PAD, :] = jnp.concatenate([piece, pad_rows], axis=0).astype(BF16)
    save = [
        pltpu.make_async_copy(w_qkv, r.w_qkv, sem.at[1]),
        pltpu.make_async_copy(w_merge, r.w_merge, sem.at[2]),
    ]
    for copy in save:
        copy.start()

    bias_full = r.bias_full
    span = r.table_v.shape[1]
    for h in range(heads):
        line = r.table_v[h : h + 1, :]
        strip = jnp.concatenate([line] + [pltpu.roll(line, span - c, 1) for c in range(1, grid_side)], axis=0)
        for row in range(grid_side):
            rolled = pltpu.roll(strip, span - row * 2 * grid_side, 1) if row else strip
            bias_full[h, row * grid_side : (row + 1) * grid_side, :] = rolled[:, : 2 * L].astype(BF16)

    normed, kept_own = r.normed, r.kept_v

    def norm_one(slot, carry):
        load_patches(slot, slot).wait()
        sel = pick_rows(r.pos, xor(mine, slot, sbits), L)
        kept = dot(sel, r.patches_v[slot], 0, 0)
        value, _ = layer_stats(kept)
        normed[pl.ds(slot * n, n), :] = value

        @pl.when(slot == 0)
        def _():
            kept_own[...] = kept[: sz.block]

        return carry

    lax.fori_loop(0, sz.samples, norm_one, 0)
    save_kept = pltpu.make_async_copy(kept_own, r.kept, sem.at[3])
    save_kept.start()

    for d in range(1, sz.mp):
        mod_copy(d, me).wait_send()
        mod_copy(d, flip(me, d)).wait_recv()
    mod_wide[...] = jnp.zeros_like(mod_wide)
    for m in range(sz.mp):
        base = m * cols // 128 * 128
        phase = m * cols - base
        piece = mod_buf[m]
        if phase:
            piece = pltpu.roll(piece, phase, 1)
        mod_wide[:, base : base + wide] += piece
    modv[...] = mod_wide[:, : 6 * D]

    factor = hd ** (-0.5)
    stores = [(r.attn_in_v, r.attn_in), (r.qkv_v, r.qkv), (r.att_v, r.att)]

    def save_slot(i, slot):
        at = pl.ds(slot * n, n)
        copies = [
            pltpu.make_async_copy(a.at[at], b.at[at], r.save_sem.at[k, slot]) for k, (a, b) in enumerate(stores)
        ]
        copies.append(pltpu.make_async_copy(r.probs_v.at[slot], r.probs.at[slot], r.save_sem.at[3, slot]))
        return copies

    def body(slot):
        s = xor(mine, slot, sbits)
        at = pl.ds(slot * n, n)
        shift = modv[pl.ds(s, 1), 0:D]
        scale = modv[pl.ds(s, 1), D : 2 * D]
        entry = (normed[at, :] * (1.0 + scale) + shift).astype(BF16)
        r.attn_in_v[at, :] = entry
        proj = dot(entry, w_qkv[...], 1, 1)
        qs = (proj[:, :lanes] + r.qv_wide[0:1, :]).astype(BF16)
        ks = proj[:, lanes : 2 * lanes].astype(BF16)
        vs = (proj[:, 2 * lanes :] + r.qv_wide[1:2, :]).astype(BF16)
        r.qkv_v[at, 0:lanes] = qs
        r.qkv_v[at, lanes : 2 * lanes] = ks
        r.qkv_v[at, 2 * lanes :] = vs
        sel = pick_rows(r.pos, s, L)
        sel_wide = pick_rows(r.pos_wide, s, 2 * L)
        live = r.pos[pl.ds(s, 1), :] >= 0
        outs = []
        for h in range(heads):
            cut = slice(h * HEAD_PAD, (h + 1) * HEAD_PAD)
            bias = dot(dot(sel, bias_full[h], 0, 0).astype(BF16), sel_wide)
            scores = jnp.where(live, dot(qs[:, cut], ks[:, cut], 1, 1) * factor + bias, MASKED)
            top = jnp.max(scores, axis=-1, keepdims=True)
            e = jnp.exp(scores - top)
            p = e / jnp.sum(e, axis=-1, keepdims=True)
            r.probs_v[slot, h] = p
            outs.append(dot(p.astype(BF16), vs[:, cut]).astype(BF16))
        joined = jnp.concatenate(outs, axis=1) if heads > 1 else outs[0]
        r.att_v[at, :] = joined
        r.part[at, :] = dot(joined, w_merge[...]).astype(BF16)
        for copy in save_slot(0, slot):
            copy.start()

    slot_loop(sz, body, red)
    red.close()
    result = red.own_sum() + r.b_merge[...].astype(F32).reshape(1, D)
    r.res_v[...] = result
    hidden = kept_own[...] + modv[pl.ds(mine, 1), 2 * D : 3 * D] * result
    r.hidden_v[...] = hidden
    value, _ = layer_stats(hidden)
    shift = modv[pl.ds(mine, 1), 3 * D : 4 * D]
    scale = modv[pl.ds(mine, 1), 4 * D : 5 * D]
    r.mlp_v[...] = (value * (1.0 + scale) + shift).astype(BF16)
    save_own = [
        pltpu.make_async_copy(r.res_v, r.res, sem.at[4]),
        pltpu.make_async_copy(r.hidden_v, r.hidden, sem.at[5]),
        pltpu.make_async_copy(r.mlp_v, r.mlp, sem.at[6]),
    ]
    for copy in save_own:
        copy.start()

    def wait_slot(slot, carry):
        for copy in save_slot(0, slot):
            copy.wait()
        return carry

    lax.fori_loop(0, sz.samples, wait_slot, 0)
    for copy in save + save_own + [save_kept]:
        copy.wait()


class Line:
    def __init__(self, r, chunk):
        self.r, self.chunk = r, chunk
        self.g, self.outer_buf, self.inner_buf = r.grads, r.z_outer, r.z_inner
        self.count = self.g.shape[1] // chunk
        self.dp, self.me = my_index()
        self.is_inner = (self.dp == 1) | (self.dp == 2)
        self.is_outer = (self.dp == 0) | (self.dp == 3)
        self.step_to = 1 + self.dp // 3
        self.back_to = (self.dp - 1) * 3
        self.other = 3 - self.dp
        self.mine = 2 - self.dp
        self.passed = self.dp - 1

    def rows(self, k):
        return pl.ds(k * self.chunk, self.chunk)

    def copy(self, src, dst, send, recv, to):
        return pltpu.make_async_remote_copy(
            src_ref=src, dst_ref=dst, send_sem=send, recv_sem=recv, device_id=(to, self.me), device_id_type=MESH
        )

    def out_copy(self, j, k):
        return self.copy(
            self.g.at[j, self.rows(k)], self.outer_buf.at[j, self.rows(k)],
            self.r.zs.at[j, k], self.r.zo.at[j, k], self.step_to,
        )

    def in_copy(self, k):
        return self.copy(
            self.g.at[self.passed, self.rows(k)], self.inner_buf.at[self.rows(k)],
            self.r.zf.at[k], self.r.zi.at[k], self.other,
        )

    def total_copy(self, j, k, which, to):
        return self.copy(
            self.outer_buf.at[j, self.rows(k)], self.outer_buf.at[j, self.rows(k)],
            self.r.zt.at[which, k], self.r.zr.at[j, k], to,
        )

    def begin(self, halves, k0, k1):
        @pl.when(self.is_outer)
        def _():
            def one(k, carry):
                for j in halves:
                    self.out_copy(j, k).start()
                return carry

            lax.fori_loop(k0, k1, one, 0)

    def add(self, to, j, k, more):
        def one(i, carry):
            at = pl.ds(k * self.chunk + i * 16, 16)
            v = self.g[j, at, :].astype(F32) + self.outer_buf[j, at, :].astype(F32)
            if more:
                v = v + self.inner_buf[at, :].astype(F32)
            to[j, at, :] = v.astype(BF16)
            return carry

        lax.fori_loop(0, self.chunk // 16, one, 0)

    def stage(self, number, j, k):
        if number == 1:

            @pl.when(self.passed == j)
            def _():
                self.out_copy(j, k).wait_recv()
                self.add(self.g, j, k, False)
                self.in_copy(k).start()

        elif number == 2:

            @pl.when(self.mine == j)
            def _():
                self.out_copy(j, k).wait_recv()
                self.in_copy(k).wait_recv()
                self.add(self.outer_buf, j, k, True)
                self.total_copy(j, k, 0, self.other).start()
                self.total_copy(j, k, 1, self.back_to).start()

        else:

            @pl.when(self.passed == j)
            def _():
                self.in_copy(k).wait_send()
                self.total_copy(j, k, 0, self.other).wait_recv()
                self.total_copy(j, k, 2, self.back_to).start()

    def finish(self):
        @pl.when(self.is_inner)
        def _():
            def one(k, carry):
                self.total_copy(self.mine, k, 0, self.other).wait_send()
                self.total_copy(self.mine, k, 1, self.back_to).wait_send()
                self.total_copy(self.passed, k, 2, self.back_to).wait_send()
                return carry

            lax.fori_loop(0, self.count, one, 0)

        @pl.when(self.is_outer)
        def _():
            def one(k, carry):
                for j in range(2):
                    self.out_copy(j, k).wait_send()
                    self.total_copy(j, k, 0, self.step_to).wait_recv()
                return carry

            lax.fori_loop(0, self.count, one, 0)


def block_backward(sz, heads, hd, grid_side, cols, dp_size, chunk, r):
    dp, me = my_index()
    mine = me // sz.per
    sbits = sz.samples.bit_length() - 1
    D, n, L = sz.width, sz.slots, grid_side * grid_side
    lanes = heads * HEAD_PAD
    local = heads * hd
    F = r.w_up_v.shape[0]
    block = sz.block
    modv = r.modv
    fwd = Reduce(sz, r.part_f, r.red_f)
    bwd = Reduce(sz, r.part_b, r.red_b)
    last = Reduce(sz, r.part_b, r.red_b[:2] + r.last_sems)
    gat_m = Gather(sz, r.mlp_v, r.gat_m)
    gat_d = Gather(sz, r.d_attn, r.gat_d)
    gat_o = Gather(sz, r.part_f, r.gat_o)
    gat_k = Gather(sz, r.mlp_v, r.gat_k)
    line = Line(r, chunk) if chunk else None
    grads = r.grads
    sem = r.sem

    per_half, per_local = (F // 2 // chunk, local // chunk) if chunk else (0, 0)
    marks = [0, per_half, 2 * per_half, 2 * per_half + per_local, 2 * per_half + 2 * per_local]
    following = {(number, j): 0 for number in (1, 2, 3) for j in range(2)}

    def tick(*steps):
        if line is None:
            return
        for number, j, count in steps:
            k0 = following[number, j]
            k1 = min(k0 + count, marks[4])
            assert number == 1 or k1 <= following[number - 1, j]
            following[number, j] = k1
            if k1 - k0 == 1:
                line.stage(number, j, k0)
            elif k1 > k0:

                def one(k, carry, number=number, j=j):
                    line.stage(number, j, k)
                    return carry

                lax.fori_loop(k0, k1, one, 0)

    def begin(group, *halves):
        if line is not None:
            line.begin(halves or (0, 1), marks[group], marks[group + 1])

    def ticks_at(i, plan):
        if line is not None:
            for when, steps in plan.items():
                pl.when(i == when)(lambda steps=steps: tick(*steps))

    load_up = pltpu.make_async_copy(r.w_up, r.w_up_v, sem.at[0])
    load_down = pltpu.make_async_copy(r.w_down, r.w_down_v, sem.at[1])
    load_up.start()
    load_down.start()

    load_own = pltpu.make_async_copy(r.mlp, r.mlp_v.at[pl.ds(0, block)], sem.at[12])
    load_own.start()

    def load_cot(slot):
        at = pl.ds(slot * n, n)
        return pltpu.make_async_copy(r.cot.at[xor(mine, slot, sbits)], r.d_mlp.at[at], r.load_sem.at[1, slot])

    def start_cot(slot, carry):
        load_cot(slot).start()
        return carry

    lax.fori_loop(0, sz.samples, start_cot, 0)
    loads = [
        pltpu.make_async_copy(r.cot.at[mine, pl.ds(0, block)], r.cot_own, sem.at[2]),
        pltpu.make_async_copy(r.hidden, r.hidden_v, sem.at[3]),
        pltpu.make_async_copy(r.res, r.res_v, sem.at[4]),
    ]
    late = [
        pltpu.make_async_copy(r.qkv, r.qkv_v, sem.at[6]),
        pltpu.make_async_copy(r.probs, r.probs_v, sem.at[7]),
        pltpu.make_async_copy(r.w_qkv, r.w_qkv_v, sem.at[9]),
        pltpu.make_async_copy(r.w_merge, r.w_merge_v, sem.at[10]),
    ]
    for copy in loads + late:
        copy.start()
    load_attn = pltpu.make_async_copy(r.attn_in, r.d_mlp, sem.at[11])
    load_kept = pltpu.make_async_copy(r.kept, r.res_v, sem.at[5])
    load_att = pltpu.make_async_copy(r.att, r.act.at[:, pl.ds(0, lanes)], sem.at[8])

    barrier = pltpu.get_barrier_semaphore()
    for d in range(1, sz.mp):
        pl.semaphore_signal(barrier, inc=1, device_id=(dp, flip(me, d)), device_id_type=MESH)
    for e in range(1, dp_size):
        pl.semaphore_signal(barrier, inc=1, device_id=(lax.rem(dp + e, dp_size), me), device_id_type=MESH)
    pl.semaphore_wait(barrier, sz.mp + dp_size - 2)
    load_own.wait()
    gat_m.start()
    r.bias_v[0:1, 0:F] = r.b_up[...].astype(F32).reshape(1, F)
    r.bias_v[1:2, :] = r.b_down[...].astype(F32).reshape(1, D)
    load_up.wait()
    load_down.wait()
    w_up, w_down, mlp = r.w_up_v, r.w_down_v, r.mlp_v
    act, d_pre, d_mlp, slope = r.act, r.d_pre, r.d_mlp, r.slope

    up_bg, down_bg = r.bias_g.at[dp, 0:1], r.bias_g.at[dp, 1:2]
    merge_bg, proj_bg = r.bias_g.at[dp, 2:3], r.bias_g.at[dp, 3:4]
    r.bias_g[dp] = jnp.zeros(r.bias_g.shape[1:], F32)
    cond = r.condition[...].astype(F32)
    r.signal_g[dp] = (cond / (1.0 + jnp.exp(-cond))).astype(BF16)
    shared = [r.bias_g, r.table_g, r.mod_g, r.signal_g]

    def dp_copy(k, e, slot):
        return pltpu.make_async_remote_copy(
            src_ref=shared[k].at[slot],
            dst_ref=shared[k].at[slot],
            send_sem=r.dp_send.at[k, e],
            recv_sem=r.dp_recv.at[k, e],
            device_id=(lax.rem(dp + e, dp_size), me),
            device_id_type=MESH,
        )

    def share(k):
        for e in range(1, dp_size):
            dp_copy(k, e, dp).start()

    share(3)

    def forward(slot, wide):
        at = pl.ds(slot * n, wide * n)
        v = dot(mlp[at, :], w_up[...], 1, 1) + r.bias_v[0:1, 0:F]
        square = v * v
        t = jnp.tanh(GELU_C * (v + GELU_A * v * square))
        active = (0.5 * v * (1.0 + t)).astype(BF16)
        act[at, :] = active
        slope[at, :] = 0.5 * (1.0 + t) + 0.5 * v * (1.0 - t * t) * (GELU_C * (1.0 + 3.0 * GELU_A * square))
        r.part_f[at, :] = dot(active, w_down[...]).astype(BF16)

    def output_grad(slot, carry):
        at = pl.ds(slot * n, n)
        s = xor(mine, slot, sbits)
        load_cot(slot).wait()
        gate = modv[pl.ds(s, 1), 5 * D : 6 * D]
        live = live_column(pick_rows(r.pos, s, L))
        dm = (gate * (d_mlp[at, :].astype(F32) * live)).astype(BF16)
        d_mlp[at, :] = dm
        down_bg[...] += jnp.sum(dm.astype(F32), axis=0, keepdims=True)
        return carry

    if sz.fast:
        def two_slots(i, carry):
            @pl.when(i == 1)
            def _():
                lax.fori_loop(0, sz.samples, output_grad, 0)
                gat_m.step(0)
                gat_m.step(1)

            @pl.when(i == 3)
            def _():
                gat_m.step(2)

            for h in range(2):
                gat_m.near_copy(2 * i, h).wait()
            forward(2 * i, 2)
            fwd.near_copy(i).start()

            @pl.when(i > 0)
            def _():
                fwd.near_add(i - 1)

            pl.when(i == 2)(functools.partial(fwd.send, 0, 2))
            pl.when(i == 3)(functools.partial(fwd.send, 1, 4))
            return carry

        lax.fori_loop(0, 4, two_slots, 0)
    else:
        for t in range(len(gat_m.stages)):
            gat_m.step(t)
        gat_m.finish()
        lax.fori_loop(0, sz.samples, output_grad, 0)
        slot_loop(sz, lambda slot: forward(slot, 1), fwd)

    def wide_grad(left, right, base):
        at = 0
        while at < F:
            size = min(256, F - at)
            value = dot(left[:, at : at + size], right[...], 0, 0).astype(BF16)
            cut = min(max(F // 2 - at, 0), size)
            if cut:
                grads[0, base + at : base + at + cut, :] = value[:cut]
            if cut < size:
                start = base + at + cut - F // 2
                grads[1, start : start + size - cut, :] = value[cut:]
            at += size

    wide_grad(act, d_mlp, 0)
    begin(0)

    def backward(slot):
        at = pl.ds(slot * n, n)
        dpre = (dot(d_mlp[at, :], w_down[...], 1, 1) * slope[at, :]).astype(BF16)
        d_pre[at, :] = dpre
        up_bg[:, :F] += jnp.sum(dpre.astype(F32), axis=0, keepdims=True)
        r.part_b[at, :] = dot(dpre, w_up[...]).astype(BF16)

    plan = {
        4: [(1, 0, 1), (1, 1, 1)],
        6: [(1, 1, 1), (2, 0, 1), (2, 1, 1)],
        7: [(1, 0, 1)],
    }

    def bwd_extra(i):
        ticks_at(i, plan)

        @pl.when(i == 5)
        def _():
            fwd.near_add(3)
            fwd.send(0, 6)
            fwd.send(1, 6)

    slot_loop(sz, backward, bwd, bwd_extra)
    load_attn.start()
    load_att.start()
    wide_grad(d_pre, mlp, F // 2)
    begin(1)
    tick((1, 1, 1), (2, 1, 1))
    for copy in loads:
        copy.wait()
    normed2, inv2 = layer_stats(r.hidden_v[...])
    r.normed_v[...] = normed2
    bwd.close()
    tick((1, 0, 1), (1, 1, 1), (2, 0, 1), (2, 1, 1), (3, 0, 1), (3, 1, 2))

    mrow = pl.ds(mine, 1)
    live = live_column(pick_rows(r.pos, mine, L)[:, :block])
    d_out = r.cot_own[...].astype(F32) * live
    d_mlp_in = bwd.own_sum()
    g = d_mlp_in * (1.0 + modv[mrow, 4 * D : 5 * D])
    dh = d_out + layer_back(g, r.normed_v[...], inv2)
    r.dh_v[...] = dh
    r.d_attn[:block, :] = (modv[mrow, 2 * D : 3 * D] * dh).astype(BF16)
    gat_d.start()
    tick((1, 0, 1))

    early, late_sums = r.early, r.late_sums
    early[me, 0:1, :] = jnp.sum(dh * r.res_v[...], axis=0, keepdims=True)
    load_kept.start()
    early[me, 1:2, :] = jnp.sum(d_mlp_in, axis=0, keepdims=True)
    early[me, 2:3, :] = jnp.sum(d_mlp_in * r.normed_v[...], axis=0, keepdims=True)

    def finish_out():
        fwd.close()
        live = live_column(pick_rows(r.pos, mine, L)[:, :block])
        mlp_out = fwd.own_sum() + r.bias_v[1:2, :]
        early[me, 3:4, :] = jnp.sum(mlp_out * (r.cot_own[...].astype(F32) * live), axis=0, keepdims=True)
        out_own = (r.hidden_v[...] + modv[mrow, 5 * D : 6 * D] * mlp_out) * live
        r.part_f[:block, :] = out_own.astype(BF16)

    def dm_copy(ref, k, d, slot):
        return pltpu.make_async_remote_copy(
            src_ref=ref.at[slot],
            dst_ref=ref.at[slot],
            send_sem=r.dm_send.at[k, d],
            recv_sem=r.dm_recv.at[k, d],
            device_id=(dp, flip(me, d)),
            device_id_type=MESH,
        )

    def attention_grad(c, half, at):
        if c < 3:
            full = dot(qkv[:, c * lanes : (c + 1) * lanes], d_mlp[...], 0, 0)
        else:
            full = dot(r.act[:, :lanes], r.d_attn[...], 0, 0)
        rows = [full[h * HEAD_PAD : h * HEAD_PAD + hd] for h in range(heads)]
        rows = jnp.concatenate(rows, axis=0) if heads > 1 else rows[0]
        grads[half, at : at + local, :] = rows.astype(BF16)

    for copy in late:
        copy.wait()
    factor = hd ** (-0.5)
    grid_g = r.grid_g
    grid_g[...] = jnp.zeros_like(grid_g)
    qkv, w_qkv, w_merge = r.qkv_v, r.w_qkv_v, r.w_merge_v
    def attention(slot):
        s = xor(mine, slot, sbits)
        at = pl.ds(slot * n, n)
        da = r.d_attn[at, :]
        merge_bg[...] += jnp.sum(da.astype(F32), axis=0, keepdims=True)
        d_att = dot(da, w_merge[...], 1, 1).astype(BF16)
        sel = pick_rows(r.pos, s, L)
        sel_wide = pick_rows(r.pos_wide, s, 2 * L)
        dq, dk, dv = [], [], []
        for h in range(heads):
            q = qkv[at, h * HEAD_PAD : (h + 1) * HEAD_PAD]
            k = qkv[at, lanes + h * HEAD_PAD : lanes + (h + 1) * HEAD_PAD]
            v = qkv[at, 2 * lanes + h * HEAD_PAD : 2 * lanes + (h + 1) * HEAD_PAD]
            d_a = d_att[:, h * HEAD_PAD : (h + 1) * HEAD_PAD]
            p = r.probs_v[slot, h]
            d_p = dot(d_a, v, 1, 1)
            dv.append(dot(p.astype(BF16), d_a, 0, 0).astype(BF16))
            ds = p * (d_p - jnp.sum(p * d_p, axis=-1, keepdims=True))
            dl = ds.astype(BF16)
            dq.append((dot(dl, k) * factor).astype(BF16))
            dk.append((dot(dl, q, 0, 0) * factor).astype(BF16))
            grid_g[h] += dot(dot(sel, dl).astype(BF16), sel_wide, 1, 1)
        joined = jnp.concatenate(dq + dk + dv, axis=1)
        qkv[at, :] = joined
        proj_bg[:, : 3 * lanes] += jnp.sum(joined.astype(F32), axis=0, keepdims=True)
        r.part_b[at, :] = dot(joined, w_qkv[...]).astype(BF16)

    if sz.fast:
        plan_one = {1: [(2, 0, 1), (2, 1, 1)], 2: [(1, 0, 1), (1, 1, 1), (3, 0, 1), (3, 1, 1)]}
        plan_two = {
            3: [(1, 0, 1), (1, 1, 1), (2, 0, 2), (2, 1, 1), (3, 0, 1)],
            4: [(1, 0, 1), (1, 1, 1), (3, 1, 1)],
            5: [(1, 1, 1), (2, 0, 1), (2, 1, 1), (3, 0, 1)],
            6: [(1, 0, 1), (2, 0, 1), (3, 0, 1), (3, 1, 1)],
            7: [(1, 0, 1), (1, 1, 1), (2, 1, 1), (3, 1, 1)],
        }

        def one(i, carry):
            q = i // 2
            pair = q + lax.rem(q, 2) * (q // 2) * -1 + (q // 2) * (1 - lax.rem(q, 2))
            slot = jnp.where(i < 2, i, 2 * pair + 1 - lax.rem(i, 2))

            ticks_at(i, plan_one)

            @pl.when(i == 1)
            def _():
                for h in range(2):
                    gat_d.near_copy(0, h).wait()

            @pl.when(i == 2)
            def _():
                gat_d.step(0)
                tick((2, 0, 1), (3, 0, 1))
                gat_d.step(1)
                fwd.take(1, *sz.sends[1, 0][1])
                fwd.take(0, *sz.sends[0, 0][1])
                fwd.send(1, 2)
                fwd.send(0, 4)
                tick((1, 0, 1), (1, 1, 1), (2, 1, 1), (3, 1, 1))
                for h in range(2):
                    gat_d.near_copy(2, h).wait()

            ticks_at(i, plan_two)

            @pl.when(i == 4)
            def _():
                gat_d.step(2)
                for d in (4, 6):
                    for h in range(2):
                        gat_d.near_copy(d, h).wait()

            attention(slot)

            @pl.when(i == 1)
            def _():
                last.near_copy(0).start()

            @pl.when((i > 1) & (lax.rem(i, 2) == 0))
            def _():
                last.near_copy(pair).start()

            @pl.when(i == 3)
            def _():
                last.near_add(0)
                last.near_add(1)
                last.send(0, 2)

            @pl.when(i == 6)
            def _():
                finish_out()

            @pl.when(i == 5)
            def _():
                last.near_add(3)
                last.send(0, 6)
                last.send(1, 6)

            @pl.when(i == 7)
            def _():
                last.near_add(2)
                last.after(2)

            return carry

        lax.fori_loop(0, 8, one, 0)
        tick((1, 1, 1), (2, 0, 1), (2, 1, 1), (3, 0, 1))
    else:
        for t in range(len(gat_d.stages)):
            gat_d.step(t)
        gat_d.finish()
        finish_out()
        slot_loop(sz, attention, last)

    load_attn.wait()
    load_att.wait()
    attention_grad(3, 1, F)
    begin(2, 1)
    tick((1, 0, 1), (2, 0, 1))
    attention_grad(0, 0, F)
    begin(2, 0)
    attention_grad(2, 1, F + local)
    begin(3, 1)
    attention_grad(1, 0, F + local)
    begin(3, 0)
    tick((1, 1, 1), (2, 1, 1), (3, 0, 1), (3, 1, 1))

    tables = r.table_g
    span = tables.shape[2]
    for h in range(heads):
        strip = jnp.zeros((grid_side, span), F32)
        for row in range(grid_side):
            piece = jnp.concatenate(
                [
                    grid_g[h, row * grid_side : (row + 1) * grid_side, :],
                    jnp.zeros((grid_side, span - 2 * L), F32),
                ],
                axis=1,
            )
            strip = strip + (pltpu.roll(piece, row * 2 * grid_side, 1) if row else piece)
        total_row = strip[0:1]
        for c in range(1, grid_side):
            total_row = total_row + pltpu.roll(strip[c : c + 1], c, 1)
        tables[dp, h : h + 1, :] = total_row

    share(0)
    share(1)
    load_kept.wait()
    normed1, inv1 = layer_stats(r.res_v[...])
    r.normed_v[...] = normed1
    last.close()
    tick((1, 0, 1), (1, 1, 1), (2, 0, 1), (2, 1, 1), (3, 1, 1))
    d_in = last.own_sum()
    g = d_in * (1.0 + modv[mrow, D : 2 * D])
    mlp[:block, :] = (r.dh_v[...] + layer_back(g, r.normed_v[...], inv1)).astype(BF16)
    late_sums[me, 0:1, :] = jnp.sum(d_in, axis=0, keepdims=True)
    late_sums[me, 1:2, :] = jnp.sum(d_in * r.normed_v[...], axis=0, keepdims=True)
    gat_k.start()
    tick((1, 1, 2), (3, 0, 1), (3, 1, 1))

    def out_copy(slot):
        return pltpu.make_async_copy(
            r.part_f.at[pl.ds(slot * n, n)], r.out.at[xor(mine, slot, sbits)], r.load_sem.at[0, slot]
        )

    def start_out(slot, carry):
        out_copy(slot).start()
        return carry

    def patch_copy(slot):
        return pltpu.make_async_copy(
            r.part_b.at[pl.ds(lax.rem(slot, 2) * L, L)], r.patch_g.at[xor(mine, slot, sbits)], r.load_sem.at[1, slot]
        )

    def patch(slot, carry):
        @pl.when(slot >= 2)
        def _():
            patch_copy(slot - 2).wait()

        sel = pick_rows(r.pos, xor(mine, slot, sbits), L)
        r.part_b[pl.ds(lax.rem(slot, 2) * L, L), :] = dot(sel, mlp[pl.ds(slot * n, n), :]).astype(BF16)
        patch_copy(slot).start()
        return carry

    for h in range(2):
        gat_k.near_copy(0, h).wait()
    if sz.fast:
        lax.fori_loop(0, 2, patch, 0)
    gat_k.step(0)
    for d in range(1, sz.mp):
        dm_copy(early, 0, d, me).start()
        dm_copy(late_sums, 1, d, me).start()
    gat_o.start()
    tick((2, 0, 1), (2, 1, 2), (3, 0, 1), (3, 1, 1))
    gat_k.step(1)
    tick((1, 0, 2), (1, 1, 1), (3, 0, 1), (3, 1, 1))
    if sz.fast:
        for d in (2, 4):
            for h in range(2):
                gat_k.near_copy(d, h).wait()
        lax.fori_loop(2, 6, patch, 0)
        gat_k.step(2)
        tick((1, 0, 1), (1, 1, 1), (2, 0, 1), (2, 1, 2), (3, 1, 1))
        for h in range(2):
            gat_k.near_copy(6, h).wait()
        lax.fori_loop(6, 8, patch, 0)
    else:
        for t in range(2, len(gat_k.stages)):
            gat_k.step(t)
        gat_k.finish(2)
        lax.fori_loop(0, sz.samples, patch, 0)
    for d in range(1, sz.mp):
        dm_copy(early, 0, d, me).wait_send()
        dm_copy(early, 0, d, flip(me, d)).wait_recv()
        dm_copy(late_sums, 1, d, me).wait_send()
        dm_copy(late_sums, 1, d, flip(me, d)).wait_recv()
    flat, mod_g = r.flat, r.mod_g
    flat[:, 6 * D :] = jnp.zeros((sz.samples, flat.shape[1] - 6 * D), F32)
    for s in range(sz.samples):
        for c in range(6):
            v = 0
            for p in range(sz.per):
                m = s * sz.per + p
                v = v + (late_sums[m, c : c + 1, :] if c < 2 else early[m, c - 2 : c - 1, :])
            flat[s : s + 1, c * D : (c + 1) * D] = v
    base = pl.multiple_of(me * cols // 128 * 128, 128)
    mod_g[dp] = flat[:, pl.ds(base, mod_g.shape[2])]
    share(2)
    tick((1, 1, 1), (2, 0, 1), (2, 1, 1), (3, 0, 1))
    tick((2, 0, 1), (2, 1, 1))
    gat_o.step(0)
    tick((1, 0, 1), (3, 1, 1), (3, 0, 1), (1, 0, 1))
    tick((3, 1, 1), (2, 1, 1))
    gat_o.step(1)
    tick((1, 0, 1), (3, 1, 1), (3, 0, 1), (3, 1, 1))
    tick((3, 0, 1), (2, 0, 1))
    for t in range(2, len(gat_o.stages)):
        gat_o.step(t)
    gat_o.finish()
    lax.fori_loop(0, sz.samples, start_out, 0)
    tick((2, 0, 1), (3, 0, 1), (3, 1, 1), (3, 0, 1))
    tick((2, 0, 1), (3, 0, 1))
    if line is not None:
        assert all(k == marks[4] for k in following.values()), following
    for k in range(4):
        for e in range(1, dp_size):
            dp_copy(k, e, dp).wait_send()
            dp_copy(k, e, lax.rem(dp + dp_size - e, dp_size)).wait_recv()
    for slot in range(sz.samples - 2, sz.samples):
        patch_copy(slot).wait()

    def wait_out(slot, carry):
        out_copy(slot).wait()
        return carry

    lax.fori_loop(0, sz.samples, wait_out, 0)
    if line is not None:
        line.finish()


def write_results(heads, hd, grid_side, cols, r):
    total = r.total
    F, local = r.up.shape[0], r.merge.shape[0]
    D = total.shape[2]
    depth = r.narrow.shape[0]
    samples = r.out.shape[0]

    def out_in(s):
        return pltpu.make_async_copy(r.out.at[s], r.out_v.at[s], r.out_sem.at[0, s])

    def out_back(s):
        return pltpu.make_async_copy(r.out_v.at[s], r.block_out.at[s], r.out_sem.at[1, s])

    jobs = []
    for s in range(samples):
        jobs.append((r.patch_g.at[s], r.patch.at[s], r.patch.shape[1]))
    rows_most = r.narrow.shape[1]

    def add(half, start, to, at, count):
        while count:
            size = min(rows_most, count)
            jobs.append((total.at[half, pl.ds(start, size)], to.at[pl.ds(at, size)], size))
            start, at, count = start + size, at + size, count - size

    for half in range(2):
        add(half, 0, r.down, half * (F // 2), F // 2)
        add(half, F // 2, r.up, half * (F // 2), F // 2)
    add(0, F, r.project, 0, 2 * local)
    add(1, F + local, r.project, 2 * local, local)
    add(1, F, r.merge, 0, local)

    def load(k):
        src, _, size = jobs[k]
        return pltpu.make_async_copy(src, r.narrow.at[k % depth, pl.ds(0, size)], r.load_sem.at[k % depth])

    def save(k):
        _, dst, size = jobs[k]
        return pltpu.make_async_copy(r.wide.at[k % depth, pl.ds(0, size)], dst, r.save_sem.at[k % depth])

    for k in range(depth):
        load(k).start()
    for s in range(samples):
        out_in(s).start()

    members, _, width = r.mod_g.shape
    shift = lax.rem(lax.axis_index("mp") * cols, 128)
    dmod = jnp.concatenate([r.mod_g[m] for m in range(members)], axis=0)
    dmod = pltpu.roll(dmod, lax.rem(width - shift, width), 1)
    upper = dmod.astype(BF16)
    parts = jnp.concatenate([upper, (dmod - upper.astype(F32)).astype(BF16)], axis=0)
    signal = jnp.concatenate([r.signal_g[m].astype(F32) for m in range(members)], axis=0).astype(BF16)
    r.mod_v[...] = dot(parts, jnp.concatenate([signal, signal], axis=0), 0, 0)[:cols]
    modulate = pltpu.make_async_copy(r.mod_v, r.modulate, r.sem.at[0])
    modulate.start()
    r.mod_bias[...] = jnp.sum(dmod, axis=0, keepdims=True)[:, :cols].reshape(cols)
    bias, table = r.bias_g[0], r.table_g[0]
    for m in range(1, members):
        bias, table = bias + r.bias_g[m], table + r.table_g[m]
    r.up_bias[...] = bias[0:1, :F].reshape(F)
    r.down_bias[...] = bias[1:2].reshape(D)
    r.merge_bias[...] = bias[2:3].reshape(D)
    lanes = heads * HEAD_PAD
    for k, c in enumerate((0, 2)):
        row = spread(bias[3:4, c * lanes : (c + 1) * lanes], heads, hd, hd - HEAD_PAD)
        r.proj_bias[k : k + 1, :] = row[:, : heads * hd]
    offsets = 2 * grid_side - 1
    r.table[...] = spread(table, offsets, offsets, -1)[:, : offsets * offsets]

    for k, (_, _, size) in enumerate(jobs):
        load(k).wait()
        if k >= depth:
            save(k - depth).wait()
        r.wide[k % depth, :size] = r.narrow[k % depth, :size].astype(F32)
        save(k).start()
        if k + depth < len(jobs):
            load(k + depth).start()
        if k < samples:
            out_in(k).wait()
            out_back(k).start()
    for k in range(max(0, len(jobs) - depth), len(jobs)):
        save(k).wait()
    for s in range(samples):
        out_back(s).wait()
    modulate.wait()


def body(
    patches,
    condition,
    lengths,
    keep_order,
    cotangent,
    projection_weight,
    query_value_bias,
    merge_weight,
    merge_output_bias,
    up_weight,
    up_projection_bias,
    down_weight,
    down_projection_bias,
    w_modulate,
    bias_modulate,
    bias_table,
):
    samples, L, D = patches.shape
    n = cotangent.shape[1]
    grid_side = math.isqrt(L)
    offsets = 2 * grid_side - 1
    heads = bias_table.shape[0]
    local = projection_weight.shape[2]
    hd = local // heads
    lanes = heads * HEAD_PAD
    F = up_weight.shape[1]
    cols = w_modulate.shape[1]
    mp, dp_size = lax.axis_size("mp"), lax.axis_size("dp")
    me = lax.axis_index("mp")
    sz = Sizes(mp, samples, n, D)
    rows, block = sz.rows, sz.block

    keep, counts, cot = keep_order, lengths, cotangent
    if sz.per > 1:
        ids = jnp.arange(n, dtype=jnp.int32)
        order = ((ids // block) ^ lax.rem(me, sz.per)) * block + ids % block
        keep = jnp.take(jnp.where(ids[None, :] < lengths[:, None], keep_order[:, :n], -1), order, axis=1)
        counts = jnp.full_like(lengths, n)
        cot = jnp.take(cot, order, axis=1)
    wide = -(-cols // 128) * 128 + 128
    modw = max(m * cols // 128 * 128 + wide for m in range(mp))
    dma = pltpu.SemaphoreType.DMA

    one = Call()
    one.arg(
        condition=condition,
        keep=keep,
        b_qv=query_value_bias,
        b_merge=merge_output_bias,
        b_mod=bias_modulate,
        b_table=bias_table,
        w_in=jnp.swapaxes(projection_weight, 1, 2),
        w_out=merge_weight,
    )
    one.arg(pltpu.SMEM, lengths=counts)
    one.arg(pl.ANY, patches=patches, w_mod=w_modulate.T)
    one.out(modv=((samples, 6 * D), F32), pos=((samples, n), jnp.int32), pos_wide=((samples, n), jnp.int32))
    one.out(
        pl.ANY,
        attn_in=((rows, D), BF16),
        qkv=((rows, 3 * lanes), BF16),
        probs=((samples, heads, n, n), F32),
        att=((rows, lanes), BF16),
        kept=((block, D), F32),
        res=((block, D), F32),
        hidden=((block, D), F32),
        mlp=((block, D), BF16),
        w_qkv=((3 * lanes, D), BF16),
        w_merge=((lanes, D), BF16),
    )
    one.vmem(
        attn_in_v=((rows, D), BF16),
        qkv_v=((rows, 3 * lanes), BF16),
        probs_v=((samples, heads, n, n), F32),
        att_v=((rows, lanes), BF16),
        kept_v=((block, D), F32),
        res_v=((block, D), F32),
        hidden_v=((block, D), F32),
        mlp_v=((block, D), BF16),
        w_qkv_v=((3 * lanes, D), BF16),
        w_merge_v=((lanes, D), BF16),
        w_mod_v=((cols, D), BF16),
        patches_v=((samples, L, D), BF16),
        mod_buf=((mp, samples, wide), F32),
        mod_wide=((samples, modw), F32),
        qv_wide=((2, lanes), F32),
        table_v=((heads, 4 * L), F32),
        normed=((rows, D), F32),
        bias_full=((heads, L, 2 * L), BF16),
        part=((rows, D), BF16),
    )
    one.scratch(
        mod_send=dma((mp,)),
        mod_recv=dma((mp,)),
        sem=dma((7,)),
        load_sem=dma((samples,)),
        save_sem=dma((4, samples)),
        red=reduce_scratch(sz),
    )
    first = one.run(
        functools.partial(attention_forward, sz, heads, hd, grid_side, cols), "attention_forward", 0, 62 << 20
    )

    chunk = 48 if dp_size == 4 and F % 96 == 0 and local % 48 == 0 else 0
    two = Call()
    two.arg(
        condition=condition,
        b_up=up_projection_bias,
        b_down=down_projection_bias,
        pos=first.pos,
        pos_wide=first.pos_wide,
        modv=first.modv,
    )
    two.arg(
        pl.ANY,
        cot=cot,
        w_up=up_weight.T,
        w_down=down_weight,
        mlp=first.mlp,
        hidden=first.hidden,
        res=first.res,
        kept=first.kept,
        qkv=first.qkv,
        probs=first.probs,
        att=first.att,
        w_qkv=first.w_qkv,
        w_merge=first.w_merge,
        attn_in=first.attn_in,
    )
    both = ((2, F + 2 * local, D), BF16)
    if chunk:
        count = (F + 2 * local) // chunk
        two.out(z_outer=both)
        two.vmem(grads=both, z_inner=((F + 2 * local, D), BF16))
        two.scratch(
            zs=dma((2, count)),
            zo=dma((2, count)),
            zf=dma((count,)),
            zi=dma((count,)),
            zt=dma((3, count)),
            zr=dma((2, count)),
        )
    else:
        two.out(grads=both)
    two.out(
        bias_g=((dp_size, 4, D), F32),
        table_g=((dp_size, heads, 4 * L), F32),
        signal_g=((dp_size, samples, D), BF16),
        mod_g=((dp_size, samples, wide), F32),
    )
    two.out(pl.ANY, out=((samples, n, D), BF16), patch_g=((samples, L, D), BF16))
    two.vmem(
        w_up_v=((F, D), BF16),
        w_down_v=((F, D), BF16),
        mlp_v=((rows, D), BF16),
        d_mlp=((rows, D), BF16),
        slope=((rows, F), F32),
        act=((rows, F), BF16),
        d_pre=((rows, F), BF16),
        part_f=((rows, D), BF16),
        part_b=((rows, D), BF16),
        d_attn=((rows, D), BF16),
        cot_own=((block, D), BF16),
        hidden_v=((block, D), F32),
        res_v=((block, D), F32),
        normed_v=((block, D), F32),
        dh_v=((block, D), F32),
        qkv_v=((rows, 3 * lanes), BF16),
        probs_v=((samples, heads, n, n), F32),
        w_qkv_v=((3 * lanes, D), BF16),
        w_merge_v=((lanes, D), BF16),
        grid_g=((heads, L, 2 * L), F32),
        early=((mp, 4, D), F32),
        late_sums=((mp, 2, D), F32),
        flat=((samples, modw), F32),
        bias_v=((2, D), F32),
    )
    two.scratch(
        sem=dma((13,)),
        load_sem=dma((3, samples)),
        dm_send=dma((2, mp)),
        dm_recv=dma((2, mp)),
        dp_send=dma((4, dp_size)),
        dp_recv=dma((4, dp_size)),
        red_f=reduce_scratch(sz),
        red_b=reduce_scratch(sz),
        last_sems=reduce_scratch(sz)[2:],
        gat_m=gather_scratch(sz),
        gat_d=gather_scratch(sz),
        gat_o=gather_scratch(sz),
        gat_k=gather_scratch(sz),
    )
    got = two.run(
        functools.partial(block_backward, sz, heads, hd, grid_side, cols, dp_size, chunk), "block_backward", 1, 64 << 20
    )

    total = got.z_outer if chunk else lax.psum(got.grads, "dp")
    three = Call()
    three.arg(mod_g=got.mod_g, signal_g=got.signal_g, bias_g=got.bias_g, table_g=got.table_g)
    three.arg(pl.ANY, total=total, out=got.out, patch_g=got.patch_g)
    three.out(
        mod_bias=((cols,), F32),
        up_bias=((F,), F32),
        down_bias=((D,), F32),
        merge_bias=((D,), F32),
        proj_bias=((2, local), F32),
        table=((heads, offsets * offsets), F32),
    )
    three.out(
        pl.ANY,
        block_out=((samples, n, D), BF16),
        patch=((samples, L, D), F32),
        up=((F, D), F32),
        down=((F, D), F32),
        project=((3 * local, D), F32),
        merge=((local, D), F32),
        modulate=((cols, D), F32),
    )
    depth = 4
    three.vmem(narrow=((depth, 288, D), BF16), wide=((depth, 288, D), F32), mod_v=((cols, D), F32), out_v=((samples, n, D), BF16))
    three.scratch(sem=dma((1,)), out_sem=dma((2, samples)), load_sem=dma((depth,)), save_sem=dma((depth,)))
    end = three.run(functools.partial(write_results, heads, hd, grid_side, cols), "write_results", None, 63 << 20)

    block_out = end.block_out
    if sz.per > 1:
        block_out = jnp.take(block_out, order, axis=1)
    return (
        block_out,
        end.patch,
        jnp.swapaxes(end.project.reshape(3, local, D), 1, 2),
        end.proj_bias,
        end.merge,
        end.merge_bias,
        end.up.T,
        end.up_bias,
        end.down,
        end.down_bias,
        end.modulate.T,
        end.mod_bias,
        end.table,
    )


def solution(mesh):
    placed = (
        P("dp", None, None),
        P("dp", None),
        P("dp"),
        P("dp", None),
        P("dp", None, None),
        P(None, None, "mp"),
        P(None, "mp"),
        P("mp", None),
        P(),
        P(None, "mp"),
        P("mp"),
        P("mp", None),
        P(),
        P(None, "mp"),
        P("mp"),
        P("mp", None),
    )
    return jax.shard_map(
        body,
        mesh=mesh,
        in_specs=placed,
        out_specs=(
            P("dp", None, None),
            P("dp", None, None),
            P(None, None, "mp"),
            P(None, "mp"),
            P("mp", None),
            P(),
            P(None, "mp"),
            P("mp"),
            P("mp", None),
            P(),
            P(None, "mp"),
            P("mp"),
            P("mp", None),
        ),
        check_vma=False,
    )
```

```python
import functools
import math
from types import SimpleNamespace

import jax
import jax.numpy as jnp
from jax import lax
from jax.experimental import pallas as pl
from jax.experimental.pallas import tpu as pltpu
from jax.sharding import PartitionSpec as P

MESH = pl.DeviceIdType.MESH
F32 = jnp.float32
BF16 = jnp.bfloat16
EPSILON = 1e-06
MASKED = -1000000000.0
GELU_C = math.sqrt(2.0 / math.pi)
GELU_A = 0.044715
VMEM = pl.BlockSpec(memory_space=pltpu.VMEM)
HEAD_PAD = 128


def dot(a, b, ca=1, cb=0):
    return lax.dot_general(a, b, (((ca,), (cb,)), ((), ())), preferred_element_type=F32)


def bit_of(value, k):
    return lax.rem(value // (1 << k), 2)


def flip(value, mask):
    out = value
    k = 0
    while (1 << k) <= mask:
        if mask & (1 << k):
            out = out + (1 << k) * (1 - 2 * bit_of(value, k))
        k += 1
    return out


def xor(a, b, bits):
    out = 0
    for k in range(bits):
        out = out + (1 << k) * lax.rem(bit_of(a, k) + bit_of(b, k), 2)
    return out


class Sizes:
    def __init__(self, mp, samples, slots, width):
        self.mp, self.samples, self.slots, self.width = mp, samples, slots, width
        self.bits = mp.bit_length() - 1
        self.rows = samples * slots
        self.block = self.rows // mp
        self.half = self.block // 2
        self.per = self.block and slots // self.block
        rest = [1 << k for k in range(1, self.bits)]
        self.orders = (rest, rest[::-1])
        self.sends = {}
        count = 0
        for h in range(2):
            live = list(range(0, mp, 2))
            for t, bit in enumerate(self.orders[h]):
                moved = [d for d in live if d & bit]
                live = [d for d in live if not d & bit]
                self.sends[h, t] = [(d, bit, count + i) for i, d in enumerate(moved)]
                count += len(moved)
        self.steps = len(rest)
        self.far = count
        self.near = mp // 2
        self.fast = self.steps == 2 and self.per == 1


def my_index():
    return lax.axis_index("dp"), lax.axis_index("mp")


def rows_of(ref, start, size):
    return ref.at[pl.ds(start, size)]


class Reduce:
    def __init__(self, sz, part, refs):
        self.sz, self.part = sz, part
        self.near_buf, self.far_buf, self.near_send, self.near_recv, self.far_send, self.far_recv = refs
        self.dp, self.me = my_index()

    def near_copy(self, pair):
        b = self.sz.block
        return pltpu.make_async_remote_copy(
            src_ref=rows_of(self.part, (2 * pair + 1) * b, b),
            dst_ref=rows_of(self.near_buf, pair * b, b),
            send_sem=self.near_send.at[pair],
            recv_sem=self.near_recv.at[pair],
            device_id=(self.dp, flip(self.me, 1)),
            device_id_type=MESH,
        )

    def far_copy(self, h, d, bit, i):
        b, hb = self.sz.block, self.sz.half
        return pltpu.make_async_remote_copy(
            src_ref=rows_of(self.part, d * b + h * hb, hb),
            dst_ref=rows_of(self.far_buf, i * hb, hb),
            send_sem=self.far_send.at[i],
            recv_sem=self.far_recv.at[i],
            device_id=(self.dp, flip(self.me, bit)),
            device_id_type=MESH,
        )

    def add(self, start, buf, at, size):
        a = self.part[pl.ds(start, size), :].astype(F32) + buf[pl.ds(at, size), :].astype(F32)
        self.part[pl.ds(start, size), :] = a.astype(BF16)

    def near_add(self, pair):
        b = self.sz.block
        self.near_copy(pair).wait()
        self.add(2 * pair * b, self.near_buf, pair * b, b)

    def send(self, h, d):
        for t in range(self.sz.steps):
            for m in self.sz.sends[h, t]:
                if m[0] == d:
                    self.far_copy(h, *m).start()

    def take(self, h, d, bit, i, add=True):
        b, hb = self.sz.block, self.sz.half
        self.far_copy(h, d, bit, i).wait()
        if add:
            self.add((d - bit) * b + h * hb, self.far_buf, i * hb, hb)

    def after(self, k):
        if k == 0:
            self.send(0, 6)
            self.send(1, 6)
        if k == 1:
            self.send(0, 2)
        if k == 2:
            self.send(1, 4)
            self.take(1, *self.sz.sends[1, 0][1])
            self.send(1, 2)
            self.take(0, *self.sz.sends[0, 0][1])
            self.send(0, 4)

    def close(self):
        sz = self.sz
        if sz.fast:
            for h in range(2):
                for t in range(2):
                    for m in sz.sends[h, t]:
                        if m[0] == m[1]:
                            self.take(h, *m, add=False)
            return

        def one(i, carry):
            self.near_add(sz.near - 1 - i)
            return carry

        lax.fori_loop(0, sz.near, one, 0)
        for t in range(sz.steps):
            for h in range(2):
                for m in sz.sends[h, t]:
                    self.far_copy(h, *m).start()
            for h in range(2):
                for m in sz.sends[h, t]:
                    self.take(h, *m, add=t < sz.steps - 1)

    def own_sum(self):
        sz, hb = self.sz, self.sz.half
        out = []
        for h in range(2):
            total = self.part[h * hb : (h + 1) * hb, :].astype(F32)
            for t in range(0 if sz.fast else sz.steps - 1, sz.steps):
                for d, bit, i in sz.sends[h, t]:
                    if d == bit:
                        total = total + self.far_buf[i * hb : (i + 1) * hb, :].astype(F32)
            out.append(total)
        return jnp.concatenate(out, axis=0)


class Gather:
    def __init__(self, sz, out, sems):
        self.sz, self.out = sz, out
        self.near_send, self.near_recv, self.far_send, self.far_recv = sems
        self.dp, self.me = my_index()
        self.first, self.stages = [], []
        if sz.fast:
            x, y = sz.orders[0]
            self.first = [(1, 0, x, 0), (0, 0, y, 1), (0, 0, x, 2), (1, 0, y, 3)]
            on = {0: (1, x, y, 5), 1: (0, y, x, 4)}
            self.stages = [
                [(self.first[1], [on[1]]), (self.first[0], [on[0]])],
                [(self.first[2], []), (self.first[3], [])],
                [(on[1], []), (on[0], [])],
            ]
        else:
            count, plan = 0, {}
            for h in range(2):
                have = [0]
                for t, bit in enumerate(sz.orders[h][::-1]):
                    plan[h, t] = [(h, d, bit, count + i) for i, d in enumerate(have)]
                    count += len(have)
                    have = have + [d | bit for d in have]
            self.first = plan[0, 0] + plan[1, 0]
            for t in range(sz.steps):
                stage = []
                for h in range(2):
                    later = plan[h, t + 1] if t + 1 < sz.steps else []
                    for k, m in enumerate(plan[h, t]):
                        stage.append((m, later if k == len(plan[h, t]) - 1 else []))
                self.stages.append(stage)

    def near_copy(self, d, h):
        b, hb = self.sz.block, self.sz.half
        return pltpu.make_async_remote_copy(
            src_ref=rows_of(self.out, d * b + h * hb, hb),
            dst_ref=rows_of(self.out, (d + 1) * b + h * hb, hb),
            send_sem=self.near_send.at[d + h],
            recv_sem=self.near_recv.at[d + h],
            device_id=(self.dp, flip(self.me, 1)),
            device_id_type=MESH,
        )

    def far_copy(self, h, d, bit, i):
        b, hb = self.sz.block, self.sz.half
        return pltpu.make_async_remote_copy(
            src_ref=rows_of(self.out, d * b + h * hb, hb),
            dst_ref=rows_of(self.out, (d + bit) * b + h * hb, hb),
            send_sem=self.far_send.at[i],
            recv_sem=self.far_recv.at[i],
            device_id=(self.dp, flip(self.me, bit)),
            device_id_type=MESH,
        )

    def start(self):
        for m in self.first:
            self.far_copy(*m).start()
        for h in range(2):
            self.near_copy(0, h).start()

    def step(self, t):
        for m, later in self.stages[t]:
            self.far_copy(*m).wait()
            for n in later:
                self.far_copy(*n).start()
            h, d, bit, _ = m
            self.near_copy(d + bit, h).start()

    def finish(self, first=0):
        for d in range(first, self.sz.mp, 2):
            for h in range(2):
                self.near_copy(d, h).wait()


def reduce_scratch(sz):
    return [
        pltpu.VMEM((sz.near * sz.block, sz.width), BF16),
        pltpu.VMEM((sz.far * sz.half, sz.width), BF16),
        pltpu.SemaphoreType.DMA((sz.near,)),
        pltpu.SemaphoreType.DMA((sz.near,)),
        pltpu.SemaphoreType.DMA((sz.far,)),
        pltpu.SemaphoreType.DMA((sz.far,)),
    ]


def gather_scratch(sz):
    return [
        pltpu.SemaphoreType.DMA((sz.mp,)),
        pltpu.SemaphoreType.DMA((sz.mp,)),
        pltpu.SemaphoreType.DMA((sz.far,)),
        pltpu.SemaphoreType.DMA((sz.far,)),
    ]


def slot_loop(sz, body, red, extra=None):
    if sz.fast:

        def one(i, carry):
            q = i // 2
            pair = 2 * (1 - lax.rem(q, 2)) + 1 - q // 2
            other = 1 - lax.rem(i, 2)
            body(2 * pair + other)

            @pl.when(other == 1)
            def _():
                red.near_copy(pair).start()

            @pl.when(other == 0)
            def _():
                red.near_add(pair)

            for k in range(3):
                pl.when(i == 2 * k + 1)(functools.partial(red.after, k))
            if extra is not None:
                extra(i)
            return carry

    else:
        pairs = sz.per // 2

        def one(i, carry):
            slot = sz.samples - 1 - i
            body(slot)
            for p in range(pairs):
                red.near_copy(slot * pairs + p).start()
            return carry

    lax.fori_loop(0, sz.samples, one, 0)


def layer_stats(values):
    centre = jnp.mean(values, axis=-1, keepdims=True)
    shifted = values - centre
    spread = jnp.mean(shifted * shifted, axis=-1, keepdims=True)
    inv_std = lax.rsqrt(spread + EPSILON)
    return shifted * inv_std, inv_std


def layer_back(gradient, normed, inv_std):
    mean_grad = jnp.mean(gradient, axis=-1, keepdims=True)
    mean_mix = jnp.mean(gradient * normed, axis=-1, keepdims=True)
    return inv_std * (gradient - mean_grad - normed * mean_mix)


def pick_rows(ids_ref, s, count):
    ids = ids_ref[pl.ds(s, 1), :]
    return (lax.broadcasted_iota(jnp.int32, (count, ids.shape[1]), 0) == ids).astype(F32).astype(BF16)


def spread(row, pieces, size, step):
    width = row.shape[1]
    lane = lax.broadcasted_iota(jnp.int32, row.shape, 1)
    total = jnp.zeros_like(row)
    for p in range(pieces):
        start = p * (size + step) if step > 0 else p * size
        moved = pltpu.roll(row, (p * step) % width, 1) if p else row
        total = jnp.where((lane >= start) & (lane < start + size), moved, total)
    return total


def spread_heads(row, heads, hd):
    return spread(row, heads, hd, HEAD_PAD - hd)


def live_column(sel):
    ones = jnp.ones((sel.shape[0], 128), BF16)
    return dot(sel, ones, 0, 0)[:, 0:1]


def stripe_of(rows):
    return 96 if rows % 192 == 0 else rows // 2


class Call:
    def __init__(self):
        self.args, self.specs, self.outs, self.out_specs, self.scratch_of = {}, [], {}, [], {}

    def arg(self, space=pltpu.VMEM, **values):
        self.args.update(values)
        self.specs += [pl.BlockSpec(memory_space=space)] * len(values)

    def out(self, space=pltpu.VMEM, **results):
        for name, (shape, dtype) in results.items():
            self.outs[name] = jax.ShapeDtypeStruct(shape, dtype)
            self.out_specs.append(pl.BlockSpec(memory_space=space))

    def scratch(self, **buffers):
        self.scratch_of.update(buffers)

    def vmem(self, **buffers):
        for name, (shape, dtype) in buffers.items():
            self.scratch_of[name] = pltpu.VMEM(shape, dtype)

    def run(self, kernel, name, cid, limit):
        flat = []
        for value in self.scratch_of.values():
            flat += value if isinstance(value, list) else [value]

        def inner(*refs):
            r, refs = SimpleNamespace(), list(refs)
            for key in list(self.args) + list(self.outs):
                setattr(r, key, refs.pop(0))
            for key, value in self.scratch_of.items():
                count = len(value) if isinstance(value, list) else 0
                setattr(r, key, [refs.pop(0) for _ in range(count)] if count else refs.pop(0))
            kernel(r)

        got = pl.pallas_call(
            inner,
            out_shape=list(self.outs.values()),
            in_specs=self.specs,
            out_specs=self.out_specs,
            scratch_shapes=flat,
            name=name,
            compiler_params=pltpu.CompilerParams(vmem_limit_bytes=limit)
            if cid is None
            else pltpu.CompilerParams(collective_id=cid, has_side_effects=True, vmem_limit_bytes=limit),
        )(*self.args.values())
        return SimpleNamespace(**dict(zip(self.outs, got)))


def attention_forward(sz, heads, hd, grid_side, cols, r):
    dp, me = my_index()
    mine = me // sz.per
    sbits = sz.samples.bit_length() - 1
    D, n, L = sz.width, sz.slots, grid_side * grid_side
    lanes = heads * HEAD_PAD
    red = Reduce(sz, r.part, r.red)
    mod_buf, mod_wide, modv = r.mod_buf, r.mod_wide, r.modv
    wide = mod_buf.shape[2]
    sem = r.sem

    barrier = pltpu.get_barrier_semaphore()
    for d in range(1, sz.mp):
        pl.semaphore_signal(barrier, inc=1, device_id=(dp, flip(me, d)), device_id_type=MESH)
    load_mod = pltpu.make_async_copy(r.w_mod, r.w_mod_v, sem.at[0])

    def load_patches(i, slot):
        return pltpu.make_async_copy(r.patches.at[xor(mine, slot, sbits)], r.patches_v.at[slot], r.load_sem.at[i])

    def start_load(slot, carry):
        load_patches(slot, slot).start()
        return carry

    load_mod.start()
    lax.fori_loop(0, sz.samples, start_load, 0)
    slots = lax.broadcasted_iota(jnp.int32, (1, n), 1)
    for s in range(sz.samples):
        pos = jnp.where(slots < r.lengths[s], r.keep[s : s + 1, 0:n], -1)
        r.pos[s : s + 1, :] = pos
        turned = L - 1 - pos
        r.pos_wide[s : s + 1, :] = jnp.where(pos < 0, -1, turned + turned // grid_side * grid_side)
    r.qv_wide[...] = jnp.zeros_like(r.qv_wide)
    r.qv_wide[:, 0 : heads * hd] = r.b_qv[...].astype(F32)
    r.qv_wide[...] = spread_heads(r.qv_wide[...], heads, hd)
    r.table_v[...] = jnp.zeros_like(r.table_v)
    offsets = 2 * grid_side - 1
    r.table_v[:, 0 : offsets * offsets] = r.b_table[...].astype(F32)
    r.table_v[...] = spread(r.table_v[...], offsets, offsets, 1)
    w_qkv, w_merge = r.w_qkv_v, r.w_merge_v
    pad_rows = jnp.zeros((HEAD_PAD - hd, D), F32)
    for h in range(heads):
        for c in range(3):
            piece = r.w_in[c].astype(F32)[h * hd : (h + 1) * hd]
            w_qkv[c * lanes + h * HEAD_PAD : c * lanes + (h + 1) * HEAD_PAD, :] = jnp.concatenate(
                [piece, pad_rows], axis=0
            ).astype(BF16)
        piece = r.w_out[...].astype(F32)[h * hd : (h + 1) * hd]
        w_merge[h * HEAD_PAD : (h + 1) * HEAD_PAD, :] = jnp.concatenate([piece, pad_rows], axis=0).astype(BF16)
    save = [
        pltpu.make_async_copy(w_qkv, r.w_qkv, sem.at[1]),
        pltpu.make_async_copy(w_merge, r.w_merge, sem.at[2]),
    ]
    for copy in save:
        copy.start()

    bias_full = r.bias_full
    span = r.table_v.shape[1]
    for h in range(heads):
        line = r.table_v[h : h + 1, :]
        strip = jnp.concatenate([line] + [pltpu.roll(line, span - c, 1) for c in range(1, grid_side)], axis=0)
        for row in range(grid_side):
            rolled = pltpu.roll(strip, span - row * 2 * grid_side, 1) if row else strip
            bias_full[h, row * grid_side : (row + 1) * grid_side, :] = rolled[:, : 2 * L].astype(BF16)

    cond = r.condition[...].astype(F32)
    signal = (cond / (1.0 + jnp.exp(-cond))).astype(BF16)
    mod_buf[me] = jnp.zeros((sz.samples, wide), F32)
    load_mod.wait()
    mod_buf[me, :, 0:cols] = dot(signal, r.w_mod_v[...], 1, 1) + r.b_mod[...].astype(F32).reshape(1, cols)
    pl.semaphore_wait(barrier, sz.mp - 1)

    def mod_copy(d, slot):
        return pltpu.make_async_remote_copy(
            src_ref=mod_buf.at[slot],
            dst_ref=mod_buf.at[slot],
            send_sem=r.mod_send.at[d],
            recv_sem=r.mod_recv.at[d],
            device_id=(dp, flip(me, d)),
            device_id_type=MESH,
        )

    for d in range(1, sz.mp):
        mod_copy(d, me).start()

    normed, kept_own = r.normed, r.kept_v

    def norm_one(slot, carry):
        load_patches(slot, slot).wait()
        sel = pick_rows(r.pos, xor(mine, slot, sbits), L)
        kept = dot(sel, r.patches_v[slot], 0, 0)
        value, _ = layer_stats(kept)
        normed[pl.ds(slot * n, n), :] = value

        @pl.when(slot == 0)
        def _():
            kept_own[...] = kept[: sz.block]

        return carry

    lax.fori_loop(0, sz.samples, norm_one, 0)
    save_kept = pltpu.make_async_copy(kept_own, r.kept, sem.at[3])
    save_kept.start()

    for d in range(1, sz.mp):
        mod_copy(d, me).wait_send()
        mod_copy(d, flip(me, d)).wait_recv()
    mod_wide[...] = jnp.zeros_like(mod_wide)
    for m in range(sz.mp):
        base = m * cols // 128 * 128
        phase = m * cols - base
        piece = mod_buf[m]
        if phase:
            piece = pltpu.roll(piece, phase, 1)
        mod_wide[:, base : base + wide] += piece
    modv[...] = mod_wide[:, : 6 * D]

    factor = hd ** (-0.5)
    stores = [(r.attn_in_v, r.attn_in), (r.qkv_v, r.qkv), (r.att_v, r.att)]

    def save_slot(i, slot):
        at = pl.ds(slot * n, n)
        copies = [
            pltpu.make_async_copy(a.at[at], b.at[at], r.save_sem.at[k, slot]) for k, (a, b) in enumerate(stores)
        ]
        copies.append(pltpu.make_async_copy(r.probs_v.at[slot], r.probs.at[slot], r.save_sem.at[3, slot]))
        return copies

    def body(slot):
        s = xor(mine, slot, sbits)
        at = pl.ds(slot * n, n)
        shift = modv[pl.ds(s, 1), 0:D]
        scale = modv[pl.ds(s, 1), D : 2 * D]
        entry = (normed[at, :] * (1.0 + scale) + shift).astype(BF16)
        r.attn_in_v[at, :] = entry
        proj = dot(entry, w_qkv[...], 1, 1)
        qs = (proj[:, :lanes] + r.qv_wide[0:1, :]).astype(BF16)
        ks = proj[:, lanes : 2 * lanes].astype(BF16)
        vs = (proj[:, 2 * lanes :] + r.qv_wide[1:2, :]).astype(BF16)
        r.qkv_v[at, 0:lanes] = qs
        r.qkv_v[at, lanes : 2 * lanes] = ks
        r.qkv_v[at, 2 * lanes :] = vs
        sel = pick_rows(r.pos, s, L)
        sel_wide = pick_rows(r.pos_wide, s, 2 * L)
        live = r.pos[pl.ds(s, 1), :] >= 0
        outs = []
        for h in range(heads):
            cut = slice(h * HEAD_PAD, (h + 1) * HEAD_PAD)
            bias = dot(dot(sel, bias_full[h], 0, 0).astype(BF16), sel_wide)
            scores = jnp.where(live, dot(qs[:, cut], ks[:, cut], 1, 1) * factor + bias, MASKED)
            top = jnp.max(scores, axis=-1, keepdims=True)
            e = jnp.exp(scores - top)
            p = e / jnp.sum(e, axis=-1, keepdims=True)
            r.probs_v[slot, h] = p
            outs.append(dot(p.astype(BF16), vs[:, cut]).astype(BF16))
        joined = jnp.concatenate(outs, axis=1) if heads > 1 else outs[0]
        r.att_v[at, :] = joined
        r.part[at, :] = dot(joined, w_merge[...]).astype(BF16)
        for copy in save_slot(0, slot):
            copy.start()

    slot_loop(sz, body, red)
    red.close()
    result = red.own_sum() + r.b_merge[...].astype(F32).reshape(1, D)
    r.res_v[...] = result
    hidden = kept_own[...] + modv[pl.ds(mine, 1), 2 * D : 3 * D] * result
    r.hidden_v[...] = hidden
    value, _ = layer_stats(hidden)
    shift = modv[pl.ds(mine, 1), 3 * D : 4 * D]
    scale = modv[pl.ds(mine, 1), 4 * D : 5 * D]
    r.mlp_v[...] = (value * (1.0 + scale) + shift).astype(BF16)
    save_own = [
        pltpu.make_async_copy(r.res_v, r.res, sem.at[4]),
        pltpu.make_async_copy(r.hidden_v, r.hidden, sem.at[5]),
        pltpu.make_async_copy(r.mlp_v, r.mlp, sem.at[6]),
    ]
    for copy in save_own:
        copy.start()

    def wait_slot(slot, carry):
        for copy in save_slot(0, slot):
            copy.wait()
        return carry

    lax.fori_loop(0, sz.samples, wait_slot, 0)
    for copy in save + save_own + [save_kept]:
        copy.wait()


class Line:
    def __init__(self, r, chunk):
        self.r, self.chunk = r, chunk
        self.g, self.outer_buf, self.inner_buf = r.grads, r.z_outer, r.z_inner
        self.count = self.g.shape[1] // chunk
        self.dp, self.me = my_index()
        self.is_inner = (self.dp == 1) | (self.dp == 2)
        self.is_outer = (self.dp == 0) | (self.dp == 3)
        self.step_to = 1 + self.dp // 3
        self.back_to = (self.dp - 1) * 3
        self.other = 3 - self.dp
        self.mine = 2 - self.dp
        self.passed = self.dp - 1

    def rows(self, k):
        return pl.ds(k * self.chunk, self.chunk)

    def copy(self, src, dst, send, recv, to):
        return pltpu.make_async_remote_copy(
            src_ref=src, dst_ref=dst, send_sem=send, recv_sem=recv, device_id=(to, self.me), device_id_type=MESH
        )

    def out_copy(self, j, k):
        return self.copy(
            self.g.at[j, self.rows(k)], self.outer_buf.at[j, self.rows(k)],
            self.r.zs.at[j, k], self.r.zo.at[j, k], self.step_to,
        )

    def in_copy(self, k):
        return self.copy(
            self.g.at[self.passed, self.rows(k)], self.inner_buf.at[self.rows(k)],
            self.r.zf.at[k], self.r.zi.at[k], self.other,
        )

    def total_copy(self, j, k, which, to):
        return self.copy(
            self.outer_buf.at[j, self.rows(k)], self.outer_buf.at[j, self.rows(k)],
            self.r.zt.at[which, k], self.r.zr.at[j, k], to,
        )

    def begin(self, halves, k0, k1):
        @pl.when(self.is_outer)
        def _():
            def one(k, carry):
                for j in halves:
                    self.out_copy(j, k).start()
                return carry

            lax.fori_loop(k0, k1, one, 0)

    def add(self, to, j, k, more):
        def one(i, carry):
            at = pl.ds(k * self.chunk + i * 16, 16)
            v = self.g[j, at, :].astype(F32) + self.outer_buf[j, at, :].astype(F32)
            if more:
                v = v + self.inner_buf[at, :].astype(F32)
            to[j, at, :] = v.astype(BF16)
            return carry

        lax.fori_loop(0, self.chunk // 16, one, 0)

    def stage(self, number, j, k):
        if number == 1:

            @pl.when(self.passed == j)
            def _():
                self.out_copy(j, k).wait_recv()
                self.add(self.g, j, k, False)
                self.in_copy(k).start()

        elif number == 2:

            @pl.when(self.mine == j)
            def _():
                self.out_copy(j, k).wait_recv()
                self.in_copy(k).wait_recv()
                self.add(self.outer_buf, j, k, True)
                self.total_copy(j, k, 0, self.other).start()
                self.total_copy(j, k, 1, self.back_to).start()

        else:

            @pl.when(self.passed == j)
            def _():
                self.in_copy(k).wait_send()
                self.total_copy(j, k, 0, self.other).wait_recv()
                self.total_copy(j, k, 2, self.back_to).start()

    def finish(self):
        @pl.when(self.is_inner)
        def _():
            def one(k, carry):
                self.total_copy(self.mine, k, 0, self.other).wait_send()
                self.total_copy(self.mine, k, 1, self.back_to).wait_send()
                self.total_copy(self.passed, k, 2, self.back_to).wait_send()
                return carry

            lax.fori_loop(0, self.count, one, 0)

        @pl.when(self.is_outer)
        def _():
            def one(k, carry):
                for j in range(2):
                    self.out_copy(j, k).wait_send()
                    self.total_copy(j, k, 0, self.step_to).wait_recv()
                return carry

            lax.fori_loop(0, self.count, one, 0)


def block_backward(sz, heads, hd, grid_side, cols, dp_size, chunk, r):
    dp, me = my_index()
    mine = me // sz.per
    sbits = sz.samples.bit_length() - 1
    D, n, L = sz.width, sz.slots, grid_side * grid_side
    lanes = heads * HEAD_PAD
    local = heads * hd
    F = r.w_up_v.shape[0]
    block = sz.block
    modv = r.modv
    fwd = Reduce(sz, r.part_f, r.red_f)
    bwd = Reduce(sz, r.part_b, r.red_b)
    last = Reduce(sz, r.part_b, r.red_b[:2] + r.last_sems)
    gat_m = Gather(sz, r.mlp_v, r.gat_m)
    gat_d = Gather(sz, r.d_attn, r.gat_d)
    gat_o = Gather(sz, r.part_f, r.gat_o)
    gat_k = Gather(sz, r.mlp_v, r.gat_k)
    line = Line(r, chunk) if chunk else None
    grads = r.grads
    sem = r.sem

    stripe = stripe_of(F)
    per_half, per_local = (F // 2 // chunk, local // chunk) if chunk else (0, 0)
    marks = [0, per_half, 2 * per_half, 2 * per_half + per_local, 2 * per_half + 2 * per_local]
    following = {(number, j): 0 for number in (1, 2, 3) for j in range(2)}

    def tick(*steps):
        if line is None:
            return
        for number, j, count in steps:
            k0 = following[number, j]
            k1 = min(k0 + count, marks[4])
            assert number == 1 or k1 <= following[number - 1, j]
            following[number, j] = k1
            if k1 - k0 == 1:
                line.stage(number, j, k0)
            elif k1 > k0:

                def one(k, carry, number=number, j=j):
                    line.stage(number, j, k)
                    return carry

                lax.fori_loop(k0, k1, one, 0)

    def begin(group, *halves):
        if line is not None:
            line.begin(halves or (0, 1), marks[group], marks[group + 1])

    def ticks_at(i, plan):
        if line is not None:
            for when, steps in plan.items():
                pl.when(i == when)(lambda steps=steps: tick(*steps))

    load_up = pltpu.make_async_copy(r.w_up, r.w_up_v, sem.at[0])
    load_down = pltpu.make_async_copy(r.w_down, r.w_down_v, sem.at[1])
    load_up.start()
    load_down.start()

    load_own = pltpu.make_async_copy(r.mlp, r.mlp_v.at[pl.ds(0, block)], sem.at[12])
    load_own.start()

    def load_cot(slot):
        at = pl.ds(slot * n, n)
        return pltpu.make_async_copy(r.cot.at[xor(mine, slot, sbits)], r.d_mlp.at[at], r.load_sem.at[1, slot])

    def start_cot(slot, carry):
        load_cot(slot).start()
        return carry

    lax.fori_loop(0, sz.samples, start_cot, 0)
    loads = [
        pltpu.make_async_copy(r.cot.at[mine, pl.ds(0, block)], r.cot_own, sem.at[2]),
        pltpu.make_async_copy(r.hidden, r.hidden_v, sem.at[3]),
        pltpu.make_async_copy(r.res, r.res_v, sem.at[4]),
    ]
    late = [
        pltpu.make_async_copy(r.qkv, r.qkv_v, sem.at[6]),
        pltpu.make_async_copy(r.probs, r.probs_v, sem.at[7]),
        pltpu.make_async_copy(r.w_qkv, r.w_qkv_v, sem.at[9]),
        pltpu.make_async_copy(r.w_merge, r.w_merge_v, sem.at[10]),
    ]
    for copy in loads + late:
        copy.start()
    load_attn = pltpu.make_async_copy(r.attn_in, r.d_mlp, sem.at[11])
    load_kept = pltpu.make_async_copy(r.kept, r.res_v, sem.at[5])
    load_att = pltpu.make_async_copy(r.att, r.act.at[:, pl.ds(0, lanes)], sem.at[8])

    barrier = pltpu.get_barrier_semaphore()
    for d in range(1, sz.mp):
        pl.semaphore_signal(barrier, inc=1, device_id=(dp, flip(me, d)), device_id_type=MESH)
    for e in range(1, dp_size):
        pl.semaphore_signal(barrier, inc=1, device_id=(lax.rem(dp + e, dp_size), me), device_id_type=MESH)
    pl.semaphore_wait(barrier, sz.mp + dp_size - 2)
    load_own.wait()
    gat_m.start()
    r.bias_v[0:1, 0:F] = r.b_up[...].astype(F32).reshape(1, F)
    r.bias_v[1:2, :] = r.b_down[...].astype(F32).reshape(1, D)
    load_up.wait()
    load_down.wait()
    w_up, w_down, mlp = r.w_up_v, r.w_down_v, r.mlp_v
    act, d_pre, d_mlp, slope = r.act, r.d_pre, r.d_mlp, r.slope

    up_bg, down_bg = r.bias_g.at[dp, 0:1], r.bias_g.at[dp, 1:2]
    merge_bg, proj_bg = r.bias_g.at[dp, 2:3], r.bias_g.at[dp, 3:4]
    r.bias_g[dp] = jnp.zeros(r.bias_g.shape[1:], F32)
    cond = r.condition[...].astype(F32)
    r.signal_g[dp] = (cond / (1.0 + jnp.exp(-cond))).astype(BF16)
    shared = [r.bias_g, r.table_g, r.mod_g, r.signal_g]

    def dp_copy(k, e, slot):
        return pltpu.make_async_remote_copy(
            src_ref=shared[k].at[slot],
            dst_ref=shared[k].at[slot],
            send_sem=r.dp_send.at[k, e],
            recv_sem=r.dp_recv.at[k, e],
            device_id=(lax.rem(dp + e, dp_size), me),
            device_id_type=MESH,
        )

    def share(k):
        for e in range(1, dp_size):
            dp_copy(k, e, dp).start()

    share(3)

    def forward(slot, wide):
        at = pl.ds(slot * n, wide * n)
        v = dot(mlp[at, :], w_up[...], 1, 1) + r.bias_v[0:1, 0:F]
        square = v * v
        h = 0.5 * jnp.tanh(v * (GELU_C * GELU_A * square + GELU_C)) + 0.5
        active = (v * h).astype(BF16)
        act[at, :] = active
        slope[at, :] = h * (1.0 + (1.0 - h) * (v * (6.0 * GELU_C * GELU_A * square + 2.0 * GELU_C)))
        r.part_f[at, :] = dot(active, w_down[...]).astype(BF16)

    def output_grad(slot, carry):
        at = pl.ds(slot * n, n)
        s = xor(mine, slot, sbits)
        load_cot(slot).wait()
        gate = modv[pl.ds(s, 1), 5 * D : 6 * D]
        live = live_column(pick_rows(r.pos, s, L))
        dm = (gate * (d_mlp[at, :].astype(F32) * live)).astype(BF16)
        d_mlp[at, :] = dm
        down_bg[...] += jnp.sum(dm.astype(F32), axis=0, keepdims=True)
        return carry

    if sz.fast:
        def two_slots(i, carry):
            @pl.when(i == 1)
            def _():
                lax.fori_loop(0, sz.samples, output_grad, 0)
                gat_m.step(0)
                gat_m.step(1)

            @pl.when(i == 3)
            def _():
                gat_m.step(2)

            for h in range(2):
                gat_m.near_copy(2 * i, h).wait()
            forward(2 * i, 2)
            fwd.near_copy(i).start()

            @pl.when(i > 0)
            def _():
                fwd.near_add(i - 1)

            pl.when(i == 2)(functools.partial(fwd.send, 0, 2))
            pl.when(i == 3)(functools.partial(fwd.send, 1, 4))
            return carry

        lax.fori_loop(0, 4, two_slots, 0)
    else:
        for t in range(len(gat_m.stages)):
            gat_m.step(t)
        gat_m.finish()
        lax.fori_loop(0, sz.samples, output_grad, 0)
        slot_loop(sz, lambda slot: forward(slot, 1), fwd)

    def wide_grad(left, right, base, group):
        at, sent = 0, 0
        while at < F:
            size = min(256, F - at)
            value = dot(left[:, at : at + size], right[...], 0, 0).astype(BF16)
            row = at
            while row < at + size:
                turn = row // stripe
                count = min((turn + 1) * stripe, at + size) - row
                to = base + turn // 2 * stripe + row % stripe
                grads[turn % 2, to : to + count, :] = value[row - at : row - at + count]
                row += count
            at += size
            if line is not None:
                ready = at // (2 * stripe) * (stripe // chunk)
                if ready > sent:
                    line.begin((0, 1), marks[group] + sent, marks[group] + ready)
                    sent = ready

    wide_grad(act, d_mlp, 0, 0)

    def backward(slot):
        at = pl.ds(slot * n, n)
        dpre = (dot(d_mlp[at, :], w_down[...], 1, 1) * slope[at, :]).astype(BF16)
        d_pre[at, :] = dpre
        up_bg[:, :F] += jnp.sum(dpre.astype(F32), axis=0, keepdims=True)
        r.part_b[at, :] = dot(dpre, w_up[...]).astype(BF16)

    plan = {
        2: [(1, 1, 1)],
        3: [(1, 0, 1)],
        5: [(1, 0, 1), (1, 1, 1), (2, 0, 1), (2, 1, 1)],
    }

    def bwd_extra(i):
        ticks_at(i, plan)

        @pl.when(i == 5)
        def _():
            fwd.near_add(3)
            fwd.send(0, 6)
            fwd.send(1, 6)

    slot_loop(sz, backward, bwd, bwd_extra)
    load_attn.start()
    load_att.start()
    wide_grad(d_pre, mlp, F // 2, 1)
    tick((1, 0, 1), (1, 1, 1), (2, 0, 1), (2, 1, 1))
    for copy in loads:
        copy.wait()
    normed2, inv2 = layer_stats(r.hidden_v[...])
    r.normed_v[...] = normed2
    bwd.close()
    tick((1, 0, 1), (1, 1, 1), (2, 0, 1), (2, 1, 1), (3, 0, 1), (3, 1, 1))

    mrow = pl.ds(mine, 1)
    live = live_column(pick_rows(r.pos, mine, L)[:, :block])
    d_out = r.cot_own[...].astype(F32) * live
    d_mlp_in = bwd.own_sum()
    g = d_mlp_in * (1.0 + modv[mrow, 4 * D : 5 * D])
    dh = d_out + layer_back(g, r.normed_v[...], inv2)
    r.dh_v[...] = dh
    r.d_attn[:block, :] = (modv[mrow, 2 * D : 3 * D] * dh).astype(BF16)
    gat_d.start()

    early, late_sums = r.early, r.late_sums
    early[me, 0:1, :] = jnp.sum(dh * r.res_v[...], axis=0, keepdims=True)
    load_kept.start()
    early[me, 1:2, :] = jnp.sum(d_mlp_in, axis=0, keepdims=True)
    early[me, 2:3, :] = jnp.sum(d_mlp_in * r.normed_v[...], axis=0, keepdims=True)

    def finish_out():
        fwd.close()
        live = live_column(pick_rows(r.pos, mine, L)[:, :block])
        mlp_out = fwd.own_sum() + r.bias_v[1:2, :]
        early[me, 3:4, :] = jnp.sum(mlp_out * (r.cot_own[...].astype(F32) * live), axis=0, keepdims=True)
        out_own = (r.hidden_v[...] + modv[mrow, 5 * D : 6 * D] * mlp_out) * live
        r.part_f[:block, :] = out_own.astype(BF16)

    def dm_copy(ref, k, d, slot):
        return pltpu.make_async_remote_copy(
            src_ref=ref.at[slot],
            dst_ref=ref.at[slot],
            send_sem=r.dm_send.at[k, d],
            recv_sem=r.dm_recv.at[k, d],
            device_id=(dp, flip(me, d)),
            device_id_type=MESH,
        )

    def attention_grad(c, half, at):
        if c < 3:
            full = dot(qkv[:, c * lanes : (c + 1) * lanes], d_mlp[...], 0, 0)
        else:
            full = dot(r.act[:, :lanes], r.d_attn[...], 0, 0)
        rows = [full[h * HEAD_PAD : h * HEAD_PAD + hd] for h in range(heads)]
        rows = jnp.concatenate(rows, axis=0) if heads > 1 else rows[0]
        grads[half, at : at + local, :] = rows.astype(BF16)

    for copy in late:
        copy.wait()
    factor = hd ** (-0.5)
    grid_g = r.grid_g
    grid_g[...] = jnp.zeros_like(grid_g)
    qkv, w_qkv, w_merge = r.qkv_v, r.w_qkv_v, r.w_merge_v
    def attention(slot):
        s = xor(mine, slot, sbits)
        at = pl.ds(slot * n, n)
        da = r.d_attn[at, :]
        merge_bg[...] += jnp.sum(da.astype(F32), axis=0, keepdims=True)
        d_att = dot(da, w_merge[...], 1, 1).astype(BF16)
        sel = pick_rows(r.pos, s, L)
        sel_wide = pick_rows(r.pos_wide, s, 2 * L)
        dq, dk, dv = [], [], []
        for h in range(heads):
            q = qkv[at, h * HEAD_PAD : (h + 1) * HEAD_PAD]
            k = qkv[at, lanes + h * HEAD_PAD : lanes + (h + 1) * HEAD_PAD]
            v = qkv[at, 2 * lanes + h * HEAD_PAD : 2 * lanes + (h + 1) * HEAD_PAD]
            d_a = d_att[:, h * HEAD_PAD : (h + 1) * HEAD_PAD]
            p = r.probs_v[slot, h]
            d_p = dot(d_a, v, 1, 1)
            dv.append(dot(p.astype(BF16), d_a, 0, 0).astype(BF16))
            ds = p * (d_p - jnp.sum(p * d_p, axis=-1, keepdims=True))
            dl = ds.astype(BF16)
            dq.append((dot(dl, k) * factor).astype(BF16))
            dk.append((dot(dl, q, 0, 0) * factor).astype(BF16))
            grid_g[h] += dot(dot(sel, dl).astype(BF16), sel_wide, 1, 1)
        joined = jnp.concatenate(dq + dk + dv, axis=1)
        qkv[at, :] = joined
        proj_bg[:, : 3 * lanes] += jnp.sum(joined.astype(F32), axis=0, keepdims=True)
        r.part_b[at, :] = dot(joined, w_qkv[...]).astype(BF16)

    if sz.fast:
        plan_one = {1: [(1, 0, 1), (1, 1, 1), (2, 0, 1), (2, 1, 1), (3, 0, 1), (3, 1, 1)], 2: [(3, 0, 1), (3, 1, 1)]}
        plan_two = {
            3: [(1, 1, 1), (2, 0, 1), (2, 1, 1), (3, 0, 1), (3, 1, 1)],
            4: [(1, 0, 1), (2, 0, 1), (2, 1, 1)],
            5: [(1, 0, 1), (1, 1, 1), (2, 1, 1), (3, 0, 1), (3, 1, 1)],
            6: [(1, 1, 1), (2, 0, 1), (3, 0, 1), (3, 1, 1)],
            7: [(1, 0, 1), (2, 0, 1), (2, 1, 1)],
        }

        def one(i, carry):
            q = i // 2
            pair = q + lax.rem(q, 2) * (q // 2) * -1 + (q // 2) * (1 - lax.rem(q, 2))
            slot = jnp.where(i < 2, i, 2 * pair + 1 - lax.rem(i, 2))

            ticks_at(i, plan_one)

            @pl.when(i == 1)
            def _():
                for h in range(2):
                    gat_d.near_copy(0, h).wait()

            @pl.when(i == 2)
            def _():
                gat_d.step(0)
                tick((1, 0, 1), (1, 1, 1), (2, 0, 1), (2, 1, 1))
                gat_d.step(1)
                fwd.take(1, *sz.sends[1, 0][1])
                fwd.take(0, *sz.sends[0, 0][1])
                fwd.send(1, 2)
                fwd.send(0, 4)
                tick((1, 0, 1), (1, 1, 1), (3, 0, 1), (3, 1, 1))
                for h in range(2):
                    gat_d.near_copy(2, h).wait()

            ticks_at(i, plan_two)

            @pl.when(i == 4)
            def _():
                gat_d.step(2)
                for d in (4, 6):
                    for h in range(2):
                        gat_d.near_copy(d, h).wait()

            attention(slot)

            @pl.when(i == 1)
            def _():
                last.near_copy(0).start()

            @pl.when((i > 1) & (lax.rem(i, 2) == 0))
            def _():
                last.near_copy(pair).start()

            @pl.when(i == 3)
            def _():
                last.near_add(0)
                last.near_add(1)
                last.send(0, 2)

            @pl.when(i == 6)
            def _():
                finish_out()

            @pl.when(i == 5)
            def _():
                last.near_add(3)
                last.send(0, 6)
                last.send(1, 6)

            @pl.when(i == 7)
            def _():
                last.near_add(2)
                last.after(2)

            return carry

        lax.fori_loop(0, 8, one, 0)
        tick((1, 0, 1), (1, 1, 1), (2, 1, 1), (3, 0, 1), (3, 1, 1))
    else:
        for t in range(len(gat_d.stages)):
            gat_d.step(t)
        gat_d.finish()
        finish_out()
        slot_loop(sz, attention, last)

    load_attn.wait()
    load_att.wait()
    attention_grad(3, 1, F)
    begin(2, 1)
    tick((2, 0, 1))
    attention_grad(0, 0, F)
    begin(2, 0)
    attention_grad(2, 1, F + local)
    begin(3, 1)
    attention_grad(1, 0, F + local)
    begin(3, 0)
    tick((1, 0, 1), (1, 1, 1), (2, 1, 1), (3, 0, 1), (3, 1, 1))

    tables = r.table_g
    span = tables.shape[2]
    for h in range(heads):
        strip = jnp.zeros((grid_side, span), F32)
        for row in range(grid_side):
            piece = jnp.concatenate(
                [
                    grid_g[h, row * grid_side : (row + 1) * grid_side, :],
                    jnp.zeros((grid_side, span - 2 * L), F32),
                ],
                axis=1,
            )
            strip = strip + (pltpu.roll(piece, row * 2 * grid_side, 1) if row else piece)
        total_row = strip[0:1]
        for c in range(1, grid_side):
            total_row = total_row + pltpu.roll(strip[c : c + 1], c, 1)
        tables[dp, h : h + 1, :] = total_row

    share(0)
    share(1)
    load_kept.wait()
    normed1, inv1 = layer_stats(r.res_v[...])
    r.normed_v[...] = normed1
    last.close()
    tick((1, 1, 2), (2, 0, 1), (3, 0, 1), (3, 1, 1))
    d_in = last.own_sum()
    g = d_in * (1.0 + modv[mrow, D : 2 * D])
    mlp[:block, :] = (r.dh_v[...] + layer_back(g, r.normed_v[...], inv1)).astype(BF16)
    late_sums[me, 0:1, :] = jnp.sum(d_in, axis=0, keepdims=True)
    late_sums[me, 1:2, :] = jnp.sum(d_in * r.normed_v[...], axis=0, keepdims=True)
    gat_k.start()
    tick((1, 1, 1), (2, 0, 1), (2, 1, 1))

    def out_copy(slot):
        return pltpu.make_async_copy(
            r.part_f.at[pl.ds(slot * n, n)], r.out.at[xor(mine, slot, sbits)], r.load_sem.at[0, slot]
        )

    def start_out(slot, carry):
        out_copy(slot).start()
        return carry

    def patch_copy(slot):
        return pltpu.make_async_copy(
            r.part_b.at[pl.ds(lax.rem(slot, 2) * L, L)], r.patch_g.at[xor(mine, slot, sbits)], r.load_sem.at[1, slot]
        )

    def patch(slot, carry):
        @pl.when(slot >= 2)
        def _():
            patch_copy(slot - 2).wait()

        sel = pick_rows(r.pos, xor(mine, slot, sbits), L)
        r.part_b[pl.ds(lax.rem(slot, 2) * L, L), :] = dot(sel, mlp[pl.ds(slot * n, n), :]).astype(BF16)
        patch_copy(slot).start()
        return carry

    for h in range(2):
        gat_k.near_copy(0, h).wait()
    if sz.fast:
        lax.fori_loop(0, 2, patch, 0)
    gat_k.step(0)
    for d in range(1, sz.mp):
        dm_copy(early, 0, d, me).start()
        dm_copy(late_sums, 1, d, me).start()
    gat_o.start()
    tick((1, 0, 1), (2, 1, 1), (3, 0, 1), (3, 1, 2))
    gat_k.step(1)
    tick((1, 0, 2), (1, 1, 1), (2, 0, 1), (2, 1, 2))
    if sz.fast:
        for d in (2, 4):
            for h in range(2):
                gat_k.near_copy(d, h).wait()
        lax.fori_loop(2, 6, patch, 0)
        gat_k.step(2)
        tick((1, 1, 2), (2, 0, 1), (2, 1, 1), (3, 0, 1), (3, 1, 1))
        for h in range(2):
            gat_k.near_copy(6, h).wait()
        lax.fori_loop(6, 8, patch, 0)
    else:
        for t in range(2, len(gat_k.stages)):
            gat_k.step(t)
        gat_k.finish(2)
        lax.fori_loop(0, sz.samples, patch, 0)
    for d in range(1, sz.mp):
        dm_copy(early, 0, d, me).wait_send()
        dm_copy(early, 0, d, flip(me, d)).wait_recv()
        dm_copy(late_sums, 1, d, me).wait_send()
        dm_copy(late_sums, 1, d, flip(me, d)).wait_recv()
    flat, mod_g = r.flat, r.mod_g
    flat[:, 6 * D :] = jnp.zeros((sz.samples, flat.shape[1] - 6 * D), F32)
    for s in range(sz.samples):
        for c in range(6):
            v = 0
            for p in range(sz.per):
                m = s * sz.per + p
                v = v + (late_sums[m, c : c + 1, :] if c < 2 else early[m, c - 2 : c - 1, :])
            flat[s : s + 1, c * D : (c + 1) * D] = v
    base = pl.multiple_of(me * cols // 128 * 128, 128)
    mod_g[dp] = flat[:, pl.ds(base, mod_g.shape[2])]
    share(2)
    tick((3, 0, 1), (3, 1, 1))
    tick((1, 0, 1), (2, 1, 1), (2, 0, 1))
    gat_o.step(0)
    tick((1, 0, 1), (3, 0, 1), (3, 1, 1), (1, 0, 1))
    tick((2, 1, 1), (3, 1, 1))
    gat_o.step(1)
    tick((3, 0, 1), (2, 0, 1), (3, 1, 1), (3, 0, 1))
    tick((2, 0, 1))
    for t in range(2, len(gat_o.stages)):
        gat_o.step(t)
    gat_o.finish()
    lax.fori_loop(0, sz.samples, start_out, 0)
    tick((2, 0, 1), (3, 0, 1), (3, 1, 1), (3, 0, 1))
    if line is not None:
        assert all(k == marks[4] for k in following.values()), following
    for k in range(4):
        for e in range(1, dp_size):
            dp_copy(k, e, dp).wait_send()
            dp_copy(k, e, lax.rem(dp + dp_size - e, dp_size)).wait_recv()
    for slot in range(sz.samples - 2, sz.samples):
        patch_copy(slot).wait()

    def wait_out(slot, carry):
        out_copy(slot).wait()
        return carry

    lax.fori_loop(0, sz.samples, wait_out, 0)
    if line is not None:
        line.finish()


def write_results(heads, hd, grid_side, cols, r):
    total = r.total
    F, local = r.up.shape[0], r.merge.shape[0]
    D = total.shape[2]
    depth = r.narrow.shape[0]
    samples = r.out.shape[0]

    def out_in(s):
        return pltpu.make_async_copy(r.out.at[s], r.out_v.at[s], r.out_sem.at[0, s])

    def out_back(s):
        return pltpu.make_async_copy(r.out_v.at[s], r.block_out.at[s], r.out_sem.at[1, s])

    jobs = []
    for s in range(samples):
        jobs.append((r.patch_g.at[s], r.patch.at[s], r.patch.shape[1]))
    rows_most = r.narrow.shape[1]

    def add(half, start, to, at, count):
        while count:
            size = min(rows_most, count)
            jobs.append((total.at[half, pl.ds(start, size)], to.at[pl.ds(at, size)], size))
            start, at, count = start + size, at + size, count - size

    stripe = stripe_of(F)
    for turn in range(F // stripe):
        add(turn % 2, turn // 2 * stripe, r.down, turn * stripe, stripe)
        add(turn % 2, F // 2 + turn // 2 * stripe, r.up, turn * stripe, stripe)
    add(0, F, r.project, 0, 2 * local)
    add(1, F + local, r.project, 2 * local, local)
    add(1, F, r.merge, 0, local)

    def load(k):
        src, _, size = jobs[k]
        return pltpu.make_async_copy(src, r.narrow.at[k % depth, pl.ds(0, size)], r.load_sem.at[k % depth])

    def save(k):
        _, dst, size = jobs[k]
        return pltpu.make_async_copy(r.wide.at[k % depth, pl.ds(0, size)], dst, r.save_sem.at[k % depth])

    for k in range(depth):
        load(k).start()
    for s in range(samples):
        out_in(s).start()

    def small_results():
        members, _, width = r.mod_g.shape
        shift = lax.rem(lax.axis_index("mp") * cols, 128)
        dmod = jnp.concatenate([r.mod_g[m] for m in range(members)], axis=0)
        dmod = pltpu.roll(dmod, lax.rem(width - shift, width), 1)
        upper = dmod.astype(BF16)
        parts = jnp.concatenate([upper, (dmod - upper.astype(F32)).astype(BF16)], axis=0)
        signal = jnp.concatenate([r.signal_g[m].astype(F32) for m in range(members)], axis=0).astype(BF16)
        r.mod_v[...] = dot(parts, jnp.concatenate([signal, signal], axis=0), 0, 0)[:cols]
        modulate = pltpu.make_async_copy(r.mod_v, r.modulate, r.sem.at[0])
        modulate.start()
        r.mod_bias[...] = jnp.sum(dmod, axis=0, keepdims=True)[:, :cols].reshape(cols)
        bias, table = r.bias_g[0], r.table_g[0]
        for m in range(1, members):
            bias, table = bias + r.bias_g[m], table + r.table_g[m]
        r.up_bias[...] = bias[0:1, :F].reshape(F)
        r.down_bias[...] = bias[1:2].reshape(D)
        r.merge_bias[...] = bias[2:3].reshape(D)
        lanes = heads * HEAD_PAD
        for k, c in enumerate((0, 2)):
            row = spread(bias[3:4, c * lanes : (c + 1) * lanes], heads, hd, hd - HEAD_PAD)
            r.proj_bias[k : k + 1, :] = row[:, : heads * hd]
        offsets = 2 * grid_side - 1
        r.table[...] = spread(table, offsets, offsets, -1)[:, : offsets * offsets]
        return modulate

    for k, (_, _, size) in enumerate(jobs):
        load(k).wait()
        if k >= depth:
            save(k - depth).wait()
        r.wide[k % depth, :size] = r.narrow[k % depth, :size].astype(F32)
        save(k).start()
        if k + depth < len(jobs):
            load(k + depth).start()
        if k < samples:
            out_in(k).wait()
            out_back(k).start()
        if k == depth:
            modulate = small_results()
    for k in range(max(0, len(jobs) - depth), len(jobs)):
        save(k).wait()
    for s in range(samples):
        out_back(s).wait()
    modulate.wait()


def body(
    patches,
    condition,
    lengths,
    keep_order,
    cotangent,
    projection_weight,
    query_value_bias,
    merge_weight,
    merge_output_bias,
    up_weight,
    up_projection_bias,
    down_weight,
    down_projection_bias,
    w_modulate,
    bias_modulate,
    bias_table,
):
    samples, L, D = patches.shape
    n = cotangent.shape[1]
    grid_side = math.isqrt(L)
    offsets = 2 * grid_side - 1
    heads = bias_table.shape[0]
    local = projection_weight.shape[2]
    hd = local // heads
    lanes = heads * HEAD_PAD
    F = up_weight.shape[1]
    cols = w_modulate.shape[1]
    mp, dp_size = lax.axis_size("mp"), lax.axis_size("dp")
    me = lax.axis_index("mp")
    sz = Sizes(mp, samples, n, D)
    rows, block = sz.rows, sz.block

    keep, counts, cot = keep_order, lengths, cotangent
    if sz.per > 1:
        ids = jnp.arange(n, dtype=jnp.int32)
        order = ((ids // block) ^ lax.rem(me, sz.per)) * block + ids % block
        keep = jnp.take(jnp.where(ids[None, :] < lengths[:, None], keep_order[:, :n], -1), order, axis=1)
        counts = jnp.full_like(lengths, n)
        cot = jnp.take(cot, order, axis=1)
    wide = -(-cols // 128) * 128 + 128
    modw = max(m * cols // 128 * 128 + wide for m in range(mp))
    dma = pltpu.SemaphoreType.DMA

    one = Call()
    one.arg(
        condition=condition,
        keep=keep,
        b_qv=query_value_bias,
        b_merge=merge_output_bias,
        b_mod=bias_modulate,
        b_table=bias_table,
        w_in=jnp.swapaxes(projection_weight, 1, 2),
        w_out=merge_weight,
    )
    one.arg(pltpu.SMEM, lengths=counts)
    one.arg(pl.ANY, patches=patches, w_mod=w_modulate.T)
    one.out(modv=((samples, 6 * D), F32), pos=((samples, n), jnp.int32), pos_wide=((samples, n), jnp.int32))
    one.out(
        pl.ANY,
        attn_in=((rows, D), BF16),
        qkv=((rows, 3 * lanes), BF16),
        probs=((samples, heads, n, n), F32),
        att=((rows, lanes), BF16),
        kept=((block, D), F32),
        res=((block, D), F32),
        hidden=((block, D), F32),
        mlp=((block, D), BF16),
        w_qkv=((3 * lanes, D), BF16),
        w_merge=((lanes, D), BF16),
    )
    one.vmem(
        attn_in_v=((rows, D), BF16),
        qkv_v=((rows, 3 * lanes), BF16),
        probs_v=((samples, heads, n, n), F32),
        att_v=((rows, lanes), BF16),
        kept_v=((block, D), F32),
        res_v=((block, D), F32),
        hidden_v=((block, D), F32),
        mlp_v=((block, D), BF16),
        w_qkv_v=((3 * lanes, D), BF16),
        w_merge_v=((lanes, D), BF16),
        w_mod_v=((cols, D), BF16),
        patches_v=((samples, L, D), BF16),
        mod_buf=((mp, samples, wide), F32),
        mod_wide=((samples, modw), F32),
        qv_wide=((2, lanes), F32),
        table_v=((heads, 4 * L), F32),
        normed=((rows, D), F32),
        bias_full=((heads, L, 2 * L), BF16),
        part=((rows, D), BF16),
    )
    one.scratch(
        mod_send=dma((mp,)),
        mod_recv=dma((mp,)),
        sem=dma((7,)),
        load_sem=dma((samples,)),
        save_sem=dma((4, samples)),
        red=reduce_scratch(sz),
    )
    first = one.run(
        functools.partial(attention_forward, sz, heads, hd, grid_side, cols), "attention_forward", 0, 62 << 20
    )

    chunk = 48 if dp_size == 4 and F % 96 == 0 and local % 48 == 0 else 0
    two = Call()
    two.arg(
        condition=condition,
        b_up=up_projection_bias,
        b_down=down_projection_bias,
        pos=first.pos,
        pos_wide=first.pos_wide,
        modv=first.modv,
    )
    two.arg(
        pl.ANY,
        cot=cot,
        w_up=up_weight.T,
        w_down=down_weight,
        mlp=first.mlp,
        hidden=first.hidden,
        res=first.res,
        kept=first.kept,
        qkv=first.qkv,
        probs=first.probs,
        att=first.att,
        w_qkv=first.w_qkv,
        w_merge=first.w_merge,
        attn_in=first.attn_in,
    )
    both = ((2, F + 2 * local, D), BF16)
    if chunk:
        count = (F + 2 * local) // chunk
        two.out(z_outer=both)
        two.vmem(grads=both, z_inner=((F + 2 * local, D), BF16))
        two.scratch(
            zs=dma((2, count)),
            zo=dma((2, count)),
            zf=dma((count,)),
            zi=dma((count,)),
            zt=dma((3, count)),
            zr=dma((2, count)),
        )
    else:
        two.out(grads=both)
    two.out(
        bias_g=((dp_size, 4, D), F32),
        table_g=((dp_size, heads, 4 * L), F32),
        signal_g=((dp_size, samples, D), BF16),
        mod_g=((dp_size, samples, wide), F32),
    )
    two.out(pl.ANY, out=((samples, n, D), BF16), patch_g=((samples, L, D), BF16))
    two.vmem(
        w_up_v=((F, D), BF16),
        w_down_v=((F, D), BF16),
        mlp_v=((rows, D), BF16),
        d_mlp=((rows, D), BF16),
        slope=((rows, F), F32),
        act=((rows, F), BF16),
        d_pre=((rows, F), BF16),
        part_f=((rows, D), BF16),
        part_b=((rows, D), BF16),
        d_attn=((rows, D), BF16),
        cot_own=((block, D), BF16),
        hidden_v=((block, D), F32),
        res_v=((block, D), F32),
        normed_v=((block, D), F32),
        dh_v=((block, D), F32),
        qkv_v=((rows, 3 * lanes), BF16),
        probs_v=((samples, heads, n, n), F32),
        w_qkv_v=((3 * lanes, D), BF16),
        w_merge_v=((lanes, D), BF16),
        grid_g=((heads, L, 2 * L), F32),
        early=((mp, 4, D), F32),
        late_sums=((mp, 2, D), F32),
        flat=((samples, modw), F32),
        bias_v=((2, D), F32),
    )
    two.scratch(
        sem=dma((13,)),
        load_sem=dma((3, samples)),
        dm_send=dma((2, mp)),
        dm_recv=dma((2, mp)),
        dp_send=dma((4, dp_size)),
        dp_recv=dma((4, dp_size)),
        red_f=reduce_scratch(sz),
        red_b=reduce_scratch(sz),
        last_sems=reduce_scratch(sz)[2:],
        gat_m=gather_scratch(sz),
        gat_d=gather_scratch(sz),
        gat_o=gather_scratch(sz),
        gat_k=gather_scratch(sz),
    )
    got = two.run(
        functools.partial(block_backward, sz, heads, hd, grid_side, cols, dp_size, chunk), "block_backward", 1, 64 << 20
    )

    total = got.z_outer if chunk else lax.psum(got.grads, "dp")
    three = Call()
    three.arg(mod_g=got.mod_g, signal_g=got.signal_g, bias_g=got.bias_g, table_g=got.table_g)
    three.arg(pl.ANY, total=total, out=got.out, patch_g=got.patch_g)
    three.out(
        mod_bias=((cols,), F32),
        up_bias=((F,), F32),
        down_bias=((D,), F32),
        merge_bias=((D,), F32),
        proj_bias=((2, local), F32),
        table=((heads, offsets * offsets), F32),
    )
    three.out(
        pl.ANY,
        block_out=((samples, n, D), BF16),
        patch=((samples, L, D), F32),
        up=((F, D), F32),
        down=((F, D), F32),
        project=((3 * local, D), F32),
        merge=((local, D), F32),
        modulate=((cols, D), F32),
    )
    depth = 8
    three.vmem(narrow=((depth, 288, D), BF16), wide=((depth, 288, D), F32), mod_v=((cols, D), F32), out_v=((samples, n, D), BF16))
    three.scratch(sem=dma((1,)), out_sem=dma((2, samples)), load_sem=dma((depth,)), save_sem=dma((depth,)))
    end = three.run(functools.partial(write_results, heads, hd, grid_side, cols), "write_results", None, 63 << 20)

    block_out = end.block_out
    if sz.per > 1:
        block_out = jnp.take(block_out, order, axis=1)
    return (
        block_out,
        end.patch,
        jnp.swapaxes(end.project.reshape(3, local, D), 1, 2),
        end.proj_bias,
        end.merge,
        end.merge_bias,
        end.up.T,
        end.up_bias,
        end.down,
        end.down_bias,
        end.modulate.T,
        end.mod_bias,
        end.table,
    )


def solution(mesh):
    placed = (
        P("dp", None, None),
        P("dp", None),
        P("dp"),
        P("dp", None),
        P("dp", None, None),
        P(None, None, "mp"),
        P(None, "mp"),
        P("mp", None),
        P(),
        P(None, "mp"),
        P("mp"),
        P("mp", None),
        P(),
        P(None, "mp"),
        P("mp"),
        P("mp", None),
    )
    return jax.shard_map(
        body,
        mesh=mesh,
        in_specs=placed,
        out_specs=(
            P("dp", None, None),
            P("dp", None, None),
            P(None, None, "mp"),
            P(None, "mp"),
            P("mp", None),
            P(),
            P(None, "mp"),
            P("mp"),
            P("mp", None),
            P(),
            P(None, "mp"),
            P("mp"),
            P("mp", None),
        ),
        check_vma=False,
    )
```

```python
import functools
import math
from types import SimpleNamespace

import jax
import jax.numpy as jnp
from jax import lax
from jax.experimental import pallas as pl
from jax.experimental.pallas import tpu as pltpu
from jax.sharding import PartitionSpec as P

MESH = pl.DeviceIdType.MESH
F32 = jnp.float32
BF16 = jnp.bfloat16
EPSILON = 1e-06
MASKED = -1000000000.0
GELU_C = math.sqrt(2.0 / math.pi)
GELU_A = 0.044715
VMEM = pl.BlockSpec(memory_space=pltpu.VMEM)
HEAD_PAD = 128


def dot(a, b, ca=1, cb=0):
    return lax.dot_general(a, b, (((ca,), (cb,)), ((), ())), preferred_element_type=F32)


def bit_of(value, k):
    return lax.rem(value // (1 << k), 2)


def flip(value, mask):
    out = value
    k = 0
    while (1 << k) <= mask:
        if mask & (1 << k):
            out = out + (1 << k) * (1 - 2 * bit_of(value, k))
        k += 1
    return out


def xor(a, b, bits):
    out = 0
    for k in range(bits):
        out = out + (1 << k) * lax.rem(bit_of(a, k) + bit_of(b, k), 2)
    return out


class Sizes:
    def __init__(self, mp, samples, slots, width):
        self.mp, self.samples, self.slots, self.width = mp, samples, slots, width
        self.bits = mp.bit_length() - 1
        self.rows = samples * slots
        self.block = self.rows // mp
        self.half = self.block // 2
        self.per = self.block and slots // self.block
        rest = [1 << k for k in range(1, self.bits)]
        self.orders = (rest, rest[::-1])
        self.sends = {}
        count = 0
        for h in range(2):
            live = list(range(0, mp, 2))
            for t, bit in enumerate(self.orders[h]):
                moved = [d for d in live if d & bit]
                live = [d for d in live if not d & bit]
                self.sends[h, t] = [(d, bit, count + i) for i, d in enumerate(moved)]
                count += len(moved)
        self.steps = len(rest)
        self.far = count
        self.near = mp // 2
        self.fast = self.steps == 2 and self.per == 1


def my_index():
    return lax.axis_index("dp"), lax.axis_index("mp")


def rows_of(ref, start, size):
    return ref.at[pl.ds(start, size)]


class Reduce:
    def __init__(self, sz, part, refs):
        self.sz, self.part = sz, part
        self.near_buf, self.far_buf, self.near_send, self.near_recv, self.far_send, self.far_recv = refs
        self.dp, self.me = my_index()

    def near_copy(self, pair):
        b = self.sz.block
        return pltpu.make_async_remote_copy(
            src_ref=rows_of(self.part, (2 * pair + 1) * b, b),
            dst_ref=rows_of(self.near_buf, pair * b, b),
            send_sem=self.near_send.at[pair],
            recv_sem=self.near_recv.at[pair],
            device_id=(self.dp, flip(self.me, 1)),
            device_id_type=MESH,
        )

    def far_copy(self, h, d, bit, i):
        b, hb = self.sz.block, self.sz.half
        return pltpu.make_async_remote_copy(
            src_ref=rows_of(self.part, d * b + h * hb, hb),
            dst_ref=rows_of(self.far_buf, i * hb, hb),
            send_sem=self.far_send.at[i],
            recv_sem=self.far_recv.at[i],
            device_id=(self.dp, flip(self.me, bit)),
            device_id_type=MESH,
        )

    def add(self, start, buf, at, size):
        a = self.part[pl.ds(start, size), :].astype(F32) + buf[pl.ds(at, size), :].astype(F32)
        self.part[pl.ds(start, size), :] = a.astype(BF16)

    def near_add(self, pair):
        b = self.sz.block
        self.near_copy(pair).wait()
        self.add(2 * pair * b, self.near_buf, pair * b, b)

    def send(self, h, d):
        for t in range(self.sz.steps):
            for m in self.sz.sends[h, t]:
                if m[0] == d:
                    self.far_copy(h, *m).start()

    def take(self, h, d, bit, i, add=True):
        b, hb = self.sz.block, self.sz.half
        self.far_copy(h, d, bit, i).wait()
        if add:
            self.add((d - bit) * b + h * hb, self.far_buf, i * hb, hb)

    def after(self, k):
        if k == 0:
            self.send(0, 6)
            self.send(1, 6)
        if k == 1:
            self.send(0, 2)
        if k == 2:
            self.send(1, 4)
            self.take(1, *self.sz.sends[1, 0][1])
            self.send(1, 2)
            self.take(0, *self.sz.sends[0, 0][1])
            self.send(0, 4)

    def close(self):
        sz = self.sz
        if sz.fast:
            for h in range(2):
                for t in range(2):
                    for m in sz.sends[h, t]:
                        if m[0] == m[1]:
                            self.take(h, *m, add=False)
            return

        def one(i, carry):
            self.near_add(sz.near - 1 - i)
            return carry

        lax.fori_loop(0, sz.near, one, 0)
        for t in range(sz.steps):
            for h in range(2):
                for m in sz.sends[h, t]:
                    self.far_copy(h, *m).start()
            for h in range(2):
                for m in sz.sends[h, t]:
                    self.take(h, *m, add=t < sz.steps - 1)

    def own_sum(self):
        sz, hb = self.sz, self.sz.half
        out = []
        for h in range(2):
            total = self.part[h * hb : (h + 1) * hb, :].astype(F32)
            for t in range(0 if sz.fast else sz.steps - 1, sz.steps):
                for d, bit, i in sz.sends[h, t]:
                    if d == bit:
                        total = total + self.far_buf[i * hb : (i + 1) * hb, :].astype(F32)
            out.append(total)
        return jnp.concatenate(out, axis=0)


class Gather:
    def __init__(self, sz, out, sems):
        self.sz, self.out = sz, out
        self.near_send, self.near_recv, self.far_send, self.far_recv = sems
        self.dp, self.me = my_index()
        self.first, self.stages = [], []
        if sz.fast:
            x, y = sz.orders[0]
            self.first = [(1, 0, x, 0), (0, 0, y, 1), (0, 0, x, 2), (1, 0, y, 3)]
            on = {0: (1, x, y, 5), 1: (0, y, x, 4)}
            self.stages = [
                [(self.first[1], [on[1]]), (self.first[0], [on[0]])],
                [(self.first[2], []), (self.first[3], [])],
                [(on[1], []), (on[0], [])],
            ]
        else:
            count, plan = 0, {}
            for h in range(2):
                have = [0]
                for t, bit in enumerate(sz.orders[h][::-1]):
                    plan[h, t] = [(h, d, bit, count + i) for i, d in enumerate(have)]
                    count += len(have)
                    have = have + [d | bit for d in have]
            self.first = plan[0, 0] + plan[1, 0]
            for t in range(sz.steps):
                stage = []
                for h in range(2):
                    later = plan[h, t + 1] if t + 1 < sz.steps else []
                    for k, m in enumerate(plan[h, t]):
                        stage.append((m, later if k == len(plan[h, t]) - 1 else []))
                self.stages.append(stage)

    def near_copy(self, d, h):
        b, hb = self.sz.block, self.sz.half
        return pltpu.make_async_remote_copy(
            src_ref=rows_of(self.out, d * b + h * hb, hb),
            dst_ref=rows_of(self.out, (d + 1) * b + h * hb, hb),
            send_sem=self.near_send.at[d + h],
            recv_sem=self.near_recv.at[d + h],
            device_id=(self.dp, flip(self.me, 1)),
            device_id_type=MESH,
        )

    def far_copy(self, h, d, bit, i):
        b, hb = self.sz.block, self.sz.half
        return pltpu.make_async_remote_copy(
            src_ref=rows_of(self.out, d * b + h * hb, hb),
            dst_ref=rows_of(self.out, (d + bit) * b + h * hb, hb),
            send_sem=self.far_send.at[i],
            recv_sem=self.far_recv.at[i],
            device_id=(self.dp, flip(self.me, bit)),
            device_id_type=MESH,
        )

    def start(self):
        for m in self.first:
            self.far_copy(*m).start()
        for h in range(2):
            self.near_copy(0, h).start()

    def step(self, t):
        for m, later in self.stages[t]:
            self.far_copy(*m).wait()
            for n in later:
                self.far_copy(*n).start()
            h, d, bit, _ = m
            self.near_copy(d + bit, h).start()

    def finish(self, first=0):
        for d in range(first, self.sz.mp, 2):
            for h in range(2):
                self.near_copy(d, h).wait()


def reduce_scratch(sz):
    return [
        pltpu.VMEM((sz.near * sz.block, sz.width), BF16),
        pltpu.VMEM((sz.far * sz.half, sz.width), BF16),
        pltpu.SemaphoreType.DMA((sz.near,)),
        pltpu.SemaphoreType.DMA((sz.near,)),
        pltpu.SemaphoreType.DMA((sz.far,)),
        pltpu.SemaphoreType.DMA((sz.far,)),
    ]


def gather_scratch(sz):
    return [
        pltpu.SemaphoreType.DMA((sz.mp,)),
        pltpu.SemaphoreType.DMA((sz.mp,)),
        pltpu.SemaphoreType.DMA((sz.far,)),
        pltpu.SemaphoreType.DMA((sz.far,)),
    ]


def slot_loop(sz, body, red, extra=None):
    if sz.fast:

        def one(i, carry):
            q = i // 2
            pair = 2 * (1 - lax.rem(q, 2)) + 1 - q // 2
            other = 1 - lax.rem(i, 2)
            body(2 * pair + other)

            @pl.when(other == 1)
            def _():
                red.near_copy(pair).start()

            @pl.when(other == 0)
            def _():
                red.near_add(pair)

            for k in range(3):
                pl.when(i == 2 * k + 1)(functools.partial(red.after, k))
            if extra is not None:
                extra(i)
            return carry

    else:
        pairs = sz.per // 2

        def one(i, carry):
            slot = sz.samples - 1 - i
            body(slot)
            for p in range(pairs):
                red.near_copy(slot * pairs + p).start()
            return carry

    lax.fori_loop(0, sz.samples, one, 0)


def layer_stats(values):
    centre = jnp.mean(values, axis=-1, keepdims=True)
    shifted = values - centre
    spread = jnp.mean(shifted * shifted, axis=-1, keepdims=True)
    inv_std = lax.rsqrt(spread + EPSILON)
    return shifted * inv_std, inv_std


def layer_back(gradient, normed, inv_std):
    mean_grad = jnp.mean(gradient, axis=-1, keepdims=True)
    mean_mix = jnp.mean(gradient * normed, axis=-1, keepdims=True)
    return inv_std * (gradient - mean_grad - normed * mean_mix)


def pick_rows(ids_ref, s, count):
    ids = ids_ref[pl.ds(s, 1), :]
    return (lax.broadcasted_iota(jnp.int32, (count, ids.shape[1]), 0) == ids).astype(F32).astype(BF16)


def spread(row, pieces, size, step):
    width = row.shape[1]
    lane = lax.broadcasted_iota(jnp.int32, row.shape, 1)
    total = jnp.zeros_like(row)
    for p in range(pieces):
        start = p * (size + step) if step > 0 else p * size
        moved = pltpu.roll(row, (p * step) % width, 1) if p else row
        total = jnp.where((lane >= start) & (lane < start + size), moved, total)
    return total


def spread_heads(row, heads, hd):
    return spread(row, heads, hd, HEAD_PAD - hd)


def live_column(sel):
    ones = jnp.ones((sel.shape[0], 128), BF16)
    return dot(sel, ones, 0, 0)[:, 0:1]


def stripe_of(rows):
    return 96 if rows % 192 == 0 else rows // 2


class Call:
    def __init__(self):
        self.args, self.specs, self.outs, self.out_specs, self.scratch_of = {}, [], {}, [], {}

    def arg(self, space=pltpu.VMEM, **values):
        self.args.update(values)
        self.specs += [pl.BlockSpec(memory_space=space)] * len(values)

    def out(self, space=pltpu.VMEM, **results):
        for name, (shape, dtype) in results.items():
            self.outs[name] = jax.ShapeDtypeStruct(shape, dtype)
            self.out_specs.append(pl.BlockSpec(memory_space=space))

    def scratch(self, **buffers):
        self.scratch_of.update(buffers)

    def vmem(self, **buffers):
        for name, (shape, dtype) in buffers.items():
            self.scratch_of[name] = pltpu.VMEM(shape, dtype)

    def run(self, kernel, name, cid, limit):
        flat = []
        for value in self.scratch_of.values():
            flat += value if isinstance(value, list) else [value]

        def inner(*refs):
            r, refs = SimpleNamespace(), list(refs)
            for key in list(self.args) + list(self.outs):
                setattr(r, key, refs.pop(0))
            for key, value in self.scratch_of.items():
                count = len(value) if isinstance(value, list) else 0
                setattr(r, key, [refs.pop(0) for _ in range(count)] if count else refs.pop(0))
            kernel(r)

        got = pl.pallas_call(
            inner,
            out_shape=list(self.outs.values()),
            in_specs=self.specs,
            out_specs=self.out_specs,
            scratch_shapes=flat,
            name=name,
            compiler_params=pltpu.CompilerParams(vmem_limit_bytes=limit)
            if cid is None
            else pltpu.CompilerParams(collective_id=cid, has_side_effects=True, vmem_limit_bytes=limit),
        )(*self.args.values())
        return SimpleNamespace(**dict(zip(self.outs, got)))


def attention_forward(sz, heads, hd, grid_side, cols, r):
    dp, me = my_index()
    mine = me // sz.per
    sbits = sz.samples.bit_length() - 1
    D, n, L = sz.width, sz.slots, grid_side * grid_side
    lanes = heads * HEAD_PAD
    red = Reduce(sz, r.part, r.red)
    mod_buf, mod_wide, modv = r.mod_buf, r.mod_wide, r.modv
    wide = mod_buf.shape[2]
    sem = r.sem

    barrier = pltpu.get_barrier_semaphore()
    for d in range(1, sz.mp):
        pl.semaphore_signal(barrier, inc=1, device_id=(dp, flip(me, d)), device_id_type=MESH)
    load_mod = pltpu.make_async_copy(r.w_mod, r.w_mod_v, sem.at[0])

    def load_patches(i, slot):
        return pltpu.make_async_copy(r.patches.at[xor(mine, slot, sbits)], r.patches_v.at[slot], r.load_sem.at[i])

    def start_load(slot, carry):
        load_patches(slot, slot).start()
        return carry

    load_mod.start()
    lax.fori_loop(0, sz.samples, start_load, 0)
    slots = lax.broadcasted_iota(jnp.int32, (1, n), 1)
    for s in range(sz.samples):
        pos = jnp.where(slots < r.lengths[s], r.keep[s : s + 1, 0:n], -1)
        r.pos[s : s + 1, :] = pos
        turned = L - 1 - pos
        r.pos_wide[s : s + 1, :] = jnp.where(pos < 0, -1, turned + turned // grid_side * grid_side)
    r.qv_wide[...] = jnp.zeros_like(r.qv_wide)
    r.qv_wide[:, 0 : heads * hd] = r.b_qv[...].astype(F32)
    r.qv_wide[...] = spread_heads(r.qv_wide[...], heads, hd)
    r.table_v[...] = jnp.zeros_like(r.table_v)
    offsets = 2 * grid_side - 1
    r.table_v[:, 0 : offsets * offsets] = r.b_table[...].astype(F32)
    r.table_v[...] = spread(r.table_v[...], offsets, offsets, 1)
    w_qkv, w_merge = r.w_qkv_v, r.w_merge_v
    pad_rows = jnp.zeros((HEAD_PAD - hd, D), F32)
    for h in range(heads):
        for c in range(3):
            piece = r.w_in[c].astype(F32)[h * hd : (h + 1) * hd]
            w_qkv[c * lanes + h * HEAD_PAD : c * lanes + (h + 1) * HEAD_PAD, :] = jnp.concatenate(
                [piece, pad_rows], axis=0
            ).astype(BF16)
        piece = r.w_out[...].astype(F32)[h * hd : (h + 1) * hd]
        w_merge[h * HEAD_PAD : (h + 1) * HEAD_PAD, :] = jnp.concatenate([piece, pad_rows], axis=0).astype(BF16)
    save = [
        pltpu.make_async_copy(w_qkv, r.w_qkv, sem.at[1]),
        pltpu.make_async_copy(w_merge, r.w_merge, sem.at[2]),
    ]
    for copy in save:
        copy.start()

    bias_full = r.bias_full
    span = r.table_v.shape[1]
    for h in range(heads):
        line = r.table_v[h : h + 1, :]
        strip = jnp.concatenate([line] + [pltpu.roll(line, span - c, 1) for c in range(1, grid_side)], axis=0)
        for row in range(grid_side):
            rolled = pltpu.roll(strip, span - row * 2 * grid_side, 1) if row else strip
            bias_full[h, row * grid_side : (row + 1) * grid_side, :] = rolled[:, : 2 * L].astype(BF16)

    cond = r.condition[...].astype(F32)
    signal = (cond / (1.0 + jnp.exp(-cond))).astype(BF16)
    mod_buf[me] = jnp.zeros((sz.samples, wide), F32)
    load_mod.wait()
    mod_buf[me, :, 0:cols] = dot(signal, r.w_mod_v[...], 1, 1) + r.b_mod[...].astype(F32).reshape(1, cols)
    pl.semaphore_wait(barrier, sz.mp - 1)

    def mod_copy(d, slot):
        return pltpu.make_async_remote_copy(
            src_ref=mod_buf.at[slot],
            dst_ref=mod_buf.at[slot],
            send_sem=r.mod_send.at[d],
            recv_sem=r.mod_recv.at[d],
            device_id=(dp, flip(me, d)),
            device_id_type=MESH,
        )

    for d in range(1, sz.mp):
        mod_copy(d, me).start()

    normed, kept_own = r.normed, r.kept_v

    def norm_one(slot, carry):
        load_patches(slot, slot).wait()
        sel = pick_rows(r.pos, xor(mine, slot, sbits), L)
        kept = dot(sel, r.patches_v[slot], 0, 0)
        value, _ = layer_stats(kept)
        normed[pl.ds(slot * n, n), :] = value

        @pl.when(slot == 0)
        def _():
            kept_own[...] = kept[: sz.block]

        return carry

    lax.fori_loop(0, sz.samples, norm_one, 0)
    save_kept = pltpu.make_async_copy(kept_own, r.kept, sem.at[3])
    save_kept.start()

    for d in range(1, sz.mp):
        mod_copy(d, me).wait_send()
        mod_copy(d, flip(me, d)).wait_recv()
    mod_wide[...] = jnp.zeros_like(mod_wide)
    for m in range(sz.mp):
        base = m * cols // 128 * 128
        phase = m * cols - base
        piece = mod_buf[m]
        if phase:
            piece = pltpu.roll(piece, phase, 1)
        mod_wide[:, base : base + wide] += piece
    modv[...] = mod_wide[:, : 6 * D]

    factor = hd ** (-0.5)
    stores = [(r.attn_in_v, r.attn_in), (r.qkv_v, r.qkv), (r.att_v, r.att)]

    def save_slot(i, slot):
        at = pl.ds(slot * n, n)
        copies = [
            pltpu.make_async_copy(a.at[at], b.at[at], r.save_sem.at[k, slot]) for k, (a, b) in enumerate(stores)
        ]
        copies.append(pltpu.make_async_copy(r.probs_v.at[slot], r.probs.at[slot], r.save_sem.at[3, slot]))
        return copies

    def body(slot):
        s = xor(mine, slot, sbits)
        at = pl.ds(slot * n, n)
        shift = modv[pl.ds(s, 1), 0:D]
        scale = modv[pl.ds(s, 1), D : 2 * D]
        entry = (normed[at, :] * (1.0 + scale) + shift).astype(BF16)
        r.attn_in_v[at, :] = entry
        proj = dot(entry, w_qkv[...], 1, 1)
        qs = (proj[:, :lanes] + r.qv_wide[0:1, :]).astype(BF16)
        ks = proj[:, lanes : 2 * lanes].astype(BF16)
        vs = (proj[:, 2 * lanes :] + r.qv_wide[1:2, :]).astype(BF16)
        r.qkv_v[at, 0:lanes] = qs
        r.qkv_v[at, lanes : 2 * lanes] = ks
        r.qkv_v[at, 2 * lanes :] = vs
        sel = pick_rows(r.pos, s, L)
        sel_wide = pick_rows(r.pos_wide, s, 2 * L)
        live = r.pos[pl.ds(s, 1), :] >= 0
        outs = []
        for h in range(heads):
            cut = slice(h * HEAD_PAD, (h + 1) * HEAD_PAD)
            bias = dot(dot(sel, bias_full[h], 0, 0).astype(BF16), sel_wide)
            scores = jnp.where(live, dot(qs[:, cut], ks[:, cut], 1, 1) * factor + bias, MASKED)
            top = jnp.max(scores, axis=-1, keepdims=True)
            e = jnp.exp(scores - top)
            p = e / jnp.sum(e, axis=-1, keepdims=True)
            r.probs_v[slot, h] = p
            outs.append(dot(p.astype(BF16), vs[:, cut]).astype(BF16))
        joined = jnp.concatenate(outs, axis=1) if heads > 1 else outs[0]
        r.att_v[at, :] = joined
        r.part[at, :] = dot(joined, w_merge[...]).astype(BF16)
        for copy in save_slot(0, slot):
            copy.start()

    slot_loop(sz, body, red)
    red.close()
    result = red.own_sum() + r.b_merge[...].astype(F32).reshape(1, D)
    r.res_v[...] = result
    hidden = kept_own[...] + modv[pl.ds(mine, 1), 2 * D : 3 * D] * result
    r.hidden_v[...] = hidden
    value, _ = layer_stats(hidden)
    shift = modv[pl.ds(mine, 1), 3 * D : 4 * D]
    scale = modv[pl.ds(mine, 1), 4 * D : 5 * D]
    r.mlp_v[...] = (value * (1.0 + scale) + shift).astype(BF16)
    save_own = [
        pltpu.make_async_copy(r.res_v, r.res, sem.at[4]),
        pltpu.make_async_copy(r.hidden_v, r.hidden, sem.at[5]),
        pltpu.make_async_copy(r.mlp_v, r.mlp, sem.at[6]),
    ]
    for copy in save_own:
        copy.start()

    def wait_slot(slot, carry):
        for copy in save_slot(0, slot):
            copy.wait()
        return carry

    lax.fori_loop(0, sz.samples, wait_slot, 0)
    for copy in save + save_own + [save_kept]:
        copy.wait()


class Line:
    def __init__(self, r, chunk):
        self.r, self.chunk = r, chunk
        self.g, self.outer_buf, self.inner_buf = r.grads, r.z_outer, r.z_inner
        self.count = self.g.shape[1] // chunk
        self.dp, self.me = my_index()
        self.is_inner = (self.dp == 1) | (self.dp == 2)
        self.is_outer = (self.dp == 0) | (self.dp == 3)
        self.step_to = 1 + self.dp // 3
        self.back_to = (self.dp - 1) * 3
        self.other = 3 - self.dp
        self.mine = 2 - self.dp
        self.passed = self.dp - 1

    def rows(self, k):
        return pl.ds(k * self.chunk, self.chunk)

    def copy(self, src, dst, send, recv, to):
        return pltpu.make_async_remote_copy(
            src_ref=src, dst_ref=dst, send_sem=send, recv_sem=recv, device_id=(to, self.me), device_id_type=MESH
        )

    def out_copy(self, j, k):
        return self.copy(
            self.g.at[j, self.rows(k)], self.outer_buf.at[j, self.rows(k)],
            self.r.zs.at[j, k], self.r.zo.at[j, k], self.step_to,
        )

    def in_copy(self, k):
        return self.copy(
            self.g.at[self.passed, self.rows(k)], self.inner_buf.at[self.rows(k)],
            self.r.zf.at[k], self.r.zi.at[k], self.other,
        )

    def total_copy(self, j, k, which, to):
        return self.copy(
            self.outer_buf.at[j, self.rows(k)], self.outer_buf.at[j, self.rows(k)],
            self.r.zt.at[which, k], self.r.zr.at[j, k], to,
        )

    def begin(self, halves, k0, k1):
        @pl.when(self.is_outer)
        def _():
            def one(k, carry):
                for j in halves:
                    self.out_copy(j, k).start()
                return carry

            lax.fori_loop(k0, k1, one, 0)

    def add(self, to, j, k, more):
        def one(i, carry):
            at = pl.ds(k * self.chunk + i * 16, 16)
            v = self.g[j, at, :].astype(F32) + self.outer_buf[j, at, :].astype(F32)
            if more:
                v = v + self.inner_buf[at, :].astype(F32)
            to[j, at, :] = v.astype(BF16)
            return carry

        lax.fori_loop(0, self.chunk // 16, one, 0)

    def stage(self, number, j, k):
        if number == 1:

            @pl.when(self.passed == j)
            def _():
                self.out_copy(j, k).wait_recv()
                self.add(self.g, j, k, False)
                self.in_copy(k).start()

        elif number == 2:

            @pl.when(self.mine == j)
            def _():
                self.out_copy(j, k).wait_recv()
                self.in_copy(k).wait_recv()
                self.add(self.outer_buf, j, k, True)
                self.total_copy(j, k, 0, self.other).start()
                self.total_copy(j, k, 1, self.back_to).start()

        else:

            @pl.when(self.passed == j)
            def _():
                self.in_copy(k).wait_send()
                self.total_copy(j, k, 0, self.other).wait_recv()
                self.total_copy(j, k, 2, self.back_to).start()

    def finish(self):
        @pl.when(self.is_inner)
        def _():
            def one(k, carry):
                self.total_copy(self.mine, k, 0, self.other).wait_send()
                self.total_copy(self.mine, k, 1, self.back_to).wait_send()
                self.total_copy(self.passed, k, 2, self.back_to).wait_send()
                return carry

            lax.fori_loop(0, self.count, one, 0)

        @pl.when(self.is_outer)
        def _():
            def one(k, carry):
                for j in range(2):
                    self.out_copy(j, k).wait_send()
                    self.total_copy(j, k, 0, self.step_to).wait_recv()
                return carry

            lax.fori_loop(0, self.count, one, 0)


def block_backward(sz, heads, hd, grid_side, cols, dp_size, chunk, r):
    dp, me = my_index()
    mine = me // sz.per
    sbits = sz.samples.bit_length() - 1
    D, n, L = sz.width, sz.slots, grid_side * grid_side
    lanes = heads * HEAD_PAD
    local = heads * hd
    F = r.w_up_v.shape[0]
    block = sz.block
    modv = r.modv
    fwd = Reduce(sz, r.part_f, r.red_f)
    bwd = Reduce(sz, r.part_b, r.red_b)
    last = Reduce(sz, r.part_b, r.red_b[:2] + r.last_sems)
    gat_m = Gather(sz, r.mlp_v, r.gat_m)
    gat_d = Gather(sz, r.d_attn, r.gat_d)
    gat_o = Gather(sz, r.part_f, r.gat_o)
    gat_k = Gather(sz, r.mlp_v, r.gat_k)
    line = Line(r, chunk) if chunk else None
    grads = r.grads
    sem = r.sem

    stripe = stripe_of(F)
    per_half, per_local = (F // 2 // chunk, local // chunk) if chunk else (0, 0)
    marks = [0, per_half, 2 * per_half, 2 * per_half + per_local, 2 * per_half + 2 * per_local]
    following = {(number, j): 0 for number in (1, 2, 3) for j in range(2)}

    def tick(*steps):
        if line is None:
            return
        for number, j, count in steps:
            k0 = following[number, j]
            k1 = min(k0 + count, marks[4])
            assert number == 1 or k1 <= following[number - 1, j]
            following[number, j] = k1
            if k1 - k0 == 1:
                line.stage(number, j, k0)
            elif k1 > k0:

                def one(k, carry, number=number, j=j):
                    line.stage(number, j, k)
                    return carry

                lax.fori_loop(k0, k1, one, 0)

    def begin(group, *halves):
        if line is not None:
            line.begin(halves or (0, 1), marks[group], marks[group + 1])

    def ticks_at(i, plan):
        if line is not None:
            for when, steps in plan.items():
                pl.when(i == when)(lambda steps=steps: tick(*steps))

    load_up = pltpu.make_async_copy(r.w_up, r.w_up_v, sem.at[0])
    load_down = pltpu.make_async_copy(r.w_down, r.w_down_v, sem.at[1])
    load_up.start()
    load_down.start()

    load_own = pltpu.make_async_copy(r.mlp, r.mlp_v.at[pl.ds(0, block)], sem.at[12])
    load_own.start()

    def load_cot(slot):
        at = pl.ds(slot * n, n)
        return pltpu.make_async_copy(r.cot.at[xor(mine, slot, sbits)], r.d_mlp.at[at], r.load_sem.at[1, slot])

    def start_cot(slot, carry):
        load_cot(slot).start()
        return carry

    lax.fori_loop(0, sz.samples, start_cot, 0)
    loads = [
        pltpu.make_async_copy(r.cot.at[mine, pl.ds(0, block)], r.cot_own, sem.at[2]),
        pltpu.make_async_copy(r.hidden, r.hidden_v, sem.at[3]),
        pltpu.make_async_copy(r.res, r.res_v, sem.at[4]),
    ]
    late = [
        pltpu.make_async_copy(r.qkv, r.qkv_v, sem.at[6]),
        pltpu.make_async_copy(r.probs, r.probs_v, sem.at[7]),
        pltpu.make_async_copy(r.w_qkv, r.w_qkv_v, sem.at[9]),
        pltpu.make_async_copy(r.w_merge, r.w_merge_v, sem.at[10]),
    ]
    for copy in loads + late:
        copy.start()
    load_attn = pltpu.make_async_copy(r.attn_in, r.d_mlp, sem.at[11])
    load_kept = pltpu.make_async_copy(r.kept, r.res_v, sem.at[5])
    load_att = pltpu.make_async_copy(r.att, r.act.at[:, pl.ds(0, lanes)], sem.at[8])

    barrier = pltpu.get_barrier_semaphore()
    for d in range(1, sz.mp):
        pl.semaphore_signal(barrier, inc=1, device_id=(dp, flip(me, d)), device_id_type=MESH)
    for e in range(1, dp_size):
        pl.semaphore_signal(barrier, inc=1, device_id=(lax.rem(dp + e, dp_size), me), device_id_type=MESH)
    pl.semaphore_wait(barrier, sz.mp + dp_size - 2)
    load_own.wait()
    gat_m.start()
    r.bias_v[0:1, 0:F] = r.b_up[...].astype(F32).reshape(1, F)
    r.bias_v[1:2, :] = r.b_down[...].astype(F32).reshape(1, D)
    load_up.wait()
    load_down.wait()
    w_up, w_down, mlp = r.w_up_v, r.w_down_v, r.mlp_v
    act, d_pre, d_mlp, slope = r.act, r.d_pre, r.d_mlp, r.slope

    up_bg, down_bg = r.bias_g.at[dp, 0:1], r.bias_g.at[dp, 1:2]
    merge_bg, proj_bg = r.bias_g.at[dp, 2:3], r.bias_g.at[dp, 3:4]
    r.bias_g[dp] = jnp.zeros(r.bias_g.shape[1:], F32)
    cond = r.condition[...].astype(F32)
    r.signal_g[dp] = (cond / (1.0 + jnp.exp(-cond))).astype(BF16)
    shared = [r.bias_g, r.table_g, r.mod_g, r.signal_g]

    def dp_copy(k, e, slot):
        return pltpu.make_async_remote_copy(
            src_ref=shared[k].at[slot],
            dst_ref=shared[k].at[slot],
            send_sem=r.dp_send.at[k, e],
            recv_sem=r.dp_recv.at[k, e],
            device_id=(lax.rem(dp + e, dp_size), me),
            device_id_type=MESH,
        )

    def share(k):
        for e in range(1, dp_size):
            dp_copy(k, e, dp).start()

    share(3)

    def forward(slot, wide):
        at = pl.ds(slot * n, wide * n)
        v = dot(mlp[at, :], w_up[...], 1, 1) + r.bias_v[0:1, 0:F]
        square = v * v
        h = 0.5 * jnp.tanh(v * (GELU_C * GELU_A * square + GELU_C)) + 0.5
        active = (v * h).astype(BF16)
        act[at, :] = active
        slope[at, :] = h * (1.0 + (1.0 - h) * (v * (6.0 * GELU_C * GELU_A * square + 2.0 * GELU_C)))
        r.part_f[at, :] = dot(active, w_down[...]).astype(BF16)

    def output_grad(slot, carry):
        at = pl.ds(slot * n, n)
        s = xor(mine, slot, sbits)
        load_cot(slot).wait()
        gate = modv[pl.ds(s, 1), 5 * D : 6 * D]
        live = live_column(pick_rows(r.pos, s, L))
        dm = (gate * (d_mlp[at, :].astype(F32) * live)).astype(BF16)
        d_mlp[at, :] = dm
        down_bg[...] += jnp.sum(dm.astype(F32), axis=0, keepdims=True)
        return carry

    if sz.fast:
        def two_slots(i, carry):
            @pl.when(i == 1)
            def _():
                lax.fori_loop(0, sz.samples, output_grad, 0)
                gat_m.step(0)
                gat_m.step(1)

            @pl.when(i == 3)
            def _():
                gat_m.step(2)

            for h in range(2):
                gat_m.near_copy(2 * i, h).wait()
            forward(2 * i, 2)
            fwd.near_copy(i).start()

            @pl.when(i > 0)
            def _():
                fwd.near_add(i - 1)

            pl.when(i == 2)(functools.partial(fwd.send, 0, 2))
            pl.when(i == 3)(functools.partial(fwd.send, 1, 4))
            return carry

        lax.fori_loop(0, 4, two_slots, 0)
    else:
        for t in range(len(gat_m.stages)):
            gat_m.step(t)
        gat_m.finish()
        lax.fori_loop(0, sz.samples, output_grad, 0)
        slot_loop(sz, lambda slot: forward(slot, 1), fwd)

    def wide_grad(left, right, base, group):
        at, sent = 0, 0
        while at < F:
            size = min(256, F - at)
            value = dot(left[:, at : at + size], right[...], 0, 0).astype(BF16)
            row = at
            while row < at + size:
                turn = row // stripe
                count = min((turn + 1) * stripe, at + size) - row
                to = base + turn // 2 * stripe + row % stripe
                grads[turn % 2, to : to + count, :] = value[row - at : row - at + count]
                row += count
            at += size
            if line is not None:
                ready = at // (2 * stripe) * (stripe // chunk)
                if ready > sent:
                    line.begin((0, 1), marks[group] + sent, marks[group] + ready)
                    sent = ready

    wide_grad(act, d_mlp, 0, 0)

    def backward(slot):
        at = pl.ds(slot * n, n)
        dpre = (dot(d_mlp[at, :], w_down[...], 1, 1) * slope[at, :]).astype(BF16)
        d_pre[at, :] = dpre
        up_bg[:, :F] += jnp.sum(dpre.astype(F32), axis=0, keepdims=True)
        r.part_b[at, :] = dot(dpre, w_up[...]).astype(BF16)

    plan = {
        2: [(1, 1, 1)],
        3: [(1, 0, 1)],
        5: [(1, 0, 1), (1, 1, 1), (2, 0, 1), (2, 1, 1)],
    }

    def bwd_extra(i):
        ticks_at(i, plan)

        @pl.when(i == 5)
        def _():
            fwd.near_add(3)
            fwd.send(0, 6)
            fwd.send(1, 6)

    slot_loop(sz, backward, bwd, bwd_extra)
    load_attn.start()
    load_att.start()
    wide_grad(d_pre, mlp, F // 2, 1)
    tick((1, 0, 1), (1, 1, 1), (2, 0, 1), (2, 1, 1))
    for copy in loads:
        copy.wait()
    normed2, inv2 = layer_stats(r.hidden_v[...])
    r.normed_v[...] = normed2
    bwd.close()
    tick((1, 0, 1), (1, 1, 1), (2, 0, 1), (2, 1, 1), (3, 0, 1), (3, 1, 1))

    mrow = pl.ds(mine, 1)
    live = live_column(pick_rows(r.pos, mine, L)[:, :block])
    d_out = r.cot_own[...].astype(F32) * live
    d_mlp_in = bwd.own_sum()
    g = d_mlp_in * (1.0 + modv[mrow, 4 * D : 5 * D])
    dh = d_out + layer_back(g, r.normed_v[...], inv2)
    r.dh_v[...] = dh
    r.d_attn[:block, :] = (modv[mrow, 2 * D : 3 * D] * dh).astype(BF16)
    gat_d.start()

    early, late_sums = r.early, r.late_sums
    early[me, 0:1, :] = jnp.sum(dh * r.res_v[...], axis=0, keepdims=True)
    load_kept.start()
    early[me, 1:2, :] = jnp.sum(d_mlp_in, axis=0, keepdims=True)
    early[me, 2:3, :] = jnp.sum(d_mlp_in * r.normed_v[...], axis=0, keepdims=True)

    def finish_out():
        fwd.close()
        live = live_column(pick_rows(r.pos, mine, L)[:, :block])
        mlp_out = fwd.own_sum() + r.bias_v[1:2, :]
        early[me, 3:4, :] = jnp.sum(mlp_out * (r.cot_own[...].astype(F32) * live), axis=0, keepdims=True)
        out_own = (r.hidden_v[...] + modv[mrow, 5 * D : 6 * D] * mlp_out) * live
        r.part_f[:block, :] = out_own.astype(BF16)

    def dm_copy(ref, k, d, slot):
        return pltpu.make_async_remote_copy(
            src_ref=ref.at[slot],
            dst_ref=ref.at[slot],
            send_sem=r.dm_send.at[k, d],
            recv_sem=r.dm_recv.at[k, d],
            device_id=(dp, flip(me, d)),
            device_id_type=MESH,
        )

    def attention_grad(c, half, at):
        if c < 3:
            full = dot(qkv[:, c * lanes : (c + 1) * lanes], d_mlp[...], 0, 0)
        else:
            full = dot(r.act[:, :lanes], r.d_attn[...], 0, 0)
        rows = [full[h * HEAD_PAD : h * HEAD_PAD + hd] for h in range(heads)]
        rows = jnp.concatenate(rows, axis=0) if heads > 1 else rows[0]
        grads[half, at : at + local, :] = rows.astype(BF16)

    for copy in late:
        copy.wait()
    factor = hd ** (-0.5)
    grid_g = r.grid_g
    grid_g[...] = jnp.zeros_like(grid_g)
    qkv, w_qkv, w_merge = r.qkv_v, r.w_qkv_v, r.w_merge_v
    def attention(slot):
        s = xor(mine, slot, sbits)
        at = pl.ds(slot * n, n)
        da = r.d_attn[at, :]
        merge_bg[...] += jnp.sum(da.astype(F32), axis=0, keepdims=True)
        d_att = dot(da, w_merge[...], 1, 1).astype(BF16)
        sel = pick_rows(r.pos, s, L)
        sel_wide = pick_rows(r.pos_wide, s, 2 * L)
        dq, dk, dv = [], [], []
        for h in range(heads):
            q = qkv[at, h * HEAD_PAD : (h + 1) * HEAD_PAD]
            k = qkv[at, lanes + h * HEAD_PAD : lanes + (h + 1) * HEAD_PAD]
            v = qkv[at, 2 * lanes + h * HEAD_PAD : 2 * lanes + (h + 1) * HEAD_PAD]
            d_a = d_att[:, h * HEAD_PAD : (h + 1) * HEAD_PAD]
            p = r.probs_v[slot, h]
            d_p = dot(d_a, v, 1, 1)
            dv.append(dot(p.astype(BF16), d_a, 0, 0).astype(BF16))
            ds = p * (d_p - jnp.sum(p * d_p, axis=-1, keepdims=True))
            dl = ds.astype(BF16)
            dq.append((dot(dl, k) * factor).astype(BF16))
            dk.append((dot(dl, q, 0, 0) * factor).astype(BF16))
            grid_g[h] += dot(dot(sel, dl).astype(BF16), sel_wide, 1, 1)
        joined = jnp.concatenate(dq + dk + dv, axis=1)
        qkv[at, :] = joined
        proj_bg[:, : 3 * lanes] += jnp.sum(joined.astype(F32), axis=0, keepdims=True)
        r.part_b[at, :] = dot(joined, w_qkv[...]).astype(BF16)

    if sz.fast:
        plan_one = {1: [(1, 0, 1), (1, 1, 1), (2, 0, 1), (2, 1, 1), (3, 0, 1), (3, 1, 1)], 2: [(3, 0, 1), (3, 1, 1)]}
        plan_two = {
            3: [(1, 1, 1), (2, 0, 1), (2, 1, 1), (3, 0, 1), (3, 1, 1)],
            4: [(1, 0, 1), (2, 0, 1), (2, 1, 1)],
            5: [(1, 0, 1), (1, 1, 1), (2, 1, 1), (3, 0, 1), (3, 1, 1)],
            6: [(1, 1, 1), (2, 0, 1), (3, 0, 1), (3, 1, 1)],
            7: [(1, 0, 1), (2, 0, 1), (2, 1, 1)],
        }

        def one(i, carry):
            q = i // 2
            pair = q + lax.rem(q, 2) * (q // 2) * -1 + (q // 2) * (1 - lax.rem(q, 2))
            slot = jnp.where(i < 2, i, 2 * pair + 1 - lax.rem(i, 2))

            ticks_at(i, plan_one)

            @pl.when(i == 1)
            def _():
                for h in range(2):
                    gat_d.near_copy(0, h).wait()

            @pl.when(i == 2)
            def _():
                gat_d.step(0)
                tick((1, 0, 1), (1, 1, 1), (2, 0, 1), (2, 1, 1))
                gat_d.step(1)
                fwd.take(1, *sz.sends[1, 0][1])
                fwd.take(0, *sz.sends[0, 0][1])
                fwd.send(1, 2)
                fwd.send(0, 4)
                tick((1, 0, 1), (1, 1, 1), (3, 0, 1), (3, 1, 1))
                for h in range(2):
                    gat_d.near_copy(2, h).wait()

            ticks_at(i, plan_two)

            @pl.when(i == 4)
            def _():
                gat_d.step(2)
                for d in (4, 6):
                    for h in range(2):
                        gat_d.near_copy(d, h).wait()

            attention(slot)

            @pl.when(i == 1)
            def _():
                last.near_copy(0).start()

            @pl.when((i > 1) & (lax.rem(i, 2) == 0))
            def _():
                last.near_copy(pair).start()

            @pl.when(i == 3)
            def _():
                last.near_add(0)
                last.near_add(1)
                last.send(0, 2)

            @pl.when(i == 6)
            def _():
                finish_out()

            @pl.when(i == 5)
            def _():
                last.near_add(3)
                last.send(0, 6)
                last.send(1, 6)

            @pl.when(i == 7)
            def _():
                last.near_add(2)
                last.after(2)

            return carry

        lax.fori_loop(0, 8, one, 0)
        tick((1, 0, 1), (1, 1, 1), (2, 1, 1), (3, 0, 1), (3, 1, 1))
    else:
        for t in range(len(gat_d.stages)):
            gat_d.step(t)
        gat_d.finish()
        finish_out()
        slot_loop(sz, attention, last)

    load_attn.wait()
    load_att.wait()
    attention_grad(3, 1, F)
    begin(2, 1)
    tick((2, 0, 1))
    attention_grad(0, 0, F)
    begin(2, 0)
    attention_grad(2, 1, F + local)
    begin(3, 1)
    attention_grad(1, 0, F + local)
    begin(3, 0)
    tick((1, 0, 1), (1, 1, 1), (2, 1, 1), (3, 0, 1), (3, 1, 1))

    tables = r.table_g
    span = tables.shape[2]
    for h in range(heads):
        strip = jnp.zeros((grid_side, span), F32)
        for row in range(grid_side):
            piece = jnp.concatenate(
                [
                    grid_g[h, row * grid_side : (row + 1) * grid_side, :],
                    jnp.zeros((grid_side, span - 2 * L), F32),
                ],
                axis=1,
            )
            strip = strip + (pltpu.roll(piece, row * 2 * grid_side, 1) if row else piece)
        total_row = strip[0:1]
        for c in range(1, grid_side):
            total_row = total_row + pltpu.roll(strip[c : c + 1], c, 1)
        tables[dp, h : h + 1, :] = total_row

    share(0)
    share(1)
    load_kept.wait()
    normed1, inv1 = layer_stats(r.res_v[...])
    r.normed_v[...] = normed1
    last.close()
    tick((1, 1, 2), (2, 0, 1), (3, 0, 1), (3, 1, 1))
    d_in = last.own_sum()
    g = d_in * (1.0 + modv[mrow, D : 2 * D])
    mlp[:block, :] = (r.dh_v[...] + layer_back(g, r.normed_v[...], inv1)).astype(BF16)
    late_sums[me, 0:1, :] = jnp.sum(d_in, axis=0, keepdims=True)
    late_sums[me, 1:2, :] = jnp.sum(d_in * r.normed_v[...], axis=0, keepdims=True)
    gat_k.start()
    tick((1, 1, 1), (2, 0, 1), (2, 1, 1))

    def out_copy(slot):
        return pltpu.make_async_copy(
            r.part_f.at[pl.ds(slot * n, n)], r.out.at[xor(mine, slot, sbits)], r.load_sem.at[0, slot]
        )

    def start_out(slot, carry):
        out_copy(slot).start()
        return carry

    def patch_copy(slot):
        return pltpu.make_async_copy(
            r.part_b.at[pl.ds(lax.rem(slot, 2) * L, L)], r.patch_g.at[xor(mine, slot, sbits)], r.load_sem.at[1, slot]
        )

    def patch(slot, carry):
        @pl.when(slot >= 2)
        def _():
            patch_copy(slot - 2).wait()

        sel = pick_rows(r.pos, xor(mine, slot, sbits), L)
        r.part_b[pl.ds(lax.rem(slot, 2) * L, L), :] = dot(sel, mlp[pl.ds(slot * n, n), :]).astype(BF16)
        patch_copy(slot).start()
        return carry

    for h in range(2):
        gat_k.near_copy(0, h).wait()
    if sz.fast:
        lax.fori_loop(0, 2, patch, 0)
    gat_k.step(0)
    for d in range(1, sz.mp):
        dm_copy(early, 0, d, me).start()
        dm_copy(late_sums, 1, d, me).start()
    gat_o.start()
    tick((1, 0, 1), (2, 1, 1), (3, 0, 1), (3, 1, 2))
    gat_k.step(1)
    tick((1, 0, 2), (1, 1, 1), (2, 0, 1), (2, 1, 2))
    if sz.fast:
        for d in (2, 4):
            for h in range(2):
                gat_k.near_copy(d, h).wait()
        lax.fori_loop(2, 6, patch, 0)
        gat_k.step(2)
        tick((1, 1, 2), (2, 0, 1), (2, 1, 1), (3, 0, 1), (3, 1, 1))
        for h in range(2):
            gat_k.near_copy(6, h).wait()
        lax.fori_loop(6, 8, patch, 0)
    else:
        for t in range(2, len(gat_k.stages)):
            gat_k.step(t)
        gat_k.finish(2)
        lax.fori_loop(0, sz.samples, patch, 0)
    for d in range(1, sz.mp):
        dm_copy(early, 0, d, me).wait_send()
        dm_copy(early, 0, d, flip(me, d)).wait_recv()
        dm_copy(late_sums, 1, d, me).wait_send()
        dm_copy(late_sums, 1, d, flip(me, d)).wait_recv()
    flat, mod_g = r.flat, r.mod_g
    flat[:, 6 * D :] = jnp.zeros((sz.samples, flat.shape[1] - 6 * D), F32)
    for s in range(sz.samples):
        for c in range(6):
            v = 0
            for p in range(sz.per):
                m = s * sz.per + p
                v = v + (late_sums[m, c : c + 1, :] if c < 2 else early[m, c - 2 : c - 1, :])
            flat[s : s + 1, c * D : (c + 1) * D] = v
    base = pl.multiple_of(me * cols // 128 * 128, 128)
    mod_g[dp] = flat[:, pl.ds(base, mod_g.shape[2])]
    share(2)
    tick((1, 0, 2), (2, 0, 1), (3, 0, 1), (3, 1, 1), (1, 0, 1))
    gat_o.step(0)
    tick((2, 0, 1), (2, 1, 1), (2, 0, 1), (3, 1, 1), (3, 0, 1))
    tick((2, 0, 1), (2, 1, 1), (3, 1, 1), (3, 0, 1))
    gat_o.step(1)
    tick((3, 0, 1), (3, 1, 1), (3, 0, 1))
    for t in range(2, len(gat_o.stages)):
        gat_o.step(t)
    gat_o.finish()
    lax.fori_loop(0, sz.samples, start_out, 0)
    tick((3, 1, 1), (3, 0, 1))
    if line is not None:
        assert all(k == marks[4] for k in following.values()), following
    for k in range(4):
        for e in range(1, dp_size):
            dp_copy(k, e, dp).wait_send()
            dp_copy(k, e, lax.rem(dp + dp_size - e, dp_size)).wait_recv()
    for slot in range(sz.samples - 2, sz.samples):
        patch_copy(slot).wait()

    def wait_out(slot, carry):
        out_copy(slot).wait()
        return carry

    lax.fori_loop(0, sz.samples, wait_out, 0)
    if line is not None:
        line.finish()


def write_results(heads, hd, grid_side, cols, r):
    total = r.total
    F, local = r.up.shape[0], r.merge.shape[0]
    D = total.shape[2]
    depth = r.narrow.shape[0]
    samples = r.out.shape[0]

    def out_in(s):
        return pltpu.make_async_copy(r.out.at[s], r.out_v.at[s], r.out_sem.at[0, s])

    def out_back(s):
        return pltpu.make_async_copy(r.out_v.at[s], r.block_out.at[s], r.out_sem.at[1, s])

    jobs = []
    for s in range(samples):
        jobs.append((r.patch_g.at[s], r.patch.at[s], r.patch.shape[1]))
    rows_most = r.narrow.shape[1]

    def add(half, start, to, at, count):
        while count:
            size = min(rows_most, count)
            jobs.append((total.at[half, pl.ds(start, size)], to.at[pl.ds(at, size)], size))
            start, at, count = start + size, at + size, count - size

    stripe = stripe_of(F)
    for turn in range(F // stripe):
        add(turn % 2, turn // 2 * stripe, r.down, turn * stripe, stripe)
        add(turn % 2, F // 2 + turn // 2 * stripe, r.up, turn * stripe, stripe)
    add(0, F, r.project, 0, 2 * local)
    add(1, F + local, r.project, 2 * local, local)
    add(1, F, r.merge, 0, local)

    def load(k):
        src, _, size = jobs[k]
        return pltpu.make_async_copy(src, r.narrow.at[k % depth, pl.ds(0, size)], r.load_sem.at[k % depth])

    def save(k):
        _, dst, size = jobs[k]
        return pltpu.make_async_copy(r.wide.at[k % depth, pl.ds(0, size)], dst, r.save_sem.at[k % depth])

    for k in range(depth):
        load(k).start()
    for s in range(samples):
        out_in(s).start()

    def small_results():
        members, _, width = r.mod_g.shape
        shift = lax.rem(lax.axis_index("mp") * cols, 128)
        dmod = jnp.concatenate([r.mod_g[m] for m in range(members)], axis=0)
        dmod = pltpu.roll(dmod, lax.rem(width - shift, width), 1)
        upper = dmod.astype(BF16)
        parts = jnp.concatenate([upper, (dmod - upper.astype(F32)).astype(BF16)], axis=0)
        signal = jnp.concatenate([r.signal_g[m].astype(F32) for m in range(members)], axis=0).astype(BF16)
        r.mod_v[...] = dot(parts, jnp.concatenate([signal, signal], axis=0), 0, 0)[:cols]
        modulate = pltpu.make_async_copy(r.mod_v, r.modulate, r.sem.at[0])
        modulate.start()
        r.mod_bias[...] = jnp.sum(dmod, axis=0, keepdims=True)[:, :cols].reshape(cols)
        bias, table = r.bias_g[0], r.table_g[0]
        for m in range(1, members):
            bias, table = bias + r.bias_g[m], table + r.table_g[m]
        r.up_bias[...] = bias[0:1, :F].reshape(F)
        r.down_bias[...] = bias[1:2].reshape(D)
        r.merge_bias[...] = bias[2:3].reshape(D)
        lanes = heads * HEAD_PAD
        for k, c in enumerate((0, 2)):
            row = spread(bias[3:4, c * lanes : (c + 1) * lanes], heads, hd, hd - HEAD_PAD)
            r.proj_bias[k : k + 1, :] = row[:, : heads * hd]
        offsets = 2 * grid_side - 1
        r.table[...] = spread(table, offsets, offsets, -1)[:, : offsets * offsets]
        return modulate

    for k, (_, _, size) in enumerate(jobs):
        load(k).wait()
        if k >= depth:
            save(k - depth).wait()
        r.wide[k % depth, :size] = r.narrow[k % depth, :size].astype(F32)
        save(k).start()
        if k + depth < len(jobs):
            load(k + depth).start()
        if k < samples:
            out_in(k).wait()
            out_back(k).start()
        if k == depth:
            modulate = small_results()
    for k in range(max(0, len(jobs) - depth), len(jobs)):
        save(k).wait()
    for s in range(samples):
        out_back(s).wait()
    modulate.wait()


def body(
    patches,
    condition,
    lengths,
    keep_order,
    cotangent,
    projection_weight,
    query_value_bias,
    merge_weight,
    merge_output_bias,
    up_weight,
    up_projection_bias,
    down_weight,
    down_projection_bias,
    w_modulate,
    bias_modulate,
    bias_table,
):
    samples, L, D = patches.shape
    n = cotangent.shape[1]
    grid_side = math.isqrt(L)
    offsets = 2 * grid_side - 1
    heads = bias_table.shape[0]
    local = projection_weight.shape[2]
    hd = local // heads
    lanes = heads * HEAD_PAD
    F = up_weight.shape[1]
    cols = w_modulate.shape[1]
    mp, dp_size = lax.axis_size("mp"), lax.axis_size("dp")
    me = lax.axis_index("mp")
    sz = Sizes(mp, samples, n, D)
    rows, block = sz.rows, sz.block

    keep, counts, cot = keep_order, lengths, cotangent
    if sz.per > 1:
        ids = jnp.arange(n, dtype=jnp.int32)
        order = ((ids // block) ^ lax.rem(me, sz.per)) * block + ids % block
        keep = jnp.take(jnp.where(ids[None, :] < lengths[:, None], keep_order[:, :n], -1), order, axis=1)
        counts = jnp.full_like(lengths, n)
        cot = jnp.take(cot, order, axis=1)
    wide = -(-cols // 128) * 128 + 128
    modw = max(m * cols // 128 * 128 + wide for m in range(mp))
    dma = pltpu.SemaphoreType.DMA

    one = Call()
    one.arg(
        condition=condition,
        keep=keep,
        b_qv=query_value_bias,
        b_merge=merge_output_bias,
        b_mod=bias_modulate,
        b_table=bias_table,
        w_in=jnp.swapaxes(projection_weight, 1, 2),
        w_out=merge_weight,
    )
    one.arg(pltpu.SMEM, lengths=counts)
    one.arg(pl.ANY, patches=patches, w_mod=w_modulate.T)
    one.out(modv=((samples, 6 * D), F32), pos=((samples, n), jnp.int32), pos_wide=((samples, n), jnp.int32))
    one.out(
        pl.ANY,
        attn_in=((rows, D), BF16),
        qkv=((rows, 3 * lanes), BF16),
        probs=((samples, heads, n, n), F32),
        att=((rows, lanes), BF16),
        kept=((block, D), F32),
        res=((block, D), F32),
        hidden=((block, D), F32),
        mlp=((block, D), BF16),
        w_qkv=((3 * lanes, D), BF16),
        w_merge=((lanes, D), BF16),
    )
    one.vmem(
        attn_in_v=((rows, D), BF16),
        qkv_v=((rows, 3 * lanes), BF16),
        probs_v=((samples, heads, n, n), F32),
        att_v=((rows, lanes), BF16),
        kept_v=((block, D), F32),
        res_v=((block, D), F32),
        hidden_v=((block, D), F32),
        mlp_v=((block, D), BF16),
        w_qkv_v=((3 * lanes, D), BF16),
        w_merge_v=((lanes, D), BF16),
        w_mod_v=((cols, D), BF16),
        patches_v=((samples, L, D), BF16),
        mod_buf=((mp, samples, wide), F32),
        mod_wide=((samples, modw), F32),
        qv_wide=((2, lanes), F32),
        table_v=((heads, 4 * L), F32),
        normed=((rows, D), F32),
        bias_full=((heads, L, 2 * L), BF16),
        part=((rows, D), BF16),
    )
    one.scratch(
        mod_send=dma((mp,)),
        mod_recv=dma((mp,)),
        sem=dma((7,)),
        load_sem=dma((samples,)),
        save_sem=dma((4, samples)),
        red=reduce_scratch(sz),
    )
    first = one.run(
        functools.partial(attention_forward, sz, heads, hd, grid_side, cols), "attention_forward", 0, 62 << 20
    )

    chunk = 48 if dp_size == 4 and F % 96 == 0 and local % 48 == 0 else 0
    two = Call()
    two.arg(
        condition=condition,
        b_up=up_projection_bias,
        b_down=down_projection_bias,
        pos=first.pos,
        pos_wide=first.pos_wide,
        modv=first.modv,
    )
    two.arg(
        pl.ANY,
        cot=cot,
        w_up=up_weight.T,
        w_down=down_weight,
        mlp=first.mlp,
        hidden=first.hidden,
        res=first.res,
        kept=first.kept,
        qkv=first.qkv,
        probs=first.probs,
        att=first.att,
        w_qkv=first.w_qkv,
        w_merge=first.w_merge,
        attn_in=first.attn_in,
    )
    both = ((2, F + 2 * local, D), BF16)
    if chunk:
        count = (F + 2 * local) // chunk
        two.out(z_outer=both)
        two.vmem(grads=both, z_inner=((F + 2 * local, D), BF16))
        two.scratch(
            zs=dma((2, count)),
            zo=dma((2, count)),
            zf=dma((count,)),
            zi=dma((count,)),
            zt=dma((3, count)),
            zr=dma((2, count)),
        )
    else:
        two.out(grads=both)
    two.out(
        bias_g=((dp_size, 4, D), F32),
        table_g=((dp_size, heads, 4 * L), F32),
        signal_g=((dp_size, samples, D), BF16),
        mod_g=((dp_size, samples, wide), F32),
    )
    two.out(pl.ANY, out=((samples, n, D), BF16), patch_g=((samples, L, D), BF16))
    two.vmem(
        w_up_v=((F, D), BF16),
        w_down_v=((F, D), BF16),
        mlp_v=((rows, D), BF16),
        d_mlp=((rows, D), BF16),
        slope=((rows, F), F32),
        act=((rows, F), BF16),
        d_pre=((rows, F), BF16),
        part_f=((rows, D), BF16),
        part_b=((rows, D), BF16),
        d_attn=((rows, D), BF16),
        cot_own=((block, D), BF16),
        hidden_v=((block, D), F32),
        res_v=((block, D), F32),
        normed_v=((block, D), F32),
        dh_v=((block, D), F32),
        qkv_v=((rows, 3 * lanes), BF16),
        probs_v=((samples, heads, n, n), F32),
        w_qkv_v=((3 * lanes, D), BF16),
        w_merge_v=((lanes, D), BF16),
        grid_g=((heads, L, 2 * L), F32),
        early=((mp, 4, D), F32),
        late_sums=((mp, 2, D), F32),
        flat=((samples, modw), F32),
        bias_v=((2, D), F32),
    )
    two.scratch(
        sem=dma((13,)),
        load_sem=dma((3, samples)),
        dm_send=dma((2, mp)),
        dm_recv=dma((2, mp)),
        dp_send=dma((4, dp_size)),
        dp_recv=dma((4, dp_size)),
        red_f=reduce_scratch(sz),
        red_b=reduce_scratch(sz),
        last_sems=reduce_scratch(sz)[2:],
        gat_m=gather_scratch(sz),
        gat_d=gather_scratch(sz),
        gat_o=gather_scratch(sz),
        gat_k=gather_scratch(sz),
    )
    got = two.run(
        functools.partial(block_backward, sz, heads, hd, grid_side, cols, dp_size, chunk), "block_backward", 1, 64 << 20
    )

    total = got.z_outer if chunk else lax.psum(got.grads, "dp")
    three = Call()
    three.arg(mod_g=got.mod_g, signal_g=got.signal_g, bias_g=got.bias_g, table_g=got.table_g)
    three.arg(pl.ANY, total=total, out=got.out, patch_g=got.patch_g)
    three.out(
        mod_bias=((cols,), F32),
        up_bias=((F,), F32),
        down_bias=((D,), F32),
        merge_bias=((D,), F32),
        proj_bias=((2, local), F32),
        table=((heads, offsets * offsets), F32),
    )
    three.out(
        pl.ANY,
        block_out=((samples, n, D), BF16),
        patch=((samples, L, D), F32),
        up=((F, D), F32),
        down=((F, D), F32),
        project=((3 * local, D), F32),
        merge=((local, D), F32),
        modulate=((cols, D), F32),
    )
    depth = 8
    three.vmem(narrow=((depth, 288, D), BF16), wide=((depth, 288, D), F32), mod_v=((cols, D), F32), out_v=((samples, n, D), BF16))
    three.scratch(sem=dma((1,)), out_sem=dma((2, samples)), load_sem=dma((depth,)), save_sem=dma((depth,)))
    end = three.run(functools.partial(write_results, heads, hd, grid_side, cols), "write_results", None, 63 << 20)

    block_out = end.block_out
    if sz.per > 1:
        block_out = jnp.take(block_out, order, axis=1)
    return (
        block_out,
        end.patch,
        jnp.swapaxes(end.project.reshape(3, local, D), 1, 2),
        end.proj_bias,
        end.merge,
        end.merge_bias,
        end.up.T,
        end.up_bias,
        end.down,
        end.down_bias,
        end.modulate.T,
        end.mod_bias,
        end.table,
    )


def solution(mesh):
    placed = (
        P("dp", None, None),
        P("dp", None),
        P("dp"),
        P("dp", None),
        P("dp", None, None),
        P(None, None, "mp"),
        P(None, "mp"),
        P("mp", None),
        P(),
        P(None, "mp"),
        P("mp"),
        P("mp", None),
        P(),
        P(None, "mp"),
        P("mp"),
        P("mp", None),
    )
    return jax.shard_map(
        body,
        mesh=mesh,
        in_specs=placed,
        out_specs=(
            P("dp", None, None),
            P("dp", None, None),
            P(None, None, "mp"),
            P(None, "mp"),
            P("mp", None),
            P(),
            P(None, "mp"),
            P("mp"),
            P("mp", None),
            P(),
            P(None, "mp"),
            P("mp"),
            P("mp", None),
        ),
        check_vma=False,
    )
```

```python
import functools
import math
from types import SimpleNamespace

import jax
import jax.numpy as jnp
from jax import lax
from jax.experimental import pallas as pl
from jax.experimental.pallas import tpu as pltpu
from jax.sharding import PartitionSpec as P

MESH = pl.DeviceIdType.MESH
F32 = jnp.float32
BF16 = jnp.bfloat16
EPSILON = 1e-06
MASKED = -1000000000.0
GELU_C = math.sqrt(2.0 / math.pi)
GELU_A = 0.044715
VMEM = pl.BlockSpec(memory_space=pltpu.VMEM)
HEAD_PAD = 128


def dot(a, b, ca=1, cb=0):
    return lax.dot_general(a, b, (((ca,), (cb,)), ((), ())), preferred_element_type=F32)


def bit_of(value, k):
    return lax.rem(value // (1 << k), 2)


def flip(value, mask):
    out = value
    k = 0
    while (1 << k) <= mask:
        if mask & (1 << k):
            out = out + (1 << k) * (1 - 2 * bit_of(value, k))
        k += 1
    return out


def xor(a, b, bits):
    out = 0
    for k in range(bits):
        out = out + (1 << k) * lax.rem(bit_of(a, k) + bit_of(b, k), 2)
    return out


class Sizes:
    def __init__(self, mp, samples, slots, width):
        self.mp, self.samples, self.slots, self.width = mp, samples, slots, width
        self.bits = mp.bit_length() - 1
        self.rows = samples * slots
        self.block = self.rows // mp
        self.half = self.block // 2
        self.per = self.block and slots // self.block
        rest = [1 << k for k in range(1, self.bits)]
        self.orders = (rest, rest[::-1])
        self.sends = {}
        count = 0
        for h in range(2):
            live = list(range(0, mp, 2))
            for t, bit in enumerate(self.orders[h]):
                moved = [d for d in live if d & bit]
                live = [d for d in live if not d & bit]
                self.sends[h, t] = [(d, bit, count + i) for i, d in enumerate(moved)]
                count += len(moved)
        self.steps = len(rest)
        self.far = count
        self.near = mp // 2
        self.fast = self.steps == 2 and self.per == 1


def my_index():
    return lax.axis_index("dp"), lax.axis_index("mp")


def rows_of(ref, start, size):
    return ref.at[pl.ds(start, size)]


class Reduce:
    def __init__(self, sz, part, refs):
        self.sz, self.part = sz, part
        self.near_buf, self.far_buf, self.near_send, self.near_recv, self.far_send, self.far_recv = refs
        self.dp, self.me = my_index()

    def near_copy(self, pair):
        b = self.sz.block
        return pltpu.make_async_remote_copy(
            src_ref=rows_of(self.part, (2 * pair + 1) * b, b),
            dst_ref=rows_of(self.near_buf, pair * b, b),
            send_sem=self.near_send.at[pair],
            recv_sem=self.near_recv.at[pair],
            device_id=(self.dp, flip(self.me, 1)),
            device_id_type=MESH,
        )

    def far_copy(self, h, d, bit, i):
        b, hb = self.sz.block, self.sz.half
        return pltpu.make_async_remote_copy(
            src_ref=rows_of(self.part, d * b + h * hb, hb),
            dst_ref=rows_of(self.far_buf, i * hb, hb),
            send_sem=self.far_send.at[i],
            recv_sem=self.far_recv.at[i],
            device_id=(self.dp, flip(self.me, bit)),
            device_id_type=MESH,
        )

    def add(self, start, buf, at, size):
        a = self.part[pl.ds(start, size), :].astype(F32) + buf[pl.ds(at, size), :].astype(F32)
        self.part[pl.ds(start, size), :] = a.astype(BF16)

    def near_add(self, pair):
        b = self.sz.block
        self.near_copy(pair).wait()
        self.add(2 * pair * b, self.near_buf, pair * b, b)

    def send(self, h, d):
        for t in range(self.sz.steps):
            for m in self.sz.sends[h, t]:
                if m[0] == d:
                    self.far_copy(h, *m).start()

    def take(self, h, d, bit, i, add=True):
        b, hb = self.sz.block, self.sz.half
        self.far_copy(h, d, bit, i).wait()
        if add:
            self.add((d - bit) * b + h * hb, self.far_buf, i * hb, hb)

    def after(self, k):
        if k == 0:
            self.send(0, 6)
            self.send(1, 6)
        if k == 1:
            self.send(0, 2)
        if k == 2:
            self.send(1, 4)
            self.take(1, *self.sz.sends[1, 0][1])
            self.send(1, 2)
            self.take(0, *self.sz.sends[0, 0][1])
            self.send(0, 4)

    def close(self):
        sz = self.sz
        if sz.fast:
            for h in range(2):
                for t in range(2):
                    for m in sz.sends[h, t]:
                        if m[0] == m[1]:
                            self.take(h, *m, add=False)
            return

        def one(i, carry):
            self.near_add(sz.near - 1 - i)
            return carry

        lax.fori_loop(0, sz.near, one, 0)
        for t in range(sz.steps):
            for h in range(2):
                for m in sz.sends[h, t]:
                    self.far_copy(h, *m).start()
            for h in range(2):
                for m in sz.sends[h, t]:
                    self.take(h, *m, add=t < sz.steps - 1)

    def own_sum(self):
        sz, hb = self.sz, self.sz.half
        out = []
        for h in range(2):
            total = self.part[h * hb : (h + 1) * hb, :].astype(F32)
            for t in range(0 if sz.fast else sz.steps - 1, sz.steps):
                for d, bit, i in sz.sends[h, t]:
                    if d == bit:
                        total = total + self.far_buf[i * hb : (i + 1) * hb, :].astype(F32)
            out.append(total)
        return jnp.concatenate(out, axis=0)


class Gather:
    def __init__(self, sz, out, sems):
        self.sz, self.out = sz, out
        self.near_send, self.near_recv, self.far_send, self.far_recv = sems
        self.dp, self.me = my_index()
        self.first, self.stages = [], []
        if sz.fast:
            x, y = sz.orders[0]
            self.first = [(1, 0, x, 0), (0, 0, y, 1), (0, 0, x, 2), (1, 0, y, 3)]
            on = {0: (1, x, y, 5), 1: (0, y, x, 4)}
            self.stages = [
                [(self.first[1], [on[1]]), (self.first[0], [on[0]])],
                [(self.first[2], []), (self.first[3], [])],
                [(on[1], []), (on[0], [])],
            ]
        else:
            count, plan = 0, {}
            for h in range(2):
                have = [0]
                for t, bit in enumerate(sz.orders[h][::-1]):
                    plan[h, t] = [(h, d, bit, count + i) for i, d in enumerate(have)]
                    count += len(have)
                    have = have + [d | bit for d in have]
            self.first = plan[0, 0] + plan[1, 0]
            for t in range(sz.steps):
                stage = []
                for h in range(2):
                    later = plan[h, t + 1] if t + 1 < sz.steps else []
                    for k, m in enumerate(plan[h, t]):
                        stage.append((m, later if k == len(plan[h, t]) - 1 else []))
                self.stages.append(stage)

    def near_copy(self, d, h):
        b, hb = self.sz.block, self.sz.half
        return pltpu.make_async_remote_copy(
            src_ref=rows_of(self.out, d * b + h * hb, hb),
            dst_ref=rows_of(self.out, (d + 1) * b + h * hb, hb),
            send_sem=self.near_send.at[d + h],
            recv_sem=self.near_recv.at[d + h],
            device_id=(self.dp, flip(self.me, 1)),
            device_id_type=MESH,
        )

    def far_copy(self, h, d, bit, i):
        b, hb = self.sz.block, self.sz.half
        return pltpu.make_async_remote_copy(
            src_ref=rows_of(self.out, d * b + h * hb, hb),
            dst_ref=rows_of(self.out, (d + bit) * b + h * hb, hb),
            send_sem=self.far_send.at[i],
            recv_sem=self.far_recv.at[i],
            device_id=(self.dp, flip(self.me, bit)),
            device_id_type=MESH,
        )

    def start(self):
        for m in self.first:
            self.far_copy(*m).start()
        for h in range(2):
            self.near_copy(0, h).start()

    def step(self, t):
        for m, later in self.stages[t]:
            self.far_copy(*m).wait()
            for n in later:
                self.far_copy(*n).start()
            h, d, bit, _ = m
            self.near_copy(d + bit, h).start()

    def finish(self, first=0):
        for d in range(first, self.sz.mp, 2):
            for h in range(2):
                self.near_copy(d, h).wait()


def reduce_scratch(sz):
    return [
        pltpu.VMEM((sz.near * sz.block, sz.width), BF16),
        pltpu.VMEM((sz.far * sz.half, sz.width), BF16),
        pltpu.SemaphoreType.DMA((sz.near,)),
        pltpu.SemaphoreType.DMA((sz.near,)),
        pltpu.SemaphoreType.DMA((sz.far,)),
        pltpu.SemaphoreType.DMA((sz.far,)),
    ]


def gather_scratch(sz):
    return [
        pltpu.SemaphoreType.DMA((sz.mp,)),
        pltpu.SemaphoreType.DMA((sz.mp,)),
        pltpu.SemaphoreType.DMA((sz.far,)),
        pltpu.SemaphoreType.DMA((sz.far,)),
    ]


def slot_loop(sz, body, red, extra=None):
    if sz.fast:

        def one(i, carry):
            q = i // 2
            pair = 2 * (1 - lax.rem(q, 2)) + 1 - q // 2
            other = 1 - lax.rem(i, 2)
            body(2 * pair + other)

            @pl.when(other == 1)
            def _():
                red.near_copy(pair).start()

            @pl.when(other == 0)
            def _():
                red.near_add(pair)

            for k in range(3):
                pl.when(i == 2 * k + 1)(functools.partial(red.after, k))
            if extra is not None:
                extra(i)
            return carry

    else:
        pairs = sz.per // 2

        def one(i, carry):
            slot = sz.samples - 1 - i
            body(slot)
            for p in range(pairs):
                red.near_copy(slot * pairs + p).start()
            return carry

    lax.fori_loop(0, sz.samples, one, 0)


def layer_stats(values):
    centre = jnp.mean(values, axis=-1, keepdims=True)
    shifted = values - centre
    spread = jnp.mean(shifted * shifted, axis=-1, keepdims=True)
    inv_std = lax.rsqrt(spread + EPSILON)
    return shifted * inv_std, inv_std


def layer_back(gradient, normed, inv_std):
    mean_grad = jnp.mean(gradient, axis=-1, keepdims=True)
    mean_mix = jnp.mean(gradient * normed, axis=-1, keepdims=True)
    return inv_std * (gradient - mean_grad - normed * mean_mix)


def pick_rows(ids_ref, s, count):
    ids = ids_ref[pl.ds(s, 1), :]
    return (lax.broadcasted_iota(jnp.int32, (count, ids.shape[1]), 0) == ids).astype(F32).astype(BF16)


def spread(row, pieces, size, step):
    width = row.shape[1]
    lane = lax.broadcasted_iota(jnp.int32, row.shape, 1)
    total = jnp.zeros_like(row)
    for p in range(pieces):
        start = p * (size + step) if step > 0 else p * size
        moved = pltpu.roll(row, (p * step) % width, 1) if p else row
        total = jnp.where((lane >= start) & (lane < start + size), moved, total)
    return total


def spread_heads(row, heads, hd):
    return spread(row, heads, hd, HEAD_PAD - hd)


def live_column(sel):
    ones = jnp.ones((sel.shape[0], 128), BF16)
    return dot(sel, ones, 0, 0)[:, 0:1]


def stripe_of(rows):
    return 96 if rows % 192 == 0 else rows // 2


class Call:
    def __init__(self):
        self.args, self.specs, self.outs, self.out_specs, self.scratch_of = {}, [], {}, [], {}

    def arg(self, space=pltpu.VMEM, **values):
        self.args.update(values)
        self.specs += [pl.BlockSpec(memory_space=space)] * len(values)

    def out(self, space=pltpu.VMEM, **results):
        for name, (shape, dtype) in results.items():
            self.outs[name] = jax.ShapeDtypeStruct(shape, dtype)
            self.out_specs.append(pl.BlockSpec(memory_space=space))

    def scratch(self, **buffers):
        self.scratch_of.update(buffers)

    def vmem(self, **buffers):
        for name, (shape, dtype) in buffers.items():
            self.scratch_of[name] = pltpu.VMEM(shape, dtype)

    def run(self, kernel, name, cid, limit):
        flat = []
        for value in self.scratch_of.values():
            flat += value if isinstance(value, list) else [value]

        def inner(*refs):
            r, refs = SimpleNamespace(), list(refs)
            for key in list(self.args) + list(self.outs):
                setattr(r, key, refs.pop(0))
            for key, value in self.scratch_of.items():
                count = len(value) if isinstance(value, list) else 0
                setattr(r, key, [refs.pop(0) for _ in range(count)] if count else refs.pop(0))
            kernel(r)

        got = pl.pallas_call(
            inner,
            out_shape=list(self.outs.values()),
            in_specs=self.specs,
            out_specs=self.out_specs,
            scratch_shapes=flat,
            name=name,
            compiler_params=pltpu.CompilerParams(vmem_limit_bytes=limit)
            if cid is None
            else pltpu.CompilerParams(collective_id=cid, has_side_effects=True, vmem_limit_bytes=limit),
        )(*self.args.values())
        return SimpleNamespace(**dict(zip(self.outs, got)))


def attention_forward(sz, heads, hd, grid_side, cols, r):
    dp, me = my_index()
    mine = me // sz.per
    sbits = sz.samples.bit_length() - 1
    D, n, L = sz.width, sz.slots, grid_side * grid_side
    lanes = heads * HEAD_PAD
    red = Reduce(sz, r.part, r.red)
    mod_buf, mod_wide, modv = r.mod_buf, r.mod_wide, r.modv
    wide = mod_buf.shape[2]
    sem = r.sem

    barrier = pltpu.get_barrier_semaphore()
    for d in range(1, sz.mp):
        pl.semaphore_signal(barrier, inc=1, device_id=(dp, flip(me, d)), device_id_type=MESH)
    load_mod = pltpu.make_async_copy(r.w_mod, r.w_mod_v, sem.at[0])

    def load_patches(i, slot):
        return pltpu.make_async_copy(r.patches.at[xor(mine, slot, sbits)], r.patches_v.at[slot], r.load_sem.at[i])

    def start_load(slot, carry):
        load_patches(slot, slot).start()
        return carry

    load_mod.start()
    lax.fori_loop(0, sz.samples, start_load, 0)
    slots = lax.broadcasted_iota(jnp.int32, (1, n), 1)
    for s in range(sz.samples):
        pos = jnp.where(slots < r.lengths[s], r.keep[s : s + 1, 0:n], -1)
        r.pos[s : s + 1, :] = pos
        turned = L - 1 - pos
        r.pos_wide[s : s + 1, :] = jnp.where(pos < 0, -1, turned + turned // grid_side * grid_side)
    r.qv_wide[...] = jnp.zeros_like(r.qv_wide)
    r.qv_wide[:, 0 : heads * hd] = r.b_qv[...].astype(F32)
    r.qv_wide[...] = spread_heads(r.qv_wide[...], heads, hd)
    r.table_v[...] = jnp.zeros_like(r.table_v)
    offsets = 2 * grid_side - 1
    r.table_v[:, 0 : offsets * offsets] = r.b_table[...].astype(F32)
    r.table_v[...] = spread(r.table_v[...], offsets, offsets, 1)
    w_qkv, w_merge = r.w_qkv_v, r.w_merge_v
    pad_rows = jnp.zeros((HEAD_PAD - hd, D), F32)
    for h in range(heads):
        for c in range(3):
            piece = r.w_in[c].astype(F32)[h * hd : (h + 1) * hd]
            w_qkv[c * lanes + h * HEAD_PAD : c * lanes + (h + 1) * HEAD_PAD, :] = jnp.concatenate(
                [piece, pad_rows], axis=0
            ).astype(BF16)
        piece = r.w_out[...].astype(F32)[h * hd : (h + 1) * hd]
        w_merge[h * HEAD_PAD : (h + 1) * HEAD_PAD, :] = jnp.concatenate([piece, pad_rows], axis=0).astype(BF16)
    save = [
        pltpu.make_async_copy(w_qkv, r.w_qkv, sem.at[1]),
        pltpu.make_async_copy(w_merge, r.w_merge, sem.at[2]),
    ]
    for copy in save:
        copy.start()

    bias_full = r.bias_full
    span = r.table_v.shape[1]
    for h in range(heads):
        line = r.table_v[h : h + 1, :]
        strip = jnp.concatenate([line] + [pltpu.roll(line, span - c, 1) for c in range(1, grid_side)], axis=0)
        for row in range(grid_side):
            rolled = pltpu.roll(strip, span - row * 2 * grid_side, 1) if row else strip
            bias_full[h, row * grid_side : (row + 1) * grid_side, :] = rolled[:, : 2 * L].astype(BF16)

    cond = r.condition[...].astype(F32)
    signal = (cond / (1.0 + jnp.exp(-cond))).astype(BF16)
    mod_buf[me] = jnp.zeros((sz.samples, wide), F32)
    load_mod.wait()
    mod_buf[me, :, 0:cols] = dot(signal, r.w_mod_v[...], 1, 1) + r.b_mod[...].astype(F32).reshape(1, cols)
    pl.semaphore_wait(barrier, sz.mp - 1)

    def mod_copy(d, slot):
        return pltpu.make_async_remote_copy(
            src_ref=mod_buf.at[slot],
            dst_ref=mod_buf.at[slot],
            send_sem=r.mod_send.at[d],
            recv_sem=r.mod_recv.at[d],
            device_id=(dp, flip(me, d)),
            device_id_type=MESH,
        )

    for d in range(1, sz.mp):
        mod_copy(d, me).start()

    normed, kept_own = r.normed, r.kept_v

    def norm_one(slot, carry):
        load_patches(slot, slot).wait()
        sel = pick_rows(r.pos, xor(mine, slot, sbits), L)
        kept = dot(sel, r.patches_v[slot], 0, 0)
        value, _ = layer_stats(kept)
        normed[pl.ds(slot * n, n), :] = value

        @pl.when(slot == 0)
        def _():
            kept_own[...] = kept[: sz.block]

        return carry

    lax.fori_loop(0, sz.samples, norm_one, 0)
    save_kept = pltpu.make_async_copy(kept_own, r.kept, sem.at[3])
    save_kept.start()

    for d in range(1, sz.mp):
        mod_copy(d, me).wait_send()
        mod_copy(d, flip(me, d)).wait_recv()
    mod_wide[...] = jnp.zeros_like(mod_wide)
    for m in range(sz.mp):
        base = m * cols // 128 * 128
        phase = m * cols - base
        piece = mod_buf[m]
        if phase:
            piece = pltpu.roll(piece, phase, 1)
        mod_wide[:, base : base + wide] += piece
    modv[...] = mod_wide[:, : 6 * D]

    factor = hd ** (-0.5)
    stores = [(r.attn_in_v, r.attn_in), (r.qkv_v, r.qkv), (r.att_v, r.att)]

    def save_slot(i, slot):
        at = pl.ds(slot * n, n)
        copies = [
            pltpu.make_async_copy(a.at[at], b.at[at], r.save_sem.at[k, slot]) for k, (a, b) in enumerate(stores)
        ]
        copies.append(pltpu.make_async_copy(r.probs_v.at[slot], r.probs.at[slot], r.save_sem.at[3, slot]))
        return copies

    def body(slot):
        s = xor(mine, slot, sbits)
        at = pl.ds(slot * n, n)
        shift = modv[pl.ds(s, 1), 0:D]
        scale = modv[pl.ds(s, 1), D : 2 * D]
        entry = (normed[at, :] * (1.0 + scale) + shift).astype(BF16)
        r.attn_in_v[at, :] = entry
        proj = dot(entry, w_qkv[...], 1, 1)
        qs = (proj[:, :lanes] + r.qv_wide[0:1, :]).astype(BF16)
        ks = proj[:, lanes : 2 * lanes].astype(BF16)
        vs = (proj[:, 2 * lanes :] + r.qv_wide[1:2, :]).astype(BF16)
        r.qkv_v[at, 0:lanes] = qs
        r.qkv_v[at, lanes : 2 * lanes] = ks
        r.qkv_v[at, 2 * lanes :] = vs
        sel = pick_rows(r.pos, s, L)
        sel_wide = pick_rows(r.pos_wide, s, 2 * L)
        live = r.pos[pl.ds(s, 1), :] >= 0
        outs = []
        for h in range(heads):
            cut = slice(h * HEAD_PAD, (h + 1) * HEAD_PAD)
            bias = dot(dot(sel, bias_full[h], 0, 0).astype(BF16), sel_wide)
            scores = jnp.where(live, dot(qs[:, cut], ks[:, cut], 1, 1) * factor + bias, MASKED)
            top = jnp.max(scores, axis=-1, keepdims=True)
            e = jnp.exp(scores - top)
            p = e / jnp.sum(e, axis=-1, keepdims=True)
            r.probs_v[slot, h] = p
            outs.append(dot(p.astype(BF16), vs[:, cut]).astype(BF16))
        joined = jnp.concatenate(outs, axis=1) if heads > 1 else outs[0]
        r.att_v[at, :] = joined
        r.part[at, :] = dot(joined, w_merge[...]).astype(BF16)
        for copy in save_slot(0, slot):
            copy.start()

    slot_loop(sz, body, red)
    red.close()
    result = red.own_sum() + r.b_merge[...].astype(F32).reshape(1, D)
    r.res_v[...] = result
    hidden = kept_own[...] + modv[pl.ds(mine, 1), 2 * D : 3 * D] * result
    r.hidden_v[...] = hidden
    value, _ = layer_stats(hidden)
    shift = modv[pl.ds(mine, 1), 3 * D : 4 * D]
    scale = modv[pl.ds(mine, 1), 4 * D : 5 * D]
    r.mlp_v[...] = (value * (1.0 + scale) + shift).astype(BF16)
    save_own = [
        pltpu.make_async_copy(r.res_v, r.res, sem.at[4]),
        pltpu.make_async_copy(r.hidden_v, r.hidden, sem.at[5]),
        pltpu.make_async_copy(r.mlp_v, r.mlp, sem.at[6]),
    ]
    for copy in save_own:
        copy.start()

    def wait_slot(slot, carry):
        for copy in save_slot(0, slot):
            copy.wait()
        return carry

    lax.fori_loop(0, sz.samples, wait_slot, 0)
    for copy in save + save_own + [save_kept]:
        copy.wait()


class Line:
    def __init__(self, r, chunk):
        self.r, self.chunk = r, chunk
        self.g, self.outer_buf, self.inner_buf = r.grads, r.z_outer, r.z_inner
        self.count = self.g.shape[1] // chunk
        self.dp, self.me = my_index()
        self.is_inner = (self.dp == 1) | (self.dp == 2)
        self.is_outer = (self.dp == 0) | (self.dp == 3)
        self.step_to = 1 + self.dp // 3
        self.back_to = (self.dp - 1) * 3
        self.other = 3 - self.dp
        self.mine = 2 - self.dp
        self.passed = self.dp - 1

    def rows(self, k):
        return pl.ds(k * self.chunk, self.chunk)

    def copy(self, src, dst, send, recv, to):
        return pltpu.make_async_remote_copy(
            src_ref=src, dst_ref=dst, send_sem=send, recv_sem=recv, device_id=(to, self.me), device_id_type=MESH
        )

    def out_copy(self, j, k):
        return self.copy(
            self.g.at[j, self.rows(k)], self.outer_buf.at[j, self.rows(k)],
            self.r.zs.at[j, k], self.r.zo.at[j, k], self.step_to,
        )

    def in_copy(self, k):
        return self.copy(
            self.g.at[self.passed, self.rows(k)], self.inner_buf.at[self.rows(k)],
            self.r.zf.at[k], self.r.zi.at[k], self.other,
        )

    def total_copy(self, j, k, which, to):
        return self.copy(
            self.outer_buf.at[j, self.rows(k)], self.outer_buf.at[j, self.rows(k)],
            self.r.zt.at[which, k], self.r.zr.at[j, k], to,
        )

    def begin(self, halves, k0, k1):
        @pl.when(self.is_outer)
        def _():
            def one(k, carry):
                for j in halves:
                    self.out_copy(j, k).start()
                return carry

            lax.fori_loop(k0, k1, one, 0)

    def add(self, to, j, k, more):
        def one(i, carry):
            at = pl.ds(k * self.chunk + i * 16, 16)
            v = self.g[j, at, :].astype(F32) + self.outer_buf[j, at, :].astype(F32)
            if more:
                v = v + self.inner_buf[at, :].astype(F32)
            to[j, at, :] = v.astype(BF16)
            return carry

        lax.fori_loop(0, self.chunk // 16, one, 0)

    def stage(self, number, j, k):
        if number == 1:

            @pl.when(self.passed == j)
            def _():
                self.out_copy(j, k).wait_recv()
                self.add(self.g, j, k, False)
                self.in_copy(k).start()

        elif number == 2:

            @pl.when(self.mine == j)
            def _():
                self.out_copy(j, k).wait_recv()
                self.in_copy(k).wait_recv()
                self.add(self.outer_buf, j, k, True)
                self.total_copy(j, k, 0, self.other).start()
                self.total_copy(j, k, 1, self.back_to).start()

        else:

            @pl.when(self.passed == j)
            def _():
                self.in_copy(k).wait_send()
                self.total_copy(j, k, 0, self.other).wait_recv()
                self.total_copy(j, k, 2, self.back_to).start()

    def finish(self):
        @pl.when(self.is_inner)
        def _():
            def one(k, carry):
                self.total_copy(self.mine, k, 0, self.other).wait_send()
                self.total_copy(self.mine, k, 1, self.back_to).wait_send()
                self.total_copy(self.passed, k, 2, self.back_to).wait_send()
                return carry

            lax.fori_loop(0, self.count, one, 0)

        @pl.when(self.is_outer)
        def _():
            def one(k, carry):
                for j in range(2):
                    self.out_copy(j, k).wait_send()
                    self.total_copy(j, k, 0, self.step_to).wait_recv()
                return carry

            lax.fori_loop(0, self.count, one, 0)


def block_backward(sz, heads, hd, grid_side, cols, dp_size, chunk, r):
    dp, me = my_index()
    mine = me // sz.per
    sbits = sz.samples.bit_length() - 1
    D, n, L = sz.width, sz.slots, grid_side * grid_side
    lanes = heads * HEAD_PAD
    local = heads * hd
    F = r.w_up_v.shape[0]
    block = sz.block
    modv = r.modv
    fwd = Reduce(sz, r.part_f, r.red_f)
    bwd = Reduce(sz, r.part_b, r.red_b)
    last = Reduce(sz, r.part_b, r.red_b[:2] + r.last_sems)
    gat_m = Gather(sz, r.mlp_v, r.gat_m)
    gat_d = Gather(sz, r.d_attn, r.gat_d)
    gat_o = Gather(sz, r.part_f, r.gat_o)
    gat_k = Gather(sz, r.mlp_v, r.gat_k)
    line = Line(r, chunk) if chunk else None
    grads = r.grads
    sem = r.sem

    stripe = stripe_of(F)
    per_half, per_local = (F // 2 // chunk, local // chunk) if chunk else (0, 0)
    marks = [0, per_half, 2 * per_half, 2 * per_half + per_local, 2 * per_half + 2 * per_local]
    following = {(number, j): 0 for number in (1, 2, 3) for j in range(2)}

    def tick(*steps):
        if line is None:
            return
        for number, j, count in steps:
            k0 = following[number, j]
            k1 = min(k0 + count, marks[4])
            assert number == 1 or k1 <= following[number - 1, j]
            following[number, j] = k1
            if k1 - k0 == 1:
                line.stage(number, j, k0)
            elif k1 > k0:

                def one(k, carry, number=number, j=j):
                    line.stage(number, j, k)
                    return carry

                lax.fori_loop(k0, k1, one, 0)

    def begin(group, *halves):
        if line is not None:
            line.begin(halves or (0, 1), marks[group], marks[group + 1])

    def ticks_at(i, plan):
        if line is not None:
            for when, steps in plan.items():
                pl.when(i == when)(lambda steps=steps: tick(*steps))

    load_up = pltpu.make_async_copy(r.w_up, r.w_up_v, sem.at[0])
    load_down = pltpu.make_async_copy(r.w_down, r.w_down_v, sem.at[1])
    load_up.start()
    load_down.start()

    load_own = pltpu.make_async_copy(r.mlp, r.mlp_v.at[pl.ds(0, block)], sem.at[12])
    load_own.start()

    def load_cot(slot):
        at = pl.ds(slot * n, n)
        return pltpu.make_async_copy(r.cot.at[xor(mine, slot, sbits)], r.d_mlp.at[at], r.load_sem.at[1, slot])

    def start_cot(slot, carry):
        load_cot(slot).start()
        return carry

    lax.fori_loop(0, sz.samples, start_cot, 0)
    loads = [
        pltpu.make_async_copy(r.cot.at[mine, pl.ds(0, block)], r.cot_own, sem.at[2]),
        pltpu.make_async_copy(r.hidden, r.hidden_v, sem.at[3]),
        pltpu.make_async_copy(r.res, r.res_v, sem.at[4]),
    ]
    late = [
        pltpu.make_async_copy(r.qkv, r.qkv_v, sem.at[6]),
        pltpu.make_async_copy(r.probs, r.probs_v, sem.at[7]),
        pltpu.make_async_copy(r.w_qkv, r.w_qkv_v, sem.at[9]),
        pltpu.make_async_copy(r.w_merge, r.w_merge_v, sem.at[10]),
    ]
    for copy in loads + late:
        copy.start()
    load_attn = pltpu.make_async_copy(r.attn_in, r.d_mlp, sem.at[11])
    load_kept = pltpu.make_async_copy(r.kept, r.res_v, sem.at[5])
    load_att = pltpu.make_async_copy(r.att, r.act.at[:, pl.ds(0, lanes)], sem.at[8])

    barrier = pltpu.get_barrier_semaphore()
    for d in range(1, sz.mp):
        pl.semaphore_signal(barrier, inc=1, device_id=(dp, flip(me, d)), device_id_type=MESH)
    for e in range(1, dp_size):
        pl.semaphore_signal(barrier, inc=1, device_id=(lax.rem(dp + e, dp_size), me), device_id_type=MESH)
    pl.semaphore_wait(barrier, sz.mp + dp_size - 2)
    load_own.wait()
    gat_m.start()
    r.bias_v[0:1, 0:F] = r.b_up[...].astype(F32).reshape(1, F)
    r.bias_v[1:2, :] = r.b_down[...].astype(F32).reshape(1, D)
    load_up.wait()
    load_down.wait()
    w_up, w_down, mlp = r.w_up_v, r.w_down_v, r.mlp_v
    act, d_pre, d_mlp, slope = r.act, r.d_pre, r.d_mlp, r.slope

    up_bg, down_bg = r.bias_g.at[dp, 0:1], r.bias_g.at[dp, 1:2]
    merge_bg, proj_bg = r.bias_g.at[dp, 2:3], r.bias_g.at[dp, 3:4]
    r.bias_g[dp] = jnp.zeros(r.bias_g.shape[1:], F32)
    cond = r.condition[...].astype(F32)
    r.signal_g[dp] = (cond / (1.0 + jnp.exp(-cond))).astype(BF16)
    shared = [r.bias_g, r.table_g, r.mod_g, r.signal_g]

    def dp_copy(k, e, slot):
        return pltpu.make_async_remote_copy(
            src_ref=shared[k].at[slot],
            dst_ref=shared[k].at[slot],
            send_sem=r.dp_send.at[k, e],
            recv_sem=r.dp_recv.at[k, e],
            device_id=(lax.rem(dp + e, dp_size), me),
            device_id_type=MESH,
        )

    def share(k):
        for e in range(1, dp_size):
            dp_copy(k, e, dp).start()

    share(3)

    def forward(slot, wide):
        at = pl.ds(slot * n, wide * n)
        v = dot(mlp[at, :], w_up[...], 1, 1) + r.bias_v[0:1, 0:F]
        square = v * v
        h = 0.5 * jnp.tanh(v * (GELU_C * GELU_A * square + GELU_C)) + 0.5
        active = (v * h).astype(BF16)
        act[at, :] = active
        slope[at, :] = h * (1.0 + (1.0 - h) * (v * (6.0 * GELU_C * GELU_A * square + 2.0 * GELU_C)))
        r.part_f[at, :] = dot(active, w_down[...]).astype(BF16)

    def output_grad(slot, carry):
        at = pl.ds(slot * n, n)
        s = xor(mine, slot, sbits)
        load_cot(slot).wait()
        gate = modv[pl.ds(s, 1), 5 * D : 6 * D]
        live = live_column(pick_rows(r.pos, s, L))
        dm = (gate * (d_mlp[at, :].astype(F32) * live)).astype(BF16)
        d_mlp[at, :] = dm
        down_bg[...] += jnp.sum(dm.astype(F32), axis=0, keepdims=True)
        return carry

    if sz.fast:
        def two_slots(i, carry):
            @pl.when(i == 1)
            def _():
                lax.fori_loop(0, sz.samples, output_grad, 0)
                gat_m.step(0)
                gat_m.step(1)

            @pl.when(i == 3)
            def _():
                gat_m.step(2)

            for h in range(2):
                gat_m.near_copy(2 * i, h).wait()
            forward(2 * i, 2)
            fwd.near_copy(i).start()

            @pl.when(i > 0)
            def _():
                fwd.near_add(i - 1)

            pl.when(i == 2)(functools.partial(fwd.send, 0, 2))
            pl.when(i == 3)(functools.partial(fwd.send, 1, 4))
            return carry

        lax.fori_loop(0, 4, two_slots, 0)
    else:
        for t in range(len(gat_m.stages)):
            gat_m.step(t)
        gat_m.finish()
        lax.fori_loop(0, sz.samples, output_grad, 0)
        slot_loop(sz, lambda slot: forward(slot, 1), fwd)

    def wide_grad(left, right, base, group):
        at, sent = 0, 0
        while at < F:
            size = min(256, F - at)
            value = dot(left[:, at : at + size], right[...], 0, 0).astype(BF16)
            row = at
            while row < at + size:
                turn = row // stripe
                count = min((turn + 1) * stripe, at + size) - row
                to = base + turn // 2 * stripe + row % stripe
                grads[turn % 2, to : to + count, :] = value[row - at : row - at + count]
                row += count
            at += size
            if line is not None:
                ready = at // (2 * stripe) * (stripe // chunk)
                if ready > sent:
                    line.begin((0, 1), marks[group] + sent, marks[group] + ready)
                    sent = ready

    wide_grad(act, d_mlp, 0, 0)

    def backward(slot):
        at = pl.ds(slot * n, n)
        dpre = (dot(d_mlp[at, :], w_down[...], 1, 1) * slope[at, :]).astype(BF16)
        d_pre[at, :] = dpre
        up_bg[:, :F] += jnp.sum(dpre.astype(F32), axis=0, keepdims=True)
        r.part_b[at, :] = dot(dpre, w_up[...]).astype(BF16)

    plan = {
        2: [(1, 1, 1)],
        3: [(1, 0, 1)],
        5: [(1, 0, 1), (1, 1, 1), (2, 0, 1), (2, 1, 1)],
    }

    def bwd_extra(i):
        ticks_at(i, plan)

        @pl.when(i == 5)
        def _():
            fwd.near_add(3)
            fwd.send(0, 6)
            fwd.send(1, 6)

    slot_loop(sz, backward, bwd, bwd_extra)
    load_attn.start()
    load_att.start()
    wide_grad(d_pre, mlp, F // 2, 1)
    tick((1, 0, 1), (1, 1, 1), (2, 0, 1), (2, 1, 1))
    for copy in loads:
        copy.wait()
    normed2, inv2 = layer_stats(r.hidden_v[...])
    r.normed_v[...] = normed2
    bwd.close()
    tick((1, 0, 1), (1, 1, 1), (2, 0, 1), (2, 1, 1), (3, 0, 1), (3, 1, 1))

    mrow = pl.ds(mine, 1)
    live = live_column(pick_rows(r.pos, mine, L)[:, :block])
    d_out = r.cot_own[...].astype(F32) * live
    d_mlp_in = bwd.own_sum()
    g = d_mlp_in * (1.0 + modv[mrow, 4 * D : 5 * D])
    dh = d_out + layer_back(g, r.normed_v[...], inv2)
    r.dh_v[...] = dh
    r.d_attn[:block, :] = (modv[mrow, 2 * D : 3 * D] * dh).astype(BF16)
    gat_d.start()

    early, late_sums = r.early, r.late_sums
    early[me, 0:1, :] = jnp.sum(dh * r.res_v[...], axis=0, keepdims=True)
    load_kept.start()
    early[me, 1:2, :] = jnp.sum(d_mlp_in, axis=0, keepdims=True)
    early[me, 2:3, :] = jnp.sum(d_mlp_in * r.normed_v[...], axis=0, keepdims=True)

    def finish_out():
        fwd.close()
        live = live_column(pick_rows(r.pos, mine, L)[:, :block])
        mlp_out = fwd.own_sum() + r.bias_v[1:2, :]
        early[me, 3:4, :] = jnp.sum(mlp_out * (r.cot_own[...].astype(F32) * live), axis=0, keepdims=True)
        out_own = (r.hidden_v[...] + modv[mrow, 5 * D : 6 * D] * mlp_out) * live
        r.part_f[:block, :] = out_own.astype(BF16)

    def dm_copy(ref, k, d, slot):
        return pltpu.make_async_remote_copy(
            src_ref=ref.at[slot],
            dst_ref=ref.at[slot],
            send_sem=r.dm_send.at[k, d],
            recv_sem=r.dm_recv.at[k, d],
            device_id=(dp, flip(me, d)),
            device_id_type=MESH,
        )

    def attention_grad(c, half, at):
        if c < 3:
            full = dot(qkv[:, c * lanes : (c + 1) * lanes], d_mlp[...], 0, 0)
        else:
            full = dot(r.act[:, :lanes], r.d_attn[...], 0, 0)
        rows = [full[h * HEAD_PAD : h * HEAD_PAD + hd] for h in range(heads)]
        rows = jnp.concatenate(rows, axis=0) if heads > 1 else rows[0]
        grads[half, at : at + local, :] = rows.astype(BF16)

    for copy in late:
        copy.wait()
    factor = hd ** (-0.5)
    grid_g = r.grid_g
    grid_g[...] = jnp.zeros_like(grid_g)
    qkv, w_qkv, w_merge = r.qkv_v, r.w_qkv_v, r.w_merge_v
    def attention(slot):
        s = xor(mine, slot, sbits)
        at = pl.ds(slot * n, n)
        da = r.d_attn[at, :]
        merge_bg[...] += jnp.sum(da.astype(F32), axis=0, keepdims=True)
        d_att = dot(da, w_merge[...], 1, 1).astype(BF16)
        sel = pick_rows(r.pos, s, L)
        sel_wide = pick_rows(r.pos_wide, s, 2 * L)
        dq, dk, dv = [], [], []
        for h in range(heads):
            q = qkv[at, h * HEAD_PAD : (h + 1) * HEAD_PAD]
            k = qkv[at, lanes + h * HEAD_PAD : lanes + (h + 1) * HEAD_PAD]
            v = qkv[at, 2 * lanes + h * HEAD_PAD : 2 * lanes + (h + 1) * HEAD_PAD]
            d_a = d_att[:, h * HEAD_PAD : (h + 1) * HEAD_PAD]
            p = r.probs_v[slot, h]
            d_p = dot(d_a, v, 1, 1)
            dv.append(dot(p.astype(BF16), d_a, 0, 0).astype(BF16))
            ds = p * (d_p - jnp.sum(p * d_p, axis=-1, keepdims=True))
            dl = ds.astype(BF16)
            dq.append((dot(dl, k) * factor).astype(BF16))
            dk.append((dot(dl, q, 0, 0) * factor).astype(BF16))
            grid_g[h] += dot(dot(sel, dl).astype(BF16), sel_wide, 1, 1)
        joined = jnp.concatenate(dq + dk + dv, axis=1)
        qkv[at, :] = joined
        proj_bg[:, : 3 * lanes] += jnp.sum(joined.astype(F32), axis=0, keepdims=True)
        r.part_b[at, :] = dot(joined, w_qkv[...]).astype(BF16)

    if sz.fast:
        plan_one = {1: [(1, 0, 1), (1, 1, 1), (2, 0, 1), (2, 1, 1), (3, 0, 1), (3, 1, 1)], 2: [(3, 0, 1), (3, 1, 1)]}
        plan_two = {
            3: [(1, 1, 1), (2, 0, 1), (2, 1, 1), (3, 0, 1), (3, 1, 1)],
            4: [(1, 0, 1), (2, 0, 1), (2, 1, 1)],
            5: [(1, 0, 1), (1, 1, 1), (2, 1, 1), (3, 0, 1), (3, 1, 1)],
            6: [(1, 1, 1), (2, 0, 1), (3, 0, 1), (3, 1, 1)],
            7: [(1, 0, 1), (2, 0, 1), (2, 1, 1)],
        }

        def one(i, carry):
            q = i // 2
            pair = q + lax.rem(q, 2) * (q // 2) * -1 + (q // 2) * (1 - lax.rem(q, 2))
            slot = jnp.where(i < 2, i, 2 * pair + 1 - lax.rem(i, 2))

            ticks_at(i, plan_one)

            @pl.when(i == 1)
            def _():
                for h in range(2):
                    gat_d.near_copy(0, h).wait()

            @pl.when(i == 2)
            def _():
                gat_d.step(0)
                tick((1, 0, 1), (1, 1, 1), (2, 0, 1), (2, 1, 1))
                gat_d.step(1)
                fwd.take(1, *sz.sends[1, 0][1])
                fwd.take(0, *sz.sends[0, 0][1])
                fwd.send(1, 2)
                fwd.send(0, 4)
                tick((1, 0, 1), (1, 1, 1), (3, 0, 1), (3, 1, 1))
                for h in range(2):
                    gat_d.near_copy(2, h).wait()

            ticks_at(i, plan_two)

            @pl.when(i == 4)
            def _():
                gat_d.step(2)
                for d in (4, 6):
                    for h in range(2):
                        gat_d.near_copy(d, h).wait()

            attention(slot)

            @pl.when(i == 1)
            def _():
                last.near_copy(0).start()

            @pl.when((i > 1) & (lax.rem(i, 2) == 0))
            def _():
                last.near_copy(pair).start()

            @pl.when(i == 3)
            def _():
                last.near_add(0)
                last.near_add(1)
                last.send(0, 2)

            @pl.when(i == 6)
            def _():
                finish_out()

            @pl.when(i == 5)
            def _():
                last.near_add(3)
                last.send(0, 6)
                last.send(1, 6)

            @pl.when(i == 7)
            def _():
                last.near_add(2)
                last.after(2)

            return carry

        lax.fori_loop(0, 8, one, 0)
        tick((1, 0, 1), (1, 1, 1), (2, 1, 1), (3, 0, 1), (3, 1, 1))
    else:
        for t in range(len(gat_d.stages)):
            gat_d.step(t)
        gat_d.finish()
        finish_out()
        slot_loop(sz, attention, last)

    load_attn.wait()
    load_att.wait()
    attention_grad(3, 1, F)
    begin(2, 1)
    tick((2, 0, 1))
    attention_grad(0, 0, F)
    begin(2, 0)
    attention_grad(2, 1, F + local)
    begin(3, 1)
    attention_grad(1, 0, F + local)
    begin(3, 0)
    tick((1, 0, 1), (1, 1, 1), (2, 1, 1), (3, 0, 1), (3, 1, 1))

    tables = r.table_g
    span = tables.shape[2]
    for h in range(heads):
        strip = jnp.zeros((grid_side, span), F32)
        for row in range(grid_side):
            piece = jnp.concatenate(
                [
                    grid_g[h, row * grid_side : (row + 1) * grid_side, :],
                    jnp.zeros((grid_side, span - 2 * L), F32),
                ],
                axis=1,
            )
            strip = strip + (pltpu.roll(piece, row * 2 * grid_side, 1) if row else piece)
        total_row = strip[0:1]
        for c in range(1, grid_side):
            total_row = total_row + pltpu.roll(strip[c : c + 1], c, 1)
        tables[dp, h : h + 1, :] = total_row

    share(0)
    share(1)
    load_kept.wait()
    normed1, inv1 = layer_stats(r.res_v[...])
    r.normed_v[...] = normed1
    last.close()
    tick((1, 1, 2), (2, 0, 1), (3, 0, 1), (3, 1, 1))
    d_in = last.own_sum()
    g = d_in * (1.0 + modv[mrow, D : 2 * D])
    mlp[:block, :] = (r.dh_v[...] + layer_back(g, r.normed_v[...], inv1)).astype(BF16)
    late_sums[me, 0:1, :] = jnp.sum(d_in, axis=0, keepdims=True)
    late_sums[me, 1:2, :] = jnp.sum(d_in * r.normed_v[...], axis=0, keepdims=True)
    gat_k.start()
    tick((1, 1, 1), (2, 0, 1), (2, 1, 1))

    def out_copy(slot):
        return pltpu.make_async_copy(
            r.part_f.at[pl.ds(slot * n, n)], r.out.at[xor(mine, slot, sbits)], r.load_sem.at[0, slot]
        )

    def start_out(slot, carry):
        out_copy(slot).start()
        return carry

    def patch_copy(slot):
        return pltpu.make_async_copy(
            r.part_b.at[pl.ds(lax.rem(slot, 2) * L, L)], r.patch_g.at[xor(mine, slot, sbits)], r.load_sem.at[1, slot]
        )

    def patch(slot, carry):
        @pl.when(slot >= 2)
        def _():
            patch_copy(slot - 2).wait()

        sel = pick_rows(r.pos, xor(mine, slot, sbits), L)
        r.part_b[pl.ds(lax.rem(slot, 2) * L, L), :] = dot(sel, mlp[pl.ds(slot * n, n), :]).astype(BF16)
        patch_copy(slot).start()
        return carry

    for h in range(2):
        gat_k.near_copy(0, h).wait()
    if sz.fast:
        lax.fori_loop(0, 2, patch, 0)
    gat_k.step(0)
    for d in range(1, sz.mp):
        dm_copy(early, 0, d, me).start()
        dm_copy(late_sums, 1, d, me).start()
    gat_o.start()
    tick((1, 0, 1), (2, 1, 1), (3, 0, 1), (3, 1, 2))
    gat_k.step(1)
    tick((1, 0, 2), (1, 1, 1), (2, 0, 1), (2, 1, 2))
    if sz.fast:
        for d in (2, 4):
            for h in range(2):
                gat_k.near_copy(d, h).wait()
        lax.fori_loop(2, 4, patch, 0)
        tick((1, 1, 1), (2, 0, 1))
        lax.fori_loop(4, 6, patch, 0)
        tick((1, 1, 1))
        gat_k.step(2)
        tick((2, 1, 1), (3, 0, 1), (3, 1, 1))
        for h in range(2):
            gat_k.near_copy(6, h).wait()
        lax.fori_loop(6, 8, patch, 0)
    else:
        for t in range(2, len(gat_k.stages)):
            gat_k.step(t)
        gat_k.finish(2)
        lax.fori_loop(0, sz.samples, patch, 0)
    for d in range(1, sz.mp):
        dm_copy(early, 0, d, me).wait_send()
        dm_copy(early, 0, d, flip(me, d)).wait_recv()
        dm_copy(late_sums, 1, d, me).wait_send()
        dm_copy(late_sums, 1, d, flip(me, d)).wait_recv()
    flat, mod_g = r.flat, r.mod_g
    flat[:, 6 * D :] = jnp.zeros((sz.samples, flat.shape[1] - 6 * D), F32)
    for s in range(sz.samples):
        for c in range(6):
            v = 0
            for p in range(sz.per):
                m = s * sz.per + p
                v = v + (late_sums[m, c : c + 1, :] if c < 2 else early[m, c - 2 : c - 1, :])
            flat[s : s + 1, c * D : (c + 1) * D] = v
    base = pl.multiple_of(me * cols // 128 * 128, 128)
    mod_g[dp] = flat[:, pl.ds(base, mod_g.shape[2])]
    share(2)
    tick((1, 0, 2), (2, 0, 1), (3, 0, 1), (3, 1, 1), (1, 0, 1))
    gat_o.step(0)
    tick((2, 0, 1), (2, 1, 1), (2, 0, 1), (3, 1, 1), (3, 0, 1))
    tick((2, 0, 1), (2, 1, 1), (3, 1, 1), (3, 0, 1))
    gat_o.step(1)
    tick((3, 0, 1), (3, 1, 1), (3, 0, 1))
    for t in range(2, len(gat_o.stages)):
        gat_o.step(t)
    gat_o.finish()
    lax.fori_loop(0, sz.samples, start_out, 0)
    tick((3, 1, 1), (3, 0, 1))
    if line is not None:
        assert all(k == marks[4] for k in following.values()), following
    for k in range(4):
        for e in range(1, dp_size):
            dp_copy(k, e, dp).wait_send()
            dp_copy(k, e, lax.rem(dp + dp_size - e, dp_size)).wait_recv()
    for slot in range(sz.samples - 2, sz.samples):
        patch_copy(slot).wait()

    def wait_out(slot, carry):
        out_copy(slot).wait()
        return carry

    lax.fori_loop(0, sz.samples, wait_out, 0)
    if line is not None:
        line.finish()


def write_results(heads, hd, grid_side, cols, r):
    total = r.total
    F, local = r.up.shape[0], r.merge.shape[0]
    D = total.shape[2]
    depth = r.narrow.shape[0]
    samples = r.out.shape[0]

    def out_in(s):
        return pltpu.make_async_copy(r.out.at[s], r.out_v.at[s], r.out_sem.at[0, s])

    def out_back(s):
        return pltpu.make_async_copy(r.out_v.at[s], r.block_out.at[s], r.out_sem.at[1, s])

    jobs = []
    for s in range(samples):
        jobs.append((r.patch_g.at[s], r.patch.at[s], r.patch.shape[1]))
    rows_most = r.narrow.shape[1]

    def add(half, start, to, at, count):
        while count:
            size = min(rows_most, count)
            jobs.append((total.at[half, pl.ds(start, size)], to.at[pl.ds(at, size)], size))
            start, at, count = start + size, at + size, count - size

    stripe = stripe_of(F)
    for turn in range(F // stripe):
        add(turn % 2, turn // 2 * stripe, r.down, turn * stripe, stripe)
        add(turn % 2, F // 2 + turn // 2 * stripe, r.up, turn * stripe, stripe)
    add(0, F, r.project, 0, 2 * local)
    add(1, F + local, r.project, 2 * local, local)
    add(1, F, r.merge, 0, local)

    def load(k):
        src, _, size = jobs[k]
        return pltpu.make_async_copy(src, r.narrow.at[k % depth, pl.ds(0, size)], r.load_sem.at[k % depth])

    def save(k):
        _, dst, size = jobs[k]
        return pltpu.make_async_copy(r.wide.at[k % depth, pl.ds(0, size)], dst, r.save_sem.at[k % depth])

    for k in range(depth):
        load(k).start()
    for s in range(samples):
        out_in(s).start()

    def small_results():
        members, _, width = r.mod_g.shape
        shift = lax.rem(lax.axis_index("mp") * cols, 128)
        dmod = jnp.concatenate([r.mod_g[m] for m in range(members)], axis=0)
        dmod = pltpu.roll(dmod, lax.rem(width - shift, width), 1)
        upper = dmod.astype(BF16)
        parts = jnp.concatenate([upper, (dmod - upper.astype(F32)).astype(BF16)], axis=0)
        signal = jnp.concatenate([r.signal_g[m].astype(F32) for m in range(members)], axis=0).astype(BF16)
        r.mod_v[...] = dot(parts, jnp.concatenate([signal, signal], axis=0), 0, 0)[:cols]
        modulate = pltpu.make_async_copy(r.mod_v, r.modulate, r.sem.at[0])
        modulate.start()
        r.mod_bias[...] = jnp.sum(dmod, axis=0, keepdims=True)[:, :cols].reshape(cols)
        bias, table = r.bias_g[0], r.table_g[0]
        for m in range(1, members):
            bias, table = bias + r.bias_g[m], table + r.table_g[m]
        r.up_bias[...] = bias[0:1, :F].reshape(F)
        r.down_bias[...] = bias[1:2].reshape(D)
        r.merge_bias[...] = bias[2:3].reshape(D)
        lanes = heads * HEAD_PAD
        for k, c in enumerate((0, 2)):
            row = spread(bias[3:4, c * lanes : (c + 1) * lanes], heads, hd, hd - HEAD_PAD)
            r.proj_bias[k : k + 1, :] = row[:, : heads * hd]
        offsets = 2 * grid_side - 1
        r.table[...] = spread(table, offsets, offsets, -1)[:, : offsets * offsets]
        return modulate

    for k, (_, _, size) in enumerate(jobs):
        load(k).wait()
        if k >= depth:
            save(k - depth).wait()
        r.wide[k % depth, :size] = r.narrow[k % depth, :size].astype(F32)
        save(k).start()
        if k + depth < len(jobs):
            load(k + depth).start()
        if k < samples:
            out_in(k).wait()
            out_back(k).start()
        if k == depth:
            modulate = small_results()
    for k in range(max(0, len(jobs) - depth), len(jobs)):
        save(k).wait()
    for s in range(samples):
        out_back(s).wait()
    modulate.wait()


def body(
    patches,
    condition,
    lengths,
    keep_order,
    cotangent,
    projection_weight,
    query_value_bias,
    merge_weight,
    merge_output_bias,
    up_weight,
    up_projection_bias,
    down_weight,
    down_projection_bias,
    w_modulate,
    bias_modulate,
    bias_table,
):
    samples, L, D = patches.shape
    n = cotangent.shape[1]
    grid_side = math.isqrt(L)
    offsets = 2 * grid_side - 1
    heads = bias_table.shape[0]
    local = projection_weight.shape[2]
    hd = local // heads
    lanes = heads * HEAD_PAD
    F = up_weight.shape[1]
    cols = w_modulate.shape[1]
    mp, dp_size = lax.axis_size("mp"), lax.axis_size("dp")
    me = lax.axis_index("mp")
    sz = Sizes(mp, samples, n, D)
    rows, block = sz.rows, sz.block

    keep, counts, cot = keep_order, lengths, cotangent
    if sz.per > 1:
        ids = jnp.arange(n, dtype=jnp.int32)
        order = ((ids // block) ^ lax.rem(me, sz.per)) * block + ids % block
        keep = jnp.take(jnp.where(ids[None, :] < lengths[:, None], keep_order[:, :n], -1), order, axis=1)
        counts = jnp.full_like(lengths, n)
        cot = jnp.take(cot, order, axis=1)
    wide = -(-cols // 128) * 128 + 128
    modw = max(m * cols // 128 * 128 + wide for m in range(mp))
    dma = pltpu.SemaphoreType.DMA

    one = Call()
    one.arg(
        condition=condition,
        keep=keep,
        b_qv=query_value_bias,
        b_merge=merge_output_bias,
        b_mod=bias_modulate,
        b_table=bias_table,
        w_in=jnp.swapaxes(projection_weight, 1, 2),
        w_out=merge_weight,
    )
    one.arg(pltpu.SMEM, lengths=counts)
    one.arg(pl.ANY, patches=patches, w_mod=w_modulate.T)
    one.out(modv=((samples, 6 * D), F32), pos=((samples, n), jnp.int32), pos_wide=((samples, n), jnp.int32))
    one.out(
        pl.ANY,
        attn_in=((rows, D), BF16),
        qkv=((rows, 3 * lanes), BF16),
        probs=((samples, heads, n, n), F32),
        att=((rows, lanes), BF16),
        kept=((block, D), F32),
        res=((block, D), F32),
        hidden=((block, D), F32),
        mlp=((block, D), BF16),
        w_qkv=((3 * lanes, D), BF16),
        w_merge=((lanes, D), BF16),
    )
    one.vmem(
        attn_in_v=((rows, D), BF16),
        qkv_v=((rows, 3 * lanes), BF16),
        probs_v=((samples, heads, n, n), F32),
        att_v=((rows, lanes), BF16),
        kept_v=((block, D), F32),
        res_v=((block, D), F32),
        hidden_v=((block, D), F32),
        mlp_v=((block, D), BF16),
        w_qkv_v=((3 * lanes, D), BF16),
        w_merge_v=((lanes, D), BF16),
        w_mod_v=((cols, D), BF16),
        patches_v=((samples, L, D), BF16),
        mod_buf=((mp, samples, wide), F32),
        mod_wide=((samples, modw), F32),
        qv_wide=((2, lanes), F32),
        table_v=((heads, 4 * L), F32),
        normed=((rows, D), F32),
        bias_full=((heads, L, 2 * L), BF16),
        part=((rows, D), BF16),
    )
    one.scratch(
        mod_send=dma((mp,)),
        mod_recv=dma((mp,)),
        sem=dma((7,)),
        load_sem=dma((samples,)),
        save_sem=dma((4, samples)),
        red=reduce_scratch(sz),
    )
    first = one.run(
        functools.partial(attention_forward, sz, heads, hd, grid_side, cols), "attention_forward", 0, 62 << 20
    )

    chunk = 48 if dp_size == 4 and F % 96 == 0 and local % 48 == 0 else 0
    two = Call()
    two.arg(
        condition=condition,
        b_up=up_projection_bias,
        b_down=down_projection_bias,
        pos=first.pos,
        pos_wide=first.pos_wide,
        modv=first.modv,
    )
    two.arg(
        pl.ANY,
        cot=cot,
        w_up=up_weight.T,
        w_down=down_weight,
        mlp=first.mlp,
        hidden=first.hidden,
        res=first.res,
        kept=first.kept,
        qkv=first.qkv,
        probs=first.probs,
        att=first.att,
        w_qkv=first.w_qkv,
        w_merge=first.w_merge,
        attn_in=first.attn_in,
    )
    both = ((2, F + 2 * local, D), BF16)
    if chunk:
        count = (F + 2 * local) // chunk
        two.out(z_outer=both)
        two.vmem(grads=both, z_inner=((F + 2 * local, D), BF16))
        two.scratch(
            zs=dma((2, count)),
            zo=dma((2, count)),
            zf=dma((count,)),
            zi=dma((count,)),
            zt=dma((3, count)),
            zr=dma((2, count)),
        )
    else:
        two.out(grads=both)
    two.out(
        bias_g=((dp_size, 4, D), F32),
        table_g=((dp_size, heads, 4 * L), F32),
        signal_g=((dp_size, samples, D), BF16),
        mod_g=((dp_size, samples, wide), F32),
    )
    two.out(pl.ANY, out=((samples, n, D), BF16), patch_g=((samples, L, D), BF16))
    two.vmem(
        w_up_v=((F, D), BF16),
        w_down_v=((F, D), BF16),
        mlp_v=((rows, D), BF16),
        d_mlp=((rows, D), BF16),
        slope=((rows, F), F32),
        act=((rows, F), BF16),
        d_pre=((rows, F), BF16),
        part_f=((rows, D), BF16),
        part_b=((rows, D), BF16),
        d_attn=((rows, D), BF16),
        cot_own=((block, D), BF16),
        hidden_v=((block, D), F32),
        res_v=((block, D), F32),
        normed_v=((block, D), F32),
        dh_v=((block, D), F32),
        qkv_v=((rows, 3 * lanes), BF16),
        probs_v=((samples, heads, n, n), F32),
        w_qkv_v=((3 * lanes, D), BF16),
        w_merge_v=((lanes, D), BF16),
        grid_g=((heads, L, 2 * L), F32),
        early=((mp, 4, D), F32),
        late_sums=((mp, 2, D), F32),
        flat=((samples, modw), F32),
        bias_v=((2, D), F32),
    )
    two.scratch(
        sem=dma((13,)),
        load_sem=dma((3, samples)),
        dm_send=dma((2, mp)),
        dm_recv=dma((2, mp)),
        dp_send=dma((4, dp_size)),
        dp_recv=dma((4, dp_size)),
        red_f=reduce_scratch(sz),
        red_b=reduce_scratch(sz),
        last_sems=reduce_scratch(sz)[2:],
        gat_m=gather_scratch(sz),
        gat_d=gather_scratch(sz),
        gat_o=gather_scratch(sz),
        gat_k=gather_scratch(sz),
    )
    got = two.run(
        functools.partial(block_backward, sz, heads, hd, grid_side, cols, dp_size, chunk), "block_backward", 1, 64 << 20
    )

    total = got.z_outer if chunk else lax.psum(got.grads, "dp")
    three = Call()
    three.arg(mod_g=got.mod_g, signal_g=got.signal_g, bias_g=got.bias_g, table_g=got.table_g)
    three.arg(pl.ANY, total=total, out=got.out, patch_g=got.patch_g)
    three.out(
        mod_bias=((cols,), F32),
        up_bias=((F,), F32),
        down_bias=((D,), F32),
        merge_bias=((D,), F32),
        proj_bias=((2, local), F32),
        table=((heads, offsets * offsets), F32),
    )
    three.out(
        pl.ANY,
        block_out=((samples, n, D), BF16),
        patch=((samples, L, D), F32),
        up=((F, D), F32),
        down=((F, D), F32),
        project=((3 * local, D), F32),
        merge=((local, D), F32),
        modulate=((cols, D), F32),
    )
    depth = 8
    three.vmem(narrow=((depth, 288, D), BF16), wide=((depth, 288, D), F32), mod_v=((cols, D), F32), out_v=((samples, n, D), BF16))
    three.scratch(sem=dma((1,)), out_sem=dma((2, samples)), load_sem=dma((depth,)), save_sem=dma((depth,)))
    end = three.run(functools.partial(write_results, heads, hd, grid_side, cols), "write_results", None, 63 << 20)

    block_out = end.block_out
    if sz.per > 1:
        block_out = jnp.take(block_out, order, axis=1)
    return (
        block_out,
        end.patch,
        jnp.swapaxes(end.project.reshape(3, local, D), 1, 2),
        end.proj_bias,
        end.merge,
        end.merge_bias,
        end.up.T,
        end.up_bias,
        end.down,
        end.down_bias,
        end.modulate.T,
        end.mod_bias,
        end.table,
    )


def solution(mesh):
    placed = (
        P("dp", None, None),
        P("dp", None),
        P("dp"),
        P("dp", None),
        P("dp", None, None),
        P(None, None, "mp"),
        P(None, "mp"),
        P("mp", None),
        P(),
        P(None, "mp"),
        P("mp"),
        P("mp", None),
        P(),
        P(None, "mp"),
        P("mp"),
        P("mp", None),
    )
    return jax.shard_map(
        body,
        mesh=mesh,
        in_specs=placed,
        out_specs=(
            P("dp", None, None),
            P("dp", None, None),
            P(None, None, "mp"),
            P(None, "mp"),
            P("mp", None),
            P(),
            P(None, "mp"),
            P("mp"),
            P("mp", None),
            P(),
            P(None, "mp"),
            P("mp"),
            P("mp", None),
        ),
        check_vma=False,
    )
```
